32 devices in a mesh: rep: 8 (over z, core), fsdp: 4 (over y, x).
Axes of the slice: x: 2, y: 2, z: 4, core: 2. Of those that a mesh axis runs over, the one named last changes fastest.
Arguments:
- tokens: bfloat16 [8192, 2048], P(('rep', 'fsdp')), may hold values from -6 to 6
- teacher: bfloat16 [8192, 2048], P(('rep', 'fsdp')), may hold values from -6 to 6
- lengths: int32 [64], replicated, may hold values from 1 to 255, as said below
- deal_order: int32 [64], replicated, may hold values from 0 to 63, as said below
- attention_gain: bfloat16 [2048], P('fsdp'), may hold values from 0.5 to 1.5
- query_gain: bfloat16 [128], P('fsdp'), may hold values from 1 to 2
- key_gain: bfloat16 [128], P('fsdp'), may hold values from 1 to 2
- w_query: bfloat16 [2048, 2048], P('fsdp'), may hold values from -0.125 to 0.125
- w_key: bfloat16 [2048, 1024], P('fsdp'), may hold values from -0.125 to 0.125
- w_value: bfloat16 [2048, 1024], P('fsdp'), may hold values from -0.125 to 0.125
- w_outgate: bfloat16 [2048, 2048], P('fsdp'), may hold values from -0.125 to 0.125
- w_output: bfloat16 [2048, 2048], P('fsdp'), may hold values from -0.75 to 0.75
- mlp_gain: bfloat16 [2048], P('fsdp'), may hold values from 0.5 to 1.5
- w_gate: bfloat16 [2048, 6144], P('fsdp'), may hold values from -0.125 to 0.125
- w_up: bfloat16 [2048, 6144], P('fsdp'), may hold values from -0.125 to 0.125
- w_down: bfloat16 [6144, 2048], P('fsdp'), may hold values from -0.078125 to 0.078125
Outputs:
- block_out: bfloat16 [8192, 2048], P(('rep', 'fsdp'))
- seq_loss: float32 [64], P(('rep', 'fsdp'))
- tokens_grad: bfloat16 [8192, 2048], P(('rep', 'fsdp'))
- attention_dgain: float32 [2048], P('fsdp')
- query_dgain: float32 [128], P('fsdp')
- key_dgain: float32 [128], P('fsdp')
- dw_query: float32 [2048, 2048], P('fsdp')
- dw_key: float32 [2048, 1024], P('fsdp')
- dw_value: float32 [2048, 1024], P('fsdp')
- dw_outgate: float32 [2048, 2048], P('fsdp')
- dw_output: float32 [2048, 2048], P('fsdp')
- mlp_dgain: float32 [2048], P('fsdp')
- dw_gate: float32 [2048, 6144], P('fsdp')
- dw_up: float32 [2048, 6144], P('fsdp')
- dw_down: float32 [6144, 2048], P('fsdp')
The draws below stay inside these ranges and needn't reach their ends.
Inputs may be any that keep to these rules, and one draw needn't show every extreme that they name: `lengths`: each block of 256 rows holds 256 tokens or fewer of its two sequences together; in every draw one block holds exactly 256. `deal_order`: A permutation of the sequence numbers.
All inputs are finite; a program needn't handle non-finite values.
Results may differ from the reference program's by a relative error of at most 0.012.
The reference program's roundings to bfloat16 on the way count: a program that leaves them out, or rounds other values in their place, can miss the bound.
Values may be sent and summed in bfloat16 or wider, within the bound.
A program may use at most 512 MiB of HBM per device.

```python
import math
import jax
import jax.numpy as jnp
from jax import lax

D = 2048
H = 16
KV = 8
HD = 128
FF = 6144
CAP = 256
TOKENS = 8192
SEQS = 64


def dealt_lengths(key):
    folded = jax.random.fold_in(key, 11)
    key_total, key_chosen, key_head, key_deal = jax.random.split(folded, 4)
    devices = SEQS // 2
    totals = jax.random.randint(key_total, (devices,), CAP // 4, CAP + 1)
    chosen = jax.random.randint(key_chosen, (), 0, devices)
    marked = jnp.arange(devices) == chosen
    totals = jnp.where(marked, CAP, totals)
    head_len = jax.random.randint(key_head, (devices,), 1, totals)
    head_len = jnp.where(marked, CAP - 1, head_len)
    slot_lengths = jnp.stack([head_len, totals - head_len], axis=1).reshape(SEQS).astype(jnp.int32)
    dealing = jax.random.permutation(key_deal, SEQS).astype(jnp.int32)
    seq_lengths = jnp.zeros((SEQS,), jnp.int32).at[dealing].set(slot_lengths)
    return (seq_lengths, dealing)


def draw_lengths(key, part):
    return dealt_lengths(key)[0]


def draw_deal_order(key, part):
    return dealt_lengths(key)[1]


def with_spikes(entries, own_key, source, target, parts, factor):
    owner, partner = [(jnp.arange(entries.shape[axis_at]) // (entries.shape[axis_at] // parts)).reshape([-1 if axis == axis_at else 1 for axis in range(entries.ndim)]) for axis_at in (source, target)]
    chosen = jax.random.permutation(own_key, parts)[partner]
    strong = (owner == chosen) | (owner == (partner + parts // 2) % parts)
    return jnp.where(strong, factor * entries, entries)


def level_of(key, dims, cuts, least, top_value):
    def one(axis_at, shards_of):
        steps = jax.random.uniform(jax.random.fold_in(jax.random.fold_in(key, 6), axis_at), (shards_of,), jnp.float32, least / len(cuts), top_value / len(cuts))
        return jnp.repeat(jnp.exp(steps), dims[axis_at] // shards_of).reshape((-1,) + (1,) * (len(dims) - axis_at - 1))

    gain = one(*cuts[0])
    for cut in cuts[1:]:
        gain = gain * one(*cut)
    return gain


def bell_draw(stream_key, shape, deviation, limit, cuts=(), kind=jnp.bfloat16):
    array = jax.random.normal(stream_key, shape, jnp.float32) * deviation
    if len(cuts) > 0:
        array = level_of(stream_key, shape, cuts, -0.22, 0.18) * array
    return jnp.clip(array, min=-limit, max=limit).astype(kind)


def bell_draw_with(stream_key, dims, width, limit, cuts, heavy, kind=jnp.bfloat16):
    values = width * jax.random.normal(stream_key, dims, jnp.float32)
    if cuts:
        values = values * level_of(stream_key, dims, cuts, -0.22, 0.18)
    return jnp.clip(with_spikes(values, jax.random.fold_in(stream_key, 3), *heavy), -limit, limit).astype(kind)


def setup_inputs(seed: int = 0) -> dict:
    key_list = jax.random.split(jax.random.key(seed), 17)
    tokens = bell_draw_with(key_list[0], (TOKENS, D), 1.0, 6.0, ((0, 32),), (0, 1, 32, 2.75))
    teacher = bell_draw(key_list[1], (TOKENS, D), 1.0, 6.0, ((0, 32),))
    lengths = draw_lengths(jax.random.fold_in(key_list[16], 71), 0)
    deal_order = draw_deal_order(jax.random.fold_in(key_list[16], 71), 0)
    attention_gain = jnp.clip(1.0 + 0.1 * jax.random.normal(key_list[4], (D,), jnp.float32), 0.5, 1.5).astype(jnp.bfloat16)
    query_gain = jnp.clip(jnp.exp(math.log(2.0) - 0.6931472 * jax.random.uniform(key_list[5], (HD,), jnp.float32) ** level_of(key_list[5], (HD,), ((0, 4),), -0.2, 0.2)), 1.0, 2.0).astype(jnp.bfloat16)
    key_gain = jnp.clip(jnp.exp(math.log(2.0) - 0.6931472 * jax.random.uniform(key_list[6], (HD,), jnp.float32) ** level_of(key_list[6], (HD,), ((0, 4),), -0.2, 0.2)), 1.0, 2.0).astype(jnp.bfloat16)
    w_query = bell_draw(key_list[7], (D, H * HD), D ** -0.5, 0.125, ((0, 4),))
    w_key = bell_draw(key_list[8], (D, KV * HD), D ** -0.5, 0.125, ((0, 4),))
    w_value = bell_draw(key_list[9], (D, KV * HD), D ** -0.5, 0.125, ((0, 4),))
    w_outgate = bell_draw(key_list[10], (D, H * HD), D ** -0.5, 0.125, ((0, 4),))
    w_output = bell_draw(key_list[11], (H * HD, D), (HD // 2) ** -0.5, 0.75, ((0, 4),))
    mlp_gain = jnp.clip(1.0 + 0.1 * jax.random.normal(key_list[12], (D,), jnp.float32), 0.5, 1.5).astype(jnp.bfloat16)
    w_gate = bell_draw(key_list[13], (D, FF), D ** -0.5, 0.125, ((0, 4),))
    w_up = bell_draw(key_list[14], (D, FF), D ** -0.5, 0.125, ((0, 4),))
    w_down = bell_draw(key_list[15], (FF, D), FF ** -0.5, 0.078125, ((0, 4),))
    return dict(tokens=tokens, teacher=teacher, lengths=lengths, deal_order=deal_order, attention_gain=attention_gain, query_gain=query_gain, key_gain=key_gain, w_query=w_query, w_key=w_key, w_value=w_value, w_outgate=w_outgate, w_output=w_output, mlp_gain=mlp_gain, w_gate=w_gate, w_up=w_up, w_down=w_down)


EPS_NORM = 1e-06
ROPE_BASE = 1000000.0
NEG_FILL = -1e+30
PRECISE = lax.Precision.HIGHEST

@jax.custom_vjp
def low(v):
    return lax.optimization_barrier(v.astype(jnp.bfloat16)).astype(jnp.float32)

@jax.custom_vjp
def low_back(v):
    return v

def low_keep(v):
    return (low(v), None)

def low_pass(kept, grad):
    return (grad,)

def back_keep(v):
    return (v, None)

def back_low(kept, grad):
    return (low(grad),)
low.defvjp(low_keep, low_pass)
low_back.defvjp(back_keep, back_low)

def rms_scale(values, gain_vec):
    return values * lax.rsqrt(lax.optimization_barrier(jnp.mean(values * values, axis=-1, keepdims=True)) + EPS_NORM) * gain_vec

def rotate(values, angle_cos, angle_sin):
    half_dim = values.shape[-1] // 2
    turned = jnp.concatenate([-values[..., half_dim:], values[..., :half_dim]], axis=-1)
    return values * angle_cos + turned * angle_sin

def row_layout(pair_len, row_count, head_dim):
    row_index = jnp.arange(row_count, dtype=jnp.int32)
    head_len = pair_len[0]
    both_len = pair_len[0] + pair_len[1]
    segment = (row_index >= head_len).astype(jnp.int32) + (row_index >= both_len).astype(jnp.int32)
    start_row = jnp.where(segment == 0, 0, jnp.where(segment == 1, head_len, both_len))
    position = (row_index - start_row).astype(jnp.float32)
    inv_freq = jnp.power(ROPE_BASE, -jnp.arange(0, head_dim, 2, dtype=jnp.float32) / head_dim)
    angles = position[:, None] * inv_freq[None, :]
    angles = jnp.concatenate([angles, angles], axis=-1)
    return (row_index, segment, jnp.cos(angles), jnp.sin(angles))

def device_block(tokens_block, teacher_block, pair_len, weight_set):
    attention_gain, query_gain, key_gain, w_query, w_key, w_value, w_outgate, w_output, mlp_gain, w_gate, w_up, w_down = weight_set
    row_count = tokens_block.shape[0]
    row_index, segment, angle_cos, angle_sin = row_layout(pair_len, row_count, HD)
    allowed = (segment[:, None] == segment[None, :]) & (row_index[None, :] <= row_index[:, None])
    normed = low(rms_scale(tokens_block, attention_gain))
    query_raw = low_back(jnp.dot(normed, w_query, precision=PRECISE))
    key_raw = low_back(jnp.dot(normed, w_key, precision=PRECISE))
    value_raw = low_back(jnp.dot(normed, w_value, precision=PRECISE))
    gate_raw = low_back(jnp.dot(normed, w_outgate, precision=PRECISE))
    queries = rms_scale(query_raw.reshape(row_count, KV, H // KV, HD), query_gain)
    queries = low(rotate(queries, angle_cos[:, None, None, :], angle_sin[:, None, None, :]))
    key_rot = rms_scale(key_raw.reshape(row_count, KV, HD), key_gain)
    key_rot = low(rotate(key_rot, angle_cos[:, None, :], angle_sin[:, None, :]))
    values = low(value_raw).reshape(row_count, KV, HD)
    scores = low_back(jnp.einsum('qkgd,pkd->kgqp', queries, key_rot, precision=PRECISE) * HD ** (-0.5))
    scores = jnp.where(allowed, scores, NEG_FILL)
    attn_probs = low(jax.nn.softmax(scores, axis=-1))
    context = low_back(jnp.einsum('kgqp,pkd->qkgd', attn_probs, values, precision=PRECISE))
    gate_heads = gate_raw.reshape(row_count, KV, H // KV, HD)
    gated_out = low((context * jax.nn.sigmoid(gate_heads)).reshape(row_count, H * HD))
    middle = tokens_block + low_back(jnp.dot(gated_out, w_output, precision=PRECISE))
    normed_mlp = low(rms_scale(middle, mlp_gain))
    gate_pre = low_back(jnp.dot(normed_mlp, w_gate, precision=PRECISE))
    up_pre = low_back(jnp.dot(normed_mlp, w_up, precision=PRECISE))
    hidden = low(jax.nn.silu(gate_pre) * up_pre)
    result = middle + low_back(jnp.dot(hidden, w_down, precision=PRECISE))
    valid_row = (segment < 2).astype(jnp.float32)
    error_rows = (result - teacher_block) * valid_row[:, None]
    return (result, lax.optimization_barrier(jnp.sum(error_rows * error_rows, axis=-1)))

def reference(tokens, teacher, lengths, deal_order, attention_gain, query_gain, key_gain, w_query, w_key, w_value, w_outgate, w_output, mlp_gain, w_gate, w_up, w_down):
    devices = TOKENS // CAP
    weight_set = tuple((weight.astype(jnp.float32) for weight in (attention_gain, query_gain, key_gain, w_query, w_key, w_value, w_outgate, w_output, mlp_gain, w_gate, w_up, w_down)))
    pair_rows = lengths[deal_order].reshape(devices, 2)
    token_count = jnp.sum(lengths).astype(jnp.float32)
    group_size = math.gcd(devices, max(1, 4096 // CAP))
    step_count = devices // group_size
    tokens_grouped = tokens.astype(jnp.float32).reshape(step_count, group_size, CAP, D)
    teacher_grouped = teacher.astype(jnp.float32).reshape(step_count, group_size, CAP, D)
    pairs_grouped = pair_rows.reshape(step_count, group_size, 2)

    def scaled_loss(tokens_in, weights_in):

        def one_step(loss_sum, inputs):
            tokens_part, teacher_part, pairs_part = inputs
            result, row_sq = jax.vmap(device_block, in_axes=(0, 0, 0, None))(tokens_part, teacher_part, pairs_part, weights_in)
            return (loss_sum + jnp.sum(row_sq), (result, row_sq))
        loss_sum, kept_rows = lax.scan(jax.checkpoint(one_step), jnp.zeros((), jnp.float32), (tokens_in, teacher_grouped, pairs_grouped))
        return (loss_sum * (TOKENS / (2.0 * token_count)), kept_rows)
    scaled, backward_fn, kept_rows = jax.vjp(scaled_loss, tokens_grouped, weight_set, has_aux=True)
    results, row_sqs = kept_rows
    grad_tokens, grad_weights = backward_fn(jnp.ones_like(scaled))
    row_index = jnp.arange(CAP, dtype=jnp.int32)
    head_rows = (row_index[None, :] < pair_rows[:, 0:1]).astype(jnp.float32)
    valid_rows = (row_index[None, :] < pair_rows[:, 0:1] + pair_rows[:, 1:2]).astype(jnp.float32)
    row_sq = row_sqs.reshape(devices, CAP)
    seq_loss = jnp.stack([lax.optimization_barrier(jnp.sum(row_sq * head_rows, axis=1)), lax.optimization_barrier(jnp.sum(row_sq * (valid_rows - head_rows), axis=1))], axis=1).reshape(SEQS)
    seq_loss = seq_loss / (2.0 * token_count)
    block_out = (results.reshape(devices, CAP, D) * valid_rows[:, :, None]).reshape(TOKENS, D).astype(jnp.bfloat16)
    tokens_grad = grad_tokens.reshape(TOKENS, D).astype(jnp.bfloat16)
    return (block_out, seq_loss, tokens_grad, grad_weights[0], grad_weights[1], grad_weights[2], grad_weights[3], grad_weights[4], grad_weights[5], grad_weights[6], grad_weights[7], grad_weights[8], grad_weights[9], grad_weights[10], grad_weights[11])
```

```python
import jax
import jax.numpy as jnp
from jax import lax
from jax.sharding import PartitionSpec as P

H = 16
KV = 8
HD = 128


EPS_NORM = 1e-06
ROPE_BASE = 1000000.0
NEG_FILL = -1e30


def rms_scale(values, gain_vec):
    return (
        values * lax.rsqrt(jnp.mean(values * values, axis=-1, keepdims=True) + EPS_NORM) * gain_vec
    )


def rotate(values, angle_cos, angle_sin):
    half_dim = values.shape[-1] // 2
    turned = jnp.concatenate([-values[..., half_dim:], values[..., :half_dim]], axis=-1)
    return values * angle_cos + turned * angle_sin


def row_layout(pair_len, row_count, head_dim):
    row_index = jnp.arange(row_count, dtype=jnp.int32)[None, :]
    head_len = pair_len[:, :1]
    both_len = pair_len[:, :1] + pair_len[:, 1:]
    segment = (row_index >= head_len).astype(jnp.int32) + (row_index >= both_len).astype(jnp.int32)
    start_row = jnp.where(segment == 0, 0, jnp.where(segment == 1, head_len, both_len))
    position = (row_index - start_row).astype(jnp.float32)
    inv_freq = jnp.power(ROPE_BASE, -jnp.arange(0, head_dim, 2, dtype=jnp.float32) / head_dim)
    angles = position[..., None] * inv_freq
    angle_cos, angle_sin = jnp.cos(angles), jnp.sin(angles)
    return (
        segment,
        jnp.concatenate([angle_cos, angle_cos], axis=-1),
        jnp.concatenate([angle_sin, angle_sin], axis=-1),
    )


def times(left_side, right_side, out=jnp.float32):
    return jnp.dot(left_side, right_side, preferred_element_type=jnp.float32).astype(out)


def times_trans(left_side, right_side, out=jnp.float32):
    return lax.dot_general(
        left_side, right_side, (((1,), (1,)), ((), ())), preferred_element_type=jnp.float32
    ).astype(out)


def trans_times(left_side, right_side, out=jnp.float32):
    return lax.dot_general(
        left_side, right_side, (((0,), (0,)), ((), ())), preferred_element_type=jnp.float32
    ).astype(out)


def gating(context, gate_heads):
    return context * jax.nn.sigmoid(gate_heads)


def swiglu(gate_pre, up_pre):
    return jax.nn.silu(gate_pre) * up_pre


def in_f32(values):
    return values.astype(jnp.float32)


def in_bf16(values):
    return values.astype(jnp.bfloat16)


def shift(values, step):
    n_fsdp = lax.axis_size("fsdp")
    return lax.ppermute(values, "fsdp", [(i, i ^ step) for i in range(n_fsdp)])


def sibling(values):
    n_rep = lax.axis_size("rep")
    return lax.ppermute(values, "rep", [(i, i ^ 1) for i in range(n_rep)])


def along_line(values, hops):
    return lax.ppermute(
        values, "rep", [(2 * a + core, 2 * b + core) for a, b in hops for core in range(2)]
    )


def line_sum(values):
    n_line = lax.axis_size("rep") // 2
    place = lax.axis_index("rep") // 2
    if n_line == 1:
        return in_bf16(values)
    half = n_line // 2
    total = in_bf16(values)
    for k in range(half - 1):
        got = along_line(total, [(k, k + 1), (n_line - 1 - k, n_line - 2 - k)])
        total = in_bf16(in_f32(total) + in_f32(got))
    got = along_line(total, [(half - 1, half), (half, half - 1)])
    total = in_bf16(in_f32(total) + in_f32(got))
    for k in range(half - 1, 0, -1):
        got = along_line(total, [(k, k - 1), (n_line - 1 - k, n_line - k)])
        total = jnp.where((place == k - 1) | (place == n_line - k), got, total)
    return total


def gather_rows(block):
    n_fsdp = lax.axis_size("fsdp")
    if n_fsdp != 4:
        return [block] + [shift(block, s) for s in range(1, n_fsdp)]
    half = block.shape[0] // 2
    top, low = block[:half], block[half:]
    x_top, y_low = shift(top, 1), shift(low, 2)
    x_low, y_top = shift(low, 1), shift(top, 2)
    d_top, d_low = shift(x_top, 2), shift(y_low, 1)
    return [
        block,
        jnp.concatenate([x_top, x_low]),
        jnp.concatenate([y_top, y_low]),
        jnp.concatenate([d_top, d_low]),
    ]


def scatter_rows(own, parts):
    n_fsdp = lax.axis_size("fsdp")
    if n_fsdp != 4:
        for s in range(1, n_fsdp):
            own = own + in_f32(shift(parts[s - 1], s))
        return own
    half = own.shape[0] // 2
    p_x, p_y, p_d = parts
    r_y = shift(p_d[:half], 1)
    r_x = shift(p_d[half:], 2)
    x_top = shift(p_x[:half], 1)
    y_low = shift(p_y[half:], 2)
    y_top = shift(in_bf16(in_f32(p_y[:half]) + in_f32(r_y)), 2)
    x_low = shift(in_bf16(in_f32(p_x[half:]) + in_f32(r_x)), 1)
    return own + jnp.concatenate(
        [in_f32(x_top) + in_f32(y_top), in_f32(y_low) + in_f32(x_low)]
    )


def shards(
    tokens,
    teacher,
    lengths,
    deal_order,
    attention_gain,
    query_gain,
    key_gain,
    w_query,
    w_key,
    w_value,
    w_outgate,
    w_output,
    mlp_gain,
    w_gate,
    w_up,
    w_down,
):
    n_rep = lax.axis_size("rep")
    n_fsdp = lax.axis_size("fsdp")
    rows, width = tokens.shape
    mine = lax.axis_index("fsdp")
    core = lax.axis_index("rep") % 2
    others = range(1, n_fsdp)
    heads_q, heads_k = H // n_fsdp, KV // n_fsdp
    cols_q, cols_k = heads_q * HD, heads_k * HD
    deep = w_query.shape[0]
    ff = w_down.shape[0]
    rows_all = rows * n_fsdp

    peers = mine ^ jnp.arange(n_fsdp, dtype=jnp.int32)
    devices = lax.axis_index("rep") * n_fsdp + peers
    slot_ids = (devices[:, None] * 2 + jnp.arange(2, dtype=jnp.int32)[None, :]).reshape(-1)
    seq_ids = jnp.arange(lengths.shape[0], dtype=jnp.int32)
    slot_seq = jnp.sum(
        jnp.where(seq_ids[None, :] == slot_ids[:, None], deal_order[None, :], 0), axis=1
    )
    pair_len = jnp.sum(
        jnp.where(seq_ids[None, :] == slot_seq[:, None], lengths[None, :], 0), axis=1
    ).reshape(n_fsdp, 2)
    token_count = jnp.sum(lengths).astype(jnp.float32)
    factor = rows * n_rep * n_fsdp / (2.0 * token_count)
    segments, angle_cos, angle_sin = row_layout(pair_len, rows, HD)
    row_index = jnp.arange(rows, dtype=jnp.int32)
    allowed = (segments[:, :, None] == segments[:, None, :]) & (
        row_index[None, None, :] <= row_index[None, :, None]
    )
    allowed = allowed[:, None, None]
    segment = segments[0]
    valid_row = (segment < 2).astype(jnp.float32)
    score_scale = HD ** (-0.5)

    def column_parts(weights, widths):
        def pick(start_of):
            return jnp.concatenate(
                [
                    lax.dynamic_slice(w, (0, start_of * cols), (deep, cols))
                    for w, cols in zip(weights, widths)
                ],
                axis=1,
            )

        return pick

    def by_columns(weights, widths):
        pick = column_parts(weights, widths)
        half = deep // 2
        cols = sum(widths)
        whole = jnp.zeros((n_fsdp * deep, cols), jnp.bfloat16)
        whole = lax.dynamic_update_slice(whole, pick(mine), (mine * deep, 0))
        for s in others:
            piece = lax.dynamic_slice(pick(mine ^ s), (core * half, 0), (half, cols))
            got = shift(piece, s)
            rest = sibling(got)
            start = (mine ^ s) * deep
            whole = lax.dynamic_update_slice(whole, got, (start + core * half, 0))
            whole = lax.dynamic_update_slice(whole, rest, (start + (1 - core) * half, 0))
        return whole

    gains_own = jnp.concatenate([attention_gain, mlp_gain, query_gain, key_gain])[None]
    gains = jnp.concatenate([gains_own] + [shift(gains_own, s) for s in others], axis=0)
    gains = in_f32(jnp.take(gains, mine ^ jnp.arange(n_fsdp), axis=0))
    small = query_gain.shape[0]
    attention_gain_f = gains[:, :deep].reshape(-1)
    mlp_gain_f = gains[:, deep : 2 * deep].reshape(-1)
    query_gain_f = gains[:, 2 * deep : 2 * deep + small].reshape(-1)
    key_gain_f = gains[:, 2 * deep + small :].reshape(-1)

    tokens_all = jnp.concatenate(gather_rows(tokens))
    w_attn = by_columns((w_query, w_key, w_outgate, w_value), (cols_q, cols_k, cols_q, cols_k))
    w_mlp = by_columns((w_gate, w_up), (ff, ff))

    tokens_f = in_f32(tokens)
    normed_all = in_bf16(rms_scale(in_f32(tokens_all), attention_gain_f))
    attn_raw = times(normed_all, w_attn)
    query_raw = attn_raw[:, :cols_q]
    key_raw = attn_raw[:, cols_q : cols_q + cols_k]
    gate_raw = attn_raw[:, cols_q + cols_k : 2 * cols_q + cols_k]
    value_b = in_bf16(attn_raw[:, 2 * cols_q + cols_k :]).reshape(n_fsdp, rows, heads_k, HD)

    def prepare_heads(query_in, key_in, query_scale, key_scale):
        query_heads = rms_scale(query_in.reshape(n_fsdp, rows, heads_q, HD), query_scale)
        query_heads = rotate(query_heads, angle_cos[:, :, None], angle_sin[:, :, None])
        key_heads = rms_scale(key_in.reshape(n_fsdp, rows, heads_k, HD), key_scale)
        key_heads = rotate(key_heads, angle_cos[:, :, None], angle_sin[:, :, None])
        return (query_heads, key_heads)

    head_pair, heads_back = jax.vjp(prepare_heads, query_raw, key_raw, query_gain_f, key_gain_f)
    queries_b = in_bf16(head_pair[0]).reshape(n_fsdp, rows, heads_k, H // KV, HD)
    keys_b = in_bf16(head_pair[1])

    def dots(spec, left, right):
        return jnp.einsum(spec, left, right, preferred_element_type=jnp.float32)

    scores = dots("sqkgd,spkd->skgqp", queries_b, keys_b) * score_scale
    scores = jnp.where(allowed, scores, NEG_FILL)
    row_top = jnp.max(scores, axis=-1, keepdims=True)
    exponent = jnp.exp(scores - row_top)
    row_total = jnp.sum(exponent, axis=-1, keepdims=True)
    probs_b = in_bf16(exponent / row_total)
    log_total = row_top + jnp.log(row_total)
    context = dots("skgqp,spkd->sqkgd", probs_b, value_b)
    gate_heads = gate_raw.reshape(n_fsdp, rows, heads_k, H // KV, HD)
    gated_out, gating_back = jax.vjp(gating, context, gate_heads)
    gated_b = in_bf16(gated_out.reshape(rows_all, cols_q))

    def summed(left, right, product):
        own = product(left[:rows], right, jnp.float32)
        parts = product(left[rows:], right, jnp.bfloat16)
        return scatter_rows(own, [parts[i * rows : (i + 1) * rows] for i in range(n_fsdp - 1)])

    middle = tokens_f + summed(gated_b, w_output, times)
    normed_mlp, mlp_norm_back = jax.vjp(rms_scale, middle, mlp_gain_f)
    normed_mlp_all = jnp.concatenate(gather_rows(in_bf16(normed_mlp)))
    gate_pre = times(normed_mlp_all, w_mlp[:, :ff])
    up_pre = times(normed_mlp_all, w_mlp[:, ff:])
    hidden, swiglu_back = jax.vjp(swiglu, gate_pre, up_pre)
    hidden_b = in_bf16(hidden)
    result = middle + summed(hidden_b, w_down, times)

    error_rows = (result - in_f32(teacher)) * valid_row[:, None]
    row_sq = jnp.sum(error_rows * error_rows, axis=-1)
    slot_mask = (segment[:, None] == jnp.arange(2, dtype=jnp.int32)[None, :]).astype(jnp.float32)
    seq_loss = jnp.sum(row_sq[:, None] * slot_mask, axis=0) / (2.0 * token_count)
    block_out = in_bf16(result * valid_row[:, None])
    grad_result = 2.0 * factor * error_rows

    def row_sharded(left, right):
        half = left.shape[1] // 2
        keep = trans_times(lax.dynamic_slice_in_dim(left, core * half, half, 1), right)
        send = trans_times(
            lax.dynamic_slice_in_dim(left, (1 - core) * half, half, 1), right, jnp.bfloat16
        )
        total = line_sum(keep + in_f32(sibling(send)))
        rest = sibling(total)
        first = jnp.where(core == 0, total, rest)
        second = jnp.where(core == 0, rest, total)
        return in_f32(jnp.concatenate([first, second], axis=0))

    def column_sharded(left, first, second, pieces):
        cols = first.shape[1] // pieces
        mine_side = jnp.where(core == 0, first, second)
        other_side = jnp.where(core == 0, second, first)
        totals = []
        for i in range(pieces):
            cut = slice(i * cols, (i + 1) * cols)
            keep = trans_times(left, mine_side[:, cut])
            send = trans_times(left, other_side[:, cut], jnp.bfloat16)
            totals.append(line_sum(keep + in_f32(sibling(send))))
        out = []
        for total in totals:
            got = [lax.dynamic_slice_in_dim(total, mine * deep, deep, 0)]
            for s in others:
                got.append(shift(lax.dynamic_slice_in_dim(total, (mine ^ s) * deep, deep, 0), s))
            out.append([(piece, sibling(piece)) for piece in got])
        return out

    def placed(pairs, which, starts, cols_of, cols):
        whole = jnp.zeros((deep, cols), jnp.float32)
        for piece_pairs, start, cut in zip(pairs, starts, cols_of):
            for s, (own, other) in enumerate(piece_pairs):
                chunk = in_f32(jnp.where(core == which, own, other)[:, cut])
                whole = lax.dynamic_update_slice(
                    whole, chunk, (0, (mine ^ s) * (cols // n_fsdp) + start)
                )
        return whole

    grad_branch_all = jnp.concatenate(gather_rows(in_bf16(grad_result)))
    dw_down = row_sharded(hidden_b, grad_branch_all)
    grad_hidden = times_trans(grad_branch_all, w_down)
    grad_gate_pre, grad_up_pre = swiglu_back(grad_hidden)
    grad_gate_b = in_bf16(grad_gate_pre)
    grad_up_b = in_bf16(grad_up_pre)
    grad_mlp_b = jnp.concatenate([grad_gate_b, grad_up_b], axis=1)
    grad_normed_mlp = summed(grad_mlp_b, w_mlp, times_trans)
    mlp_pieces = 2
    mlp_pairs = column_sharded(normed_mlp_all, grad_gate_b, grad_up_b, mlp_pieces)
    starts = [i * (ff // mlp_pieces) for i in range(mlp_pieces)]
    cuts = [slice(None)] * mlp_pieces
    dw_gate = placed(mlp_pairs, 0, starts, cuts, w_gate.shape[1])
    dw_up = placed(mlp_pairs, 1, starts, cuts, w_up.shape[1])
    grad_middle_norm, grad_mlp_gain = mlp_norm_back(grad_normed_mlp)
    grad_middle = grad_result + grad_middle_norm

    grad_attn_all = jnp.concatenate(gather_rows(in_bf16(grad_middle)))
    dw_output = row_sharded(gated_b, grad_attn_all)
    grad_gated = times_trans(grad_attn_all, w_output).reshape(
        n_fsdp, rows, heads_k, H // KV, HD
    )
    grad_context, grad_gate_heads = gating_back(grad_gated)
    grad_context_b = in_bf16(grad_context)
    grad_outgate_b = in_bf16(grad_gate_heads.reshape(rows_all, cols_q))
    scores_again = dots("sqkgd,spkd->skgqp", queries_b, keys_b) * score_scale
    probs_again = jnp.where(allowed, jnp.exp(scores_again - log_total), 0.0)
    grad_value = dots("skgqp,sqkgd->spkd", in_bf16(probs_again), grad_context_b)
    grad_probs = dots("sqkgd,spkd->skgqp", grad_context_b, value_b)
    grad_scores = probs_again * (
        grad_probs - jnp.sum(probs_again * grad_probs, axis=-1, keepdims=True)
    )
    grad_scores_b = in_bf16(grad_scores)
    grad_queries = dots("skgqp,spkd->sqkgd", grad_scores_b, keys_b) * score_scale
    grad_keys = dots("skgqp,sqkgd->spkd", grad_scores_b, queries_b) * score_scale
    grad_query_raw, grad_key_raw, grad_query_gain, grad_key_gain = heads_back(
        (grad_queries.reshape(n_fsdp, rows, heads_q, HD), grad_keys)
    )
    grad_query_b = in_bf16(grad_query_raw)
    grad_key_b = in_bf16(grad_key_raw)
    grad_value_b = in_bf16(grad_value.reshape(rows_all, cols_k))
    first = jnp.concatenate([grad_query_b, grad_key_b], axis=1)
    second = jnp.concatenate([grad_outgate_b, grad_value_b], axis=1)
    attn_pairs = column_sharded(normed_all, first, second, 1)
    query_cut, key_cut = slice(0, cols_q), slice(cols_q, None)
    dw_query = placed(attn_pairs, 0, [0], [query_cut], w_query.shape[1])
    dw_key = placed(attn_pairs, 0, [0], [key_cut], w_key.shape[1])
    dw_outgate = placed(attn_pairs, 1, [0], [query_cut], w_outgate.shape[1])
    dw_value = placed(attn_pairs, 1, [0], [key_cut], w_value.shape[1])
    grad_normed = summed(jnp.concatenate([first, second], axis=1), w_attn, times_trans)
    _, norm_back = jax.vjp(rms_scale, tokens_f, attention_gain_f)
    grad_tokens_norm, grad_attention_gain = norm_back(grad_normed)
    tokens_grad = in_bf16(grad_middle + grad_tokens_norm)

    dgains = lax.psum(
        jnp.concatenate([grad_attention_gain, grad_mlp_gain, grad_query_gain, grad_key_gain]),
        ("rep", "fsdp"),
    )

    def own_part(start, cols):
        return lax.dynamic_slice(dgains, (start + mine * cols,), (cols,))

    return (
        block_out,
        seq_loss,
        tokens_grad,
        own_part(0, deep),
        own_part(2 * width, small),
        own_part(2 * width + HD, small),
        dw_query,
        dw_key,
        dw_value,
        dw_outgate,
        dw_output,
        own_part(width, deep),
        dw_gate,
        dw_up,
        dw_down,
    )


def solution(mesh):
    return jax.shard_map(
        shards,
        mesh=mesh,
        in_specs=(
            P(("rep", "fsdp"), None),
            P(("rep", "fsdp"), None),
            P(),
            P(),
            P("fsdp"),
            P("fsdp"),
            P("fsdp"),
            P("fsdp", None),
            P("fsdp", None),
            P("fsdp", None),
            P("fsdp", None),
            P("fsdp", None),
            P("fsdp"),
            P("fsdp", None),
            P("fsdp", None),
            P("fsdp", None),
        ),
        out_specs=(
            P(("rep", "fsdp"), None),
            P(("rep", "fsdp")),
            P(("rep", "fsdp"), None),
            P("fsdp"),
            P("fsdp"),
            P("fsdp"),
            P("fsdp", None),
            P("fsdp", None),
            P("fsdp", None),
            P("fsdp", None),
            P("fsdp", None),
            P("fsdp"),
            P("fsdp", None),
            P("fsdp", None),
            P("fsdp", None),
        ),
        check_vma=False,
    )
```

```python
import functools

import jax
import jax.numpy as jnp
from jax import lax
from jax.experimental import pallas as pl
from jax.experimental.pallas import tpu as pltpu
from jax.sharding import PartitionSpec as P

MESH = pl.DeviceIdType.MESH

H = 16
KV = 8
HD = 128


EPS_NORM = 1e-06
ROPE_BASE = 1000000.0
NEG_FILL = -1e30


def rms_scale(values, gain_vec):
    return (
        values * lax.rsqrt(jnp.mean(values * values, axis=-1, keepdims=True) + EPS_NORM) * gain_vec
    )


def rotate(values, angle_cos, angle_sin):
    half_dim = values.shape[-1] // 2
    turned = jnp.concatenate([-values[..., half_dim:], values[..., :half_dim]], axis=-1)
    return values * angle_cos + turned * angle_sin


def row_layout(pair_len, row_count, head_dim):
    row_index = jnp.arange(row_count, dtype=jnp.int32)[None, :]
    head_len = pair_len[:, :1]
    both_len = pair_len[:, :1] + pair_len[:, 1:]
    segment = (row_index >= head_len).astype(jnp.int32) + (row_index >= both_len).astype(jnp.int32)
    start_row = jnp.where(segment == 0, 0, jnp.where(segment == 1, head_len, both_len))
    position = (row_index - start_row).astype(jnp.float32)
    inv_freq = jnp.power(ROPE_BASE, -jnp.arange(0, head_dim, 2, dtype=jnp.float32) / head_dim)
    angles = position[..., None] * inv_freq
    angle_cos, angle_sin = jnp.cos(angles), jnp.sin(angles)
    return (
        segment,
        jnp.concatenate([angle_cos, angle_cos], axis=-1),
        jnp.concatenate([angle_sin, angle_sin], axis=-1),
    )


def times(left_side, right_side, out=jnp.float32):
    return jnp.dot(left_side, right_side, preferred_element_type=jnp.float32).astype(out)


def times_trans(left_side, right_side, out=jnp.float32):
    return lax.dot_general(
        left_side, right_side, (((1,), (1,)), ((), ())), preferred_element_type=jnp.float32
    ).astype(out)


def trans_times(left_side, right_side, out=jnp.float32):
    return lax.dot_general(
        left_side, right_side, (((0,), (0,)), ((), ())), preferred_element_type=jnp.float32
    ).astype(out)


def gating(context, gate_heads):
    return context * jax.nn.sigmoid(gate_heads)


def swiglu(gate_pre, up_pre):
    return jax.nn.silu(gate_pre) * up_pre


def in_f32(values):
    return values.astype(jnp.float32)


def in_bf16(values):
    return values.astype(jnp.bfloat16)


def shift(values, step):
    n_fsdp = lax.axis_size("fsdp")
    return lax.ppermute(values, "fsdp", [(i, i ^ step) for i in range(n_fsdp)])


def sibling(values):
    n_rep = lax.axis_size("rep")
    return lax.ppermute(values, "rep", [(i, i ^ 1) for i in range(n_rep)])


def sum_everywhere(values):
    for axis in ("fsdp", "rep"):
        n = lax.axis_size(axis)
        step = 1
        while step < n:
            values = values + lax.ppermute(values, axis, [(i, i ^ step) for i in range(n)])
            step *= 2
    return values


def flipped(index, step, n):
    out, bit = index, 1
    while bit < n:
        has = (step // bit) % 2
        out = out + has * bit * (1 - 2 * ((index // bit) % 2))
        bit *= 2
    return out


def at_least(value, bound, span):
    span = max(span, bound)
    return (value + (span - bound)) // span


class Unit:
    def __init__(self, base, by_owner, row_blocks, col_blocks):
        self.base, self.by_owner = base, by_owner
        self.row_blocks, self.col_blocks = row_blocks, col_blocks
        self.count = row_blocks * col_blocks


LAG_B, LAG_C, LAG_D, LAG_E, LAG_G = 2, 4, 6, 8, 11
RING = 4


def reduce_kernel(
    n_fsdp, n_rep, units, piece_rows, piece_cols, *refs
):
    lefts, rights = refs[: len(units)], refs[len(units) : 2 * len(units)]
    out = refs[2 * len(units)]
    (lm, lo, rh, sb, kb, r1, inb, xb) = refs[2 * len(units) + 1 : 2 * len(units) + 9]
    (tile_sem, r1s, r1r, ins, inr, xs, xr, os_, fs, fr, gs, gr, ls) = refs[2 * len(units) + 9 :]
    total = sum(unit.count for unit in units)
    rep, mine = lax.axis_index("rep"), lax.axis_index("fsdp")
    core, place = rep % 2, rep // 2
    n_line = n_rep // 2
    half = n_line // 2
    side = place // half
    depth = place * (1 - side) + (n_line - 1 - place) * side
    inward = (place + 1 - 2 * side) * 2 + core
    outward = (place - 1 + 2 * side) * 2 + core
    sib = rep + 1 - 2 * core
    middle = depth == half - 1

    barrier = pltpu.get_barrier_semaphore()

    def greet(device):
        pl.semaphore_signal(barrier, inc=1, device_id=device, device_id_type=MESH)

    greet({"rep": sib, "fsdp": mine})
    greet({"rep": inward, "fsdp": mine})
    for s in range(1, n_fsdp):
        greet({"rep": rep, "fsdp": flipped(mine, s, n_fsdp)})

    @pl.when(depth == 0)
    def _():
        pl.semaphore_wait(barrier, 1 + n_fsdp)

    @pl.when(depth > 0)
    def _():
        greet({"rep": outward, "fsdp": mine})
        pl.semaphore_wait(barrier, 2 + n_fsdp)

    def remote(src, dst, send, recv, to_rep, to_fsdp):
        return pltpu.make_async_remote_copy(
            src_ref=src,
            dst_ref=dst,
            send_sem=send,
            recv_sem=recv,
            device_id={"rep": to_rep, "fsdp": to_fsdp},
            device_id_type=MESH,
        )

    def r1_copy(p):
        return remote(sb.at[p % RING], r1.at[p], r1s.at[p], r1r.at[p], sib, mine)

    def in_copy(p):
        return remote(r1.at[p], inb.at[p], ins.at[p], inr.at[p], inward, mine)

    def x_copy(p):
        return remote(r1.at[p], xb.at[p], xs.at[p], xr.at[p], inward, mine)

    def o_copy(p, src):
        return remote(src.at[p], xb.at[p], os_.at[p], xr.at[p], outward, mine)

    def owner_of(p):
        step, place_at, keep = 0, p, 1
        for u, unit in enumerate(units):
            if unit.by_owner:
                inside = at_least(p, unit.base, total - unit.base)
                if unit.base + unit.count < total:
                    stop = unit.base + unit.count
                    inside = inside * (1 - at_least(p, stop, total - stop))
                i = p - unit.base
                step = step + inside * (n_fsdp - 1 - i // unit.col_blocks)
        return step

    def spot(p, source):
        where = p
        for unit in units:
            if unit.by_owner:
                inside = at_least(p, unit.base, total - unit.base)
                if unit.base + unit.count < total:
                    stop = unit.base + unit.count
                    inside = inside * (1 - at_least(p, stop, total - stop))
                i = p - unit.base
                spread = unit.base + source * unit.col_blocks + i % unit.col_blocks
                where = where + inside * (spread - p)
        return where

    def f_copy(p, step):
        return remote(
            r1.at[p],
            out.at[spot(p, mine), core],
            fs.at[p],
            fr.at[p],
            rep,
            flipped(mine, step, n_fsdp),
        )

    def g_copy(p, src, where):
        return remote(src, out.at[where, core], gs.at[p], gr.at[p], sib, mine)

    def l_copy(p):
        return pltpu.make_async_copy(r1.at[p], out.at[spot(p, mine), core], ls.at[p])

    def add_into(p, other):
        r1[p] = (r1[p].astype(jnp.float32) + other.astype(jnp.float32)).astype(jnp.bfloat16)

    def stage_b(p):
        r1_copy(p).wait_recv()
        add_into(p, kb[p % RING])
        if half > 1:

            @pl.when(depth == 0)
            def _():
                in_copy(p).start()
        else:
            x_copy(p).start()

    def stage_c(p):
        @pl.when(depth > 0)
        def _():
            in_copy(p).wait_recv()
            add_into(p, inb[p])

            @pl.when(depth < half - 1)
            def _():
                in_copy(p).start()

            @pl.when(middle)
            def _():
                x_copy(p).start()

    def stage_d(p):
        @pl.when(middle)
        def _():
            x_copy(p).wait()
            add_into(p, xb[p])

            @pl.when(depth > 0)
            def _():
                o_copy(p, r1).start()

    def stage_e(p):
        @pl.when(depth < half - 1)
        def _():
            o_copy(p, xb).wait_recv()

            @pl.when(depth > 0)
            def _():
                o_copy(p, xb).start()

            in_copy(p).wait_send()
            r1[p] = xb[p]

        step = owner_of(p)

        @pl.when(step == 0)
        def _():
            l_copy(p).start()
            g_copy(p, r1.at[p], spot(p, mine)).start()

        @pl.when(step > 0)
        def _():
            f_copy(p, step).start()

    def stage_g(p):
        step = owner_of(p)

        @pl.when(step > 0)
        def _():
            f_copy(p, step).wait_recv()
            where = spot(p, flipped(mine, step, n_fsdp))
            g_copy(p, out.at[where, core], where).start()

    stages = [(LAG_B, stage_b), (LAG_C, stage_c), (LAG_D, stage_d), (LAG_E, stage_e), (LAG_G, stage_g)]

    def service(t):
        for lag, stage in stages:
            pl.when((t >= lag) & (t < total + lag))(functools.partial(stage, t - lag))

    def tiles(u, i, slot):
        unit = units[u]
        r, j = i // unit.col_blocks, i % unit.col_blocks
        if unit.by_owner:
            owner = flipped(mine, n_fsdp - 1 - r, n_fsdp)
            first = owner * 2 * piece_rows + core * piece_rows
            second = owner * 2 * piece_rows + (1 - core) * piece_rows
        else:
            first = core * unit.row_blocks * piece_rows + r * piece_rows
            second = (1 - core) * unit.row_blocks * piece_rows + r * piece_rows
        first = pl.multiple_of(first, piece_rows)
        second = pl.multiple_of(second, piece_rows)
        cols = pl.multiple_of(j * piece_cols, piece_cols)
        return [
            pltpu.make_async_copy(
                lefts[u].at[:, pl.ds(first, piece_rows)], lm.at[slot], tile_sem.at[slot, 0]
            ),
            pltpu.make_async_copy(
                lefts[u].at[:, pl.ds(second, piece_rows)], lo.at[slot], tile_sem.at[slot, 1]
            ),
            pltpu.make_async_copy(
                rights[u].at[:, pl.ds(cols, piece_cols)], rh.at[slot], tile_sem.at[slot, 2]
            ),
        ]

    def product(left, right):
        return lax.dot_general(
            left, right, (((0,), (0,)), ((), ())), preferred_element_type=jnp.float32
        )

    for copy in tiles(0, 0, 0):
        copy.start()
    for u, unit in enumerate(units):

        def step(i, carry, u=u, unit=unit):
            t = unit.base + i
            slot = t % 2
            for copy in tiles(u, i, slot):
                copy.wait()

            @pl.when(i + 1 < unit.count)
            def _():
                for copy in tiles(u, i + 1, 1 - slot):
                    copy.start()

            if u + 1 < len(units):

                @pl.when(i + 1 == unit.count)
                def _():
                    for copy in tiles(u + 1, 0, 1 - slot):
                        copy.start()

            @pl.when(t >= RING)
            def _():
                r1_copy(t - RING).wait_send()

            sb[t % RING] = product(lo[slot], rh[slot]).astype(jnp.bfloat16)
            r1_copy(t).start()
            kb[t % RING] = product(lm[slot], rh[slot])
            service(t)
            return carry

        lax.fori_loop(0, unit.count, step, 0)

    def drain(t, carry):
        service(t)
        return carry

    lax.fori_loop(total, total + LAG_G, drain, 0)

    def finish(p, carry):
        @pl.when(p >= total - RING)
        def _():
            r1_copy(p).wait_send()

        @pl.when(depth > 0)
        def _():
            o_copy(p, r1).wait_send()

        step = owner_of(p)

        @pl.when(step == 0)
        def _():
            l_copy(p).wait()

        @pl.when(step > 0)
        def _():
            f_copy(p, step).wait_send()

        g_copy(p, r1.at[p], p).wait()
        return carry

    lax.fori_loop(0, total, finish, 0)


def reduced(n_fsdp, n_rep, units, piece_rows, piece_cols, lefts, rights):
    total = sum(unit.count for unit in units)
    rows = lefts[0].shape[0]
    half = n_rep // 4
    dma = pltpu.SemaphoreType.DMA
    piece = (piece_rows, piece_cols)
    any_spec = pl.BlockSpec(memory_space=pl.ANY)
    flops = sum(4 * unit.count for unit in units) * rows * piece_rows * piece_cols
    return pl.pallas_call(
        functools.partial(reduce_kernel, n_fsdp, n_rep, units, piece_rows, piece_cols),
        out_shape=jax.ShapeDtypeStruct((total, 2) + piece, jnp.bfloat16),
        in_specs=[any_spec] * (2 * len(units)),
        out_specs=any_spec,
        scratch_shapes=[
            pltpu.VMEM((2, rows, piece_rows), jnp.bfloat16),
            pltpu.VMEM((2, rows, piece_rows), jnp.bfloat16),
            pltpu.VMEM((2, rows, piece_cols), jnp.bfloat16),
            pltpu.VMEM((RING,) + piece, jnp.bfloat16),
            pltpu.VMEM((RING,) + piece, jnp.float32),
            pltpu.VMEM((total,) + piece, jnp.bfloat16),
            pltpu.VMEM((total,) + piece, jnp.bfloat16),
            pltpu.VMEM((total,) + piece, jnp.bfloat16),
            dma((2, 3)),
        ]
        + [dma((total,)) for _ in range(12)],
        compiler_params=pltpu.CompilerParams(
            collective_id=0, has_side_effects=True, vmem_limit_bytes=60 << 20
        ),
        cost_estimate=pl.CostEstimate(flops=flops, bytes_accessed=1 << 30, transcendentals=0),
        name="reduce_weight_gradients",
    )(*lefts, *rights)


def widen_kernel(in_ref, out_ref):
    cols = in_ref.shape[-1]
    for i in range(in_ref.shape[0]):
        out_ref[:, i * cols : (i + 1) * cols] = in_ref[i, 0].astype(jnp.float32)


def widened(pieces, grid, together, where, shape, place):
    rows, cols = pieces.shape[2:]
    return pl.pallas_call(
        widen_kernel,
        grid=grid,
        out_shape=jax.ShapeDtypeStruct(shape, jnp.float32),
        in_specs=[pl.BlockSpec((together, 1, rows, cols), where)],
        out_specs=pl.BlockSpec((rows, together * cols), place),
        name="widen",
    )(pieces)


def widen_heads_kernel(query_in, gate_in, pair_in, query_out, gate_out, key_out, value_out):
    half = key_out.shape[1]
    query_out[...] = query_in[0, 0].astype(jnp.float32)
    gate_out[...] = gate_in[0, 0].astype(jnp.float32)
    key_out[...] = pair_in[0, 0, :, :half].astype(jnp.float32)
    value_out[...] = pair_in[0, 0, :, half:].astype(jnp.float32)


def widened_heads(pieces, base, n_fsdp, shapes):
    rows, cols = pieces.shape[2:]

    def where(j):
        return lambda c, f: (base + 3 * f + j, c, 0, 0)

    widths = (cols, cols, cols // 2, cols // 2)
    return pl.pallas_call(
        widen_heads_kernel,
        grid=(2, n_fsdp),
        out_shape=[jax.ShapeDtypeStruct(shape, jnp.float32) for shape in shapes],
        in_specs=[pl.BlockSpec((1, 1, rows, cols), where(j)) for j in range(3)],
        out_specs=[pl.BlockSpec((rows, wide), lambda c, f: (c, f)) for wide in widths],
        name="widen_heads",
    )(pieces, pieces, pieces)


def gather_rows(block):
    n_fsdp = lax.axis_size("fsdp")
    if n_fsdp != 4:
        return [block] + [shift(block, s) for s in range(1, n_fsdp)]
    half = block.shape[0] // 2
    top, low = block[:half], block[half:]
    x_top, y_low = shift(top, 1), shift(low, 2)
    x_low, y_top = shift(low, 1), shift(top, 2)
    d_top, d_low = shift(x_top, 2), shift(y_low, 1)
    return [
        block,
        jnp.concatenate([x_top, x_low]),
        jnp.concatenate([y_top, y_low]),
        jnp.concatenate([d_top, d_low]),
    ]


def scatter_rows(own, parts):
    n_fsdp = lax.axis_size("fsdp")
    if n_fsdp != 4:
        for s in range(1, n_fsdp):
            own = own + in_f32(shift(parts[s - 1], s))
        return own
    half = own.shape[0] // 2
    p_x, p_y, p_d = parts
    r_y = shift(p_d[:half], 1)
    r_x = shift(p_d[half:], 2)
    x_top = shift(p_x[:half], 1)
    y_low = shift(p_y[half:], 2)
    y_top = shift(in_bf16(in_f32(p_y[:half]) + in_f32(r_y)), 2)
    x_low = shift(in_bf16(in_f32(p_x[half:]) + in_f32(r_x)), 1)
    return own + jnp.concatenate(
        [in_f32(x_top) + in_f32(y_top), in_f32(y_low) + in_f32(x_low)]
    )


def shards(
    tokens,
    teacher,
    lengths,
    deal_order,
    attention_gain,
    query_gain,
    key_gain,
    w_query,
    w_key,
    w_value,
    w_outgate,
    w_output,
    mlp_gain,
    w_gate,
    w_up,
    w_down,
):
    n_rep = lax.axis_size("rep")
    n_fsdp = lax.axis_size("fsdp")
    rows, width = tokens.shape
    mine = lax.axis_index("fsdp")
    core = lax.axis_index("rep") % 2
    others = range(1, n_fsdp)
    heads_q, heads_k = H // n_fsdp, KV // n_fsdp
    cols_q, cols_k = heads_q * HD, heads_k * HD
    deep = w_query.shape[0]
    ff = w_down.shape[0]
    rows_all = rows * n_fsdp

    peers = mine ^ jnp.arange(n_fsdp, dtype=jnp.int32)
    devices = lax.axis_index("rep") * n_fsdp + peers
    slot_ids = (devices[:, None] * 2 + jnp.arange(2, dtype=jnp.int32)[None, :]).reshape(-1)
    seq_ids = jnp.arange(lengths.shape[0], dtype=jnp.int32)
    slot_seq = jnp.sum(
        jnp.where(seq_ids[None, :] == slot_ids[:, None], deal_order[None, :], 0), axis=1
    )
    pair_len = jnp.sum(
        jnp.where(seq_ids[None, :] == slot_seq[:, None], lengths[None, :], 0), axis=1
    ).reshape(n_fsdp, 2)
    token_count = jnp.sum(lengths).astype(jnp.float32)
    factor = rows * n_rep * n_fsdp / (2.0 * token_count)
    segments, angle_cos, angle_sin = row_layout(pair_len, rows, HD)
    row_index = jnp.arange(rows, dtype=jnp.int32)
    allowed = (segments[:, :, None] == segments[:, None, :]) & (
        row_index[None, None, :] <= row_index[None, :, None]
    )
    allowed = allowed[:, None, None]
    segment = segments[0]
    valid_row = (segment < 2).astype(jnp.float32)
    score_scale = HD ** (-0.5)

    def column_parts(weights, widths):
        def pick(start_of):
            return jnp.concatenate(
                [
                    lax.dynamic_slice(w, (0, start_of * cols), (deep, cols))
                    for w, cols in zip(weights, widths)
                ],
                axis=1,
            )

        return pick

    def by_columns(weights, widths):
        pick = column_parts(weights, widths)
        half = deep // 2
        cols = sum(widths)
        whole = jnp.zeros((n_fsdp * deep, cols), jnp.bfloat16)
        whole = lax.dynamic_update_slice(whole, pick(mine), (mine * deep, 0))
        for s in others:
            piece = lax.dynamic_slice(pick(mine ^ s), (core * half, 0), (half, cols))
            got = shift(piece, s)
            rest = sibling(got)
            start = (mine ^ s) * deep
            whole = lax.dynamic_update_slice(whole, got, (start + core * half, 0))
            whole = lax.dynamic_update_slice(whole, rest, (start + (1 - core) * half, 0))
        return whole

    gains_own = jnp.concatenate([attention_gain, mlp_gain, query_gain, key_gain])[None]
    gains = jnp.concatenate([gains_own] + [shift(gains_own, s) for s in others], axis=0)
    gains = in_f32(jnp.take(gains, mine ^ jnp.arange(n_fsdp), axis=0))
    small = query_gain.shape[0]
    attention_gain_f = gains[:, :deep].reshape(-1)
    mlp_gain_f = gains[:, deep : 2 * deep].reshape(-1)
    query_gain_f = gains[:, 2 * deep : 2 * deep + small].reshape(-1)
    key_gain_f = gains[:, 2 * deep + small :].reshape(-1)

    tokens_all = jnp.concatenate(gather_rows(tokens))
    w_attn = by_columns((w_query, w_outgate, w_key, w_value), (cols_q, cols_q, cols_k, cols_k))
    w_mlp = by_columns((w_gate, w_up), (ff, ff))

    tokens_f = in_f32(tokens)
    normed_all = in_bf16(rms_scale(in_f32(tokens_all), attention_gain_f))
    attn_raw = times(normed_all, w_attn)
    query_raw = attn_raw[:, :cols_q]
    gate_raw = attn_raw[:, cols_q : 2 * cols_q]
    key_raw = attn_raw[:, 2 * cols_q : 2 * cols_q + cols_k]
    value_b = in_bf16(attn_raw[:, 2 * cols_q + cols_k :]).reshape(n_fsdp, rows, heads_k, HD)

    def prepare_heads(query_in, key_in, query_scale, key_scale):
        query_heads = rms_scale(query_in.reshape(n_fsdp, rows, heads_q, HD), query_scale)
        query_heads = rotate(query_heads, angle_cos[:, :, None], angle_sin[:, :, None])
        key_heads = rms_scale(key_in.reshape(n_fsdp, rows, heads_k, HD), key_scale)
        key_heads = rotate(key_heads, angle_cos[:, :, None], angle_sin[:, :, None])
        return (query_heads, key_heads)

    head_pair, heads_back = jax.vjp(prepare_heads, query_raw, key_raw, query_gain_f, key_gain_f)
    queries_b = in_bf16(head_pair[0]).reshape(n_fsdp, rows, heads_k, H // KV, HD)
    keys_b = in_bf16(head_pair[1])

    def dots(spec, left, right):
        return jnp.einsum(spec, left, right, preferred_element_type=jnp.float32)

    scores = dots("sqkgd,spkd->skgqp", queries_b, keys_b) * score_scale
    scores = jnp.where(allowed, scores, NEG_FILL)
    row_top = jnp.max(scores, axis=-1, keepdims=True)
    exponent = jnp.exp(scores - row_top)
    row_total = jnp.sum(exponent, axis=-1, keepdims=True)
    probs_b = in_bf16(exponent / row_total)
    log_total = row_top + jnp.log(row_total)
    context = dots("skgqp,spkd->sqkgd", probs_b, value_b)
    gate_heads = gate_raw.reshape(n_fsdp, rows, heads_k, H // KV, HD)
    gated_out, gating_back = jax.vjp(gating, context, gate_heads)
    gated_b = in_bf16(gated_out.reshape(rows_all, cols_q))

    def summed(left, right, product):
        own = product(left[:rows], right, jnp.float32)
        parts = product(left[rows:], right, jnp.bfloat16)
        return scatter_rows(own, [parts[i * rows : (i + 1) * rows] for i in range(n_fsdp - 1)])

    middle = tokens_f + summed(gated_b, w_output, times)
    normed_mlp, mlp_norm_back = jax.vjp(rms_scale, middle, mlp_gain_f)
    normed_mlp_all = jnp.concatenate(gather_rows(in_bf16(normed_mlp)))
    gate_pre = times(normed_mlp_all, w_mlp[:, :ff])
    up_pre = times(normed_mlp_all, w_mlp[:, ff:])
    hidden, swiglu_back = jax.vjp(swiglu, gate_pre, up_pre)
    hidden_b = in_bf16(hidden)
    result = middle + summed(hidden_b, w_down, times)

    error_rows = (result - in_f32(teacher)) * valid_row[:, None]
    row_sq = jnp.sum(error_rows * error_rows, axis=-1)
    slot_mask = (segment[:, None] == jnp.arange(2, dtype=jnp.int32)[None, :]).astype(jnp.float32)
    seq_loss = jnp.sum(row_sq[:, None] * slot_mask, axis=0) / (2.0 * token_count)
    block_out = in_bf16(result * valid_row[:, None])
    grad_result = 2.0 * factor * error_rows

    grad_branch_all = jnp.concatenate(gather_rows(in_bf16(grad_result)))
    grad_hidden = times_trans(grad_branch_all, w_down)
    grad_gate_pre, grad_up_pre = swiglu_back(grad_hidden)
    grad_gate_b = in_bf16(grad_gate_pre)
    grad_up_b = in_bf16(grad_up_pre)
    grad_mlp_b = jnp.concatenate([grad_gate_b, grad_up_b], axis=1)
    grad_normed_mlp = summed(grad_mlp_b, w_mlp, times_trans)
    grad_middle_norm, grad_mlp_gain = mlp_norm_back(grad_normed_mlp)
    grad_middle = grad_result + grad_middle_norm

    grad_attn_all = jnp.concatenate(gather_rows(in_bf16(grad_middle)))
    grad_gated = times_trans(grad_attn_all, w_output).reshape(
        n_fsdp, rows, heads_k, H // KV, HD
    )
    grad_context, grad_gate_heads = gating_back(grad_gated)
    grad_context_b = in_bf16(grad_context)
    grad_outgate_b = in_bf16(grad_gate_heads.reshape(rows_all, cols_q))
    scores_again = dots("sqkgd,spkd->skgqp", queries_b, keys_b) * score_scale
    probs_again = jnp.where(allowed, jnp.exp(scores_again - log_total), 0.0)
    grad_value = dots("skgqp,sqkgd->spkd", in_bf16(probs_again), grad_context_b)
    grad_probs = dots("sqkgd,spkd->skgqp", grad_context_b, value_b)
    grad_scores = probs_again * (
        grad_probs - jnp.sum(probs_again * grad_probs, axis=-1, keepdims=True)
    )
    grad_scores_b = in_bf16(grad_scores)
    grad_queries = dots("skgqp,spkd->sqkgd", grad_scores_b, keys_b) * score_scale
    grad_keys = dots("skgqp,sqkgd->spkd", grad_scores_b, queries_b) * score_scale
    grad_query_raw, grad_key_raw, grad_query_gain, grad_key_gain = heads_back(
        (grad_queries.reshape(n_fsdp, rows, heads_q, HD), grad_keys)
    )
    grad_query_b = in_bf16(grad_query_raw)
    grad_key_b = in_bf16(grad_key_raw)
    grad_value_b = in_bf16(grad_value.reshape(rows_all, cols_k))
    grad_raw_b = jnp.concatenate(
        [grad_query_b, grad_outgate_b, grad_key_b, grad_value_b], axis=1
    )
    grad_normed = summed(grad_raw_b, w_attn, times_trans)
    _, norm_back = jax.vjp(rms_scale, tokens_f, attention_gain_f)
    grad_tokens_norm, grad_attention_gain = norm_back(grad_normed)
    tokens_grad = in_bf16(grad_middle + grad_tokens_norm)

    dgains = sum_everywhere(
        jnp.concatenate([grad_attention_gain, grad_mlp_gain, grad_query_gain, grad_key_gain])[None]
    )[0]

    piece_rows, piece_cols = deep // 2, width // n_fsdp
    units, base = [], 0
    for by_owner, row_blocks, cols in (
        (False, ff // 2 // piece_rows, width),
        (True, n_fsdp, 2 * ff),
        (False, cols_q // 2 // piece_rows, width),
        (True, n_fsdp, 2 * cols_q + 2 * cols_k),
    ):
        units.append(Unit(base, by_owner, row_blocks, cols // piece_cols))
        base += units[-1].count
    pieces = reduced(
        n_fsdp,
        n_rep,
        units,
        piece_rows,
        piece_cols,
        (hidden_b, normed_mlp_all, gated_b, normed_all),
        (grad_branch_all, grad_mlp_b, grad_attn_all, grad_raw_b),
    )
    down, mlp, outp, attn = units

    def by_rows(unit, weight):
        blocks, together = unit.row_blocks, unit.col_blocks
        return widened(
            pieces,
            (2, blocks),
            together,
            lambda c, r: (unit.base // together + r, c, 0, 0),
            weight.shape,
            lambda c, r: (c * blocks + r, 0),
        )

    def by_owners(unit, weight, which):
        together = unit.col_blocks // 2
        return widened(
            pieces,
            (2, n_fsdp),
            together,
            lambda c, f: (unit.base // together + 2 * f + which, c, 0, 0),
            weight.shape,
            lambda c, f: (c, f),
        )

    dw_down = by_rows(down, w_down)
    dw_output = by_rows(outp, w_output)
    dw_gate = by_owners(mlp, w_gate, 0)
    dw_up = by_owners(mlp, w_up, 1)
    dw_query, dw_outgate, dw_key, dw_value = widened_heads(
        pieces,
        attn.base,
        n_fsdp,
        (w_query.shape, w_outgate.shape, w_key.shape, w_value.shape),
    )

    def own_part(start, cols):
        return lax.dynamic_slice(dgains, (start + mine * cols,), (cols,))

    return (
        block_out,
        seq_loss,
        tokens_grad,
        own_part(0, deep),
        own_part(2 * width, small),
        own_part(2 * width + HD, small),
        dw_query,
        dw_key,
        dw_value,
        dw_outgate,
        dw_output,
        own_part(width, deep),
        dw_gate,
        dw_up,
        dw_down,
    )


def solution(mesh):
    return jax.shard_map(
        shards,
        mesh=mesh,
        in_specs=(
            P(("rep", "fsdp"), None),
            P(("rep", "fsdp"), None),
            P(),
            P(),
            P("fsdp"),
            P("fsdp"),
            P("fsdp"),
            P("fsdp", None),
            P("fsdp", None),
            P("fsdp", None),
            P("fsdp", None),
            P("fsdp", None),
            P("fsdp"),
            P("fsdp", None),
            P("fsdp", None),
            P("fsdp", None),
        ),
        out_specs=(
            P(("rep", "fsdp"), None),
            P(("rep", "fsdp")),
            P(("rep", "fsdp"), None),
            P("fsdp"),
            P("fsdp"),
            P("fsdp"),
            P("fsdp", None),
            P("fsdp", None),
            P("fsdp", None),
            P("fsdp", None),
            P("fsdp", None),
            P("fsdp"),
            P("fsdp", None),
            P("fsdp", None),
            P("fsdp", None),
        ),
        check_vma=False,
    )
```

```python
import functools

import jax
import jax.numpy as jnp
from jax import lax
from jax.experimental import pallas as pl
from jax.experimental.pallas import tpu as pltpu
from jax.sharding import PartitionSpec as P

MESH = pl.DeviceIdType.MESH

H = 16
KV = 8
HD = 128


EPS_NORM = 1e-06
ROPE_BASE = 1000000.0
NEG_FILL = -1e30


def rms_scale(values, gain_vec):
    return (
        values * lax.rsqrt(jnp.mean(values * values, axis=-1, keepdims=True) + EPS_NORM) * gain_vec
    )


def row_layout(pair_len, row_count, head_dim):
    row_index = jnp.arange(row_count, dtype=jnp.int32)[None, :]
    head_len = pair_len[:, :1]
    both_len = pair_len[:, :1] + pair_len[:, 1:]
    segment = (row_index >= head_len).astype(jnp.int32) + (row_index >= both_len).astype(jnp.int32)
    start_row = jnp.where(segment == 0, 0, jnp.where(segment == 1, head_len, both_len))
    position = (row_index - start_row).astype(jnp.float32)
    inv_freq = jnp.power(ROPE_BASE, -jnp.arange(0, head_dim, 2, dtype=jnp.float32) / head_dim)
    angles = position[..., None] * inv_freq
    angle_cos, angle_sin = jnp.cos(angles), jnp.sin(angles)
    return (
        segment,
        jnp.concatenate([angle_cos, angle_cos], axis=-1),
        jnp.concatenate([angle_sin, angle_sin], axis=-1),
    )


def times(left_side, right_side, out=jnp.float32):
    return jnp.dot(left_side, right_side, preferred_element_type=jnp.float32).astype(out)


def times_trans(left_side, right_side, out=jnp.float32):
    return lax.dot_general(
        left_side, right_side, (((1,), (1,)), ((), ())), preferred_element_type=jnp.float32
    ).astype(out)


def trans_times(left_side, right_side, out=jnp.float32):
    return lax.dot_general(
        left_side, right_side, (((0,), (0,)), ((), ())), preferred_element_type=jnp.float32
    ).astype(out)


def swiglu(gate_pre, up_pre):
    return jax.nn.silu(gate_pre) * up_pre


def in_f32(values):
    return values.astype(jnp.float32)


def in_bf16(values):
    return values.astype(jnp.bfloat16)


def shift(values, step):
    n_fsdp = lax.axis_size("fsdp")
    return lax.ppermute(values, "fsdp", [(i, i ^ step) for i in range(n_fsdp)])


def sibling(values):
    n_rep = lax.axis_size("rep")
    return lax.ppermute(values, "rep", [(i, i ^ 1) for i in range(n_rep)])


def sum_everywhere(values):
    for axis in ("fsdp", "rep"):
        n = lax.axis_size(axis)
        step = 1
        while step < n:
            values = values + lax.ppermute(values, axis, [(i, i ^ step) for i in range(n)])
            step *= 2
    return values


def flipped(index, step, n):
    out, bit = index, 1
    while bit < n:
        has = (step // bit) % 2
        out = out + has * bit * (1 - 2 * ((index // bit) % 2))
        bit *= 2
    return out


def at_least(value, bound, span):
    span = max(span, bound)
    return (value + (span - bound)) // span


class Unit:
    def __init__(self, base, by_owner, row_blocks, col_blocks):
        self.base, self.by_owner = base, by_owner
        self.row_blocks, self.col_blocks = row_blocks, col_blocks
        self.count = row_blocks * col_blocks


LAG_B, LAG_C, LAG_D, LAG_E, LAG_G = 2, 4, 6, 8, 11
RING = 4


def reduce_kernel(
    n_fsdp, n_rep, units, piece_rows, piece_cols, *refs
):
    lefts, rights = refs[: len(units)], refs[len(units) : 2 * len(units)]
    out = refs[2 * len(units)]
    (lm, lo, rh, sb, kb, r1, inb, xb) = refs[2 * len(units) + 1 : 2 * len(units) + 9]
    (tile_sem, r1s, r1r, ins, inr, xs, xr, os_, fs, fr, gs, gr, ls) = refs[2 * len(units) + 9 :]
    total = sum(unit.count for unit in units)
    rep, mine = lax.axis_index("rep"), lax.axis_index("fsdp")
    core, place = rep % 2, rep // 2
    n_line = n_rep // 2
    half = n_line // 2
    side = place // half
    depth = place * (1 - side) + (n_line - 1 - place) * side
    inward = (place + 1 - 2 * side) * 2 + core
    outward = (place - 1 + 2 * side) * 2 + core
    sib = rep + 1 - 2 * core
    middle = depth == half - 1

    barrier = pltpu.get_barrier_semaphore()

    def greet(device):
        pl.semaphore_signal(barrier, inc=1, device_id=device, device_id_type=MESH)

    greet({"rep": sib, "fsdp": mine})
    greet({"rep": inward, "fsdp": mine})
    for s in range(1, n_fsdp):
        greet({"rep": rep, "fsdp": flipped(mine, s, n_fsdp)})

    @pl.when(depth == 0)
    def _():
        pl.semaphore_wait(barrier, 1 + n_fsdp)

    @pl.when(depth > 0)
    def _():
        greet({"rep": outward, "fsdp": mine})
        pl.semaphore_wait(barrier, 2 + n_fsdp)

    def remote(src, dst, send, recv, to_rep, to_fsdp):
        return pltpu.make_async_remote_copy(
            src_ref=src,
            dst_ref=dst,
            send_sem=send,
            recv_sem=recv,
            device_id={"rep": to_rep, "fsdp": to_fsdp},
            device_id_type=MESH,
        )

    def r1_copy(p):
        return remote(sb.at[p % RING], r1.at[p], r1s.at[p], r1r.at[p], sib, mine)

    def in_copy(p):
        return remote(r1.at[p], inb.at[p], ins.at[p], inr.at[p], inward, mine)

    def x_copy(p):
        return remote(r1.at[p], xb.at[p], xs.at[p], xr.at[p], inward, mine)

    def o_copy(p, src):
        return remote(src.at[p], xb.at[p], os_.at[p], xr.at[p], outward, mine)

    def owner_of(p):
        step, place_at, keep = 0, p, 1
        for u, unit in enumerate(units):
            if unit.by_owner:
                inside = at_least(p, unit.base, total - unit.base)
                if unit.base + unit.count < total:
                    stop = unit.base + unit.count
                    inside = inside * (1 - at_least(p, stop, total - stop))
                i = p - unit.base
                step = step + inside * (n_fsdp - 1 - i // unit.col_blocks)
        return step

    def spot(p, source):
        where = p
        for unit in units:
            if unit.by_owner:
                inside = at_least(p, unit.base, total - unit.base)
                if unit.base + unit.count < total:
                    stop = unit.base + unit.count
                    inside = inside * (1 - at_least(p, stop, total - stop))
                i = p - unit.base
                spread = unit.base + source * unit.col_blocks + i % unit.col_blocks
                where = where + inside * (spread - p)
        return where

    def f_copy(p, step):
        return remote(
            r1.at[p],
            out.at[spot(p, mine), core],
            fs.at[p],
            fr.at[p],
            rep,
            flipped(mine, step, n_fsdp),
        )

    def g_copy(p, src, where):
        return remote(src, out.at[where, core], gs.at[p], gr.at[p], sib, mine)

    def l_copy(p):
        return pltpu.make_async_copy(r1.at[p], out.at[spot(p, mine), core], ls.at[p])

    def add_into(p, other):
        r1[p] = (r1[p].astype(jnp.float32) + other.astype(jnp.float32)).astype(jnp.bfloat16)

    def stage_b(p):
        r1_copy(p).wait_recv()
        add_into(p, kb[p % RING])
        if half > 1:

            @pl.when(depth == 0)
            def _():
                in_copy(p).start()
        else:
            x_copy(p).start()

    def stage_c(p):
        @pl.when(depth > 0)
        def _():
            in_copy(p).wait_recv()
            add_into(p, inb[p])

            @pl.when(depth < half - 1)
            def _():
                in_copy(p).start()

            @pl.when(middle)
            def _():
                x_copy(p).start()

    def stage_d(p):
        @pl.when(middle)
        def _():
            x_copy(p).wait()
            add_into(p, xb[p])

            @pl.when(depth > 0)
            def _():
                o_copy(p, r1).start()

    def stage_e(p):
        @pl.when(depth < half - 1)
        def _():
            o_copy(p, xb).wait_recv()

            @pl.when(depth > 0)
            def _():
                o_copy(p, xb).start()

            in_copy(p).wait_send()
            r1[p] = xb[p]

        step = owner_of(p)

        @pl.when(step == 0)
        def _():
            l_copy(p).start()
            g_copy(p, r1.at[p], spot(p, mine)).start()

        @pl.when(step > 0)
        def _():
            f_copy(p, step).start()

    def stage_g(p):
        step = owner_of(p)

        @pl.when(step > 0)
        def _():
            f_copy(p, step).wait_recv()
            where = spot(p, flipped(mine, step, n_fsdp))
            g_copy(p, out.at[where, core], where).start()

    stages = [(LAG_B, stage_b), (LAG_C, stage_c), (LAG_D, stage_d), (LAG_E, stage_e), (LAG_G, stage_g)]

    def service(t):
        for lag, stage in stages:
            pl.when((t >= lag) & (t < total + lag))(functools.partial(stage, t - lag))

    def tiles(u, i, slot):
        unit = units[u]
        r, j = i // unit.col_blocks, i % unit.col_blocks
        if unit.by_owner:
            owner = flipped(mine, n_fsdp - 1 - r, n_fsdp)
            first = owner * 2 * piece_rows + core * piece_rows
            second = owner * 2 * piece_rows + (1 - core) * piece_rows
        else:
            first = core * unit.row_blocks * piece_rows + r * piece_rows
            second = (1 - core) * unit.row_blocks * piece_rows + r * piece_rows
        first = pl.multiple_of(first, piece_rows)
        second = pl.multiple_of(second, piece_rows)
        cols = pl.multiple_of(j * piece_cols, piece_cols)
        return [
            pltpu.make_async_copy(
                lefts[u].at[:, pl.ds(first, piece_rows)], lm.at[slot], tile_sem.at[slot, 0]
            ),
            pltpu.make_async_copy(
                lefts[u].at[:, pl.ds(second, piece_rows)], lo.at[slot], tile_sem.at[slot, 1]
            ),
            pltpu.make_async_copy(
                rights[u].at[:, pl.ds(cols, piece_cols)], rh.at[slot], tile_sem.at[slot, 2]
            ),
        ]

    def product(left, right):
        return lax.dot_general(
            left, right, (((0,), (0,)), ((), ())), preferred_element_type=jnp.float32
        )

    for copy in tiles(0, 0, 0):
        copy.start()
    for u, unit in enumerate(units):

        def step(i, carry, u=u, unit=unit):
            t = unit.base + i
            slot = t % 2
            for copy in tiles(u, i, slot):
                copy.wait()

            @pl.when(i + 1 < unit.count)
            def _():
                for copy in tiles(u, i + 1, 1 - slot):
                    copy.start()

            if u + 1 < len(units):

                @pl.when(i + 1 == unit.count)
                def _():
                    for copy in tiles(u + 1, 0, 1 - slot):
                        copy.start()

            @pl.when(t >= RING)
            def _():
                r1_copy(t - RING).wait_send()

            sb[t % RING] = product(lo[slot], rh[slot]).astype(jnp.bfloat16)
            r1_copy(t).start()
            kb[t % RING] = product(lm[slot], rh[slot])
            service(t)
            return carry

        lax.fori_loop(0, unit.count, step, 0)

    def drain(t, carry):
        service(t)
        return carry

    lax.fori_loop(total, total + LAG_G, drain, 0)

    def finish(p, carry):
        @pl.when(p >= total - RING)
        def _():
            r1_copy(p).wait_send()

        @pl.when(depth > 0)
        def _():
            o_copy(p, r1).wait_send()

        step = owner_of(p)

        @pl.when(step == 0)
        def _():
            l_copy(p).wait()

        @pl.when(step > 0)
        def _():
            f_copy(p, step).wait_send()

        g_copy(p, r1.at[p], p).wait()
        return carry

    lax.fori_loop(0, total, finish, 0)


def reduced(n_fsdp, n_rep, units, piece_rows, piece_cols, lefts, rights):
    total = sum(unit.count for unit in units)
    rows = lefts[0].shape[0]
    half = n_rep // 4
    dma = pltpu.SemaphoreType.DMA
    piece = (piece_rows, piece_cols)
    any_spec = pl.BlockSpec(memory_space=pl.ANY)
    flops = sum(4 * unit.count for unit in units) * rows * piece_rows * piece_cols
    return pl.pallas_call(
        functools.partial(reduce_kernel, n_fsdp, n_rep, units, piece_rows, piece_cols),
        out_shape=jax.ShapeDtypeStruct((total, 2) + piece, jnp.bfloat16),
        in_specs=[any_spec] * (2 * len(units)),
        out_specs=any_spec,
        scratch_shapes=[
            pltpu.VMEM((2, rows, piece_rows), jnp.bfloat16),
            pltpu.VMEM((2, rows, piece_rows), jnp.bfloat16),
            pltpu.VMEM((2, rows, piece_cols), jnp.bfloat16),
            pltpu.VMEM((RING,) + piece, jnp.bfloat16),
            pltpu.VMEM((RING,) + piece, jnp.float32),
            pltpu.VMEM((total,) + piece, jnp.bfloat16),
            pltpu.VMEM((total,) + piece, jnp.bfloat16),
            pltpu.VMEM((total,) + piece, jnp.bfloat16),
            dma((2, 3)),
        ]
        + [dma((total,)) for _ in range(12)],
        compiler_params=pltpu.CompilerParams(
            collective_id=0, has_side_effects=True, vmem_limit_bytes=60 << 20
        ),
        cost_estimate=pl.CostEstimate(flops=flops, bytes_accessed=1 << 30, transcendentals=0),
        name="reduce_weight_gradients",
    )(*lefts, *rights)


def widen_kernel(in_ref, out_ref):
    cols = in_ref.shape[-1]
    for i in range(in_ref.shape[0]):
        out_ref[:, i * cols : (i + 1) * cols] = in_ref[i, 0].astype(jnp.float32)


def widened(pieces, grid, together, where, shape, place):
    rows, cols = pieces.shape[2:]
    return pl.pallas_call(
        widen_kernel,
        grid=grid,
        out_shape=jax.ShapeDtypeStruct(shape, jnp.float32),
        in_specs=[pl.BlockSpec((together, 1, rows, cols), where)],
        out_specs=pl.BlockSpec((rows, together * cols), place),
        name="widen",
    )(pieces)


def widen_heads_kernel(query_in, gate_in, pair_in, query_out, gate_out, key_out, value_out):
    half = key_out.shape[1]
    query_out[...] = query_in[0, 0].astype(jnp.float32)
    gate_out[...] = gate_in[0, 0].astype(jnp.float32)
    key_out[...] = pair_in[0, 0, :, :half].astype(jnp.float32)
    value_out[...] = pair_in[0, 0, :, half:].astype(jnp.float32)


def widened_heads(pieces, base, n_fsdp, shapes):
    rows, cols = pieces.shape[2:]

    def where(j):
        return lambda c, f: (base + 3 * f + j, c, 0, 0)

    widths = (cols, cols, cols // 2, cols // 2)
    return pl.pallas_call(
        widen_heads_kernel,
        grid=(2, n_fsdp),
        out_shape=[jax.ShapeDtypeStruct(shape, jnp.float32) for shape in shapes],
        in_specs=[pl.BlockSpec((1, 1, rows, cols), where(j)) for j in range(3)],
        out_specs=[pl.BlockSpec((rows, wide), lambda c, f: (c, f)) for wide in widths],
        name="widen_heads",
    )(pieces, pieces, pieces)


def block_mask(pair_ref, rows):
    block = pl.program_id(0)
    head_len = pair_ref[block, 0]
    both_len = head_len + pair_ref[block, 1]
    query_row = lax.broadcasted_iota(jnp.int32, (rows, rows), 0)
    key_row = lax.broadcasted_iota(jnp.int32, (rows, rows), 1)

    def segment(index):
        return (index >= head_len).astype(jnp.int32) + (index >= both_len).astype(jnp.int32)

    return (segment(query_row) == segment(key_row)) & (key_row <= query_row)


def turn(values):
    half_dim = values.shape[-1] // 2
    return jnp.concatenate([-values[:, half_dim:], values[:, :half_dim]], axis=-1)


def head_forward(raw, gain, angle_cos, angle_sin):
    values = raw * lax.rsqrt(jnp.mean(raw * raw, axis=-1, keepdims=True) + EPS_NORM) * gain
    return in_bf16(values * angle_cos + turn(values) * angle_sin)


def head_backward(grad, raw, gain, angle_cos, angle_sin):
    grad = grad * angle_cos - turn(grad * angle_sin)
    scale = lax.rsqrt(jnp.mean(raw * raw, axis=-1, keepdims=True) + EPS_NORM)
    unit = raw * scale
    gain_rows = grad * unit
    inner = grad * gain
    return scale * (inner - unit * jnp.mean(inner * unit, axis=-1, keepdims=True)), gain_rows


def product_of(left, right, left_dim, right_dim):
    return lax.dot_general(
        left, right, (((left_dim,), (right_dim,)), ((), ())), preferred_element_type=jnp.float32
    )


def softmax_of(queries, keys, allowed):
    scores = jnp.where(allowed, product_of(queries, keys, 1, 1) * HD ** (-0.5), NEG_FILL)
    exponent = jnp.exp(scores - jnp.max(scores, axis=-1, keepdims=True))
    return exponent / jnp.sum(exponent, axis=-1, keepdims=True)


def attend_kernel(
    heads_k, pair_ref, raw_ref, cos_ref, sin_ref, qg_ref, kg_ref, q_ref, k_ref, v_ref, gated_ref
):
    group = H // KV
    cols_q, cols_k = heads_k * group * HD, heads_k * HD
    allowed = block_mask(pair_ref, raw_ref.shape[0])
    angle_cos, angle_sin = cos_ref[...], sin_ref[...]
    for j in range(heads_k):
        own = slice(j * HD, (j + 1) * HD)
        keys = head_forward(
            raw_ref[:, 2 * cols_q + j * HD : 2 * cols_q + (j + 1) * HD],
            kg_ref[...],
            angle_cos,
            angle_sin,
        )
        start = 2 * cols_q + cols_k + j * HD
        values = in_bf16(raw_ref[:, start : start + HD])
        k_ref[:, own] = keys
        v_ref[:, own] = values
        for h in range(j * group, (j + 1) * group):
            cut = slice(h * HD, (h + 1) * HD)
            queries = head_forward(raw_ref[:, cut], qg_ref[...], angle_cos, angle_sin)
            q_ref[:, cut] = queries
            probs = in_bf16(softmax_of(queries, keys, allowed))
            context = product_of(probs, values, 1, 0)
            gate = raw_ref[:, cols_q + h * HD : cols_q + (h + 1) * HD]
            gated_ref[:, cut] = in_bf16(context * jax.nn.sigmoid(gate))


def attend_back_kernel(
    heads_k,
    pair_ref,
    raw_ref,
    cos_ref,
    sin_ref,
    qg_ref,
    kg_ref,
    q_ref,
    k_ref,
    v_ref,
    grad_ref,
    out_ref,
    gain_ref,
):
    group = H // KV
    cols_q, cols_k = heads_k * group * HD, heads_k * HD
    allowed = block_mask(pair_ref, raw_ref.shape[0])
    angle_cos, angle_sin = cos_ref[...], sin_ref[...]

    @pl.when(pl.program_id(0) == 0)
    def _():
        gain_ref[...] = jnp.zeros_like(gain_ref)

    for j in range(heads_k):
        own = slice(j * HD, (j + 1) * HD)
        keys, values = k_ref[:, own], v_ref[:, own]
        grad_keys, grad_values = 0.0, 0.0
        for h in range(j * group, (j + 1) * group):
            cut = slice(h * HD, (h + 1) * HD)
            gate_cut = slice(cols_q + h * HD, cols_q + (h + 1) * HD)
            queries, grad_gated = q_ref[:, cut], grad_ref[:, cut]
            probs = softmax_of(queries, keys, allowed)
            probs_b = in_bf16(probs)
            context = product_of(probs_b, values, 1, 0)
            gate = jax.nn.sigmoid(raw_ref[:, gate_cut])
            grad_context = in_bf16(grad_gated * gate)
            out_ref[:, gate_cut] = in_bf16(grad_gated * context * gate * (1.0 - gate))
            grad_probs = product_of(grad_context, values, 1, 1)
            grad_scores = in_bf16(
                probs * (grad_probs - jnp.sum(probs * grad_probs, axis=-1, keepdims=True))
            )
            grad_values += product_of(probs_b, grad_context, 0, 0)
            grad_keys += product_of(grad_scores, queries, 0, 0)
            grad_queries = product_of(grad_scores, keys, 1, 0) * HD ** (-0.5)
            grad_raw, gain_rows = head_backward(
                grad_queries, raw_ref[:, cut], qg_ref[...], angle_cos, angle_sin
            )
            out_ref[:, cut] = in_bf16(grad_raw)
            gain_ref[0:1, :] += jnp.sum(gain_rows, axis=0, keepdims=True)
        key_start = 2 * cols_q + j * HD
        grad_raw, gain_rows = head_backward(
            grad_keys * HD ** (-0.5),
            raw_ref[:, key_start : key_start + HD],
            kg_ref[...],
            angle_cos,
            angle_sin,
        )
        out_ref[:, key_start : key_start + HD] = in_bf16(grad_raw)
        gain_ref[1:2, :] += jnp.sum(gain_rows, axis=0, keepdims=True)
        value_start = 2 * cols_q + cols_k + j * HD
        out_ref[:, value_start : value_start + HD] = in_bf16(grad_values)


def rows_spec(rows, cols):
    return pl.BlockSpec((rows, cols), lambda s: (s, 0))


def whole_spec(shape):
    return pl.BlockSpec(shape, lambda s: (0, 0))


def attend(heads_k, rows, pair_len, raw, angle_cos, angle_sin, query_gain, key_gain):
    rows_all, cols = raw.shape
    cols_q, cols_k = heads_k * (H // KV) * HD, heads_k * HD
    outs = (cols_q, cols_k, cols_k, cols_q)
    return pl.pallas_call(
        functools.partial(attend_kernel, heads_k),
        grid=(rows_all // rows,),
        in_specs=[
            pl.BlockSpec(memory_space=pltpu.SMEM),
            rows_spec(rows, cols),
            rows_spec(rows, HD),
            rows_spec(rows, HD),
            whole_spec((1, HD)),
            whole_spec((1, HD)),
        ],
        out_shape=[jax.ShapeDtypeStruct((rows_all, c), jnp.bfloat16) for c in outs],
        out_specs=[rows_spec(rows, c) for c in outs],
        cost_estimate=pl.CostEstimate(
            flops=4 * rows_all * rows * cols_q,
            bytes_accessed=8 * rows_all * cols,
            transcendentals=rows_all * rows * heads_k * 2,
        ),
        compiler_params=pltpu.CompilerParams(vmem_limit_bytes=32 << 20),
        name="attend",
    )(pair_len, raw, angle_cos, angle_sin, query_gain, key_gain)


def attend_back(
    heads_k, rows, pair_len, raw, angle_cos, angle_sin, query_gain, key_gain, q, k, v, grad_gated
):
    rows_all, cols = raw.shape
    cols_q, cols_k = heads_k * (H // KV) * HD, heads_k * HD
    return pl.pallas_call(
        functools.partial(attend_back_kernel, heads_k),
        grid=(rows_all // rows,),
        in_specs=[
            pl.BlockSpec(memory_space=pltpu.SMEM),
            rows_spec(rows, cols),
            rows_spec(rows, HD),
            rows_spec(rows, HD),
            whole_spec((1, HD)),
            whole_spec((1, HD)),
            rows_spec(rows, cols_q),
            rows_spec(rows, cols_k),
            rows_spec(rows, cols_k),
            rows_spec(rows, cols_q),
        ],
        out_shape=[
            jax.ShapeDtypeStruct((rows_all, cols), jnp.bfloat16),
            jax.ShapeDtypeStruct((8, HD), jnp.float32),
        ],
        out_specs=[rows_spec(rows, cols), whole_spec((8, HD))],
        cost_estimate=pl.CostEstimate(
            flops=14 * rows_all * rows * cols_q,
            bytes_accessed=10 * rows_all * cols,
            transcendentals=rows_all * rows * heads_k * 2,
        ),
        compiler_params=pltpu.CompilerParams(vmem_limit_bytes=32 << 20),
        name="attend_back",
    )(pair_len, raw, angle_cos, angle_sin, query_gain, key_gain, q, k, v, grad_gated)


def after(values, *others):
    return lax.optimization_barrier((values, *others))[0]


def remote_copy(src, dst, send, recv, to_rep, to_fsdp):
    return pltpu.make_async_remote_copy(
        src_ref=src,
        dst_ref=dst,
        send_sem=send,
        recv_sem=recv,
        device_id={"rep": to_rep, "fsdp": to_fsdp},
        device_id_type=MESH,
    )


def greet_all(peers):
    barrier = pltpu.get_barrier_semaphore()
    for to_rep, to_fsdp in peers:
        pl.semaphore_signal(
            barrier, inc=1, device_id={"rep": to_rep, "fsdp": to_fsdp}, device_id_type=MESH
        )
    pl.semaphore_wait(barrier, len(peers))


class GatherRows:
    def __init__(self, n_fsdp, rep, mine, source, target, sems):
        self.n_fsdp, self.rep, self.mine = n_fsdp, rep, mine
        self.source, self.target = source, target
        self.send, self.recv, self.local = sems
        self.half = source.shape[0] // 2

    def copy(self, s, h, to=None, src=None):
        rows = pl.ds(h * self.half, self.half)
        to = s if to is None else to
        return remote_copy(
            self.source.at[rows] if src is None else self.target.at[src, rows],
            self.target.at[s, rows],
            self.send.at[s, h],
            self.recv.at[s, h],
            self.rep,
            flipped(self.mine, to, self.n_fsdp),
        )

    def own(self):
        return pltpu.make_async_copy(self.source, self.target.at[0], self.local)

    def start(self):
        for s, h in ((1, 0), (2, 1), (1, 1), (2, 0)):
            if s < self.n_fsdp:
                self.copy(s, h).start()
        if self.n_fsdp != 4:
            for s in range(3, self.n_fsdp):
                for h in range(2):
                    self.copy(s, h).start()
        self.own().start()

    def forward(self):
        if self.n_fsdp == 4:
            self.copy(1, 0).wait_recv()
            self.copy(3, 0, to=2, src=1).start()
            self.copy(2, 1).wait_recv()
            self.copy(3, 1, to=1, src=2).start()

    def finish(self):
        for s in range(1, self.n_fsdp):
            for h in range(2):
                copy = self.copy(s, h)
                if self.n_fsdp == 4 and (s, h) in ((1, 0), (2, 1)):
                    copy.wait_send()
                else:
                    copy.wait()
        self.own().wait()


def fetch_kernel(n_fsdp, n_rep, widths, ff, *refs):
    (tokens, gains, wq, wg, wk, wv, w_gate, w_up) = refs[:8]
    (tokens_all, gains_all, w_attn, mlp_part) = refs[8:12]
    (ts, tr, tl, gs, gr, ws, wr, zs, zr, cs, cr, ms, mr, ls) = refs[12:]
    rep, mine = lax.axis_index("rep"), lax.axis_index("fsdp")
    core, place = rep % 2, rep // 2
    sib = rep + 1 - 2 * core
    partner = (place + 1 - 2 * (place % 2)) * 2 + core
    deep = wq.shape[0]
    block, part_rows = deep // 4, deep // n_rep
    others = range(1, n_fsdp)
    greet_all([(sib, mine), (partner, mine)] + [(rep, flipped(mine, s, n_fsdp)) for s in others])

    weights = (wq, wg, wk, wv)
    starts = [sum(widths[:i]) for i in range(4)]
    band = (place % 2) * 2 + core
    other_band = (1 - place % 2) * 2 + core

    def gain_copy(s):
        return remote_copy(
            gains, gains_all.at[mine], gs.at[s], gr.at[s], rep, flipped(mine, s, n_fsdp)
        )

    def weight_copy(s, i):
        peer = flipped(mine, s, n_fsdp)
        cols = pl.ds(pl.multiple_of(peer * widths[i], widths[i]), widths[i])
        return remote_copy(
            weights[i].at[pl.ds(band * block, block), cols],
            w_attn.at[pl.ds(mine * deep + band * block, block), pl.ds(starts[i], widths[i])],
            ws.at[s, i],
            wr.at[s, i],
            rep,
            peer,
        )

    def band_at(s, which):
        return w_attn.at[pl.ds(flipped(mine, s, n_fsdp) * deep + which * block, block)]

    def partner_copy(s):
        return remote_copy(band_at(s, band), band_at(s, band), zs.at[s], zr.at[s], partner, mine)

    def sibling_copy(s, k):
        which = band if k == 0 else other_band
        return remote_copy(
            band_at(s, which), band_at(s, which), cs.at[s, k], cr.at[s, k], sib, mine
        )

    def mlp_copy(s, i):
        peer = flipped(mine, s, n_fsdp)
        cols = pl.ds(pl.multiple_of(peer * ff, ff), ff)
        return remote_copy(
            (w_gate, w_up)[i].at[pl.ds(rep * part_rows, part_rows), cols],
            mlp_part.at[s - 1, :, pl.ds(i * ff, ff)],
            ms.at[s, i],
            mr.at[s, i],
            rep,
            peer,
        )

    def own_copy(i):
        cols = pl.ds(pl.multiple_of(mine * widths[i], widths[i]), widths[i])
        return pltpu.make_async_copy(
            weights[i].at[:, cols],
            w_attn.at[pl.ds(mine * deep, deep), pl.ds(starts[i], widths[i])],
            ls.at[i],
        )

    own_gain = pltpu.make_async_copy(gains, gains_all.at[mine], ls.at[4])
    rows = GatherRows(n_fsdp, rep, mine, tokens, tokens_all, (ts, tr, tl))
    for s in others:
        gain_copy(s).start()
        for i in range(4):
            weight_copy(s, i).start()
    rows.start()
    own_gain.start()
    for i in range(4):
        own_copy(i).start()
    for s in others:
        for i in range(4):
            weight_copy(s, i).wait_recv()
        partner_copy(s).start()
        sibling_copy(s, 0).start()
    rows.forward()
    for s in others:
        for i in range(2):
            mlp_copy(s, i).start()
    for s in others:
        partner_copy(s).wait_recv()
        sibling_copy(s, 1).start()
    rows.finish()
    for s in others:
        gain_copy(s).wait()
        partner_copy(s).wait_send()
        for i in range(4):
            weight_copy(s, i).wait_send()
        for i in range(2):
            sibling_copy(s, i).wait()
            mlp_copy(s, i).wait()
    own_gain.wait()
    for i in range(4):
        own_copy(i).wait()


def fetched(n_fsdp, n_rep, widths, ff, tokens, gains, *weights):
    deep = weights[0].shape[0]
    rows, width = tokens.shape
    dma = pltpu.SemaphoreType.DMA
    any_spec = pl.BlockSpec(memory_space=pl.ANY)
    shapes = (
        (n_fsdp, rows, width),
        (n_fsdp,) + gains.shape,
        (n_fsdp * deep, sum(widths)),
        (n_fsdp - 1, deep // n_rep, 2 * ff),
    )
    pair, four = dma((n_fsdp, 2)), dma((n_fsdp, 4))
    one = dma((n_fsdp,))
    return pl.pallas_call(
        functools.partial(fetch_kernel, n_fsdp, n_rep, widths, ff),
        out_shape=[jax.ShapeDtypeStruct(shape, jnp.bfloat16) for shape in shapes],
        in_specs=[any_spec] * 8,
        out_specs=[any_spec] * 4,
        scratch_shapes=[
            pair, pair, dma, one, one, four, four, one, one, pair, pair, pair, pair, dma((5,))
        ],
        compiler_params=pltpu.CompilerParams(collective_id=1, has_side_effects=True),
        name="fetch",
    )(tokens, gains, *weights)


def gather_rows(block):
    n_fsdp = lax.axis_size("fsdp")
    if n_fsdp != 4:
        return [block] + [shift(block, s) for s in range(1, n_fsdp)]
    half = block.shape[0] // 2
    top, low = block[:half], block[half:]
    x_top, y_low = shift(top, 1), shift(low, 2)
    x_low, y_top = shift(low, 1), shift(top, 2)
    d_top, d_low = shift(x_top, 2), shift(y_low, 1)
    return [
        block,
        jnp.concatenate([x_top, x_low]),
        jnp.concatenate([y_top, y_low]),
        jnp.concatenate([d_top, d_low]),
    ]


def scatter_rows(own, parts):
    n_fsdp = lax.axis_size("fsdp")
    if n_fsdp != 4:
        for s in range(1, n_fsdp):
            own = own + in_f32(shift(parts[s - 1], s))
        return own
    half = own.shape[0] // 2
    p_x, p_y, p_d = parts
    r_y = shift(p_d[:half], 1)
    r_x = shift(p_d[half:], 2)
    x_top = shift(p_x[:half], 1)
    y_low = shift(p_y[half:], 2)
    y_top = shift(in_bf16(in_f32(p_y[:half]) + in_f32(r_y)), 2)
    x_low = shift(in_bf16(in_f32(p_x[half:]) + in_f32(r_x)), 1)
    return own + jnp.concatenate(
        [in_f32(x_top) + in_f32(y_top), in_f32(y_low) + in_f32(x_low)]
    )


def shards(
    tokens,
    teacher,
    lengths,
    deal_order,
    attention_gain,
    query_gain,
    key_gain,
    w_query,
    w_key,
    w_value,
    w_outgate,
    w_output,
    mlp_gain,
    w_gate,
    w_up,
    w_down,
):
    n_rep = lax.axis_size("rep")
    n_fsdp = lax.axis_size("fsdp")
    rows, width = tokens.shape
    mine = lax.axis_index("fsdp")
    core = lax.axis_index("rep") % 2
    others = range(1, n_fsdp)
    heads_q, heads_k = H // n_fsdp, KV // n_fsdp
    cols_q, cols_k = heads_q * HD, heads_k * HD
    deep = w_query.shape[0]
    ff = w_down.shape[0]
    rows_all = rows * n_fsdp

    peers = mine ^ jnp.arange(n_fsdp, dtype=jnp.int32)
    devices = lax.axis_index("rep") * n_fsdp + peers
    slot_ids = (devices[:, None] * 2 + jnp.arange(2, dtype=jnp.int32)[None, :]).reshape(-1)
    seq_ids = jnp.arange(lengths.shape[0], dtype=jnp.int32)
    slot_seq = jnp.sum(
        jnp.where(seq_ids[None, :] == slot_ids[:, None], deal_order[None, :], 0), axis=1
    )
    pair_len = jnp.sum(
        jnp.where(seq_ids[None, :] == slot_seq[:, None], lengths[None, :], 0), axis=1
    ).reshape(n_fsdp, 2)
    token_count = jnp.sum(lengths).astype(jnp.float32)
    factor = rows * n_rep * n_fsdp / (2.0 * token_count)
    segments, angle_cos, angle_sin = row_layout(pair_len, rows, HD)
    angle_cos, angle_sin = angle_cos.reshape(rows_all, HD), angle_sin.reshape(rows_all, HD)
    segment = segments[0]
    valid_row = (segment < 2).astype(jnp.float32)

    small = query_gain.shape[0]
    gains_own = jnp.concatenate([attention_gain, mlp_gain, query_gain, key_gain])
    gains_own = jnp.pad(gains_own, (0, 16 * HD - gains_own.shape[0])).reshape(16, HD)
    tokens_all, gains, w_attn, mlp_part = fetched(
        n_fsdp,
        n_rep,
        (cols_q, cols_q, cols_k, cols_k),
        ff,
        tokens,
        gains_own,
        w_query,
        w_outgate,
        w_key,
        w_value,
        w_gate,
        w_up,
    )
    tokens_all = tokens_all.reshape(rows_all, width)
    gains = in_f32(gains.reshape(n_fsdp, 16 * HD))
    attention_gain_f = gains[:, :deep].reshape(-1)
    mlp_gain_f = gains[:, deep : 2 * deep].reshape(-1)
    query_gain_f = gains[:, 2 * deep : 2 * deep + small].reshape(-1)
    key_gain_f = gains[:, 2 * deep + small : 2 * deep + 2 * small].reshape(-1)

    mlp_parts = lax.all_gather(mlp_part, "rep", axis=0)
    w_mlp = jnp.zeros((n_fsdp * deep, 2 * ff), jnp.bfloat16)
    for i, weight in enumerate((w_gate, w_up)):
        own = lax.dynamic_slice(weight, (0, mine * ff), (deep, ff))
        w_mlp = lax.dynamic_update_slice(w_mlp, own, (mine * deep, i * ff))
    for s in others:
        rows_of = mlp_parts[:, s - 1].reshape(deep, 2 * ff)
        w_mlp = lax.dynamic_update_slice(w_mlp, rows_of, ((mine ^ s) * deep, 0))

    tokens_f = in_f32(tokens)
    normed_all = in_bf16(rms_scale(in_f32(tokens_all), attention_gain_f))
    attn_raw = times(normed_all, w_attn)
    head_args = (
        heads_k,
        rows,
        pair_len,
        attn_raw,
        angle_cos,
        angle_sin,
        query_gain_f[None],
        key_gain_f[None],
    )
    queries_b, keys_b, values_b, gated_b = attend(*head_args)

    def summed(left, right, product):
        own = product(left[:rows], right, jnp.float32)
        parts = product(left[rows:], right, jnp.bfloat16)
        return scatter_rows(own, [parts[i * rows : (i + 1) * rows] for i in range(n_fsdp - 1)])

    middle = tokens_f + summed(gated_b, w_output, times)
    normed_mlp, mlp_norm_back = jax.vjp(rms_scale, middle, mlp_gain_f)
    normed_mlp_all = jnp.concatenate(gather_rows(in_bf16(normed_mlp)))
    gate_pre = times(normed_mlp_all, w_mlp[:, :ff])
    up_pre = times(normed_mlp_all, w_mlp[:, ff:])
    hidden, swiglu_back = jax.vjp(swiglu, gate_pre, up_pre)
    hidden_b = in_bf16(hidden)
    result = middle + summed(hidden_b, w_down, times)

    error_rows = (result - in_f32(teacher)) * valid_row[:, None]
    row_sq = jnp.sum(error_rows * error_rows, axis=-1)
    slot_mask = (segment[:, None] == jnp.arange(2, dtype=jnp.int32)[None, :]).astype(jnp.float32)
    seq_loss = jnp.sum(row_sq[:, None] * slot_mask, axis=0) / (2.0 * token_count)
    block_out = in_bf16(result * valid_row[:, None])
    grad_result = 2.0 * factor * error_rows

    grad_branch_all = jnp.concatenate(gather_rows(in_bf16(grad_result)))
    grad_hidden = times_trans(grad_branch_all, w_down)
    grad_gate_pre, grad_up_pre = swiglu_back(grad_hidden)
    grad_gate_b = in_bf16(grad_gate_pre)
    grad_up_b = in_bf16(grad_up_pre)
    grad_mlp_b = jnp.concatenate([grad_gate_b, grad_up_b], axis=1)
    grad_normed_mlp = summed(grad_mlp_b, w_mlp, times_trans)
    grad_middle_norm, grad_mlp_gain = mlp_norm_back(grad_normed_mlp)
    grad_middle = grad_result + grad_middle_norm

    grad_attn_all = jnp.concatenate(gather_rows(in_bf16(grad_middle)))
    grad_gated = times_trans(grad_attn_all, w_output)
    grad_raw_b, head_gains = attend_back(*head_args, queries_b, keys_b, values_b, grad_gated)
    grad_query_gain, grad_key_gain = head_gains[0], head_gains[1]
    grad_normed = summed(grad_raw_b, w_attn, times_trans)
    _, norm_back = jax.vjp(rms_scale, tokens_f, attention_gain_f)
    grad_tokens_norm, grad_attention_gain = norm_back(grad_normed)
    tokens_grad = in_bf16(grad_middle + grad_tokens_norm)

    dgains = sum_everywhere(
        jnp.concatenate([grad_attention_gain, grad_mlp_gain, grad_query_gain, grad_key_gain])[None]
    )[0]

    piece_rows, piece_cols = deep // 2, width // n_fsdp
    units, base = [], 0
    for by_owner, row_blocks, cols in (
        (False, ff // 2 // piece_rows, width),
        (True, n_fsdp, 2 * ff),
        (False, cols_q // 2 // piece_rows, width),
        (True, n_fsdp, 2 * cols_q + 2 * cols_k),
    ):
        units.append(Unit(base, by_owner, row_blocks, cols // piece_cols))
        base += units[-1].count
    pieces = reduced(
        n_fsdp,
        n_rep,
        units,
        piece_rows,
        piece_cols,
        (hidden_b, normed_mlp_all, gated_b, normed_all),
        (grad_branch_all, grad_mlp_b, grad_attn_all, grad_raw_b),
    )
    down, mlp, outp, attn = units

    def by_rows(unit, weight):
        blocks, together = unit.row_blocks, unit.col_blocks
        return widened(
            pieces,
            (2, blocks),
            together,
            lambda c, r: (unit.base // together + r, c, 0, 0),
            weight.shape,
            lambda c, r: (c * blocks + r, 0),
        )

    def by_owners(unit, weight, which):
        together = unit.col_blocks // 2
        return widened(
            pieces,
            (2, n_fsdp),
            together,
            lambda c, f: (unit.base // together + 2 * f + which, c, 0, 0),
            weight.shape,
            lambda c, f: (c, f),
        )

    dw_down = by_rows(down, w_down)
    dw_output = by_rows(outp, w_output)
    dw_gate = by_owners(mlp, w_gate, 0)
    dw_up = by_owners(mlp, w_up, 1)
    dw_query, dw_outgate, dw_key, dw_value = widened_heads(
        pieces,
        attn.base,
        n_fsdp,
        (w_query.shape, w_outgate.shape, w_key.shape, w_value.shape),
    )

    def own_part(start, cols):
        return lax.dynamic_slice(dgains, (start + mine * cols,), (cols,))

    return (
        block_out,
        seq_loss,
        tokens_grad,
        own_part(0, deep),
        own_part(2 * width, small),
        own_part(2 * width + HD, small),
        dw_query,
        dw_key,
        dw_value,
        dw_outgate,
        dw_output,
        own_part(width, deep),
        dw_gate,
        dw_up,
        dw_down,
    )


def solution(mesh):
    return jax.shard_map(
        shards,
        mesh=mesh,
        in_specs=(
            P(("rep", "fsdp"), None),
            P(("rep", "fsdp"), None),
            P(),
            P(),
            P("fsdp"),
            P("fsdp"),
            P("fsdp"),
            P("fsdp", None),
            P("fsdp", None),
            P("fsdp", None),
            P("fsdp", None),
            P("fsdp", None),
            P("fsdp"),
            P("fsdp", None),
            P("fsdp", None),
            P("fsdp", None),
        ),
        out_specs=(
            P(("rep", "fsdp"), None),
            P(("rep", "fsdp")),
            P(("rep", "fsdp"), None),
            P("fsdp"),
            P("fsdp"),
            P("fsdp"),
            P("fsdp", None),
            P("fsdp", None),
            P("fsdp", None),
            P("fsdp", None),
            P("fsdp", None),
            P("fsdp"),
            P("fsdp", None),
            P("fsdp", None),
            P("fsdp", None),
        ),
        check_vma=False,
    )
```

```python
import functools

import jax
import jax.numpy as jnp
from jax import lax
from jax.experimental import pallas as pl
from jax.experimental.pallas import tpu as pltpu
from jax.sharding import PartitionSpec as P

MESH = pl.DeviceIdType.MESH

H = 16
KV = 8
HD = 128


EPS_NORM = 1e-06
ROPE_BASE = 1000000.0
NEG_FILL = -1e30


def rms_scale(values, gain_vec):
    return (
        values * lax.rsqrt(jnp.mean(values * values, axis=-1, keepdims=True) + EPS_NORM) * gain_vec
    )


def row_layout(pair_len, row_count, head_dim):
    row_index = jnp.arange(row_count, dtype=jnp.int32)[None, :]
    head_len = pair_len[:, :1]
    both_len = pair_len[:, :1] + pair_len[:, 1:]
    segment = (row_index >= head_len).astype(jnp.int32) + (row_index >= both_len).astype(jnp.int32)
    start_row = jnp.where(segment == 0, 0, jnp.where(segment == 1, head_len, both_len))
    position = (row_index - start_row).astype(jnp.float32)
    inv_freq = jnp.power(ROPE_BASE, -jnp.arange(0, head_dim, 2, dtype=jnp.float32) / head_dim)
    angles = position[..., None] * inv_freq
    angle_cos, angle_sin = jnp.cos(angles), jnp.sin(angles)
    return (
        segment,
        jnp.concatenate([angle_cos, angle_cos], axis=-1),
        jnp.concatenate([angle_sin, angle_sin], axis=-1),
    )


def times(left_side, right_side, out=jnp.float32):
    return jnp.dot(left_side, right_side, preferred_element_type=jnp.float32).astype(out)


def times_trans(left_side, right_side, out=jnp.float32):
    return lax.dot_general(
        left_side, right_side, (((1,), (1,)), ((), ())), preferred_element_type=jnp.float32
    ).astype(out)


def trans_times(left_side, right_side, out=jnp.float32):
    return lax.dot_general(
        left_side, right_side, (((0,), (0,)), ((), ())), preferred_element_type=jnp.float32
    ).astype(out)


def swiglu(gate_pre, up_pre):
    return jax.nn.silu(gate_pre) * up_pre


def in_f32(values):
    return values.astype(jnp.float32)


def in_bf16(values):
    return values.astype(jnp.bfloat16)


def shift(values, step):
    n_fsdp = lax.axis_size("fsdp")
    return lax.ppermute(values, "fsdp", [(i, i ^ step) for i in range(n_fsdp)])


def sibling(values):
    n_rep = lax.axis_size("rep")
    return lax.ppermute(values, "rep", [(i, i ^ 1) for i in range(n_rep)])


def sum_everywhere(values):
    for axis in ("fsdp", "rep"):
        n = lax.axis_size(axis)
        step = 1
        while step < n:
            values = values + lax.ppermute(values, axis, [(i, i ^ step) for i in range(n)])
            step *= 2
    return values


def flipped(index, step, n):
    out, bit = index, 1
    while bit < n:
        has = (step // bit) % 2
        out = out + has * bit * (1 - 2 * ((index // bit) % 2))
        bit *= 2
    return out


def at_least(value, bound, span):
    span = max(span, bound)
    return (value + (span - bound)) // span


class Unit:
    def __init__(self, base, by_owner, row_blocks, col_blocks):
        self.base, self.by_owner = base, by_owner
        self.row_blocks, self.col_blocks = row_blocks, col_blocks
        self.count = row_blocks * col_blocks


LAG_B, LAG_C, LAG_D, LAG_E, LAG_G = 2, 4, 6, 8, 11
RING = 4


ROW_STEP = 32
TILES = 8


def norm_back(grad, raw, gain):
    scale = lax.rsqrt(jnp.mean(raw * raw, axis=-1, keepdims=True) + EPS_NORM)
    unit = raw * scale
    inner = grad * gain
    return scale * (inner - unit * jnp.mean(inner * unit, axis=-1, keepdims=True)), grad * unit


def backward_kernel(n_fsdp, n_rep, heads_k, units, piece_rows, piece_cols, *refs):
    (hidden, normed_mlp, gated, normed, grad_branch, grad_mlp, w_mlp, w_output, w_attn) = refs[:9]
    (middle, grad_result, tokens, attn_raw, all_cos, all_sin, all_q, all_k, all_v) = refs[9:18]
    (gains, head_gains, pair_ref) = refs[18:21]
    (out, grad_attn, grad_raw, inb, xb, tokens_grad, gain_out, head_gain_out) = refs[21:29]
    (lm, lo, rh, sb, kb, r1, c_slot, d_slot, big, wt, own, pbuf, land_a, land_b) = refs[29:43]
    (mid, gres, tok, ga, wo, raw, cs, sn, qb, kvb, vb, gb, gg, ob) = refs[43:57]
    (tile_sem, r1s, r1r, ins, inr, xs, xr, os_, fs, fr, gs, gr, ls) = refs[57:70]
    (load_sem, first_sem, wt_sem, ps, pr, qs, qr, ag_s, ag_r, ag_l, block_sem) = refs[70:]
    lefts = (hidden, normed_mlp, gated, normed)
    rights = (grad_branch, grad_mlp, grad_attn, grad_raw)
    total = sum(unit.count for unit in units)
    rows, width = own.shape
    rows_all = n_fsdp * rows
    ff = grad_mlp.shape[1] // 2
    tile = width // TILES
    others = range(1, n_fsdp)
    rep, mine = lax.axis_index("rep"), lax.axis_index("fsdp")
    core, place = rep % 2, rep // 2
    n_line = n_rep // 2
    half = n_line // 2
    side = place // half
    depth = place * (1 - side) + (n_line - 1 - place) * side
    inward = (place + 1 - 2 * side) * 2 + core
    outward = (place - 1 + 2 * side) * 2 + core
    sib = rep + 1 - 2 * core
    at_middle = depth == half - 1

    barrier = pltpu.get_barrier_semaphore()

    def greet(to_rep, to_fsdp):
        pl.semaphore_signal(
            barrier, inc=1, device_id={"rep": to_rep, "fsdp": to_fsdp}, device_id_type=MESH
        )

    greet(sib, mine)
    greet(inward, mine)
    for s in others:
        greet(rep, flipped(mine, s, n_fsdp))

    @pl.when(depth == 0)
    def _():
        pl.semaphore_wait(barrier, 1 + n_fsdp)

    @pl.when(depth > 0)
    def _():
        greet(outward, mine)
        pl.semaphore_wait(barrier, 2 + n_fsdp)


    def r1_copy(p):
        return remote_copy(sb.at[p % RING], r1.at[p], r1s.at[p], r1r.at[p], sib, mine)

    def in_copy(p):
        return remote_copy(r1.at[p], inb.at[p], ins.at[p], inr.at[p], inward, mine)

    def x_copy(p):
        return remote_copy(r1.at[p], xb.at[p], xs.at[p], xr.at[p], inward, mine)

    def o_copy(p, src):
        return remote_copy(src.at[p], xb.at[p], os_.at[p], xr.at[p], outward, mine)

    def inside_of(p, unit):
        inside = at_least(p, unit.base, total - unit.base)
        stop = unit.base + unit.count
        if stop < total:
            inside = inside * (1 - at_least(p, stop, total - stop))
        return inside

    def owner_of(p):
        step = 0
        for unit in units:
            if unit.by_owner:
                i = p - unit.base
                step = step + inside_of(p, unit) * (n_fsdp - 1 - i // unit.col_blocks)
        return step

    def spot(p, source):
        where = p
        for unit in units:
            if unit.by_owner:
                i = p - unit.base
                spread = unit.base + source * unit.col_blocks + i % unit.col_blocks
                where = where + inside_of(p, unit) * (spread - p)
        return where

    def f_copy(p, step):
        return remote_copy(
            r1.at[p],
            out.at[spot(p, mine), core],
            fs.at[p],
            fr.at[p],
            rep,
            flipped(mine, step, n_fsdp),
        )

    def g_copy(p, src, where):
        return remote_copy(src, out.at[where, core], gs.at[p], gr.at[p], sib, mine)

    def l_copy(p):
        return pltpu.make_async_copy(r1.at[p], out.at[spot(p, mine), core], ls.at[p])

    def c_load(p):
        return pltpu.make_async_copy(inb.at[p], c_slot, load_sem.at[0])

    def d_load(p):
        return pltpu.make_async_copy(xb.at[p], d_slot, load_sem.at[1])

    def e_load(p):
        return pltpu.make_async_copy(xb.at[p], r1.at[p], load_sem.at[2])

    def add_into(p, other):
        r1[p] = in_bf16(in_f32(r1[p]) + in_f32(other))

    def begin_c(p):
        @pl.when(depth > 0)
        def _():
            in_copy(p).wait_recv()
            c_load(p).start()

    def begin_d(p):
        @pl.when(at_middle)
        def _():
            x_copy(p).wait_recv()
            d_load(p).start()

    def begin_e(p):
        @pl.when(depth < half - 1)
        def _():
            o_copy(p, xb).wait_recv()

            @pl.when(depth > 0)
            def _():
                o_copy(p, xb).start()

            in_copy(p).wait_send()
            e_load(p).start()

    def end_b(p):
        r1_copy(p).wait_recv()
        add_into(p, kb[p % RING])
        if half > 1:

            @pl.when(depth == 0)
            def _():
                in_copy(p).start()
        else:
            x_copy(p).start()

    def end_c(p):
        @pl.when(depth > 0)
        def _():
            c_load(p).wait()
            add_into(p, c_slot[...])

            @pl.when(depth < half - 1)
            def _():
                in_copy(p).start()

            @pl.when(at_middle)
            def _():
                x_copy(p).start()

    def end_d(p):
        @pl.when(at_middle)
        def _():
            d_load(p).wait()
            x_copy(p).wait_send()
            add_into(p, d_slot[...])

            @pl.when(depth > 0)
            def _():
                o_copy(p, r1).start()

    def end_e(p):
        @pl.when(depth < half - 1)
        def _():
            e_load(p).wait()

        step = owner_of(p)

        @pl.when(step == 0)
        def _():
            l_copy(p).start()
            g_copy(p, r1.at[p], spot(p, mine)).start()

        @pl.when(step > 0)
        def _():
            f_copy(p, step).start()

    def end_g(p):
        step = owner_of(p)

        @pl.when(step > 0)
        def _():
            f_copy(p, step).wait_recv()
            where = spot(p, flipped(mine, step, n_fsdp))
            g_copy(p, out.at[where, core], where).start()

    def run(stages, t):
        for lag, stage in stages:
            pl.when((t >= lag) & (t < total + lag))(functools.partial(stage, t - lag))

    def begin(t):
        run([(LAG_C, begin_c), (LAG_D, begin_d), (LAG_E, begin_e)], t)

    def end(t):
        run([(LAG_B, end_b), (LAG_C, end_c), (LAG_D, end_d), (LAG_E, end_e), (LAG_G, end_g)], t)

    def tiles(u, i, slot):
        unit = units[u]
        r, j = i // unit.col_blocks, i % unit.col_blocks
        if unit.by_owner:
            owner = flipped(mine, n_fsdp - 1 - r, n_fsdp)
            first = owner * 2 * piece_rows + core * piece_rows
            second = owner * 2 * piece_rows + (1 - core) * piece_rows
        else:
            first = core * unit.row_blocks * piece_rows + r * piece_rows
            second = (1 - core) * unit.row_blocks * piece_rows + r * piece_rows
        first = pl.ds(pl.multiple_of(first, piece_rows), piece_rows)
        second = pl.ds(pl.multiple_of(second, piece_rows), piece_rows)
        cols = pl.ds(pl.multiple_of(j * piece_cols, piece_cols), piece_cols)
        return [
            pltpu.make_async_copy(lefts[u].at[:, first], lm.at[slot], tile_sem.at[slot, 0]),
            pltpu.make_async_copy(lefts[u].at[:, second], lo.at[slot], tile_sem.at[slot, 1]),
            pltpu.make_async_copy(rights[u].at[:, cols], rh.at[slot], tile_sem.at[slot, 2]),
        ]


    first_pairs = (
        (grad_mlp.at[:, pl.ds(0, ff)], big.at[pl.ds(0, rows_all)]),
        (grad_mlp.at[:, pl.ds(ff, ff)], big.at[pl.ds(rows_all, rows_all)]),
        (middle, mid),
        (grad_result, gres),
        (tokens, tok),
        (w_output, wo),
    )

    def first_loads(which):
        return [pltpu.make_async_copy(*first_pairs[i], first_sem.at[i]) for i in which]

    def attn_load():
        return pltpu.make_async_copy(w_attn, big.at[pl.ds(0, width)], first_sem.at[6])

    def tile_of(j):
        return pl.ds(pl.multiple_of(j * tile, tile), tile)

    def wt_load(j):
        return pltpu.make_async_copy(w_mlp.at[tile_of(j)], wt.at[j % 2], wt_sem.at[j % 2])

    def p_copy(s, j):
        return remote_copy(
            pbuf.at[s - 1, :, tile_of(j)],
            land_a.at[s - 1, :, tile_of(j)],
            ps.at[s, j],
            pr.at[s, j],
            rep,
            flipped(mine, s, n_fsdp),
        )

    def q_copy(s):
        return remote_copy(
            pbuf.at[s - 1], land_b.at[s - 1], qs.at[s], qr.at[s], rep, flipped(mine, s, n_fsdp)
        )

    gather = GatherRows(n_fsdp, rep, mine, ga, grad_attn, (ag_s, ag_r, ag_l))

    def mlp_products(j):
        @pl.when(j == 0)
        def _():
            for copy in first_loads((0, 1)):
                copy.wait()

        wt_load(j).wait()

        @pl.when(j + 1 < TILES)
        def _():
            wt_load(j + 1).start()

        for s in (*others, 0):
            part = product_of(big[s * rows : (s + 1) * rows], wt[j % 2, :, :ff], 1, 1)
            part += product_of(
                big[rows_all + s * rows : rows_all + (s + 1) * rows], wt[j % 2, :, ff:], 1, 1
            )
            if s == 0:
                own[:, tile_of(j)] = part
            else:
                pbuf[s - 1, :, tile_of(j)] = in_bf16(part)
                p_copy(s, j).start()

    def middle_back():
        attn_load().start()
        for copy in first_loads((2, 3)):
            copy.wait()

        def wait_tiles(j, carry):
            for s in others:
                p_copy(s, j).wait()
            return carry

        lax.fori_loop(0, TILES, wait_tiles, 0)
        gain_out[...] = jnp.zeros_like(gain_out)
        head_gain_out[...] = jnp.zeros_like(head_gain_out)

        def some_rows(r, carry):
            cut = pl.ds(pl.multiple_of(r * ROW_STEP, ROW_STEP), ROW_STEP)
            grad = own[cut]
            for s in others:
                grad += in_f32(land_a[s - 1, cut])
            back, gain_rows = norm_back(grad, mid[cut], gains[1:2])
            gain_out[1:2] += jnp.sum(gain_rows, axis=0, keepdims=True)
            back = gres[cut] + back
            gres[cut] = back
            ga[cut] = in_bf16(back)
            return carry

        lax.fori_loop(0, rows // ROW_STEP, some_rows, 0)
        gather.start()

    def block_loads(s):
        cut = pl.ds(pl.multiple_of(s * rows, rows), rows)
        pairs = (
            (attn_raw, raw), (all_cos, cs), (all_sin, sn), (all_q, qb), (all_k, kvb), (all_v, vb)
        )
        copies = [
            pltpu.make_async_copy(src.at[cut], dst, block_sem.at[i])
            for i, (src, dst) in enumerate(pairs)
        ]
        return copies

    def grad_load(s):
        cut = pl.ds(pl.multiple_of(s * rows, rows), rows)
        return pltpu.make_async_copy(grad_attn.at[cut], gb, block_sem.at[6])

    def store(s):
        cut = pl.ds(pl.multiple_of(s * rows, rows), rows)
        return pltpu.make_async_copy(ob, grad_raw.at[cut], block_sem.at[7])

    def heads_back(s, heads):
        attend_back(
            heads_k,
            heads,
            block_mask(pair_ref, rows, s),
            cs[...],
            sn[...],
            head_gains[0:1],
            head_gains[1:2],
            raw,
            qb,
            kvb,
            vb,
            gg,
            ob,
            head_gain_out,
        )

    early = heads_k // 2

    def block_first(s):
        copies = block_loads(s)
        for copy in copies:
            copy.start()

        @pl.when(s == 0)
        def _():
            first_loads((5,))[0].wait()
            gb[...] = ga[...]

        for k in others:

            @pl.when(s == k)
            def _(k=k):
                gather.arrive(k)

        @pl.when(s > 0)
        def _():
            copy = grad_load(s)
            copy.start()
            copy.wait()

        gg[...] = product_of(gb[...], wo[...], 1, 1)
        for copy in copies:
            copy.wait()
        heads_back(s, range(early))

    def block_second(s):
        heads_back(s, range(early, heads_k))
        store(s).start()

    def block_third(s):
        store(s).wait()

        @pl.when(s == 0)
        def _():
            attn_load().wait()

        def one_tile(j, carry):
            part = product_of(ob[...], big[tile_of(j)], 1, 1)

            @pl.when(s == 0)
            def _():
                own[:, tile_of(j)] = part

            @pl.when(s > 0)
            def _():
                pbuf[s - 1, :, tile_of(j)] = in_bf16(part)

            return carry

        lax.fori_loop(0, TILES, one_tile, 0)

        @pl.when(s > 0)
        def _():
            q_copy(s).start()

    def tokens_back():
        first_loads((4,))[0].wait()
        for s in others:
            q_copy(s).wait()

        def some_rows(r, carry):
            cut = pl.ds(pl.multiple_of(r * ROW_STEP, ROW_STEP), ROW_STEP)
            grad = own[cut]
            for s in others:
                grad += in_f32(land_b[s - 1, cut])
            back, gain_rows = norm_back(grad, in_f32(tok[cut]), gains[0:1])
            gain_out[0:1] += jnp.sum(gain_rows, axis=0, keepdims=True)
            tokens_grad[cut] = in_bf16(gres[cut] + back)
            return carry

        lax.fori_loop(0, rows // ROW_STEP, some_rows, 0)

    def tasks(u, i):
        if u == 0:
            pl.when(i < TILES)(lambda: mlp_products(i))
        if u == 1:
            pl.when(i == 2)(middle_back)
            pl.when(i == 6)(gather.forward)
            pl.when(i == 12)(lambda: gather.own().wait())
            last = 12 + 3 * (n_fsdp - 1)
            busy = ((i >= 6) & (i < 9)) | ((i >= 12) & (i < last))
            s = at_least(i, 9, units[1].count) * ((i - 9) // 3)
            for phase, task in enumerate((block_first, block_second, block_third)):
                pl.when(busy & (i % 3 == phase))(functools.partial(task, s))
        if u == 2:

            @pl.when(i == 2)
            def _():
                gather.sent()
                tokens_back()

    def product(left, right):
        return product_of(left, right, 0, 0)

    for copy in first_loads(range(6)):
        copy.start()
    wt_load(0).start()
    for copy in tiles(0, 0, 0):
        copy.start()
    for u, unit in enumerate(units):

        def step(i, carry, u=u, unit=unit):
            t = unit.base + i
            slot = t % 2
            begin(t)
            for copy in tiles(u, i, slot):
                copy.wait()

            @pl.when(i + 1 < unit.count)
            def _():
                for copy in tiles(u, i + 1, 1 - slot):
                    copy.start()

            if u + 1 < len(units):

                @pl.when(i + 1 == unit.count)
                def _():
                    for copy in tiles(u + 1, 0, 1 - slot):
                        copy.start()

            @pl.when(t >= RING)
            def _():
                r1_copy(t - RING).wait_send()

            sb[t % RING] = in_bf16(product(lo[slot], rh[slot]))
            r1_copy(t).start()
            kb[t % RING] = product(lm[slot], rh[slot])
            end(t)
            tasks(u, i)
            return carry

        lax.fori_loop(0, unit.count, step, 0)

    def drain(t, carry):
        begin(t)
        end(t)
        return carry

    lax.fori_loop(total, total + LAG_G, drain, 0)

    def finish(p, carry):
        @pl.when(p >= total - RING)
        def _():
            r1_copy(p).wait_send()

        @pl.when(depth > 0)
        def _():
            o_copy(p, r1).wait_send()

        step = owner_of(p)

        @pl.when(step == 0)
        def _():
            l_copy(p).wait()

        @pl.when(step > 0)
        def _():
            f_copy(p, step).wait_send()

        g_copy(p, r1.at[p], p).wait()
        return carry

    lax.fori_loop(0, total, finish, 0)


def backward(n_fsdp, n_rep, heads_k, units, piece_rows, piece_cols, args):
    total = sum(unit.count for unit in units)
    rows_all, rows = args[0].shape[0], args[9].shape[0]
    width, cols = args[8].shape
    cols_q, cols_k = heads_k * (H // KV) * HD, heads_k * HD
    two_ff = args[5].shape[1]
    dma = pltpu.SemaphoreType.DMA
    piece = (piece_rows, piece_cols)
    low, full = jnp.bfloat16, jnp.float32
    any_spec = pl.BlockSpec(memory_space=pl.ANY)
    vmem = pl.BlockSpec(memory_space=pltpu.VMEM)
    flops = sum(4 * unit.count for unit in units) * rows_all * piece_rows * piece_cols
    outs = (
        ((total, 2) + piece, low),
        ((rows_all, width), low),
        ((rows_all, cols), low),
        ((total,) + piece, low),
        ((total,) + piece, low),
        ((rows, width), low),
        ((8, width), full),
        ((8, HD), full),
    )
    scratch = (
        ((2, rows_all, piece_rows), low),
        ((2, rows_all, piece_rows), low),
        ((2, rows_all, piece_cols), low),
        ((RING,) + piece, low),
        ((RING,) + piece, full),
        ((total,) + piece, low),
        (piece, low),
        (piece, low),
        ((max(2 * rows_all, width), cols), low),
        ((2, width // TILES, two_ff), low),
        ((rows, width), full),
        ((n_fsdp - 1, rows, width), low),
        ((n_fsdp - 1, rows, width), low),
        ((n_fsdp - 1, rows, width), low),
        ((rows, width), full),
        ((rows, width), full),
        ((rows, width), low),
        ((rows, width), low),
        ((cols_q, width), low),
        ((rows, cols), full),
        ((rows, HD), full),
        ((rows, HD), full),
        ((rows, cols_q), low),
        ((rows, cols_k), low),
        ((rows, cols_k), low),
        ((rows, width), low),
        ((rows, cols_q), full),
        ((rows, cols), low),
    )
    return pl.pallas_call(
        functools.partial(
            backward_kernel, n_fsdp, n_rep, heads_k, units, piece_rows, piece_cols
        ),
        out_shape=[jax.ShapeDtypeStruct(shape, kind) for shape, kind in outs],
        in_specs=[any_spec] * 18 + [vmem] * 2 + [pl.BlockSpec(memory_space=pltpu.SMEM)],
        out_specs=[any_spec] * 5 + [vmem] * 3,
        scratch_shapes=[pltpu.VMEM(shape, kind) for shape, kind in scratch]
        + [dma((2, 3))]
        + [dma((total,)) for _ in range(12)]
        + [
            dma((3,)),
            dma((7,)),
            dma((2,)),
            dma((n_fsdp, TILES)),
            dma((n_fsdp, TILES)),
            dma((n_fsdp,)),
            dma((n_fsdp,)),
            dma((n_fsdp, 2)),
            dma((n_fsdp, 2)),
            dma,
            dma((8,)),
        ],
        compiler_params=pltpu.CompilerParams(
            collective_id=0, has_side_effects=True, vmem_limit_bytes=62 << 20
        ),
        cost_estimate=pl.CostEstimate(flops=2 * flops, bytes_accessed=1 << 30, transcendentals=0),
        name="backward",
    )(*args)


def widen_kernel(in_ref, out_ref):
    cols = in_ref.shape[-1]
    for i in range(in_ref.shape[0]):
        out_ref[:, i * cols : (i + 1) * cols] = in_ref[i, 0].astype(jnp.float32)


def widened(pieces, grid, together, where, shape, place):
    rows, cols = pieces.shape[2:]
    return pl.pallas_call(
        widen_kernel,
        grid=grid,
        out_shape=jax.ShapeDtypeStruct(shape, jnp.float32),
        in_specs=[pl.BlockSpec((together, 1, rows, cols), where)],
        out_specs=pl.BlockSpec((rows, together * cols), place),
        name="widen",
    )(pieces)


def widen_heads_kernel(query_in, gate_in, pair_in, query_out, gate_out, key_out, value_out):
    half = key_out.shape[1]
    query_out[...] = query_in[0, 0].astype(jnp.float32)
    gate_out[...] = gate_in[0, 0].astype(jnp.float32)
    key_out[...] = pair_in[0, 0, :, :half].astype(jnp.float32)
    value_out[...] = pair_in[0, 0, :, half:].astype(jnp.float32)


def widened_heads(pieces, base, n_fsdp, shapes):
    rows, cols = pieces.shape[2:]

    def where(j):
        return lambda c, f: (base + 3 * f + j, c, 0, 0)

    widths = (cols, cols, cols // 2, cols // 2)
    return pl.pallas_call(
        widen_heads_kernel,
        grid=(2, n_fsdp),
        out_shape=[jax.ShapeDtypeStruct(shape, jnp.float32) for shape in shapes],
        in_specs=[pl.BlockSpec((1, 1, rows, cols), where(j)) for j in range(3)],
        out_specs=[pl.BlockSpec((rows, wide), lambda c, f: (c, f)) for wide in widths],
        name="widen_heads",
    )(pieces, pieces, pieces)


def block_mask(pair_ref, rows, block):
    head_len = pair_ref[block, 0]
    both_len = head_len + pair_ref[block, 1]
    query_row = lax.broadcasted_iota(jnp.int32, (rows, rows), 0)
    key_row = lax.broadcasted_iota(jnp.int32, (rows, rows), 1)

    def segment(index):
        return (index >= head_len).astype(jnp.int32) + (index >= both_len).astype(jnp.int32)

    return (segment(query_row) == segment(key_row)) & (key_row <= query_row)


def turn(values):
    half_dim = values.shape[-1] // 2
    return jnp.concatenate([-values[:, half_dim:], values[:, :half_dim]], axis=-1)


def head_forward(raw, gain, angle_cos, angle_sin):
    values = raw * lax.rsqrt(jnp.mean(raw * raw, axis=-1, keepdims=True) + EPS_NORM) * gain
    return in_bf16(values * angle_cos + turn(values) * angle_sin)


def head_backward(grad, raw, gain, angle_cos, angle_sin):
    grad = grad * angle_cos - turn(grad * angle_sin)
    scale = lax.rsqrt(jnp.mean(raw * raw, axis=-1, keepdims=True) + EPS_NORM)
    unit = raw * scale
    gain_rows = grad * unit
    inner = grad * gain
    return scale * (inner - unit * jnp.mean(inner * unit, axis=-1, keepdims=True)), gain_rows


def product_of(left, right, left_dim, right_dim):
    return lax.dot_general(
        left, right, (((left_dim,), (right_dim,)), ((), ())), preferred_element_type=jnp.float32
    )


def softmax_of(queries, keys, allowed):
    scores = jnp.where(allowed, product_of(queries, keys, 1, 1) * HD ** (-0.5), NEG_FILL)
    exponent = jnp.exp(scores - jnp.max(scores, axis=-1, keepdims=True))
    return exponent / jnp.sum(exponent, axis=-1, keepdims=True)


def attend_kernel(
    heads_k, pair_ref, raw_ref, cos_ref, sin_ref, qg_ref, kg_ref, q_ref, k_ref, v_ref, gated_ref
):
    group = H // KV
    cols_q, cols_k = heads_k * group * HD, heads_k * HD
    allowed = block_mask(pair_ref, raw_ref.shape[0], pl.program_id(0))
    angle_cos, angle_sin = cos_ref[...], sin_ref[...]
    for j in range(heads_k):
        own = slice(j * HD, (j + 1) * HD)
        keys = head_forward(
            raw_ref[:, 2 * cols_q + j * HD : 2 * cols_q + (j + 1) * HD],
            kg_ref[...],
            angle_cos,
            angle_sin,
        )
        start = 2 * cols_q + cols_k + j * HD
        values = in_bf16(raw_ref[:, start : start + HD])
        k_ref[:, own] = keys
        v_ref[:, own] = values
        for h in range(j * group, (j + 1) * group):
            cut = slice(h * HD, (h + 1) * HD)
            queries = head_forward(raw_ref[:, cut], qg_ref[...], angle_cos, angle_sin)
            q_ref[:, cut] = queries
            probs = in_bf16(softmax_of(queries, keys, allowed))
            context = product_of(probs, values, 1, 0)
            gate = raw_ref[:, cols_q + h * HD : cols_q + (h + 1) * HD]
            gated_ref[:, cut] = in_bf16(context * jax.nn.sigmoid(gate))


def attend_back(
    heads_k,
    heads,
    allowed,
    angle_cos,
    angle_sin,
    query_gain,
    key_gain,
    raw_ref,
    q_ref,
    k_ref,
    v_ref,
    grad_ref,
    out_ref,
    gain_ref,
):
    group = H // KV
    cols_q, cols_k = heads_k * group * HD, heads_k * HD
    for j in heads:
        own = slice(j * HD, (j + 1) * HD)
        keys, values = k_ref[:, own], v_ref[:, own]
        grad_keys, grad_values = 0.0, 0.0
        for h in range(j * group, (j + 1) * group):
            cut = slice(h * HD, (h + 1) * HD)
            gate_cut = slice(cols_q + h * HD, cols_q + (h + 1) * HD)
            queries, grad_gated = q_ref[:, cut], grad_ref[:, cut]
            probs = softmax_of(queries, keys, allowed)
            probs_b = in_bf16(probs)
            context = product_of(probs_b, values, 1, 0)
            gate = jax.nn.sigmoid(raw_ref[:, gate_cut])
            grad_context = in_bf16(grad_gated * gate)
            out_ref[:, gate_cut] = in_bf16(grad_gated * context * gate * (1.0 - gate))
            grad_probs = product_of(grad_context, values, 1, 1)
            grad_scores = in_bf16(
                probs * (grad_probs - jnp.sum(probs * grad_probs, axis=-1, keepdims=True))
            )
            grad_values += product_of(probs_b, grad_context, 0, 0)
            grad_keys += product_of(grad_scores, queries, 0, 0)
            grad_queries = product_of(grad_scores, keys, 1, 0) * HD ** (-0.5)
            grad_raw, gain_rows = head_backward(
                grad_queries, raw_ref[:, cut], query_gain, angle_cos, angle_sin
            )
            out_ref[:, cut] = in_bf16(grad_raw)
            gain_ref[0:1, :] += jnp.sum(gain_rows, axis=0, keepdims=True)
        key_start = 2 * cols_q + j * HD
        grad_raw, gain_rows = head_backward(
            grad_keys * HD ** (-0.5),
            raw_ref[:, key_start : key_start + HD],
            key_gain,
            angle_cos,
            angle_sin,
        )
        out_ref[:, key_start : key_start + HD] = in_bf16(grad_raw)
        gain_ref[1:2, :] += jnp.sum(gain_rows, axis=0, keepdims=True)
        value_start = 2 * cols_q + cols_k + j * HD
        out_ref[:, value_start : value_start + HD] = in_bf16(grad_values)


def rows_spec(rows, cols):
    return pl.BlockSpec((rows, cols), lambda s: (s, 0))


def whole_spec(shape):
    return pl.BlockSpec(shape, lambda s: (0, 0))


def attend(heads_k, rows, pair_len, raw, angle_cos, angle_sin, query_gain, key_gain):
    rows_all, cols = raw.shape
    cols_q, cols_k = heads_k * (H // KV) * HD, heads_k * HD
    outs = (cols_q, cols_k, cols_k, cols_q)
    return pl.pallas_call(
        functools.partial(attend_kernel, heads_k),
        grid=(rows_all // rows,),
        in_specs=[
            pl.BlockSpec(memory_space=pltpu.SMEM),
            rows_spec(rows, cols),
            rows_spec(rows, HD),
            rows_spec(rows, HD),
            whole_spec((1, HD)),
            whole_spec((1, HD)),
        ],
        out_shape=[jax.ShapeDtypeStruct((rows_all, c), jnp.bfloat16) for c in outs],
        out_specs=[rows_spec(rows, c) for c in outs],
        cost_estimate=pl.CostEstimate(
            flops=4 * rows_all * rows * cols_q,
            bytes_accessed=8 * rows_all * cols,
            transcendentals=rows_all * rows * heads_k * 2,
        ),
        compiler_params=pltpu.CompilerParams(vmem_limit_bytes=32 << 20),
        name="attend",
    )(pair_len, raw, angle_cos, angle_sin, query_gain, key_gain)


def after(values, *others):
    return lax.optimization_barrier((values, *others))[0]


def remote_copy(src, dst, send, recv, to_rep, to_fsdp):
    return pltpu.make_async_remote_copy(
        src_ref=src,
        dst_ref=dst,
        send_sem=send,
        recv_sem=recv,
        device_id={"rep": to_rep, "fsdp": to_fsdp},
        device_id_type=MESH,
    )


def greet_all(peers):
    barrier = pltpu.get_barrier_semaphore()
    for to_rep, to_fsdp in peers:
        pl.semaphore_signal(
            barrier, inc=1, device_id={"rep": to_rep, "fsdp": to_fsdp}, device_id_type=MESH
        )
    pl.semaphore_wait(barrier, len(peers))


class GatherRows:
    def __init__(self, n_fsdp, rep, mine, source, target, sems):
        self.n_fsdp, self.rep, self.mine = n_fsdp, rep, mine
        self.source, self.target = source, target
        self.send, self.recv, self.local = sems
        self.rows = source.shape[0]
        self.half = self.rows // 2
        self.relay = ((1, 0), (2, 1)) if n_fsdp == 4 else ()

    def copy(self, s, h, to=None, src=None):
        to = s if to is None else to
        return remote_copy(
            self.source.at[pl.ds(h * self.half, self.half)]
            if src is None
            else self.target.at[pl.ds(src * self.rows + h * self.half, self.half)],
            self.target.at[pl.ds(s * self.rows + h * self.half, self.half)],
            self.send.at[s, h],
            self.recv.at[s, h],
            self.rep,
            flipped(self.mine, to, self.n_fsdp),
        )

    def own(self):
        return pltpu.make_async_copy(
            self.source, self.target.at[pl.ds(0, self.rows)], self.local
        )

    def start(self):
        for s, h in ((1, 0), (2, 1), (1, 1), (2, 0)):
            if s < self.n_fsdp:
                self.copy(s, h).start()
        if self.n_fsdp != 4:
            for s in range(3, self.n_fsdp):
                for h in range(2):
                    self.copy(s, h).start()
        self.own().start()

    def forward(self):
        if self.n_fsdp == 4:
            self.copy(1, 0).wait_recv()
            self.copy(3, 0, to=2, src=1).start()
            self.copy(2, 1).wait_recv()
            self.copy(3, 1, to=1, src=2).start()

    def arrive(self, s):
        for h in range(2):
            if (s, h) not in self.relay:
                self.copy(s, h).wait_recv()

    def sent(self):
        for s in range(1, self.n_fsdp):
            for h in range(2):
                self.copy(s, h).wait_send()

    def finish(self):
        for s in range(1, self.n_fsdp):
            self.arrive(s)
        self.sent()
        self.own().wait()


def fetch_kernel(n_fsdp, n_rep, widths, ff, *refs):
    (tokens, gains, wq, wg, wk, wv, w_gate, w_up) = refs[:8]
    (tokens_all, gains_all, w_attn, mlp_part) = refs[8:12]
    (ts, tr, tl, gs, gr, ws, wr, zs, zr, cs, cr, ms, mr, ls) = refs[12:]
    rep, mine = lax.axis_index("rep"), lax.axis_index("fsdp")
    core, place = rep % 2, rep // 2
    sib = rep + 1 - 2 * core
    partner = (place + 1 - 2 * (place % 2)) * 2 + core
    deep = wq.shape[0]
    block, part_rows = deep // 4, deep // n_rep
    others = range(1, n_fsdp)
    greet_all([(sib, mine), (partner, mine)] + [(rep, flipped(mine, s, n_fsdp)) for s in others])

    weights = (wq, wg, wk, wv)
    starts = [sum(widths[:i]) for i in range(4)]
    band = (place % 2) * 2 + core
    other_band = (1 - place % 2) * 2 + core

    def gain_copy(s):
        return remote_copy(
            gains, gains_all.at[mine], gs.at[s], gr.at[s], rep, flipped(mine, s, n_fsdp)
        )

    def weight_copy(s, i):
        peer = flipped(mine, s, n_fsdp)
        cols = pl.ds(pl.multiple_of(peer * widths[i], widths[i]), widths[i])
        return remote_copy(
            weights[i].at[pl.ds(band * block, block), cols],
            w_attn.at[pl.ds(mine * deep + band * block, block), pl.ds(starts[i], widths[i])],
            ws.at[s, i],
            wr.at[s, i],
            rep,
            peer,
        )

    def band_at(s, which):
        return w_attn.at[pl.ds(flipped(mine, s, n_fsdp) * deep + which * block, block)]

    def partner_copy(s):
        return remote_copy(band_at(s, band), band_at(s, band), zs.at[s], zr.at[s], partner, mine)

    def sibling_copy(s, k):
        which = band if k == 0 else other_band
        return remote_copy(
            band_at(s, which), band_at(s, which), cs.at[s, k], cr.at[s, k], sib, mine
        )

    def mlp_copy(s, i):
        peer = flipped(mine, s, n_fsdp)
        cols = pl.ds(pl.multiple_of(peer * ff, ff), ff)
        return remote_copy(
            (w_gate, w_up)[i].at[pl.ds(rep * part_rows, part_rows), cols],
            mlp_part.at[s - 1, :, pl.ds(i * ff, ff)],
            ms.at[s, i],
            mr.at[s, i],
            rep,
            peer,
        )

    def own_copy(i):
        cols = pl.ds(pl.multiple_of(mine * widths[i], widths[i]), widths[i])
        return pltpu.make_async_copy(
            weights[i].at[:, cols],
            w_attn.at[pl.ds(mine * deep, deep), pl.ds(starts[i], widths[i])],
            ls.at[i],
        )

    own_gain = pltpu.make_async_copy(gains, gains_all.at[mine], ls.at[4])
    rows = GatherRows(n_fsdp, rep, mine, tokens, tokens_all, (ts, tr, tl))
    for s in others:
        gain_copy(s).start()
        for i in range(4):
            weight_copy(s, i).start()
    rows.start()
    own_gain.start()
    for i in range(4):
        own_copy(i).start()
    for s in others:
        for i in range(4):
            weight_copy(s, i).wait_recv()
        partner_copy(s).start()
        sibling_copy(s, 0).start()
    rows.forward()
    for s in others:
        for i in range(2):
            mlp_copy(s, i).start()
    for s in others:
        partner_copy(s).wait_recv()
        sibling_copy(s, 1).start()
    rows.finish()
    for s in others:
        gain_copy(s).wait()
        partner_copy(s).wait_send()
        for i in range(4):
            weight_copy(s, i).wait_send()
        for i in range(2):
            sibling_copy(s, i).wait()
            mlp_copy(s, i).wait()
    own_gain.wait()
    for i in range(4):
        own_copy(i).wait()


def fetched(n_fsdp, n_rep, widths, ff, tokens, gains, *weights):
    deep = weights[0].shape[0]
    rows, width = tokens.shape
    dma = pltpu.SemaphoreType.DMA
    any_spec = pl.BlockSpec(memory_space=pl.ANY)
    shapes = (
        (n_fsdp * rows, width),
        (n_fsdp,) + gains.shape,
        (n_fsdp * deep, sum(widths)),
        (n_fsdp - 1, deep // n_rep, 2 * ff),
    )
    pair, four = dma((n_fsdp, 2)), dma((n_fsdp, 4))
    one = dma((n_fsdp,))
    return pl.pallas_call(
        functools.partial(fetch_kernel, n_fsdp, n_rep, widths, ff),
        out_shape=[jax.ShapeDtypeStruct(shape, jnp.bfloat16) for shape in shapes],
        in_specs=[any_spec] * 8,
        out_specs=[any_spec] * 4,
        scratch_shapes=[
            pair, pair, dma, one, one, four, four, one, one, pair, pair, pair, pair, dma((5,))
        ],
        compiler_params=pltpu.CompilerParams(collective_id=1, has_side_effects=True),
        name="fetch",
    )(tokens, gains, *weights)


def gather_rows(block):
    n_fsdp = lax.axis_size("fsdp")
    if n_fsdp != 4:
        return [block] + [shift(block, s) for s in range(1, n_fsdp)]
    half = block.shape[0] // 2
    top, low = block[:half], block[half:]
    x_top, y_low = shift(top, 1), shift(low, 2)
    x_low, y_top = shift(low, 1), shift(top, 2)
    d_top, d_low = shift(x_top, 2), shift(y_low, 1)
    return [
        block,
        jnp.concatenate([x_top, x_low]),
        jnp.concatenate([y_top, y_low]),
        jnp.concatenate([d_top, d_low]),
    ]


def scatter_rows(own, parts):
    n_fsdp = lax.axis_size("fsdp")
    if n_fsdp != 4:
        for s in range(1, n_fsdp):
            own = own + in_f32(shift(parts[s - 1], s))
        return own
    half = own.shape[0] // 2
    p_x, p_y, p_d = parts
    r_y = shift(p_d[:half], 1)
    r_x = shift(p_d[half:], 2)
    x_top = shift(p_x[:half], 1)
    y_low = shift(p_y[half:], 2)
    y_top = shift(in_bf16(in_f32(p_y[:half]) + in_f32(r_y)), 2)
    x_low = shift(in_bf16(in_f32(p_x[half:]) + in_f32(r_x)), 1)
    return own + jnp.concatenate(
        [in_f32(x_top) + in_f32(y_top), in_f32(y_low) + in_f32(x_low)]
    )


def shards(
    tokens,
    teacher,
    lengths,
    deal_order,
    attention_gain,
    query_gain,
    key_gain,
    w_query,
    w_key,
    w_value,
    w_outgate,
    w_output,
    mlp_gain,
    w_gate,
    w_up,
    w_down,
):
    n_rep = lax.axis_size("rep")
    n_fsdp = lax.axis_size("fsdp")
    rows, width = tokens.shape
    mine = lax.axis_index("fsdp")
    core = lax.axis_index("rep") % 2
    others = range(1, n_fsdp)
    heads_q, heads_k = H // n_fsdp, KV // n_fsdp
    cols_q, cols_k = heads_q * HD, heads_k * HD
    deep = w_query.shape[0]
    ff = w_down.shape[0]
    rows_all = rows * n_fsdp

    peers = mine ^ jnp.arange(n_fsdp, dtype=jnp.int32)
    devices = lax.axis_index("rep") * n_fsdp + peers
    slot_ids = (devices[:, None] * 2 + jnp.arange(2, dtype=jnp.int32)[None, :]).reshape(-1)
    seq_ids = jnp.arange(lengths.shape[0], dtype=jnp.int32)
    slot_seq = jnp.sum(
        jnp.where(seq_ids[None, :] == slot_ids[:, None], deal_order[None, :], 0), axis=1
    )
    pair_len = jnp.sum(
        jnp.where(seq_ids[None, :] == slot_seq[:, None], lengths[None, :], 0), axis=1
    ).reshape(n_fsdp, 2)
    token_count = jnp.sum(lengths).astype(jnp.float32)
    factor = rows * n_rep * n_fsdp / (2.0 * token_count)
    segments, angle_cos, angle_sin = row_layout(pair_len, rows, HD)
    angle_cos, angle_sin = angle_cos.reshape(rows_all, HD), angle_sin.reshape(rows_all, HD)
    segment = segments[0]
    valid_row = (segment < 2).astype(jnp.float32)

    small = query_gain.shape[0]
    gains_own = jnp.concatenate([attention_gain, mlp_gain, query_gain, key_gain])
    gains_own = jnp.pad(gains_own, (0, 16 * HD - gains_own.shape[0])).reshape(16, HD)
    tokens_all, gains, w_attn, mlp_part = fetched(
        n_fsdp,
        n_rep,
        (cols_q, cols_q, cols_k, cols_k),
        ff,
        tokens,
        gains_own,
        w_query,
        w_outgate,
        w_key,
        w_value,
        w_gate,
        w_up,
    )
    gains = in_f32(gains.reshape(n_fsdp, 16 * HD))
    attention_gain_f = gains[:, :deep].reshape(-1)
    mlp_gain_f = gains[:, deep : 2 * deep].reshape(-1)
    query_gain_f = gains[:, 2 * deep : 2 * deep + small].reshape(-1)
    key_gain_f = gains[:, 2 * deep + small : 2 * deep + 2 * small].reshape(-1)

    mlp_parts = lax.all_gather(mlp_part, "rep", axis=0)
    w_mlp = jnp.zeros((n_fsdp * deep, 2 * ff), jnp.bfloat16)
    for i, weight in enumerate((w_gate, w_up)):
        own = lax.dynamic_slice(weight, (0, mine * ff), (deep, ff))
        w_mlp = lax.dynamic_update_slice(w_mlp, own, (mine * deep, i * ff))
    for s in others:
        rows_of = mlp_parts[:, s - 1].reshape(deep, 2 * ff)
        w_mlp = lax.dynamic_update_slice(w_mlp, rows_of, ((mine ^ s) * deep, 0))

    tokens_f = in_f32(tokens)
    normed_all = in_bf16(rms_scale(in_f32(tokens_all), attention_gain_f))
    attn_raw = times(normed_all, w_attn)
    head_args = (
        heads_k,
        rows,
        pair_len,
        attn_raw,
        angle_cos,
        angle_sin,
        query_gain_f[None],
        key_gain_f[None],
    )
    queries_b, keys_b, values_b, gated_b = attend(*head_args)

    def summed(left, right, product):
        own = product(left[:rows], right, jnp.float32)
        parts = product(left[rows:], right, jnp.bfloat16)
        return scatter_rows(own, [parts[i * rows : (i + 1) * rows] for i in range(n_fsdp - 1)])

    middle = tokens_f + summed(gated_b, w_output, times)
    normed_mlp = rms_scale(middle, mlp_gain_f)
    normed_mlp_all = jnp.concatenate(gather_rows(in_bf16(normed_mlp)))
    gate_pre = times(normed_mlp_all, w_mlp[:, :ff])
    up_pre = times(normed_mlp_all, w_mlp[:, ff:])
    hidden, swiglu_back = jax.vjp(swiglu, gate_pre, up_pre)
    hidden_b = in_bf16(hidden)
    result = middle + summed(hidden_b, w_down, times)

    error_rows = (result - in_f32(teacher)) * valid_row[:, None]
    row_sq = jnp.sum(error_rows * error_rows, axis=-1)
    slot_mask = (segment[:, None] == jnp.arange(2, dtype=jnp.int32)[None, :]).astype(jnp.float32)
    seq_loss = jnp.sum(row_sq[:, None] * slot_mask, axis=0) / (2.0 * token_count)
    block_out = in_bf16(result * valid_row[:, None])
    grad_result = 2.0 * factor * error_rows

    grad_branch_all = jnp.concatenate(gather_rows(in_bf16(grad_result)))
    grad_hidden = times_trans(grad_branch_all, w_down)
    grad_gate_pre, grad_up_pre = swiglu_back(grad_hidden)
    grad_gate_b = in_bf16(grad_gate_pre)
    grad_up_b = in_bf16(grad_up_pre)
    grad_mlp_b = jnp.concatenate([grad_gate_b, grad_up_b], axis=1)
    piece_rows, piece_cols = deep // 2, width // n_fsdp
    units, base = [], 0
    for by_owner, row_blocks, cols in (
        (False, ff // 2 // piece_rows, width),
        (True, n_fsdp, 2 * ff),
        (False, cols_q // 2 // piece_rows, width),
        (True, n_fsdp, 2 * cols_q + 2 * cols_k),
    ):
        units.append(Unit(base, by_owner, row_blocks, cols // piece_cols))
        base += units[-1].count
    gain_rows = jnp.concatenate(
        [attention_gain_f[None], mlp_gain_f[None], jnp.zeros((6, width), jnp.float32)]
    )
    head_gains = jnp.concatenate(
        [query_gain_f[None], key_gain_f[None], jnp.zeros((6, HD), jnp.float32)]
    )
    pieces, _, _, _, _, tokens_grad, gain_parts, head_gain_parts = backward(
        n_fsdp,
        n_rep,
        heads_k,
        units,
        piece_rows,
        piece_cols,
        (
            hidden_b,
            normed_mlp_all,
            gated_b,
            normed_all,
            grad_branch_all,
            grad_mlp_b,
            w_mlp,
            w_output,
            w_attn,
            middle,
            grad_result,
            tokens,
            attn_raw,
            angle_cos,
            angle_sin,
            queries_b,
            keys_b,
            values_b,
            gain_rows,
            head_gains,
            pair_len,
        ),
    )
    dgains = sum_everywhere(
        jnp.concatenate([gain_parts[:2].reshape(1, -1), head_gain_parts[:2].reshape(1, -1)], axis=1)
    )[0]
    down, mlp, outp, attn = units

    def by_rows(unit, weight):
        blocks, together = unit.row_blocks, unit.col_blocks
        return widened(
            pieces,
            (2, blocks),
            together,
            lambda c, r: (unit.base // together + r, c, 0, 0),
            weight.shape,
            lambda c, r: (c * blocks + r, 0),
        )

    def by_owners(unit, weight, which):
        together = unit.col_blocks // 2
        return widened(
            pieces,
            (2, n_fsdp),
            together,
            lambda c, f: (unit.base // together + 2 * f + which, c, 0, 0),
            weight.shape,
            lambda c, f: (c, f),
        )

    dw_down = by_rows(down, w_down)
    dw_output = by_rows(outp, w_output)
    dw_gate = by_owners(mlp, w_gate, 0)
    dw_up = by_owners(mlp, w_up, 1)
    dw_query, dw_outgate, dw_key, dw_value = widened_heads(
        pieces,
        attn.base,
        n_fsdp,
        (w_query.shape, w_outgate.shape, w_key.shape, w_value.shape),
    )

    def own_part(start, cols):
        return lax.dynamic_slice(dgains, (start + mine * cols,), (cols,))

    return (
        block_out,
        seq_loss,
        tokens_grad,
        own_part(0, deep),
        own_part(2 * width, small),
        own_part(2 * width + HD, small),
        dw_query,
        dw_key,
        dw_value,
        dw_outgate,
        dw_output,
        own_part(width, deep),
        dw_gate,
        dw_up,
        dw_down,
    )


def solution(mesh):
    return jax.shard_map(
        shards,
        mesh=mesh,
        in_specs=(
            P(("rep", "fsdp"), None),
            P(("rep", "fsdp"), None),
            P(),
            P(),
            P("fsdp"),
            P("fsdp"),
            P("fsdp"),
            P("fsdp", None),
            P("fsdp", None),
            P("fsdp", None),
            P("fsdp", None),
            P("fsdp", None),
            P("fsdp"),
            P("fsdp", None),
            P("fsdp", None),
            P("fsdp", None),
        ),
        out_specs=(
            P(("rep", "fsdp"), None),
            P(("rep", "fsdp")),
            P(("rep", "fsdp"), None),
            P("fsdp"),
            P("fsdp"),
            P("fsdp"),
            P("fsdp", None),
            P("fsdp", None),
            P("fsdp", None),
            P("fsdp", None),
            P("fsdp", None),
            P("fsdp"),
            P("fsdp", None),
            P("fsdp", None),
            P("fsdp", None),
        ),
        check_vma=False,
    )
```

```python
import functools

import jax
import jax.numpy as jnp
from jax import lax
from jax.experimental import pallas as pl
from jax.experimental.pallas import tpu as pltpu
from jax.sharding import PartitionSpec as P

MESH = pl.DeviceIdType.MESH

H = 16
KV = 8
HD = 128


EPS_NORM = 1e-06
ROPE_BASE = 1000000.0
NEG_FILL = -1e30


def row_layout(pair_len, row_count, head_dim):
    row_index = jnp.arange(row_count, dtype=jnp.int32)[None, :]
    head_len = pair_len[:, :1]
    both_len = pair_len[:, :1] + pair_len[:, 1:]
    segment = (row_index >= head_len).astype(jnp.int32) + (row_index >= both_len).astype(jnp.int32)
    start_row = jnp.where(segment == 0, 0, jnp.where(segment == 1, head_len, both_len))
    position = (row_index - start_row).astype(jnp.float32)
    inv_freq = jnp.power(ROPE_BASE, -jnp.arange(0, head_dim, 2, dtype=jnp.float32) / head_dim)
    angles = position[..., None] * inv_freq
    angle_cos, angle_sin = jnp.cos(angles), jnp.sin(angles)
    return (
        jnp.concatenate([angle_cos, angle_cos], axis=-1),
        jnp.concatenate([angle_sin, angle_sin], axis=-1),
    )


def in_f32(values):
    return values.astype(jnp.float32)


def in_bf16(values):
    return values.astype(jnp.bfloat16)


def flipped(index, step, n):
    out, bit = index, 1
    while bit < n:
        has = (step // bit) % 2
        out = out + has * bit * (1 - 2 * ((index // bit) % 2))
        bit *= 2
    return out


def at_least(value, bound, span):
    span = max(span, bound)
    return (value + (span - bound)) // span


class Unit:
    def __init__(self, base, by_owner, row_blocks, col_blocks):
        self.base, self.by_owner = base, by_owner
        self.row_blocks, self.col_blocks = row_blocks, col_blocks
        self.count = row_blocks * col_blocks


LAG_B, LAG_C, LAG_D, LAG_E, LAG_G = 2, 4, 6, 8, 11
RING = 4


ROW_STEP = 32
TILES = 8


def norm_back(grad, raw, gain):
    scale = lax.rsqrt(jnp.mean(raw * raw, axis=-1, keepdims=True) + EPS_NORM)
    unit = raw * scale
    inner = grad * gain
    return scale * (inner - unit * jnp.mean(inner * unit, axis=-1, keepdims=True)), grad * unit


def backward_kernel(n_fsdp, n_rep, heads_k, units, piece_rows, piece_cols, *refs):
    (hidden, normed_mlp, gated, normed, grad_branch, grad_mlp, w_mlp, w_output, w_attn) = refs[:9]
    (middle, grad_result, tokens, attn_raw, all_cos, all_sin, all_q, all_k, all_v) = refs[9:18]
    (gains, head_gains, pair_ref) = refs[18:21]
    (out, grad_attn, grad_raw, inb, xb, tokens_grad, gain_out) = refs[21:28]
    (lm, lo, rh, sb, kb, r1, c_slot, d_slot, big, wt, own, pbuf, land_a, land_b) = refs[28:42]
    (mid, gres, tok, ga, wo, raw, cs, sn, qb, kvb, vb, gb, gg, ob) = refs[42:56]
    (tile_sem, r1s, r1r, ins, inr, xs, xr, os_, fs, fr, gs, gr, ls) = refs[56:69]
    (load_sem, first_sem, wt_sem, ps, pr, qs, qr, ag_s, ag_r, ag_l, block_sem) = refs[69:80]
    (near_land, pair_land, in_land, far_land, near_s, near_r, line_s, line_r) = refs[80:]
    head_gain_out = gain_out.at[:, pl.ds(own.shape[1], HD)]
    lefts = (hidden, normed_mlp, gated, normed)
    rights = (grad_branch, grad_mlp, grad_attn, grad_raw)
    total = sum(unit.count for unit in units)
    rows, width = own.shape
    rows_all = n_fsdp * rows
    ff = grad_mlp.shape[1] // 2
    tile = width // TILES
    others = range(1, n_fsdp)
    rep, mine = lax.axis_index("rep"), lax.axis_index("fsdp")
    core, place = rep % 2, rep // 2
    n_line = n_rep // 2
    half = n_line // 2
    side = place // half
    depth = place * (1 - side) + (n_line - 1 - place) * side
    inward = (place + 1 - 2 * side) * 2 + core
    outward = (place - 1 + 2 * side) * 2 + core
    sib = rep + 1 - 2 * core
    at_middle = depth == half - 1

    barrier = pltpu.get_barrier_semaphore()

    def greet(to_rep, to_fsdp):
        pl.semaphore_signal(
            barrier, inc=1, device_id={"rep": to_rep, "fsdp": to_fsdp}, device_id_type=MESH
        )

    greet(sib, mine)
    greet(inward, mine)
    for s in others:
        greet(rep, flipped(mine, s, n_fsdp))

    @pl.when(depth == 0)
    def _():
        pl.semaphore_wait(barrier, 1 + n_fsdp)

    @pl.when(depth > 0)
    def _():
        greet(outward, mine)
        pl.semaphore_wait(barrier, 2 + n_fsdp)


    def r1_copy(p):
        return remote_copy(sb.at[p % RING], r1.at[p], r1s.at[p], r1r.at[p], sib, mine)

    def in_copy(p):
        return remote_copy(r1.at[p], inb.at[p], ins.at[p], inr.at[p], inward, mine)

    def x_copy(p):
        return remote_copy(r1.at[p], xb.at[p], xs.at[p], xr.at[p], inward, mine)

    def o_copy(p, src):
        return remote_copy(src.at[p], xb.at[p], os_.at[p], xr.at[p], outward, mine)

    def inside_of(p, unit):
        inside = at_least(p, unit.base, total - unit.base)
        stop = unit.base + unit.count
        if stop < total:
            inside = inside * (1 - at_least(p, stop, total - stop))
        return inside

    def owner_of(p):
        step = 0
        for unit in units:
            if unit.by_owner:
                i = p - unit.base
                step = step + inside_of(p, unit) * (n_fsdp - 1 - i // unit.col_blocks)
        return step

    def spot(p, source):
        where = p
        for unit in units:
            if unit.by_owner:
                i = p - unit.base
                spread = unit.base + source * unit.col_blocks + i % unit.col_blocks
                where = where + inside_of(p, unit) * (spread - p)
        return where

    def f_copy(p, step):
        return remote_copy(
            r1.at[p],
            out.at[spot(p, mine), core],
            fs.at[p],
            fr.at[p],
            rep,
            flipped(mine, step, n_fsdp),
        )

    def g_copy(p, src, where):
        return remote_copy(src, out.at[where, core], gs.at[p], gr.at[p], sib, mine)

    def l_copy(p):
        return pltpu.make_async_copy(r1.at[p], out.at[spot(p, mine), core], ls.at[p])

    def c_load(p):
        return pltpu.make_async_copy(inb.at[p], c_slot, load_sem.at[0])

    def d_load(p):
        return pltpu.make_async_copy(xb.at[p], d_slot, load_sem.at[1])

    def e_load(p):
        return pltpu.make_async_copy(xb.at[p], r1.at[p], load_sem.at[2])

    def add_into(p, other):
        r1[p] = in_bf16(in_f32(r1[p]) + in_f32(other))

    def begin_c(p):
        @pl.when(depth > 0)
        def _():
            in_copy(p).wait_recv()
            c_load(p).start()

    def begin_d(p):
        @pl.when(at_middle)
        def _():
            x_copy(p).wait_recv()
            d_load(p).start()

    def begin_e(p):
        @pl.when(depth < half - 1)
        def _():
            o_copy(p, xb).wait_recv()

            @pl.when(depth > 0)
            def _():
                o_copy(p, xb).start()

            in_copy(p).wait_send()
            e_load(p).start()

    def end_b(p):
        r1_copy(p).wait_recv()
        add_into(p, kb[p % RING])
        if half > 1:

            @pl.when(depth == 0)
            def _():
                in_copy(p).start()
        else:
            x_copy(p).start()

    def end_c(p):
        @pl.when(depth > 0)
        def _():
            c_load(p).wait()
            add_into(p, c_slot[...])

            @pl.when(depth < half - 1)
            def _():
                in_copy(p).start()

            @pl.when(at_middle)
            def _():
                x_copy(p).start()

    def end_d(p):
        @pl.when(at_middle)
        def _():
            d_load(p).wait()
            x_copy(p).wait_send()
            add_into(p, d_slot[...])

            @pl.when(depth > 0)
            def _():
                o_copy(p, r1).start()

    def end_e(p):
        @pl.when(depth < half - 1)
        def _():
            e_load(p).wait()

        step = owner_of(p)

        @pl.when(step == 0)
        def _():
            l_copy(p).start()
            g_copy(p, r1.at[p], spot(p, mine)).start()

        @pl.when(step > 0)
        def _():
            f_copy(p, step).start()

    def end_g(p):
        step = owner_of(p)

        @pl.when(step > 0)
        def _():
            f_copy(p, step).wait_recv()
            where = spot(p, flipped(mine, step, n_fsdp))
            g_copy(p, out.at[where, core], where).start()

    def run(stages, t):
        for lag, stage in stages:
            pl.when((t >= lag) & (t < total + lag))(functools.partial(stage, t - lag))

    def begin(t):
        run([(LAG_C, begin_c), (LAG_D, begin_d), (LAG_E, begin_e)], t)

    def end(t):
        run([(LAG_B, end_b), (LAG_C, end_c), (LAG_D, end_d), (LAG_E, end_e), (LAG_G, end_g)], t)

    def tiles(u, i, slot):
        unit = units[u]
        r, j = i // unit.col_blocks, i % unit.col_blocks
        if unit.by_owner:
            owner = flipped(mine, n_fsdp - 1 - r, n_fsdp)
            first = owner * 2 * piece_rows + core * piece_rows
            second = owner * 2 * piece_rows + (1 - core) * piece_rows
        else:
            first = core * unit.row_blocks * piece_rows + r * piece_rows
            second = (1 - core) * unit.row_blocks * piece_rows + r * piece_rows
        first = pl.ds(pl.multiple_of(first, piece_rows), piece_rows)
        second = pl.ds(pl.multiple_of(second, piece_rows), piece_rows)
        cols = pl.ds(pl.multiple_of(j * piece_cols, piece_cols), piece_cols)
        return [
            pltpu.make_async_copy(lefts[u].at[:, first], lm.at[slot], tile_sem.at[slot, 0]),
            pltpu.make_async_copy(lefts[u].at[:, second], lo.at[slot], tile_sem.at[slot, 1]),
            pltpu.make_async_copy(rights[u].at[:, cols], rh.at[slot], tile_sem.at[slot, 2]),
        ]


    first_pairs = (
        (grad_mlp.at[:, pl.ds(0, ff)], big.at[pl.ds(0, rows_all)]),
        (grad_mlp.at[:, pl.ds(ff, ff)], big.at[pl.ds(rows_all, rows_all)]),
        (middle, mid),
        (grad_result, gres),
        (tokens, tok),
        (w_output, wo),
    )

    def first_loads(which):
        return [pltpu.make_async_copy(*first_pairs[i], first_sem.at[i]) for i in which]

    def attn_load():
        return pltpu.make_async_copy(w_attn, big.at[pl.ds(0, width)], first_sem.at[6])

    def tile_of(j):
        return pl.ds(pl.multiple_of(j * tile, tile), tile)

    def wt_load(j):
        return pltpu.make_async_copy(w_mlp.at[tile_of(j)], wt.at[j % 2], wt_sem.at[j % 2])

    def p_copy(s, j):
        return remote_copy(
            pbuf.at[s - 1, :, tile_of(j)],
            land_a.at[s - 1, :, tile_of(j)],
            ps.at[s, j],
            pr.at[s, j],
            rep,
            flipped(mine, s, n_fsdp),
        )

    def q_copy(s):
        return remote_copy(
            pbuf.at[s - 1], land_b.at[s - 1], qs.at[s], qr.at[s], rep, flipped(mine, s, n_fsdp)
        )

    gather = GatherRows(n_fsdp, rep, mine, ga, grad_attn, (ag_s, ag_r, ag_l))

    def mlp_products(j):
        @pl.when(j == 0)
        def _():
            for copy in first_loads((0, 1)):
                copy.wait()

        wt_load(j).wait()

        @pl.when(j + 1 < TILES)
        def _():
            wt_load(j + 1).start()

        for s in (*others, 0):
            part = product_of(big[s * rows : (s + 1) * rows], wt[j % 2, :, :ff], 1, 1)
            part += product_of(
                big[rows_all + s * rows : rows_all + (s + 1) * rows], wt[j % 2, :, ff:], 1, 1
            )
            if s == 0:
                own[:, tile_of(j)] = part
            else:
                pbuf[s - 1, :, tile_of(j)] = in_bf16(part)
                p_copy(s, j).start()

    row_steps = rows // ROW_STEP

    def middle_back(part):
        if part == 0:
            middle_sums()

        def some_rows(r, carry):
            cut = pl.ds(pl.multiple_of(r * ROW_STEP, ROW_STEP), ROW_STEP)
            grad = own[cut]
            for s in others:
                grad += in_f32(land_a[s - 1, cut])
            back, gain_rows = norm_back(grad, mid[cut], gains[1:2])
            gain_out[1:2, :width] += jnp.sum(gain_rows, axis=0, keepdims=True)
            back = gres[cut] + back
            gres[cut] = back
            ga[cut] = in_bf16(back)
            return carry

        lax.fori_loop(part * row_steps // 2, (part + 1) * row_steps // 2, some_rows, 0)
        if part == 1:
            gather.start()
            for copy in block_loads(0):
                copy.start()

    def middle_sums():
        attn_load().start()
        for copy in first_loads((2, 3)):
            copy.wait()

        def wait_tiles(j, carry):
            for s in others:
                p_copy(s, j).wait()
            return carry

        lax.fori_loop(0, TILES, wait_tiles, 0)
        gain_out[...] = jnp.zeros_like(gain_out)

    def block_loads(s):
        cut = pl.ds(pl.multiple_of(s * rows, rows), rows)
        pairs = (
            (attn_raw, raw), (all_cos, cs), (all_sin, sn), (all_q, qb), (all_k, kvb), (all_v, vb)
        )
        copies = [
            pltpu.make_async_copy(src.at[cut], dst, block_sem.at[i])
            for i, (src, dst) in enumerate(pairs)
        ]
        return copies

    def grad_load(s):
        cut = pl.ds(pl.multiple_of(s * rows, rows), rows)
        return pltpu.make_async_copy(grad_attn.at[cut], gb, block_sem.at[6])

    def store(s):
        cut = pl.ds(pl.multiple_of(s * rows, rows), rows)
        return pltpu.make_async_copy(ob, grad_raw.at[cut], block_sem.at[7])

    def heads_back(s, heads):
        attend_back(
            heads_k,
            heads,
            block_mask(pair_ref, rows, s),
            cs[...],
            sn[...],
            head_gains[0:1],
            head_gains[1:2],
            raw,
            qb,
            kvb,
            vb,
            gg,
            ob,
            head_gain_out,
        )

    early = heads_k // 2

    def block_first(s):
        @pl.when(s == 0)
        def _():
            first_loads((5,))[0].wait()
            gb[...] = ga[...]

        for k in others:

            @pl.when(s == k)
            def _(k=k):
                gather.arrive(k)

        @pl.when(s > 0)
        def _():
            copy = grad_load(s)
            copy.start()
            copy.wait()

        gg[...] = product_of(gb[...], wo[...], 1, 1)
        for copy in block_loads(s):
            copy.wait()
        heads_back(s, range(early))

    def block_second(s):
        heads_back(s, range(early, heads_k))
        store(s).start()

        @pl.when(s + 1 < n_fsdp)
        def _():
            for copy in block_loads(s + 1):
                copy.start()

    def block_third(s):
        store(s).wait()

        @pl.when(s == 0)
        def _():
            attn_load().wait()

        def one_tile(j, carry):
            part = product_of(ob[...], big[tile_of(j)], 1, 1)

            @pl.when(s == 0)
            def _():
                own[:, tile_of(j)] = part

            @pl.when(s > 0)
            def _():
                pbuf[s - 1, :, tile_of(j)] = in_bf16(part)

            return carry

        lax.fori_loop(0, TILES, one_tile, 0)

        @pl.when(s > 0)
        def _():
            q_copy(s).start()

    def tokens_back(part):
        if part == 0:
            gather.sent()
            first_loads((4,))[0].wait()
            for s in others:
                q_copy(s).wait()

        def some_rows(r, carry):
            cut = pl.ds(pl.multiple_of(r * ROW_STEP, ROW_STEP), ROW_STEP)
            grad = own[cut]
            for s in others:
                grad += in_f32(land_b[s - 1, cut])
            back, gain_rows = norm_back(grad, in_f32(tok[cut]), gains[0:1])
            gain_out[0:1, :width] += jnp.sum(gain_rows, axis=0, keepdims=True)
            tokens_grad[cut] = in_bf16(gres[cut] + back)
            return carry

        lax.fori_loop(part * row_steps // 2, (part + 1) * row_steps // 2, some_rows, 0)
        if part == 1:
            near_land[mine] = gain_out[...]
            for s in others:
                near_copy(s).start()


    def near_copy(s):
        return remote_copy(
            gain_out,
            near_land.at[mine],
            near_s.at[s],
            near_r.at[s],
            rep,
            flipped(mine, s, n_fsdp),
        )

    def line_copy(k, target, to_rep):
        return remote_copy(gain_out, target, line_s.at[k], line_r.at[k], to_rep, mine)

    def pair_copy():
        return line_copy(0, pair_land, sib)

    def gain_in():
        return line_copy(1, in_land, inward)

    def gain_across():
        return line_copy(2, far_land, inward)

    def gain_back():
        return line_copy(3, far_land, outward)

    def gains_near():
        for s in others:
            near_copy(s).wait()
        summed = near_land[0]
        for k in others:
            summed += near_land[k]
        gain_out[...] = summed
        pair_copy().start()

    def gains_pair():
        pair_copy().wait()
        gain_out[...] += pair_land[...]

        @pl.when(depth == 0)
        def _():
            (gain_in if half > 1 else gain_across)().start()

    def gains_in(k):
        @pl.when(depth == k)
        def _():
            gain_in().wait_recv()
            gain_out[...] += in_land[...]
            (gain_in if k < half - 1 else gain_across)().start()

    def gains_across():
        @pl.when(at_middle)
        def _():
            gain_across().wait()
            gain_out[...] += far_land[...]
            if half > 1:
                gain_back().start()

    def gains_back(k):
        @pl.when(depth == k)
        def _():
            gain_back().wait_recv()
            gain_in().wait_send()
            gain_out[...] = far_land[...]
            if k > 0:
                gain_back().start()

    def tasks(u, i):
        if u == 0:
            pl.when((i >= 4) & (i < 4 + TILES))(lambda: mlp_products(i - 4))
        if u == 1:
            for part in range(2):
                pl.when(i == 7 + part)(functools.partial(middle_back, part))
            pl.when(i == 12)(gather.forward)
            pl.when(i == 15)(lambda: gather.own().wait())
            last = 15 + 3 * (n_fsdp - 1)
            busy = ((i >= 9) & (i < 12)) | ((i >= 15) & (i < last))
            s = at_least(i, 12, units[1].count) * ((i - 12) // 3)
            for phase, task in enumerate((block_first, block_second, block_third)):
                pl.when(busy & (i % 3 == phase))(functools.partial(task, s))
        if u == 3:
            for part in range(2):
                pl.when(i == 2 + part)(functools.partial(tokens_back, part))
            pl.when(i == 6)(gains_near)
            pl.when(i == 8)(gains_pair)

    def product(left, right):
        return product_of(left, right, 0, 0)

    for copy in first_loads(range(6)):
        copy.start()
    wt_load(0).start()
    for copy in tiles(0, 0, 0):
        copy.start()
    for u, unit in enumerate(units):

        def step(i, carry, u=u, unit=unit):
            t = unit.base + i
            slot = t % 2
            begin(t)
            for copy in tiles(u, i, slot):
                copy.wait()

            @pl.when(i + 1 < unit.count)
            def _():
                for copy in tiles(u, i + 1, 1 - slot):
                    copy.start()

            if u + 1 < len(units):

                @pl.when(i + 1 == unit.count)
                def _():
                    for copy in tiles(u + 1, 0, 1 - slot):
                        copy.start()

            @pl.when(t >= RING)
            def _():
                r1_copy(t - RING).wait_send()

            sb[t % RING] = in_bf16(product(lo[slot], rh[slot]))
            r1_copy(t).start()
            kb[t % RING] = product(lm[slot], rh[slot])
            end(t)
            tasks(u, i)
            return carry

        lax.fori_loop(0, unit.count, step, 0)

    def drain(t, carry):
        begin(t)
        end(t)
        return carry

    lax.fori_loop(total, total + LAG_G, drain, 0)

    def finish(p, carry):
        @pl.when(p >= total - RING)
        def _():
            r1_copy(p).wait_send()

        @pl.when(depth > 0)
        def _():
            o_copy(p, r1).wait_send()

        step = owner_of(p)

        @pl.when(step == 0)
        def _():
            l_copy(p).wait()

        @pl.when(step > 0)
        def _():
            f_copy(p, step).wait_send()

        g_copy(p, r1.at[p], p).wait()
        return carry

    lax.fori_loop(0, total, finish, 0)
    for k in range(1, half):
        gains_in(k)
    gains_across()
    for k in range(half - 2, -1, -1):
        gains_back(k)
    if half > 1:

        @pl.when(depth > 0)
        def _():
            gain_back().wait_send()


def backward(n_fsdp, n_rep, heads_k, units, piece_rows, piece_cols, args):
    total = sum(unit.count for unit in units)
    rows_all, rows = args[0].shape[0], args[9].shape[0]
    width, cols = args[8].shape
    cols_q, cols_k = heads_k * (H // KV) * HD, heads_k * HD
    two_ff = args[5].shape[1]
    dma = pltpu.SemaphoreType.DMA
    piece = (piece_rows, piece_cols)
    low, full = jnp.bfloat16, jnp.float32
    any_spec = pl.BlockSpec(memory_space=pl.ANY)
    vmem = pl.BlockSpec(memory_space=pltpu.VMEM)
    flops = sum(4 * unit.count for unit in units) * rows_all * piece_rows * piece_cols
    outs = (
        ((total, 2) + piece, low),
        ((rows_all, width), low),
        ((rows_all, cols), low),
        ((total,) + piece, low),
        ((total,) + piece, low),
        ((rows, width), low),
        ((8, width + HD), full),
    )
    scratch = (
        ((2, rows_all, piece_rows), low),
        ((2, rows_all, piece_rows), low),
        ((2, rows_all, piece_cols), low),
        ((RING,) + piece, low),
        ((RING,) + piece, full),
        ((total,) + piece, low),
        (piece, low),
        (piece, low),
        ((max(2 * rows_all, width), cols), low),
        ((2, width // TILES, two_ff), low),
        ((rows, width), full),
        ((n_fsdp - 1, rows, width), low),
        ((n_fsdp - 1, rows, width), low),
        ((n_fsdp - 1, rows, width), low),
        ((rows, width), full),
        ((rows, width), full),
        ((rows, width), low),
        ((rows, width), low),
        ((cols_q, width), low),
        ((rows, cols), full),
        ((rows, HD), full),
        ((rows, HD), full),
        ((rows, cols_q), low),
        ((rows, cols_k), low),
        ((rows, cols_k), low),
        ((rows, width), low),
        ((rows, cols_q), full),
        ((rows, cols), low),
    )
    return pl.pallas_call(
        functools.partial(
            backward_kernel, n_fsdp, n_rep, heads_k, units, piece_rows, piece_cols
        ),
        out_shape=[jax.ShapeDtypeStruct(shape, kind) for shape, kind in outs],
        in_specs=[any_spec] * 18 + [vmem] * 2 + [pl.BlockSpec(memory_space=pltpu.SMEM)],
        out_specs=[any_spec] * 5 + [vmem] * 2,
        scratch_shapes=[pltpu.VMEM(shape, kind) for shape, kind in scratch]
        + [dma((2, 3))]
        + [dma((total,)) for _ in range(12)]
        + [
            dma((3,)),
            dma((7,)),
            dma((2,)),
            dma((n_fsdp, TILES)),
            dma((n_fsdp, TILES)),
            dma((n_fsdp,)),
            dma((n_fsdp,)),
            dma((n_fsdp, 2)),
            dma((n_fsdp, 2)),
            dma,
            dma((8,)),
            pltpu.VMEM((n_fsdp, 8, width + HD), full),
            pltpu.VMEM((8, width + HD), full),
            pltpu.VMEM((8, width + HD), full),
            pltpu.VMEM((8, width + HD), full),
            dma((n_fsdp,)),
            dma((n_fsdp,)),
            dma((4,)),
            dma((4,)),
        ],
        compiler_params=pltpu.CompilerParams(
            collective_id=0, has_side_effects=True, vmem_limit_bytes=62 << 20
        ),
        cost_estimate=pl.CostEstimate(flops=2 * flops, bytes_accessed=1 << 30, transcendentals=0),
        name="backward",
    )(*args)


def widen_kernel(in_ref, out_ref):
    cols = in_ref.shape[-1]
    for i in range(in_ref.shape[0]):
        out_ref[:, i * cols : (i + 1) * cols] = in_ref[i, 0].astype(jnp.float32)


def widened(pieces, grid, together, where, shape, place):
    rows, cols = pieces.shape[2:]
    return pl.pallas_call(
        widen_kernel,
        grid=grid,
        out_shape=jax.ShapeDtypeStruct(shape, jnp.float32),
        in_specs=[pl.BlockSpec((together, 1, rows, cols), where)],
        out_specs=pl.BlockSpec((rows, together * cols), place),
        name="widen",
    )(pieces)


def widen_heads_kernel(query_in, gate_in, pair_in, query_out, gate_out, key_out, value_out):
    half = key_out.shape[1]
    query_out[...] = query_in[0, 0].astype(jnp.float32)
    gate_out[...] = gate_in[0, 0].astype(jnp.float32)
    key_out[...] = pair_in[0, 0, :, :half].astype(jnp.float32)
    value_out[...] = pair_in[0, 0, :, half:].astype(jnp.float32)


def widened_heads(pieces, base, n_fsdp, shapes):
    rows, cols = pieces.shape[2:]

    def where(j):
        return lambda c, f: (base + 3 * f + j, c, 0, 0)

    widths = (cols, cols, cols // 2, cols // 2)
    return pl.pallas_call(
        widen_heads_kernel,
        grid=(2, n_fsdp),
        out_shape=[jax.ShapeDtypeStruct(shape, jnp.float32) for shape in shapes],
        in_specs=[pl.BlockSpec((1, 1, rows, cols), where(j)) for j in range(3)],
        out_specs=[pl.BlockSpec((rows, wide), lambda c, f: (c, f)) for wide in widths],
        name="widen_heads",
    )(pieces, pieces, pieces)


def block_mask(pair_ref, rows, block):
    head_len = pair_ref[block, 0]
    both_len = head_len + pair_ref[block, 1]
    query_row = lax.broadcasted_iota(jnp.int32, (rows, rows), 0)
    key_row = lax.broadcasted_iota(jnp.int32, (rows, rows), 1)

    def segment(index):
        return (index >= head_len).astype(jnp.int32) + (index >= both_len).astype(jnp.int32)

    return (segment(query_row) == segment(key_row)) & (key_row <= query_row)


def turn(values):
    half_dim = values.shape[-1] // 2
    return jnp.concatenate([-values[:, half_dim:], values[:, :half_dim]], axis=-1)


def head_forward(raw, gain, angle_cos, angle_sin):
    values = raw * lax.rsqrt(jnp.mean(raw * raw, axis=-1, keepdims=True) + EPS_NORM) * gain
    return in_bf16(values * angle_cos + turn(values) * angle_sin)


def head_backward(grad, raw, gain, angle_cos, angle_sin):
    grad = grad * angle_cos - turn(grad * angle_sin)
    scale = lax.rsqrt(jnp.mean(raw * raw, axis=-1, keepdims=True) + EPS_NORM)
    unit = raw * scale
    gain_rows = grad * unit
    inner = grad * gain
    return scale * (inner - unit * jnp.mean(inner * unit, axis=-1, keepdims=True)), gain_rows


def product_of(left, right, left_dim, right_dim):
    return lax.dot_general(
        left, right, (((left_dim,), (right_dim,)), ((), ())), preferred_element_type=jnp.float32
    )


def softmax_of(queries, keys, allowed):
    scores = jnp.where(allowed, product_of(queries, keys, 1, 1) * HD ** (-0.5), NEG_FILL)
    exponent = jnp.exp(scores - jnp.max(scores, axis=-1, keepdims=True))
    return exponent / jnp.sum(exponent, axis=-1, keepdims=True)


def attend(
    heads_k,
    allowed,
    angle_cos,
    angle_sin,
    query_gain,
    key_gain,
    raw_ref,
    q_ref,
    k_ref,
    v_ref,
    gated_ref,
):
    group = H // KV
    cols_q, cols_k = heads_k * group * HD, heads_k * HD
    for j in range(heads_k):
        own = slice(j * HD, (j + 1) * HD)
        keys = head_forward(
            raw_ref[:, 2 * cols_q + j * HD : 2 * cols_q + (j + 1) * HD],
            key_gain,
            angle_cos,
            angle_sin,
        )
        start = 2 * cols_q + cols_k + j * HD
        values = in_bf16(raw_ref[:, start : start + HD])
        k_ref[:, own] = keys
        v_ref[:, own] = values
        for h in range(j * group, (j + 1) * group):
            cut = slice(h * HD, (h + 1) * HD)
            queries = head_forward(raw_ref[:, cut], query_gain, angle_cos, angle_sin)
            q_ref[:, cut] = queries
            probs = in_bf16(softmax_of(queries, keys, allowed))
            context = product_of(probs, values, 1, 0)
            gate = raw_ref[:, cols_q + h * HD : cols_q + (h + 1) * HD]
            gated_ref[:, cut] = in_bf16(context * jax.nn.sigmoid(gate))


def attend_back(
    heads_k,
    heads,
    allowed,
    angle_cos,
    angle_sin,
    query_gain,
    key_gain,
    raw_ref,
    q_ref,
    k_ref,
    v_ref,
    grad_ref,
    out_ref,
    gain_ref,
):
    group = H // KV
    cols_q, cols_k = heads_k * group * HD, heads_k * HD
    for j in heads:
        own = slice(j * HD, (j + 1) * HD)
        keys, values = k_ref[:, own], v_ref[:, own]
        grad_keys, grad_values = 0.0, 0.0
        for h in range(j * group, (j + 1) * group):
            cut = slice(h * HD, (h + 1) * HD)
            gate_cut = slice(cols_q + h * HD, cols_q + (h + 1) * HD)
            queries, grad_gated = q_ref[:, cut], grad_ref[:, cut]
            probs = softmax_of(queries, keys, allowed)
            probs_b = in_bf16(probs)
            context = product_of(probs_b, values, 1, 0)
            gate = jax.nn.sigmoid(raw_ref[:, gate_cut])
            grad_context = in_bf16(grad_gated * gate)
            out_ref[:, gate_cut] = in_bf16(grad_gated * context * gate * (1.0 - gate))
            grad_probs = product_of(grad_context, values, 1, 1)
            grad_scores = in_bf16(
                probs * (grad_probs - jnp.sum(probs * grad_probs, axis=-1, keepdims=True))
            )
            grad_values += product_of(probs_b, grad_context, 0, 0)
            grad_keys += product_of(grad_scores, queries, 0, 0)
            grad_queries = product_of(grad_scores, keys, 1, 0) * HD ** (-0.5)
            grad_raw, gain_rows = head_backward(
                grad_queries, raw_ref[:, cut], query_gain, angle_cos, angle_sin
            )
            out_ref[:, cut] = in_bf16(grad_raw)
            gain_ref[0:1, :] += jnp.sum(gain_rows, axis=0, keepdims=True)
        key_start = 2 * cols_q + j * HD
        grad_raw, gain_rows = head_backward(
            grad_keys * HD ** (-0.5),
            raw_ref[:, key_start : key_start + HD],
            key_gain,
            angle_cos,
            angle_sin,
        )
        out_ref[:, key_start : key_start + HD] = in_bf16(grad_raw)
        gain_ref[1:2, :] += jnp.sum(gain_rows, axis=0, keepdims=True)
        value_start = 2 * cols_q + cols_k + j * HD
        out_ref[:, value_start : value_start + HD] = in_bf16(grad_values)


def remote_copy(src, dst, send, recv, to_rep, to_fsdp):
    return pltpu.make_async_remote_copy(
        src_ref=src,
        dst_ref=dst,
        send_sem=send,
        recv_sem=recv,
        device_id={"rep": to_rep, "fsdp": to_fsdp},
        device_id_type=MESH,
    )


def greet_all(peers):
    barrier = pltpu.get_barrier_semaphore()
    for to_rep, to_fsdp in peers:
        pl.semaphore_signal(
            barrier, inc=1, device_id={"rep": to_rep, "fsdp": to_fsdp}, device_id_type=MESH
        )
    pl.semaphore_wait(barrier, len(peers))


class GatherRows:
    def __init__(self, n_fsdp, rep, mine, source, target, sems):
        self.n_fsdp, self.rep, self.mine = n_fsdp, rep, mine
        self.source, self.target = source, target
        self.send, self.recv, self.local = sems
        self.rows = source.shape[0]
        self.half = self.rows // 2
        self.relay = ((1, 0), (2, 1)) if n_fsdp == 4 else ()

    def copy(self, s, h, to=None, src=None):
        to = s if to is None else to
        return remote_copy(
            self.source.at[pl.ds(h * self.half, self.half)]
            if src is None
            else self.target.at[pl.ds(src * self.rows + h * self.half, self.half)],
            self.target.at[pl.ds(s * self.rows + h * self.half, self.half)],
            self.send.at[s, h],
            self.recv.at[s, h],
            self.rep,
            flipped(self.mine, to, self.n_fsdp),
        )

    def own(self):
        return pltpu.make_async_copy(
            self.source, self.target.at[pl.ds(0, self.rows)], self.local
        )

    def start(self):
        for s, h in ((1, 0), (2, 1), (1, 1), (2, 0)):
            if s < self.n_fsdp:
                self.copy(s, h).start()
        if self.n_fsdp != 4:
            for s in range(3, self.n_fsdp):
                for h in range(2):
                    self.copy(s, h).start()
        self.own().start()

    def forward(self):
        if self.n_fsdp == 4:
            self.copy(1, 0).wait_recv()
            self.copy(3, 0, to=2, src=1).start()
            self.copy(2, 1).wait_recv()
            self.copy(3, 1, to=1, src=2).start()

    def arrive(self, s):
        for h in range(2):
            if (s, h) not in self.relay:
                self.copy(s, h).wait_recv()

    def sent(self):
        for s in range(1, self.n_fsdp):
            for h in range(2):
                self.copy(s, h).wait_send()

    def finish(self):
        for s in range(1, self.n_fsdp):
            self.arrive(s)
        self.sent()
        self.own().wait()


def forward_kernel(n_fsdp, n_rep, heads_k, *refs):
    (tokens, gains, wq, wg, wk, wv, w_gate, w_up, w_output, w_down, teacher) = refs[:11]
    (all_cos, all_sin, pair_ref, factor_ref) = refs[11:15]
    (normed_all, raw_all, q_all, k_all, v_all, gated_all, w_attn, w_mlp) = refs[15:23]
    (middle_out, nmlp_all, hidden_all, gbranch_all, gmlp_all, gres_out, block_out) = refs[23:30]
    (gu_all, gain_out, head_gain_out, loss_out) = refs[30:34]
    (tok, gl, wa, wo, wd, wm, nb, raw, cs, sn, qb, kvb, vb, gb, own, pbuf, land) = refs[34:51]
    (mid, nm, te, gu, hb, gm) = refs[51:57]
    (ts, tr, tl, us, ur, ul, bs, br, bl, gain_s, gain_r, ws, wr, zs, zr, cps, cpr) = refs[57:74]
    (ms, mr, hs, hr, ss, sr, ps, pr, qs, qr, load, keep, mine_sem) = refs[74:]
    rows, width = own.shape
    cols, ff = raw.shape[1], hb.shape[1]
    deep = wq.shape[0]
    widths = tuple(w.shape[1] // n_fsdp for w in (wq, wg, wk, wv))
    starts = [sum(widths[:i]) for i in range(4)]
    others = range(1, n_fsdp)
    n_line = n_rep // 2
    rep, mine = lax.axis_index("rep"), lax.axis_index("fsdp")
    core, place = rep % 2, rep // 2
    sib = rep + 1 - 2 * core
    partner = (place + 1 - 2 * (place % 2)) * 2 + core
    block, part = deep // 4, deep // n_rep
    band = (place % 2) * 2 + core
    other_band = (1 - place % 2) * 2 + core
    hops = range(1, n_line)
    row_steps = rows // ROW_STEP
    near = sorted({1, n_line - 1})
    greet_all(
        [(sib, mine)]
        + [(((place + k) % n_line) * 2 + core, mine) for k in near]
        + [(rep, flipped(mine, s, n_fsdp)) for s in others]
    )


    def columns(peer, wide):
        return pl.ds(pl.multiple_of(peer * wide, wide), wide)

    def mlp_copy(s, i):
        peer = flipped(mine, s, n_fsdp)
        return remote_copy(
            (w_gate, w_up)[i].at[pl.ds(rep * part, part), columns(peer, ff)],
            w_mlp.at[pl.ds(mine * deep + rep * part, part), pl.ds(i * ff, ff)],
            ms.at[s, i],
            mr.at[s, i],
            rep,
            peer,
        )

    def part_at(s, of_rep):
        return w_mlp.at[pl.ds(flipped(mine, s, n_fsdp) * deep + of_rep * part, part)]

    def line_copy(s, k, up):
        step = 1 if up else -1
        src = part_at(s, ((place - step * (k - 1) + n_line) % n_line) * 2 + core)
        to_rep = ((place + step + n_line) % n_line) * 2 + core
        way = 0 if up else 1
        return remote_copy(src, src, hs.at[way, s, k], hr.at[way, s, k], to_rep, mine)

    def line_sends(k):
        for up in (True, False):
            first, last = (k - 1, n_line - 2) if up else (1, n_line - k)

            @pl.when((place >= first) & (place <= last))
            def _(up=up):
                for s in others:
                    line_copy(s, k, up).start()

    def line_arrivals(k):
        for up in (True, False):
            first, last = (k, n_line - 1) if up else (0, n_line - 1 - k)

            @pl.when((place >= first) & (place <= last))
            def _(up=up):
                for s in others:
                    line_copy(s, k, up).wait_recv()
                    share_copy(s, k, up).start()

        if k + 1 < n_line:
            line_sends(k + 1)

    def share_copy(s, k, up):
        step = 1 if up else -1
        src = part_at(s, ((place - step * k + n_line) % n_line) * 2 + core)
        way = 0 if up else 1
        return remote_copy(src, src, ss.at[way, s, k], sr.at[way, s, k], sib, mine)

    def shares(action):
        for s in others:
            action(share_copy(s, 0, True))
        for k in hops:
            for up in (True, False):
                first, last = (k, n_line - 1) if up else (0, n_line - 1 - k)

                @pl.when((place >= first) & (place <= last))
                def _(k=k, up=up):
                    for s in others:
                        action(share_copy(s, k, up))

    def lines_sent():
        for k in hops:
            for up in (True, False):
                first, last = (k - 1, n_line - 2) if up else (1, n_line - k)

                @pl.when((place >= first) & (place <= last))
                def _(k=k, up=up):
                    for s in others:
                        line_copy(s, k, up).wait_send()

    weights = (wq, wg, wk, wv)

    def weight_copy(s, i):
        peer = flipped(mine, s, n_fsdp)
        return remote_copy(
            weights[i].at[pl.ds(band * block, block), columns(peer, widths[i])],
            w_attn.at[pl.ds(mine * deep + band * block, block), pl.ds(starts[i], widths[i])],
            ws.at[s, i],
            wr.at[s, i],
            rep,
            peer,
        )

    def band_at(s, which):
        return w_attn.at[pl.ds(flipped(mine, s, n_fsdp) * deep + which * block, block)]

    def partner_copy(s):
        return remote_copy(band_at(s, band), band_at(s, band), zs.at[s], zr.at[s], partner, mine)

    def sibling_copy(s, k):
        which = band if k == 0 else other_band
        return remote_copy(
            band_at(s, which), band_at(s, which), cps.at[s, k], cpr.at[s, k], sib, mine
        )

    def gain_copy(s):
        return remote_copy(
            gains, gl.at[mine], gain_s.at[s], gain_r.at[s], rep, flipped(mine, s, n_fsdp)
        )

    mine_rows = pl.ds(mine * deep, deep)
    mine_pairs = [
        (weights[i].at[:, columns(mine, widths[i])], w_attn.at[mine_rows, pl.ds(starts[i], widths[i])])
        for i in range(4)
    ]
    mine_pairs += [
        (w.at[:, columns(mine, ff)], w_mlp.at[mine_rows, pl.ds(i * ff, ff)])
        for i, w in enumerate((w_gate, w_up))
    ]
    mine_pairs += [(gains, gl.at[mine]), (w_output, wo), (w_down, wd), (teacher, te)]

    def local(which):
        return [pltpu.make_async_copy(*mine_pairs[i], mine_sem.at[i]) for i in which]

    def attn_load():
        return pltpu.make_async_copy(w_attn, wa, load.at[0])

    def mlp_load():
        return pltpu.make_async_copy(w_mlp, wm, load.at[1])

    token_rows = GatherRows(n_fsdp, rep, mine, tokens, tok, (ts, tr, tl))
    up_rows = GatherRows(n_fsdp, rep, mine, nm, nmlp_all, (us, ur, ul))
    back_rows = GatherRows(n_fsdp, rep, mine, nm, gbranch_all, (bs, br, bl))

    for s in others:
        gain_copy(s).start()
        for i in range(4):
            weight_copy(s, i).start()
    token_rows.start()
    for copy in local(range(10)):
        copy.start()
    for s in others:
        for i in range(4):
            weight_copy(s, i).wait_recv()
        partner_copy(s).start()
        sibling_copy(s, 0).start()
    for s in others:
        for i in range(2):
            mlp_copy(s, i).start()
    token_rows.forward()
    local((6,))[0].wait()
    gain_out[...] = jnp.zeros_like(gain_out)
    head_gain_out[...] = jnp.zeros_like(head_gain_out)
    for s in others:
        gain_copy(s).wait()
    lines = deep // HD
    for f in range(n_fsdp):
        piece = in_f32(gl[f])
        for kind in range(2):
            for r in range(lines):
                at = f * deep + r * HD
                gain_out[kind : kind + 1, at : at + HD] = piece[
                    kind * lines + r : kind * lines + r + 1
                ]
            head_gain_out[kind : kind + 1] += piece[2 * lines + kind : 2 * lines + kind + 1]
    for s in others:
        partner_copy(s).wait_recv()
        sibling_copy(s, 1).start()
    for s in others:
        for k in range(2):
            sibling_copy(s, k).wait_recv()
    for copy in local((0, 1, 2, 3)):
        copy.wait()
    attn_load().start()
    for s in others:
        for i in range(2):
            mlp_copy(s, i).wait_recv()
        share_copy(s, 0, True).start()
    line_sends(1)
    for copy in local((7, 8, 9)):
        copy.wait()

    def block_rows(s):
        return pl.ds(pl.multiple_of(s * rows, rows), rows)

    def some_rows(base, r):
        return pl.ds(pl.multiple_of(base + r * ROW_STEP, ROW_STEP), ROW_STEP)

    def tiled(count, wide, body):
        def one(j, carry):
            body(pl.ds(pl.multiple_of(j * wide, wide), wide))
            return carry

        lax.fori_loop(0, count, one, 0)

    def by_rows(body):
        def one(r, carry):
            body(r)
            return carry

        lax.fori_loop(0, row_steps, one, 0)

    tile = width // 4

    def leave(s, left, right):
        def one(cut):
            product = product_of(left[...], right[:, cut], 1, 0)

            @pl.when(s == 0)
            def _():
                own[:, cut] = product

            @pl.when(s > 0)
            def _():
                pbuf[s - 1, :, cut] = in_bf16(product)

        tiled(4, tile, one)

    def out_copy(s, sends, recvs):
        return remote_copy(
            pbuf.at[s - 1],
            land.at[s - 1],
            sends.at[s],
            recvs.at[s],
            rep,
            flipped(mine, s, n_fsdp),
        )

    def summed(cut):
        total = own[cut]
        for s in others:
            total += in_f32(land[s - 1, cut])
        return total

    def scaled(values, gain):
        scale = lax.rsqrt(jnp.mean(values * values, axis=-1, keepdims=True) + EPS_NORM)
        return in_bf16(values * scale * gain)


    def attention_stores(s):
        cut = block_rows(s)
        pairs = (
            (nb, normed_all), (raw, raw_all), (qb, q_all), (kvb, k_all), (vb, v_all), (gb, gated_all)
        )
        return [
            pltpu.make_async_copy(src, dst.at[cut], keep.at[i])
            for i, (src, dst) in enumerate(pairs)
        ]

    def angle_loads(s):
        cut = block_rows(s)
        return [
            pltpu.make_async_copy(all_cos.at[cut], cs, load.at[2]),
            pltpu.make_async_copy(all_sin.at[cut], sn, load.at[3]),
        ]

    def attention(i, carry):
        s = (i + 1) % n_fsdp
        for copy in angle_loads(s):
            copy.start()
        for k in range(n_fsdp):

            @pl.when(s == k)
            def _(k=k):
                if k == 0:
                    token_rows.own().wait()
                else:
                    token_rows.arrive(k)

        @pl.when(i > 0)
        def _():
            for copy in attention_stores(s):
                copy.wait()

        def normed_rows(r):
            values = in_f32(tok[some_rows(s * rows, r)])
            nb[some_rows(0, r)] = scaled(values, gain_out[0:1])

        by_rows(normed_rows)

        @pl.when(i == 0)
        def _():
            attn_load().wait()

        def raw_tile(cut):
            raw[:, cut] = product_of(nb[...], wa[:, cut], 1, 0)

        tiled(3, cols // 3, raw_tile)
        for copy in angle_loads(s):
            copy.wait()
        attend(
            heads_k,
            block_mask(pair_ref, rows, s),
            cs[...],
            sn[...],
            head_gain_out[0:1],
            head_gain_out[1:2],
            raw,
            qb,
            kvb,
            vb,
            gb,
        )
        for copy in attention_stores(s):
            copy.start()
        leave(s, gb, wo)

        @pl.when(s > 0)
        def _():
            out_copy(s, ps, pr).start()

        return carry

    lax.fori_loop(0, n_fsdp, attention, 0)
    for k in range(1, n_line // 2):
        line_arrivals(k)
    for s in others:
        out_copy(s, ps, pr).wait()

    def middle_rows(r):
        cut = some_rows(0, r)
        values = in_f32(tok[cut]) + summed(cut)
        mid[cut] = values
        nm[cut] = scaled(values, gain_out[1:2])

    by_rows(middle_rows)
    up_rows.start()

    def middle_store():
        return pltpu.make_async_copy(mid, middle_out, load.at[4])

    middle_store().start()
    for copy in attention_stores(0):
        copy.wait()


    for k in range(n_line // 2, n_line - 1):
        line_arrivals(k)
    up_rows.forward()
    line_arrivals(n_line - 1)
    shares(lambda copy: copy.wait_recv())
    for copy in local((4, 5)):
        copy.wait()
    mlp_load().start()
    mlp_load().wait()

    def block_load(source, s):
        return pltpu.make_async_copy(source.at[block_rows(s)], nb, load.at[2])

    def ff_stores(s):
        cut = block_rows(s)
        return [
            pltpu.make_async_copy(hb, hidden_all.at[cut], keep.at[0]),
            pltpu.make_async_copy(gu, gu_all.at[cut], keep.at[1]),
        ]

    def into_nb(gather, source, s):
        @pl.when(s == 0)
        def _():
            nb[...] = nm[...]

        for k in others:

            @pl.when(s == k)
            def _(k=k):
                gather.arrive(k)

        @pl.when(s > 0)
        def _():
            copy = block_load(source, s)
            copy.start()
            copy.wait()

    def feed_forward(i, carry):
        s = (i + 1) % n_fsdp
        into_nb(up_rows, nmlp_all, s)

        @pl.when(i > 0)
        def _():
            for copy in ff_stores(s):
                copy.wait()

        def pre_tile(cut):
            gu[:, cut] = product_of(nb[...], wm[:, cut], 1, 0)

        tiled(6, ff // 3, pre_tile)

        def hidden_rows(r):
            cut = some_rows(0, r)
            gate_pre = gu[cut, :ff]
            hb[cut] = in_bf16(gate_pre * jax.nn.sigmoid(gate_pre) * gu[cut, ff:])

        by_rows(hidden_rows)
        for copy in ff_stores(s):
            copy.start()
        leave(s, hb, wd)

        @pl.when(s > 0)
        def _():
            out_copy(s, qs, qr).start()

        return carry

    lax.fori_loop(0, n_fsdp, feed_forward, 0)
    up_rows.sent()
    up_rows.own().wait()
    middle_store().wait()
    for copy in ff_stores(0):
        copy.wait()


    def gu_load(s):
        return pltpu.make_async_copy(gu_all.at[block_rows(s)], gu, load.at[5])

    gu_load(0).start()
    for s in others:
        out_copy(s, qs, qr).wait()
    head_len = pair_ref[0, 0]
    both_len = head_len + pair_ref[0, 1]
    loss_out[...] = jnp.zeros_like(loss_out)

    def error_rows(r):
        cut = some_rows(0, r)
        index = r * ROW_STEP + lax.broadcasted_iota(jnp.int32, (ROW_STEP, 1), 0)
        valid = (index < both_len).astype(jnp.float32)
        result = mid[cut] + summed(cut)
        error = (result - in_f32(te[cut])) * valid
        square = jnp.sum(error * error, axis=-1, keepdims=True)
        first = jnp.where(index < head_len, square, 0.0)
        loss_out[0:1] += jnp.sum(first, axis=0, keepdims=True)
        loss_out[1:2] += jnp.sum(square - first, axis=0, keepdims=True)
        te[cut] = in_bf16(result * valid)
        grad = error * factor_ref[0, 0]
        mid[cut] = grad
        nm[cut] = in_bf16(grad)

    by_rows(error_rows)
    back_rows.start()
    last_stores = [
        pltpu.make_async_copy(te, block_out, load.at[3]),
        pltpu.make_async_copy(mid, gres_out, load.at[4]),
    ]
    for copy in last_stores:
        copy.start()

    def grad_store(s):
        return pltpu.make_async_copy(gm, gmlp_all.at[block_rows(s)], keep.at[2])

    def feed_back(s, carry):
        @pl.when(s == 1)
        def _():
            back_rows.forward()

        into_nb(back_rows, gbranch_all, s)

        def hidden_tile(cut):
            raw[:, cut] = product_of(nb[...], wd[cut], 1, 1)

        tiled(3, ff // 3, hidden_tile)
        gu_load(s).wait()

        @pl.when(s > 0)
        def _():
            grad_store(s).wait()

        def grad_rows(r):
            cut = some_rows(0, r)
            gate_pre, grad = gu[cut, :ff], raw[cut]
            gate = jax.nn.sigmoid(gate_pre)
            silu = gate_pre * gate
            gm[cut, :ff] = in_bf16(grad * gu[cut, ff:] * (gate + silu * (1.0 - gate)))
            gm[cut, ff:] = in_bf16(grad * silu)

        by_rows(grad_rows)
        grad_store(s).start()

        @pl.when(s + 1 < n_fsdp)
        def _():
            gu_load(s + 1).start()

        return carry

    lax.fori_loop(0, n_fsdp, feed_back, 0)

    grad_store(0).wait()
    for copy in last_stores:
        copy.wait()
    back_rows.sent()
    back_rows.own().wait()
    token_rows.sent()
    for s in others:
        partner_copy(s).wait_send()
        for i in range(4):
            weight_copy(s, i).wait_send()
        for i in range(2):
            sibling_copy(s, i).wait_send()
            mlp_copy(s, i).wait_send()
    lines_sent()
    shares(lambda copy: copy.wait_send())


def forward(n_fsdp, n_rep, heads_k, args):
    rows, width = args[0].shape
    rows_all = n_fsdp * rows
    cols_q, cols_k = heads_k * (H // KV) * HD, heads_k * HD
    cols = 2 * cols_q + 2 * cols_k
    ff = args[9].shape[0]
    n_line = n_rep // 2
    low, full = jnp.bfloat16, jnp.float32
    dma = pltpu.SemaphoreType.DMA
    any_spec = pl.BlockSpec(memory_space=pl.ANY)
    vmem, smem = pl.BlockSpec(memory_space=pltpu.VMEM), pl.BlockSpec(memory_space=pltpu.SMEM)
    outs = (
        ((rows_all, width), low),
        ((rows_all, cols), full),
        ((rows_all, cols_q), low),
        ((rows_all, cols_k), low),
        ((rows_all, cols_k), low),
        ((rows_all, cols_q), low),
        ((width, cols), low),
        ((width, 2 * ff), low),
        ((rows, width), full),
        ((rows_all, width), low),
        ((rows_all, ff), low),
        ((rows_all, width), low),
        ((rows_all, 2 * ff), low),
        ((rows, width), full),
        ((rows, width), low),
        ((rows_all, 2 * ff), full),
        ((8, width), full),
        ((8, HD), full),
        ((8, HD), full),
    )
    scratch = (
        ((rows_all, width), low),
        ((n_fsdp, 16, HD), low),
        ((width, cols), low),
        ((cols_q, width), low),
        ((ff, width), low),
        ((width, 2 * ff), low),
        ((rows, width), low),
        ((rows, cols), full),
        ((rows, HD), full),
        ((rows, HD), full),
        ((rows, cols_q), low),
        ((rows, cols_k), low),
        ((rows, cols_k), low),
        ((rows, cols_q), low),
        ((rows, width), full),
        ((n_fsdp - 1, rows, width), low),
        ((n_fsdp - 1, rows, width), low),
        ((rows, width), full),
        ((rows, width), low),
        ((rows, width), low),
        ((rows, 2 * ff), full),
        ((rows, ff), low),
        ((rows, 2 * ff), low),
    )
    one, pair, four = dma((n_fsdp,)), dma((n_fsdp, 2)), dma((n_fsdp, 4))
    line = dma((2, n_fsdp, n_line))
    return pl.pallas_call(
        functools.partial(forward_kernel, n_fsdp, n_rep, heads_k),
        out_shape=[jax.ShapeDtypeStruct(shape, kind) for shape, kind in outs],
        in_specs=[any_spec] * 13 + [smem] * 2,
        out_specs=[any_spec] * 16 + [vmem] * 3,
        scratch_shapes=[pltpu.VMEM(shape, kind) for shape, kind in scratch]
        + [pair, pair, dma] * 3
        + [one, one, four, four, one, one, pair, pair]
        + [pair, pair, line, line, line, line, one, one, one, one]
        + [dma((6,)), dma((6,)), dma((10,))],
        compiler_params=pltpu.CompilerParams(
            collective_id=1, has_side_effects=True, vmem_limit_bytes=62 << 20
        ),
        name="forward",
    )(*args)


def shards(
    tokens,
    teacher,
    lengths,
    deal_order,
    attention_gain,
    query_gain,
    key_gain,
    w_query,
    w_key,
    w_value,
    w_outgate,
    w_output,
    mlp_gain,
    w_gate,
    w_up,
    w_down,
):
    n_rep = lax.axis_size("rep")
    n_fsdp = lax.axis_size("fsdp")
    rows, width = tokens.shape
    mine = lax.axis_index("fsdp")
    core = lax.axis_index("rep") % 2
    others = range(1, n_fsdp)
    heads_q, heads_k = H // n_fsdp, KV // n_fsdp
    cols_q, cols_k = heads_q * HD, heads_k * HD
    deep = w_query.shape[0]
    ff = w_down.shape[0]
    rows_all = rows * n_fsdp

    peers = mine ^ jnp.arange(n_fsdp, dtype=jnp.int32)
    devices = lax.axis_index("rep") * n_fsdp + peers
    slot_ids = (devices[:, None] * 2 + jnp.arange(2, dtype=jnp.int32)[None, :]).reshape(-1)
    seq_ids = jnp.arange(lengths.shape[0], dtype=jnp.int32)
    slot_seq = jnp.sum(
        jnp.where(seq_ids[None, :] == slot_ids[:, None], deal_order[None, :], 0), axis=1
    )
    pair_len = jnp.sum(
        jnp.where(seq_ids[None, :] == slot_seq[:, None], lengths[None, :], 0), axis=1
    ).reshape(n_fsdp, 2)
    token_count = jnp.sum(lengths).astype(jnp.float32)
    factor = rows * n_rep * n_fsdp / (2.0 * token_count)
    angle_cos, angle_sin = row_layout(pair_len, rows, HD)
    angle_cos, angle_sin = angle_cos.reshape(rows_all, HD), angle_sin.reshape(rows_all, HD)

    small = query_gain.shape[0]

    def spread(gain):
        return lax.dynamic_update_slice(
            jnp.zeros((1, HD), jnp.bfloat16), gain[None], (0, mine * small)
        )

    gain_block = jnp.concatenate(
        [
            attention_gain.reshape(-1, HD),
            mlp_gain.reshape(-1, HD),
            spread(query_gain),
            spread(key_gain),
            jnp.zeros((14 - 2 * deep // HD, HD), jnp.bfloat16),
        ]
    )
    (
        normed_all,
        attn_raw,
        queries_b,
        keys_b,
        values_b,
        gated_b,
        w_attn,
        w_mlp,
        middle,
        normed_mlp_all,
        hidden_b,
        grad_branch_all,
        grad_mlp_b,
        grad_result,
        block_out,
        _,
        gain_rows,
        head_gains,
        losses,
    ) = forward(
        n_fsdp,
        n_rep,
        heads_k,
        (
            tokens,
            gain_block,
            w_query,
            w_outgate,
            w_key,
            w_value,
            w_gate,
            w_up,
            w_output,
            w_down,
            teacher,
            angle_cos,
            angle_sin,
            pair_len,
            (2.0 * factor).reshape(1, 1),
        ),
    )
    seq_loss = losses[:2, 0] / (2.0 * token_count)
    piece_rows, piece_cols = deep // 2, width // n_fsdp
    units, base = [], 0
    for by_owner, row_blocks, cols in (
        (False, ff // 2 // piece_rows, width),
        (True, n_fsdp, 2 * ff),
        (False, cols_q // 2 // piece_rows, width),
        (True, n_fsdp, 2 * cols_q + 2 * cols_k),
    ):
        units.append(Unit(base, by_owner, row_blocks, cols // piece_cols))
        base += units[-1].count
    pieces, _, _, _, _, tokens_grad, gain_sums = backward(
        n_fsdp,
        n_rep,
        heads_k,
        units,
        piece_rows,
        piece_cols,
        (
            hidden_b,
            normed_mlp_all,
            gated_b,
            normed_all,
            grad_branch_all,
            grad_mlp_b,
            w_mlp,
            w_output,
            w_attn,
            middle,
            grad_result,
            tokens,
            attn_raw,
            angle_cos,
            angle_sin,
            queries_b,
            keys_b,
            values_b,
            gain_rows,
            head_gains,
            pair_len,
        ),
    )
    down, mlp, outp, attn = units

    def by_rows(unit, weight):
        blocks, together = unit.row_blocks, unit.col_blocks
        return widened(
            pieces,
            (2, blocks),
            together,
            lambda c, r: (unit.base // together + r, c, 0, 0),
            weight.shape,
            lambda c, r: (c * blocks + r, 0),
        )

    def by_owners(unit, weight, which):
        together = unit.col_blocks // 2
        return widened(
            pieces,
            (2, n_fsdp),
            together,
            lambda c, f: (unit.base // together + 2 * f + which, c, 0, 0),
            weight.shape,
            lambda c, f: (c, f),
        )

    dw_down = by_rows(down, w_down)
    dw_output = by_rows(outp, w_output)
    dw_gate = by_owners(mlp, w_gate, 0)
    dw_up = by_owners(mlp, w_up, 1)
    dw_query, dw_outgate, dw_key, dw_value = widened_heads(
        pieces,
        attn.base,
        n_fsdp,
        (w_query.shape, w_outgate.shape, w_key.shape, w_value.shape),
    )

    def own_part(row, start, cols):
        return lax.dynamic_slice(gain_sums, (row, start + mine * cols), (1, cols))[0]

    return (
        block_out,
        seq_loss,
        tokens_grad,
        own_part(0, 0, deep),
        own_part(0, width, small),
        own_part(1, width, small),
        dw_query,
        dw_key,
        dw_value,
        dw_outgate,
        dw_output,
        own_part(1, 0, deep),
        dw_gate,
        dw_up,
        dw_down,
    )


def solution(mesh):
    return jax.shard_map(
        shards,
        mesh=mesh,
        in_specs=(
            P(("rep", "fsdp"), None),
            P(("rep", "fsdp"), None),
            P(),
            P(),
            P("fsdp"),
            P("fsdp"),
            P("fsdp"),
            P("fsdp", None),
            P("fsdp", None),
            P("fsdp", None),
            P("fsdp", None),
            P("fsdp", None),
            P("fsdp"),
            P("fsdp", None),
            P("fsdp", None),
            P("fsdp", None),
        ),
        out_specs=(
            P(("rep", "fsdp"), None),
            P(("rep", "fsdp")),
            P(("rep", "fsdp"), None),
            P("fsdp"),
            P("fsdp"),
            P("fsdp"),
            P("fsdp", None),
            P("fsdp", None),
            P("fsdp", None),
            P("fsdp", None),
            P("fsdp", None),
            P("fsdp"),
            P("fsdp", None),
            P("fsdp", None),
            P("fsdp", None),
        ),
        check_vma=False,
    )
```

```python
import functools

import jax
import jax.numpy as jnp
import numpy as np
from jax import lax
from jax.experimental import pallas as pl
from jax.experimental.pallas import tpu as pltpu
from jax.sharding import PartitionSpec as P

MESH = pl.DeviceIdType.MESH

H = 16
KV = 8
HD = 128


EPS_NORM = 1e-06
ROPE_BASE = 1000000.0
NEG_FILL = -1e30


def in_f32(values):
    return values.astype(jnp.float32)


def in_bf16(values):
    return values.astype(jnp.bfloat16)


def flipped(index, step, n):
    out, bit = index, 1
    while bit < n:
        has = (step // bit) % 2
        out = out + has * bit * (1 - 2 * ((index // bit) % 2))
        bit *= 2
    return out


def at_least(value, bound, span):
    span = max(span, bound)
    return (value + (span - bound)) // span


class Unit:
    def __init__(self, base, by_owner, row_blocks, col_blocks):
        self.base, self.by_owner = base, by_owner
        self.row_blocks, self.col_blocks = row_blocks, col_blocks
        self.count = row_blocks * col_blocks


LAG_B, LAG_C, LAG_D, LAG_E, LAG_G = 2, 4, 6, 8, 14
RING = 4


ROW_STEP = 32
TILES = 8


def norm_back(grad, raw, gain):
    scale = lax.rsqrt(jnp.mean(raw * raw, axis=-1, keepdims=True) + EPS_NORM)
    unit = raw * scale
    inner = grad * gain
    return scale * (inner - unit * jnp.mean(inner * unit, axis=-1, keepdims=True)), grad * unit


def backward_kernel(n_fsdp, n_rep, heads_k, units, piece_rows, piece_cols, *refs):
    (hidden, normed_mlp, gated, normed, grad_branch, grad_mlp, w_mlp, w_output, w_attn) = refs[:9]
    (middle, grad_result, tokens, attn_raw, all_cos, all_sin, all_q, all_k, all_v) = refs[9:18]
    (gains, head_gains, lengths_ref, deal_ref) = refs[18:22]
    (out, grad_attn, grad_raw, inb, xb, tokens_grad, gain_out) = refs[22:29]
    (lm, lo, rh, sb, kb, r1, c_slot, d_slot, big, wt, own, pbuf, land_a, land_b) = refs[29:43]
    (mid, gres, tok, ga, wo, raw, cs, sn, qb, kvb, vb, gb, gg, ob) = refs[43:57]
    (tile_sem, r1s, r1r, ins, inr, xs, xr, os_, fs, fr, gs, gr, ls) = refs[57:70]
    (load_sem, first_sem, wt_sem, ps, pr, qs, qr, ag_s, ag_r, ag_l, block_sem) = refs[70:81]
    (near_land, pair_land, in_land, far_land, near_s, near_r, line_s, line_r) = refs[81:]
    head_gain_out = gain_out.at[:, pl.ds(own.shape[1], HD)]
    lefts = (hidden, normed_mlp, gated, normed)
    rights = (grad_branch, grad_mlp, grad_attn, grad_raw)
    total = sum(unit.count for unit in units)
    rows, width = own.shape
    rows_all = n_fsdp * rows
    ff = grad_mlp.shape[1] // 2
    tile = width // TILES
    others = range(1, n_fsdp)
    rep, mine = lax.axis_index("rep"), lax.axis_index("fsdp")
    core, place = rep % 2, rep // 2
    n_line = n_rep // 2
    half = n_line // 2
    side = place // half
    depth = place * (1 - side) + (n_line - 1 - place) * side
    inward = (place + 1 - 2 * side) * 2 + core
    outward = (place - 1 + 2 * side) * 2 + core
    sib = rep + 1 - 2 * core
    at_middle = depth == half - 1

    barrier = pltpu.get_barrier_semaphore()

    def greet(to_rep, to_fsdp):
        pl.semaphore_signal(
            barrier, inc=1, device_id={"rep": to_rep, "fsdp": to_fsdp}, device_id_type=MESH
        )

    greet(sib, mine)
    greet(inward, mine)
    for s in others:
        greet(rep, flipped(mine, s, n_fsdp))

    @pl.when(depth == 0)
    def _():
        pl.semaphore_wait(barrier, 1 + n_fsdp)

    @pl.when(depth > 0)
    def _():
        greet(outward, mine)
        pl.semaphore_wait(barrier, 2 + n_fsdp)


    def r1_copy(p):
        return remote_copy(sb.at[p % RING], r1.at[p], r1s.at[p], r1r.at[p], sib, mine)

    def in_copy(p):
        return remote_copy(r1.at[p], inb.at[p], ins.at[p], inr.at[p], inward, mine)

    def x_copy(p):
        return remote_copy(r1.at[p], xb.at[p], xs.at[p], xr.at[p], inward, mine)

    def o_copy(p, src):
        return remote_copy(src.at[p], xb.at[p], os_, xr.at[p], outward, mine)

    def inside_of(p, unit):
        inside = at_least(p, unit.base, total - unit.base)
        stop = unit.base + unit.count
        if stop < total:
            inside = inside * (1 - at_least(p, stop, total - stop))
        return inside

    def owner_of(p):
        step = 0
        for unit in units:
            if unit.by_owner:
                i = p - unit.base
                step = step + inside_of(p, unit) * (n_fsdp - 1 - i // unit.col_blocks)
        return step

    def spot(p, source):
        where = p
        for unit in units:
            if unit.by_owner:
                i = p - unit.base
                spread = unit.base + source * unit.col_blocks + i % unit.col_blocks
                where = where + inside_of(p, unit) * (spread - p)
        return where

    def f_copy(p, step):
        return remote_copy(
            r1.at[p],
            out.at[spot(p, mine), core],
            fs,
            fr.at[p],
            rep,
            flipped(mine, step, n_fsdp),
        )

    def g_copy(src, where):
        return remote_copy(src, out.at[where, core], gs, gr, sib, mine)

    def l_copy(p):
        return pltpu.make_async_copy(r1.at[p], out.at[spot(p, mine), core], ls)

    def c_load(p):
        return pltpu.make_async_copy(inb.at[p], c_slot, load_sem.at[0])

    def d_load(p):
        return pltpu.make_async_copy(xb.at[p], d_slot, load_sem.at[1])

    def e_load(p):
        return pltpu.make_async_copy(xb.at[p], r1.at[p], load_sem.at[2])

    def add_into(p, other):
        r1[p] = in_bf16(in_f32(r1[p]) + in_f32(other))

    def begin_c(p):
        @pl.when(depth > 0)
        def _():
            in_copy(p).wait_recv()
            c_load(p).start()

    def begin_d(p):
        @pl.when(at_middle)
        def _():
            x_copy(p).wait_recv()
            d_load(p).start()

    def begin_e(p):
        @pl.when(depth < half - 1)
        def _():
            o_copy(p, xb).wait_recv()

            @pl.when(depth > 0)
            def _():
                o_copy(p, xb).start()

            in_copy(p).wait_send()
            e_load(p).start()

    def end_b(p):
        r1_copy(p).wait_recv()
        add_into(p, kb[p % RING])
        if half > 1:

            @pl.when(depth == 0)
            def _():
                in_copy(p).start()
        else:
            x_copy(p).start()

    def end_c(p):
        @pl.when(depth > 0)
        def _():
            c_load(p).wait()
            add_into(p, c_slot[...])

            @pl.when(depth < half - 1)
            def _():
                in_copy(p).start()

            @pl.when(at_middle)
            def _():
                x_copy(p).start()

    def end_d(p):
        @pl.when(at_middle)
        def _():
            d_load(p).wait()
            x_copy(p).wait_send()
            add_into(p, d_slot[...])

            @pl.when(depth > 0)
            def _():
                o_copy(p, r1).start()

    def end_e(p):
        @pl.when(depth < half - 1)
        def _():
            e_load(p).wait()

        step = owner_of(p)

        @pl.when(step == 0)
        def _():
            l_copy(p).start()
            g_copy(r1.at[p], spot(p, mine)).start()

        @pl.when(step > 0)
        def _():
            f_copy(p, step).start()

    def end_g(p):
        step = owner_of(p)

        @pl.when(step > 0)
        def _():
            f_copy(p, step).wait_recv()
            where = spot(p, flipped(mine, step, n_fsdp))
            g_copy(out.at[where, core], where).start()

    def run(stages, t):
        for lag, stage in stages:
            pl.when((t >= lag) & (t < total + lag))(functools.partial(stage, t - lag))

    def begin(t):
        run([(LAG_C, begin_c), (LAG_D, begin_d), (LAG_E, begin_e)], t)

    def end(t):
        run([(LAG_B, end_b), (LAG_C, end_c), (LAG_D, end_d), (LAG_E, end_e), (LAG_G, end_g)], t)

    def tiles(u, i, slot):
        unit = units[u]
        r, j = i // unit.col_blocks, i % unit.col_blocks
        if unit.by_owner:
            owner = flipped(mine, n_fsdp - 1 - r, n_fsdp)
            first = owner * 2 * piece_rows + core * piece_rows
            second = owner * 2 * piece_rows + (1 - core) * piece_rows
        else:
            first = core * unit.row_blocks * piece_rows + r * piece_rows
            second = (1 - core) * unit.row_blocks * piece_rows + r * piece_rows
        first = pl.ds(pl.multiple_of(first, piece_rows), piece_rows)
        second = pl.ds(pl.multiple_of(second, piece_rows), piece_rows)
        cols = pl.ds(pl.multiple_of(j * piece_cols, piece_cols), piece_cols)
        return [
            pltpu.make_async_copy(lefts[u].at[:, first], lm.at[slot], tile_sem.at[slot, 0]),
            pltpu.make_async_copy(lefts[u].at[:, second], lo.at[slot], tile_sem.at[slot, 1]),
            pltpu.make_async_copy(rights[u].at[:, cols], rh.at[slot], tile_sem.at[slot, 2]),
        ]


    first_pairs = (
        (grad_mlp.at[:, pl.ds(0, ff)], big.at[pl.ds(0, rows_all)]),
        (grad_mlp.at[:, pl.ds(ff, ff)], big.at[pl.ds(rows_all, rows_all)]),
        (middle, mid),
        (grad_result, gres),
        (tokens, tok),
        (w_output, wo),
    )

    def first_loads(which):
        return [pltpu.make_async_copy(*first_pairs[i], first_sem.at[i]) for i in which]

    def attn_load():
        return pltpu.make_async_copy(w_attn, big.at[pl.ds(0, width)], first_sem.at[6])

    def tile_of(j):
        return pl.ds(pl.multiple_of(j * tile, tile), tile)

    def wt_load(j):
        return pltpu.make_async_copy(w_mlp.at[tile_of(j)], wt.at[j % 2], wt_sem.at[j % 2])

    def p_copy(s, j):
        return remote_copy(
            pbuf.at[s - 1, :, tile_of(j)],
            land_a.at[s - 1, :, tile_of(j)],
            ps.at[s, j],
            pr.at[s, j],
            rep,
            flipped(mine, s, n_fsdp),
        )

    def q_copy(s):
        return remote_copy(
            pbuf.at[s - 1], land_b.at[s - 1], qs.at[s], qr.at[s], rep, flipped(mine, s, n_fsdp)
        )

    gather = GatherRows(n_fsdp, rep, mine, ga, grad_attn, (ag_s, ag_r, ag_l))

    def mlp_products(j):
        @pl.when(j == 0)
        def _():
            for copy in first_loads((0, 1)):
                copy.wait()

        wt_load(j).wait()

        @pl.when(j + 1 < TILES)
        def _():
            wt_load(j + 1).start()

        for s in (*others, 0):
            part = product_of(big[s * rows : (s + 1) * rows], wt[j % 2, :, :ff], 1, 1)
            part += product_of(
                big[rows_all + s * rows : rows_all + (s + 1) * rows], wt[j % 2, :, ff:], 1, 1
            )
            if s == 0:
                own[:, tile_of(j)] = part
            else:
                pbuf[s - 1, :, tile_of(j)] = in_bf16(part)
                p_copy(s, j).start()

    row_steps = rows // ROW_STEP

    def middle_back(part):
        if part == 0:
            middle_sums()

        def some_rows(r, carry):
            cut = pl.ds(pl.multiple_of(r * ROW_STEP, ROW_STEP), ROW_STEP)
            grad = own[cut]
            for s in others:
                grad += in_f32(land_a[s - 1, cut])
            back, gain_rows = norm_back(grad, mid[cut], gains[1:2])
            gain_out[1:2, :width] += jnp.sum(gain_rows, axis=0, keepdims=True)
            back = gres[cut] + back
            gres[cut] = back
            ga[cut] = in_bf16(back)
            return carry

        lax.fori_loop(part * row_steps // 2, (part + 1) * row_steps // 2, some_rows, 0)
        if part == 1:
            gather.start()
            for copy in block_loads(0):
                copy.start()

    def middle_sums():
        attn_load().start()
        for copy in first_loads((2, 3)):
            copy.wait()

        def wait_tiles(j, carry):
            for s in others:
                p_copy(s, j).wait()
            return carry

        lax.fori_loop(0, TILES, wait_tiles, 0)
        gain_out[...] = jnp.zeros_like(gain_out)

    def block_loads(s):
        cut = pl.ds(pl.multiple_of(s * rows, rows), rows)
        pairs = (
            (attn_raw, raw), (all_cos, cs), (all_sin, sn), (all_q, qb), (all_k, kvb), (all_v, vb)
        )
        copies = [
            pltpu.make_async_copy(src.at[cut], dst, block_sem.at[i])
            for i, (src, dst) in enumerate(pairs)
        ]
        return copies

    def grad_load(s):
        cut = pl.ds(pl.multiple_of(s * rows, rows), rows)
        return pltpu.make_async_copy(grad_attn.at[cut], gb, block_sem.at[6])

    def store(s):
        cut = pl.ds(pl.multiple_of(s * rows, rows), rows)
        return pltpu.make_async_copy(ob, grad_raw.at[cut], block_sem.at[7])

    def heads_back(s, heads):
        attend_back(
            heads_k,
            heads,
            block_mask(
                block_lengths(lengths_ref, deal_ref, rep * n_fsdp + flipped(mine, s, n_fsdp)), rows
            ),
            cs[...],
            sn[...],
            head_gains[0:1],
            head_gains[1:2],
            raw,
            qb,
            kvb,
            vb,
            gg,
            ob,
            head_gain_out,
        )

    early = heads_k // 2

    def block_first(s):
        @pl.when(s == 0)
        def _():
            first_loads((5,))[0].wait()
            gb[...] = ga[...]

        for k in others:

            @pl.when(s == k)
            def _(k=k):
                gather.arrive(k)

        @pl.when(s > 0)
        def _():
            copy = grad_load(s)
            copy.start()
            copy.wait()

        gg[...] = product_of(gb[...], wo[...], 1, 1)
        for copy in block_loads(s):
            copy.wait()
        heads_back(s, range(early))

    def block_second(s):
        heads_back(s, range(early, heads_k))
        store(s).start()

        @pl.when(s + 1 < n_fsdp)
        def _():
            for copy in block_loads(s + 1):
                copy.start()

    def block_third(s):
        store(s).wait()

        @pl.when(s == 0)
        def _():
            attn_load().wait()

        def one_tile(j, carry):
            part = product_of(ob[...], big[tile_of(j)], 1, 1)

            @pl.when(s == 0)
            def _():
                own[:, tile_of(j)] = part

            @pl.when(s > 0)
            def _():
                pbuf[s - 1, :, tile_of(j)] = in_bf16(part)

            return carry

        lax.fori_loop(0, TILES, one_tile, 0)

        @pl.when(s > 0)
        def _():
            q_copy(s).start()

    def tokens_back(part):
        if part == 0:
            gather.sent()
            first_loads((4,))[0].wait()
            for s in others:
                q_copy(s).wait()

        def some_rows(r, carry):
            cut = pl.ds(pl.multiple_of(r * ROW_STEP, ROW_STEP), ROW_STEP)
            grad = own[cut]
            for s in others:
                grad += in_f32(land_b[s - 1, cut])
            back, gain_rows = norm_back(grad, in_f32(tok[cut]), gains[0:1])
            gain_out[0:1, :width] += jnp.sum(gain_rows, axis=0, keepdims=True)
            tokens_grad[cut] = in_bf16(gres[cut] + back)
            return carry

        lax.fori_loop(part * row_steps // 2, (part + 1) * row_steps // 2, some_rows, 0)
        if part == 1:
            near_land[mine] = gain_out[...]
            for s in others:
                near_copy(s).start()


    def near_copy(s):
        return remote_copy(
            gain_out,
            near_land.at[mine],
            near_s.at[s],
            near_r.at[s],
            rep,
            flipped(mine, s, n_fsdp),
        )

    def line_copy(k, target, to_rep):
        return remote_copy(gain_out, target, line_s.at[k], line_r.at[k], to_rep, mine)

    def pair_copy():
        return line_copy(0, pair_land, sib)

    def gain_in():
        return line_copy(1, in_land, inward)

    def gain_across():
        return line_copy(2, far_land, inward)

    def gain_back():
        return line_copy(3, far_land, outward)

    def gains_near():
        for s in others:
            near_copy(s).wait()
        summed = near_land[0]
        for k in others:
            summed += near_land[k]
        gain_out[...] = summed
        pair_copy().start()

    def gains_pair():
        pair_copy().wait()
        gain_out[...] += pair_land[...]

        @pl.when(depth == 0)
        def _():
            (gain_in if half > 1 else gain_across)().start()

    def gains_in(k):
        @pl.when(depth == k)
        def _():
            gain_in().wait_recv()
            gain_out[...] += in_land[...]
            (gain_in if k < half - 1 else gain_across)().start()

    def gains_across():
        @pl.when(at_middle)
        def _():
            gain_across().wait()
            gain_out[...] += far_land[...]
            if half > 1:
                gain_back().start()

    def gains_back(k):
        @pl.when(depth == k)
        def _():
            gain_back().wait_recv()
            gain_in().wait_send()
            gain_out[...] = far_land[...]
            if k > 0:
                gain_back().start()

    def tasks(u, i):
        if u == 0:

            @pl.when(i == 1)
            def _():
                wt_load(0).start()
                for copy in first_loads((0, 1)):
                    copy.start()

            @pl.when(i == 6)
            def _():
                for copy in first_loads((2, 3, 4, 5)):
                    copy.start()

            pl.when((i >= 4) & (i < 4 + TILES))(lambda: mlp_products(i - 4))
        if u == 1:
            for part in range(2):
                pl.when(i == 7 + part)(functools.partial(middle_back, part))
            pl.when(i == 12)(gather.forward)
            pl.when(i == 15)(lambda: gather.own().wait())
            last = 15 + 3 * (n_fsdp - 1)
            busy = ((i >= 9) & (i < 12)) | ((i >= 15) & (i < last))
            s = at_least(i, 12, units[1].count) * ((i - 12) // 3)
            for phase, task in enumerate((block_first, block_second, block_third)):
                pl.when(busy & (i % 3 == phase))(functools.partial(task, s))
        if u == 3:
            for part in range(2):
                pl.when(i == 2 + part)(functools.partial(tokens_back, part))
            pl.when(i == 6)(gains_near)
            pl.when(i == 8)(gains_pair)

    def product(left, right):
        return product_of(left, right, 0, 0)

    for copy in tiles(0, 0, 0):
        copy.start()
    for u, unit in enumerate(units):

        def step(i, carry, u=u, unit=unit):
            t = unit.base + i
            slot = t % 2
            begin(t)
            for copy in tiles(u, i, slot):
                copy.wait()

            @pl.when(i + 1 < unit.count)
            def _():
                for copy in tiles(u, i + 1, 1 - slot):
                    copy.start()

            if u + 1 < len(units):

                @pl.when(i + 1 == unit.count)
                def _():
                    for copy in tiles(u + 1, 0, 1 - slot):
                        copy.start()

            @pl.when(t >= RING)
            def _():
                r1_copy(t - RING).wait_send()

            sb[t % RING] = in_bf16(product(lo[slot], rh[slot]))
            r1_copy(t).start()
            kb[t % RING] = product(lm[slot], rh[slot])
            end(t)
            tasks(u, i)
            return carry

        lax.fori_loop(0, unit.count, step, 0)

    def drain(t, carry):
        begin(t)
        end(t)
        return carry

    lax.fori_loop(total, total + LAG_G, drain, 0)

    for p in range(total - RING, total):
        r1_copy(p).wait_send()
    kept = sum(u.col_blocks if u.by_owner else u.count for u in units)
    some, rest = pl.ds(0, kept), pl.ds(0, total - kept)
    every = remote_copy(r1, out.at[:, core], gs, gr, sib, mine)
    every.wait()
    pltpu.make_async_copy(r1.at[some], out.at[some, core], ls).wait()
    remote_copy(r1.at[rest], out.at[rest, core], fs, fr.at[0], sib, mine).wait_send()

    @pl.when(depth > 0)
    def _():
        remote_copy(r1, xb, os_, xr.at[0], outward, mine).wait_send()

    for k in range(1, half):
        gains_in(k)
    gains_across()
    for k in range(half - 2, -1, -1):
        gains_back(k)
    if half > 1:

        @pl.when(depth > 0)
        def _():
            gain_back().wait_send()


def backward(n_fsdp, n_rep, heads_k, units, piece_rows, piece_cols, args):
    total = sum(unit.count for unit in units)
    rows_all, rows = args[0].shape[0], args[9].shape[0]
    width, cols = args[8].shape
    cols_q, cols_k = heads_k * (H // KV) * HD, heads_k * HD
    two_ff = args[5].shape[1]
    dma = pltpu.SemaphoreType.DMA
    piece = (piece_rows, piece_cols)
    low, full = jnp.bfloat16, jnp.float32
    any_spec = pl.BlockSpec(memory_space=pl.ANY)
    vmem = pl.BlockSpec(memory_space=pltpu.VMEM)
    flops = sum(4 * unit.count for unit in units) * rows_all * piece_rows * piece_cols
    outs = (
        ((total, 2) + piece, low),
        ((rows_all, width), low),
        ((rows_all, cols), low),
        ((total,) + piece, low),
        ((total,) + piece, low),
        ((rows, width), low),
        ((8, width + HD), full),
    )
    scratch = (
        ((2, rows_all, piece_rows), low),
        ((2, rows_all, piece_rows), low),
        ((2, rows_all, piece_cols), low),
        ((RING,) + piece, low),
        ((RING,) + piece, full),
        ((total,) + piece, low),
        (piece, low),
        (piece, low),
        ((max(2 * rows_all, width), cols), low),
        ((2, width // TILES, two_ff), low),
        ((rows, width), full),
        ((n_fsdp - 1, rows, width), low),
        ((n_fsdp - 1, rows, width), low),
        ((n_fsdp - 1, rows, width), low),
        ((rows, width), full),
        ((rows, width), full),
        ((rows, width), low),
        ((rows, width), low),
        ((cols_q, width), low),
        ((rows, cols), full),
        ((rows, HD), full),
        ((rows, HD), full),
        ((rows, cols_q), low),
        ((rows, cols_k), low),
        ((rows, cols_k), low),
        ((rows, width), low),
        ((rows, cols_q), full),
        ((rows, cols), low),
    )
    return pl.pallas_call(
        functools.partial(
            backward_kernel, n_fsdp, n_rep, heads_k, units, piece_rows, piece_cols
        ),
        out_shape=[jax.ShapeDtypeStruct(shape, kind) for shape, kind in outs],
        in_specs=[any_spec] * 18 + [vmem] * 2 + [pl.BlockSpec(memory_space=pltpu.SMEM)] * 2,
        out_specs=[any_spec] * 5 + [vmem] * 2,
        scratch_shapes=[pltpu.VMEM(shape, kind) for shape, kind in scratch]
        + [dma((2, 3))]
        + [dma((total,)) for _ in range(6)]
        + [dma, dma, dma((total,)), dma, dma, dma]
        + [
            dma((3,)),
            dma((7,)),
            dma((2,)),
            dma((n_fsdp, TILES)),
            dma((n_fsdp, TILES)),
            dma((n_fsdp,)),
            dma((n_fsdp,)),
            dma((n_fsdp, 2)),
            dma((n_fsdp, 2)),
            dma,
            dma((8,)),
            pltpu.VMEM((n_fsdp, 8, width + HD), full),
            pltpu.VMEM((8, width + HD), full),
            pltpu.VMEM((8, width + HD), full),
            pltpu.VMEM((8, width + HD), full),
            dma((n_fsdp,)),
            dma((n_fsdp,)),
            dma((4,)),
            dma((4,)),
        ],
        compiler_params=pltpu.CompilerParams(
            collective_id=0, has_side_effects=True, vmem_limit_bytes=62 << 20
        ),
        cost_estimate=pl.CostEstimate(flops=2 * flops, bytes_accessed=1 << 30, transcendentals=0),
        name="backward",
    )(*args)


def widen_kernel(in_ref, out_ref):
    cols = in_ref.shape[-1]
    for i in range(in_ref.shape[0]):
        out_ref[:, i * cols : (i + 1) * cols] = in_ref[i, 0].astype(jnp.float32)


def widened(pieces, grid, together, where, shape, place):
    rows, cols = pieces.shape[2:]
    return pl.pallas_call(
        widen_kernel,
        grid=grid,
        out_shape=jax.ShapeDtypeStruct(shape, jnp.float32),
        in_specs=[pl.BlockSpec((together, 1, rows, cols), where)],
        out_specs=pl.BlockSpec((rows, together * cols), place),
        name="widen",
    )(pieces)


def widen_both_kernel(in_ref, first_ref, second_ref):
    cols, count = in_ref.shape[-1], in_ref.shape[0] // 2
    for i in range(count):
        first_ref[:, i * cols : (i + 1) * cols] = in_f32(in_ref[i, 0])
        second_ref[:, i * cols : (i + 1) * cols] = in_f32(in_ref[count + i, 0])


def widened_both(pieces, base, together, n_fsdp, shape):
    rows, cols = pieces.shape[2:]
    return pl.pallas_call(
        widen_both_kernel,
        grid=(2, n_fsdp),
        out_shape=[jax.ShapeDtypeStruct(shape, jnp.float32)] * 2,
        in_specs=[
            pl.BlockSpec((together, 1, rows, cols), lambda c, f: (base // together + f, c, 0, 0))
        ],
        out_specs=[pl.BlockSpec((rows, together // 2 * cols), lambda c, f: (c, f))] * 2,
        compiler_params=pltpu.CompilerParams(vmem_limit_bytes=32 << 20),
        name="widen_both",
    )(pieces)


def widen_heads_kernel(query_in, gate_in, pair_in, query_out, gate_out, key_out, value_out):
    half = key_out.shape[1]
    query_out[...] = query_in[0, 0].astype(jnp.float32)
    gate_out[...] = gate_in[0, 0].astype(jnp.float32)
    key_out[...] = pair_in[0, 0, :, :half].astype(jnp.float32)
    value_out[...] = pair_in[0, 0, :, half:].astype(jnp.float32)


def widened_heads(pieces, base, n_fsdp, shapes):
    rows, cols = pieces.shape[2:]

    def where(j):
        return lambda c, f: (base + 3 * f + j, c, 0, 0)

    widths = (cols, cols, cols // 2, cols // 2)
    return pl.pallas_call(
        widen_heads_kernel,
        grid=(2, n_fsdp),
        out_shape=[jax.ShapeDtypeStruct(shape, jnp.float32) for shape in shapes],
        in_specs=[pl.BlockSpec((1, 1, rows, cols), where(j)) for j in range(3)],
        out_specs=[pl.BlockSpec((rows, wide), lambda c, f: (c, f)) for wide in widths],
        name="widen_heads",
    )(pieces, pieces, pieces)


def block_lengths(lengths_ref, deal_ref, device):
    head_len = lengths_ref[deal_ref[2 * device]]
    return head_len, head_len + lengths_ref[deal_ref[2 * device + 1]]


def block_mask(block, rows):
    head_len, both_len = block
    query_row = lax.broadcasted_iota(jnp.int32, (rows, rows), 0)
    key_row = lax.broadcasted_iota(jnp.int32, (rows, rows), 1)

    def segment(index):
        return (index >= head_len).astype(jnp.int32) + (index >= both_len).astype(jnp.int32)

    return (segment(query_row) == segment(key_row)) & (key_row <= query_row)


def turn(values):
    half_dim = values.shape[-1] // 2
    return jnp.concatenate([-values[:, half_dim:], values[:, :half_dim]], axis=-1)


def head_forward(raw, gain, angle_cos, angle_sin):
    values = raw * lax.rsqrt(jnp.mean(raw * raw, axis=-1, keepdims=True) + EPS_NORM) * gain
    return in_bf16(values * angle_cos + turn(values) * angle_sin)


def head_backward(grad, raw, gain, angle_cos, angle_sin):
    grad = grad * angle_cos - turn(grad * angle_sin)
    scale = lax.rsqrt(jnp.mean(raw * raw, axis=-1, keepdims=True) + EPS_NORM)
    unit = raw * scale
    gain_rows = grad * unit
    inner = grad * gain
    return scale * (inner - unit * jnp.mean(inner * unit, axis=-1, keepdims=True)), gain_rows


def product_of(left, right, left_dim, right_dim):
    return lax.dot_general(
        left, right, (((left_dim,), (right_dim,)), ((), ())), preferred_element_type=jnp.float32
    )


def softmax_of(queries, keys, allowed):
    scores = jnp.where(allowed, product_of(queries, keys, 1, 1) * HD ** (-0.5), NEG_FILL)
    exponent = jnp.exp(scores - jnp.max(scores, axis=-1, keepdims=True))
    return exponent / jnp.sum(exponent, axis=-1, keepdims=True)


def attend(
    heads_k,
    allowed,
    angle_cos,
    angle_sin,
    query_gain,
    key_gain,
    raw_ref,
    q_ref,
    k_ref,
    v_ref,
    gated_ref,
):
    group = H // KV
    cols_q, cols_k = heads_k * group * HD, heads_k * HD
    for j in range(heads_k):
        own = slice(j * HD, (j + 1) * HD)
        keys = head_forward(
            raw_ref[:, 2 * cols_q + j * HD : 2 * cols_q + (j + 1) * HD],
            key_gain,
            angle_cos,
            angle_sin,
        )
        start = 2 * cols_q + cols_k + j * HD
        values = in_bf16(raw_ref[:, start : start + HD])
        k_ref[:, own] = keys
        v_ref[:, own] = values
        for h in range(j * group, (j + 1) * group):
            cut = slice(h * HD, (h + 1) * HD)
            queries = head_forward(raw_ref[:, cut], query_gain, angle_cos, angle_sin)
            q_ref[:, cut] = queries
            probs = in_bf16(softmax_of(queries, keys, allowed))
            context = product_of(probs, values, 1, 0)
            gate = raw_ref[:, cols_q + h * HD : cols_q + (h + 1) * HD]
            gated_ref[:, cut] = in_bf16(context * jax.nn.sigmoid(gate))


def attend_back(
    heads_k,
    heads,
    allowed,
    angle_cos,
    angle_sin,
    query_gain,
    key_gain,
    raw_ref,
    q_ref,
    k_ref,
    v_ref,
    grad_ref,
    out_ref,
    gain_ref,
):
    group = H // KV
    cols_q, cols_k = heads_k * group * HD, heads_k * HD
    for j in heads:
        own = slice(j * HD, (j + 1) * HD)
        keys, values = k_ref[:, own], v_ref[:, own]
        grad_keys, grad_values = 0.0, 0.0
        for h in range(j * group, (j + 1) * group):
            cut = slice(h * HD, (h + 1) * HD)
            gate_cut = slice(cols_q + h * HD, cols_q + (h + 1) * HD)
            queries, grad_gated = q_ref[:, cut], grad_ref[:, cut]
            probs = softmax_of(queries, keys, allowed)
            probs_b = in_bf16(probs)
            context = product_of(probs_b, values, 1, 0)
            gate = jax.nn.sigmoid(raw_ref[:, gate_cut])
            grad_context = in_bf16(grad_gated * gate)
            out_ref[:, gate_cut] = in_bf16(grad_gated * context * gate * (1.0 - gate))
            grad_probs = product_of(grad_context, values, 1, 1)
            grad_scores = in_bf16(
                probs * (grad_probs - jnp.sum(probs * grad_probs, axis=-1, keepdims=True))
            )
            grad_values += product_of(probs_b, grad_context, 0, 0)
            grad_keys += product_of(grad_scores, queries, 0, 0)
            grad_queries = product_of(grad_scores, keys, 1, 0) * HD ** (-0.5)
            grad_raw, gain_rows = head_backward(
                grad_queries, raw_ref[:, cut], query_gain, angle_cos, angle_sin
            )
            out_ref[:, cut] = in_bf16(grad_raw)
            gain_ref[0:1, :] += jnp.sum(gain_rows, axis=0, keepdims=True)
        key_start = 2 * cols_q + j * HD
        grad_raw, gain_rows = head_backward(
            grad_keys * HD ** (-0.5),
            raw_ref[:, key_start : key_start + HD],
            key_gain,
            angle_cos,
            angle_sin,
        )
        out_ref[:, key_start : key_start + HD] = in_bf16(grad_raw)
        gain_ref[1:2, :] += jnp.sum(gain_rows, axis=0, keepdims=True)
        value_start = 2 * cols_q + cols_k + j * HD
        out_ref[:, value_start : value_start + HD] = in_bf16(grad_values)


def remote_copy(src, dst, send, recv, to_rep, to_fsdp):
    return pltpu.make_async_remote_copy(
        src_ref=src,
        dst_ref=dst,
        send_sem=send,
        recv_sem=recv,
        device_id={"rep": to_rep, "fsdp": to_fsdp},
        device_id_type=MESH,
    )


def greet_all(peers):
    barrier = pltpu.get_barrier_semaphore()
    for to_rep, to_fsdp in peers:
        pl.semaphore_signal(
            barrier, inc=1, device_id={"rep": to_rep, "fsdp": to_fsdp}, device_id_type=MESH
        )
    pl.semaphore_wait(barrier, len(peers))


class GatherRows:
    def __init__(self, n_fsdp, rep, mine, source, target, sems):
        self.n_fsdp, self.rep, self.mine = n_fsdp, rep, mine
        self.source, self.target = source, target
        self.send, self.recv, self.local = sems
        self.rows = source.shape[0]
        self.half = self.rows // 2
        self.relay = ((1, 0), (2, 1)) if n_fsdp == 4 else ()

    def copy(self, s, h, to=None, src=None):
        to = s if to is None else to
        return remote_copy(
            self.source.at[pl.ds(h * self.half, self.half)]
            if src is None
            else self.target.at[pl.ds(src * self.rows + h * self.half, self.half)],
            self.target.at[pl.ds(s * self.rows + h * self.half, self.half)],
            self.send.at[s, h],
            self.recv.at[s, h],
            self.rep,
            flipped(self.mine, to, self.n_fsdp),
        )

    def own(self):
        return pltpu.make_async_copy(
            self.source, self.target.at[pl.ds(0, self.rows)], self.local
        )

    def start(self):
        for s, h in ((1, 0), (2, 1), (1, 1), (2, 0)):
            if s < self.n_fsdp:
                self.copy(s, h).start()
        if self.n_fsdp != 4:
            for s in range(3, self.n_fsdp):
                for h in range(2):
                    self.copy(s, h).start()
        self.own().start()

    def forward(self):
        if self.n_fsdp == 4:
            self.copy(1, 0).wait_recv()
            self.copy(3, 0, to=2, src=1).start()
            self.copy(2, 1).wait_recv()
            self.copy(3, 1, to=1, src=2).start()

    def arrive(self, s):
        for h in range(2):
            if (s, h) not in self.relay:
                self.copy(s, h).wait_recv()

    def sent(self):
        for s in range(1, self.n_fsdp):
            for h in range(2):
                self.copy(s, h).wait_send()

    def finish(self):
        for s in range(1, self.n_fsdp):
            self.arrive(s)
        self.sent()
        self.own().wait()


def forward_kernel(n_fsdp, n_rep, heads_k, *refs):
    (tokens, gains, wq, wg, wk, wv, w_gate, w_up, w_output, w_down, teacher) = refs[:11]
    (lengths_ref, deal_ref, lengths_row, freq_ref) = refs[11:15]
    (normed_all, raw_all, q_all, k_all, v_all, gated_all, w_attn, w_mlp) = refs[15:23]
    (middle_out, nmlp_all, hidden_all, gbranch_all, gmlp_all, gres_out, block_out) = refs[23:30]
    (gu_all, all_cos, all_sin, gain_out, head_gain_out, loss_out) = refs[30:36]
    (tok, gl, wa, wo, wd, wm, nb, raw, cs, sn, qb, kvb, vb, gb, own, pbuf, land) = refs[36:53]
    (mid, nm, te, gu, hb, gm) = refs[53:59]
    (ts, tr, tl, us, ur, ul, bs, br, bl, gain_s, gain_r, ws, wr, zs, zr, cps, cpr) = refs[59:76]
    (ms, mr, hs, hr, ss, sr, ps, pr, qs, qr, load, keep, mine_sem) = refs[76:]
    rows, width = own.shape
    rows_all = n_fsdp * rows
    cols, ff = raw.shape[1], hb.shape[1]
    deep = wq.shape[0]
    widths = tuple(w.shape[1] // n_fsdp for w in (wq, wg, wk, wv))
    starts = [sum(widths[:i]) for i in range(4)]
    others = range(1, n_fsdp)
    n_line = n_rep // 2
    rep, mine = lax.axis_index("rep"), lax.axis_index("fsdp")
    core, place = rep % 2, rep // 2
    sib = rep + 1 - 2 * core
    partner = (place + 1 - 2 * (place % 2)) * 2 + core
    block, part = deep // 4, deep // n_rep
    band = (place % 2) * 2 + core
    other_band = (1 - place % 2) * 2 + core
    hops = range(1, n_line)
    row_steps = rows // ROW_STEP
    near = sorted({1, n_line - 1})
    greet_all(
        [(sib, mine)]
        + [(((place + k) % n_line) * 2 + core, mine) for k in near]
        + [(rep, flipped(mine, s, n_fsdp)) for s in others]
    )


    def columns(peer, wide):
        return pl.ds(pl.multiple_of(peer * wide, wide), wide)

    def mlp_copy(s, i):
        peer = flipped(mine, s, n_fsdp)
        return remote_copy(
            (w_gate, w_up)[i].at[pl.ds(rep * part, part), columns(peer, ff)],
            w_mlp.at[pl.ds(mine * deep + rep * part, part), pl.ds(i * ff, ff)],
            ms.at[s, i],
            mr.at[s, i],
            rep,
            peer,
        )

    def part_at(s, of_rep):
        return w_mlp.at[pl.ds(flipped(mine, s, n_fsdp) * deep + of_rep * part, part)]

    def line_copy(s, k, up):
        step = 1 if up else -1
        src = part_at(s, ((place - step * (k - 1) + n_line) % n_line) * 2 + core)
        to_rep = ((place + step + n_line) % n_line) * 2 + core
        way = 0 if up else 1
        return remote_copy(src, src, hs.at[way, s, k], hr.at[way, s, k], to_rep, mine)

    def line_sends(k):
        for up in (True, False):
            first, last = (k - 1, n_line - 2) if up else (1, n_line - k)

            @pl.when((place >= first) & (place <= last))
            def _(up=up):
                for s in others:
                    line_copy(s, k, up).start()

    def line_arrivals(k):
        for up in (True, False):
            first, last = (k, n_line - 1) if up else (0, n_line - 1 - k)

            @pl.when((place >= first) & (place <= last))
            def _(up=up):
                for s in others:
                    line_copy(s, k, up).wait_recv()
                    share_copy(s, k, up).start()

        if k + 1 < n_line:
            line_sends(k + 1)

    def share_copy(s, k, up):
        step = 1 if up else -1
        src = part_at(s, ((place - step * k + n_line) % n_line) * 2 + core)
        way = 0 if up else 1
        return remote_copy(src, src, ss.at[way, s, k], sr.at[way, s, k], sib, mine)

    def shares(action):
        for s in others:
            action(share_copy(s, 0, True))
        for k in hops:
            for up in (True, False):
                first, last = (k, n_line - 1) if up else (0, n_line - 1 - k)

                @pl.when((place >= first) & (place <= last))
                def _(k=k, up=up):
                    for s in others:
                        action(share_copy(s, k, up))

    def lines_sent():
        for k in hops:
            for up in (True, False):
                first, last = (k - 1, n_line - 2) if up else (1, n_line - k)

                @pl.when((place >= first) & (place <= last))
                def _(k=k, up=up):
                    for s in others:
                        line_copy(s, k, up).wait_send()

    weights = (wq, wg, wk, wv)

    def weight_copy(s, i):
        peer = flipped(mine, s, n_fsdp)
        return remote_copy(
            weights[i].at[pl.ds(band * block, block), columns(peer, widths[i])],
            w_attn.at[pl.ds(mine * deep + band * block, block), pl.ds(starts[i], widths[i])],
            ws.at[s, i],
            wr.at[s, i],
            rep,
            peer,
        )

    def band_at(s, which):
        return w_attn.at[pl.ds(flipped(mine, s, n_fsdp) * deep + which * block, block)]

    def partner_copy(s):
        return remote_copy(band_at(s, band), band_at(s, band), zs.at[s], zr.at[s], partner, mine)

    def sibling_copy(s, k):
        which = band if k == 0 else other_band
        return remote_copy(
            band_at(s, which), band_at(s, which), cps.at[s, k], cpr.at[s, k], sib, mine
        )

    def gain_copy(s):
        return remote_copy(
            gains, gl.at[mine], gain_s.at[s], gain_r.at[s], rep, flipped(mine, s, n_fsdp)
        )

    mine_rows = pl.ds(mine * deep, deep)
    mine_pairs = [
        (weights[i].at[:, columns(mine, widths[i])], w_attn.at[mine_rows, pl.ds(starts[i], widths[i])])
        for i in range(4)
    ]
    mine_pairs += [
        (w.at[:, columns(mine, ff)], w_mlp.at[mine_rows, pl.ds(i * ff, ff)])
        for i, w in enumerate((w_gate, w_up))
    ]
    mine_pairs += [(gains, gl.at[mine]), (w_output, wo), (w_down, wd), (teacher, te)]

    def local(which):
        return [pltpu.make_async_copy(*mine_pairs[i], mine_sem.at[i]) for i in which]

    def attn_load():
        return pltpu.make_async_copy(w_attn, wa, load.at[0])

    def mlp_load():
        return pltpu.make_async_copy(w_mlp, wm, load.at[1])

    token_rows = GatherRows(n_fsdp, rep, mine, tokens, tok, (ts, tr, tl))
    up_rows = GatherRows(n_fsdp, rep, mine, nm, nmlp_all, (us, ur, ul))
    back_rows = GatherRows(n_fsdp, rep, mine, nm, gbranch_all, (bs, br, bl))

    for s in others:
        gain_copy(s).start()
        for i in range(4):
            weight_copy(s, i).start()
    for copy in local(range(10)):
        copy.start()
    for s in others:
        for i in range(4):
            weight_copy(s, i).wait_recv()
        partner_copy(s).start()
        sibling_copy(s, 0).start()
    for s in others:
        for i in range(2):
            mlp_copy(s, i).start()

    def block_rows(s):
        return pl.ds(pl.multiple_of(s * rows, rows), rows)

    def lengths_of(s):
        return block_lengths(lengths_ref, deal_ref, rep * n_fsdp + flipped(mine, s, n_fsdp))

    def angles(s, carry):
        head_len, both_len = lengths_of(s)
        index = lax.broadcasted_iota(jnp.int32, (rows, HD), 0)
        start = jnp.where(index < head_len, 0, jnp.where(index < both_len, head_len, both_len))
        angle = (index - start).astype(jnp.float32) * freq_ref[...]
        cs[block_rows(s)] = jnp.cos(angle)
        sn[block_rows(s)] = jnp.sin(angle)
        return carry

    lax.fori_loop(0, n_fsdp, angles, 0)
    angle_stores = [
        pltpu.make_async_copy(cs, all_cos, load.at[2]),
        pltpu.make_async_copy(sn, all_sin, load.at[3]),
    ]
    for copy in angle_stores:
        copy.start()
    token_count = jnp.sum(in_f32(lengths_row[...]), axis=1, keepdims=True)
    local((6,))[0].wait()
    gain_out[...] = jnp.zeros_like(gain_out)
    head_gain_out[...] = jnp.zeros_like(head_gain_out)
    for s in others:
        gain_copy(s).wait()
    lines = deep // HD
    for f in range(n_fsdp):
        piece = in_f32(gl[f])
        for kind in range(2):
            for r in range(lines):
                at = f * deep + r * HD
                gain_out[kind : kind + 1, at : at + HD] = piece[
                    kind * lines + r : kind * lines + r + 1
                ]
            head_gain_out[kind : kind + 1] += piece[2 * lines + kind : 2 * lines + kind + 1]
    for s in others:
        for i in range(2):
            mlp_copy(s, i).wait_recv()
        share_copy(s, 0, True).start()
    token_rows.start()
    for s in others:
        partner_copy(s).wait_recv()
        sibling_copy(s, 1).start()
    line_sends(1)
    for s in others:
        for k in range(2):
            sibling_copy(s, k).wait_recv()
    for copy in local((0, 1, 2, 3)):
        copy.wait()
    attn_load().start()
    for copy in local((7, 8, 9)):
        copy.wait()

    def some_rows(base, r):
        return pl.ds(pl.multiple_of(base + r * ROW_STEP, ROW_STEP), ROW_STEP)

    def tiled(count, wide, body):
        def one(j, carry):
            body(pl.ds(pl.multiple_of(j * wide, wide), wide))
            return carry

        lax.fori_loop(0, count, one, 0)

    def by_rows(body):
        def one(r, carry):
            body(r)
            return carry

        lax.fori_loop(0, row_steps, one, 0)

    tile = width // 4

    def leave(s, left, right):
        def one(cut):
            product = product_of(left[...], right[:, cut], 1, 0)

            @pl.when(s == 0)
            def _():
                own[:, cut] = product

            @pl.when(s > 0)
            def _():
                pbuf[s - 1, :, cut] = in_bf16(product)

        tiled(4, tile, one)

    def out_copy(s, sends, recvs):
        return remote_copy(
            pbuf.at[s - 1],
            land.at[s - 1],
            sends.at[s],
            recvs.at[s],
            rep,
            flipped(mine, s, n_fsdp),
        )

    def summed(cut):
        total = own[cut]
        for s in others:
            total += in_f32(land[s - 1, cut])
        return total

    def scaled(values, gain):
        scale = lax.rsqrt(jnp.mean(values * values, axis=-1, keepdims=True) + EPS_NORM)
        return in_bf16(values * scale * gain)


    def attention_stores(s):
        cut = block_rows(s)
        pairs = (
            (nb, normed_all), (raw, raw_all), (qb, q_all), (kvb, k_all), (vb, v_all), (gb, gated_all)
        )
        return [
            pltpu.make_async_copy(src, dst.at[cut], keep.at[i])
            for i, (src, dst) in enumerate(pairs)
        ]

    def attention(s, carry):
        pl.when(s == 1)(token_rows.forward)
        for k in range(n_fsdp):

            @pl.when(s == k)
            def _(k=k):
                if k == 0:
                    token_rows.own().wait()
                else:
                    token_rows.arrive(k)

        @pl.when(s > 0)
        def _():
            for copy in attention_stores(s):
                copy.wait()

        def normed_rows(r):
            values = in_f32(tok[some_rows(s * rows, r)])
            nb[some_rows(0, r)] = scaled(values, gain_out[0:1])

        by_rows(normed_rows)

        @pl.when(s == 0)
        def _():
            attn_load().wait()

        def raw_tile(cut):
            raw[:, cut] = product_of(nb[...], wa[:, cut], 1, 0)

        tiled(3, cols // 3, raw_tile)
        attend(
            heads_k,
            block_mask(lengths_of(s), rows),
            cs[block_rows(s)],
            sn[block_rows(s)],
            head_gain_out[0:1],
            head_gain_out[1:2],
            raw,
            qb,
            kvb,
            vb,
            gb,
        )
        for copy in attention_stores(s):
            copy.start()
        leave(s, gb, wo)

        @pl.when(s > 0)
        def _():
            out_copy(s, ps, pr).start()

        if n_line > 2:
            pl.when(s == n_fsdp - 2)(lambda: line_arrivals(1))
        return carry

    lax.fori_loop(0, n_fsdp, attention, 0)
    for copy in angle_stores:
        copy.wait()
    for k in range(2, n_line - 1):
        line_arrivals(k)
    for s in others:
        out_copy(s, ps, pr).wait()

    def middle_rows(r):
        cut = some_rows(0, r)
        values = in_f32(tok[cut]) + summed(cut)
        mid[cut] = values
        nm[cut] = scaled(values, gain_out[1:2])

    by_rows(middle_rows)
    up_rows.start()

    def middle_store():
        return pltpu.make_async_copy(mid, middle_out, load.at[4])

    middle_store().start()
    for copy in attention_stores(0):
        copy.wait()


    line_arrivals(n_line - 1)
    shares(lambda copy: copy.wait_recv())
    for copy in local((4, 5)):
        copy.wait()
    mlp_load().start()
    mlp_load().wait()

    def block_load(source, s):
        return pltpu.make_async_copy(source.at[block_rows(s)], nb, load.at[2])

    def ff_stores(s):
        cut = block_rows(s)
        return [
            pltpu.make_async_copy(hb, hidden_all.at[cut], keep.at[0]),
            pltpu.make_async_copy(gu, gu_all.at[cut], keep.at[1]),
        ]

    def into_nb(gather, source, s):
        @pl.when(s == 0)
        def _():
            nb[...] = nm[...]

        for k in others:

            @pl.when(s == k)
            def _(k=k):
                gather.arrive(k)

        @pl.when(s > 0)
        def _():
            copy = block_load(source, s)
            copy.start()
            copy.wait()

    def feed_forward(i, carry):
        s = (i + 1) % n_fsdp
        pl.when(i == 0)(up_rows.forward)
        into_nb(up_rows, nmlp_all, s)

        @pl.when(i > 0)
        def _():
            for copy in ff_stores(s):
                copy.wait()

        def pre_tile(cut):
            gu[:, cut] = product_of(nb[...], wm[:, cut], 1, 0)

        tiled(6, ff // 3, pre_tile)

        def hidden_rows(r):
            cut = some_rows(0, r)
            gate_pre = gu[cut, :ff]
            hb[cut] = in_bf16(gate_pre * jax.nn.sigmoid(gate_pre) * gu[cut, ff:])

        by_rows(hidden_rows)
        for copy in ff_stores(s):
            copy.start()
        leave(s, hb, wd)

        @pl.when(s > 0)
        def _():
            out_copy(s, qs, qr).start()

        return carry

    lax.fori_loop(0, n_fsdp, feed_forward, 0)
    up_rows.sent()
    up_rows.own().wait()
    middle_store().wait()
    for copy in ff_stores(0):
        copy.wait()


    def gu_load(s):
        return pltpu.make_async_copy(gu_all.at[block_rows(s)], gu, load.at[5])

    gu_load(0).start()
    for s in others:
        out_copy(s, qs, qr).wait()
    head_len, both_len = lengths_of(0)
    factor = (n_rep * rows_all) / token_count
    loss_out[...] = jnp.zeros_like(loss_out)

    def error_rows(r):
        cut = some_rows(0, r)
        index = r * ROW_STEP + lax.broadcasted_iota(jnp.int32, (ROW_STEP, 1), 0)
        valid = (index < both_len).astype(jnp.float32)
        result = mid[cut] + summed(cut)
        error = (result - in_f32(te[cut])) * valid
        square = jnp.sum(error * error, axis=-1, keepdims=True)
        first = jnp.where(index < head_len, square, 0.0)
        loss_out[0:1] += jnp.sum(first, axis=0, keepdims=True)
        loss_out[1:2] += jnp.sum(square - first, axis=0, keepdims=True)
        te[cut] = in_bf16(result * valid)
        grad = error * factor
        mid[cut] = grad
        nm[cut] = in_bf16(grad)

    by_rows(error_rows)
    loss_out[...] = loss_out[...] / (2.0 * token_count)
    back_rows.start()
    last_stores = [
        pltpu.make_async_copy(te, block_out, load.at[3]),
        pltpu.make_async_copy(mid, gres_out, load.at[4]),
    ]
    for copy in last_stores:
        copy.start()

    def grad_store(s):
        return pltpu.make_async_copy(gm, gmlp_all.at[block_rows(s)], keep.at[2])

    def feed_back(s, carry):
        pl.when(s == 1)(back_rows.forward)
        into_nb(back_rows, gbranch_all, s)

        def hidden_tile(cut):
            raw[:, cut] = product_of(nb[...], wd[cut], 1, 1)

        tiled(3, ff // 3, hidden_tile)
        gu_load(s).wait()

        @pl.when(s > 0)
        def _():
            grad_store(s).wait()

        def grad_rows(r):
            cut = some_rows(0, r)
            gate_pre, grad = gu[cut, :ff], raw[cut]
            gate = jax.nn.sigmoid(gate_pre)
            silu = gate_pre * gate
            gm[cut, :ff] = in_bf16(grad * gu[cut, ff:] * (gate + silu * (1.0 - gate)))
            gm[cut, ff:] = in_bf16(grad * silu)

        by_rows(grad_rows)
        grad_store(s).start()

        @pl.when(s + 1 < n_fsdp)
        def _():
            gu_load(s + 1).start()

        return carry

    lax.fori_loop(0, n_fsdp, feed_back, 0)

    grad_store(0).wait()
    for copy in last_stores:
        copy.wait()
    back_rows.sent()
    back_rows.own().wait()
    token_rows.sent()
    for s in others:
        partner_copy(s).wait_send()
        for i in range(4):
            weight_copy(s, i).wait_send()
        for i in range(2):
            sibling_copy(s, i).wait_send()
            mlp_copy(s, i).wait_send()
    lines_sent()
    shares(lambda copy: copy.wait_send())


def forward(n_fsdp, n_rep, heads_k, args):
    rows, width = args[0].shape
    rows_all = n_fsdp * rows
    cols_q, cols_k = heads_k * (H // KV) * HD, heads_k * HD
    cols = 2 * cols_q + 2 * cols_k
    ff = args[9].shape[0]
    n_line = n_rep // 2
    low, full = jnp.bfloat16, jnp.float32
    dma = pltpu.SemaphoreType.DMA
    any_spec = pl.BlockSpec(memory_space=pl.ANY)
    vmem, smem = pl.BlockSpec(memory_space=pltpu.VMEM), pl.BlockSpec(memory_space=pltpu.SMEM)
    outs = (
        ((rows_all, width), low),
        ((rows_all, cols), full),
        ((rows_all, cols_q), low),
        ((rows_all, cols_k), low),
        ((rows_all, cols_k), low),
        ((rows_all, cols_q), low),
        ((width, cols), low),
        ((width, 2 * ff), low),
        ((rows, width), full),
        ((rows_all, width), low),
        ((rows_all, ff), low),
        ((rows_all, width), low),
        ((rows_all, 2 * ff), low),
        ((rows, width), full),
        ((rows, width), low),
        ((rows_all, 2 * ff), full),
        ((rows_all, HD), full),
        ((rows_all, HD), full),
        ((8, width), full),
        ((8, HD), full),
        ((8, HD), full),
    )
    scratch = (
        ((rows_all, width), low),
        ((n_fsdp, 16, HD), low),
        ((width, cols), low),
        ((cols_q, width), low),
        ((ff, width), low),
        ((width, 2 * ff), low),
        ((rows, width), low),
        ((rows, cols), full),
        ((rows_all, HD), full),
        ((rows_all, HD), full),
        ((rows, cols_q), low),
        ((rows, cols_k), low),
        ((rows, cols_k), low),
        ((rows, cols_q), low),
        ((rows, width), full),
        ((n_fsdp - 1, rows, width), low),
        ((n_fsdp - 1, rows, width), low),
        ((rows, width), full),
        ((rows, width), low),
        ((rows, width), low),
        ((rows, 2 * ff), full),
        ((rows, ff), low),
        ((rows, 2 * ff), low),
    )
    one, pair, four = dma((n_fsdp,)), dma((n_fsdp, 2)), dma((n_fsdp, 4))
    line = dma((2, n_fsdp, n_line))
    return pl.pallas_call(
        functools.partial(forward_kernel, n_fsdp, n_rep, heads_k),
        out_shape=[jax.ShapeDtypeStruct(shape, kind) for shape, kind in outs],
        in_specs=[any_spec] * 11 + [smem] * 2 + [vmem] * 2,
        out_specs=[any_spec] * 18 + [vmem] * 3,
        scratch_shapes=[pltpu.VMEM(shape, kind) for shape, kind in scratch]
        + [pair, pair, dma] * 3
        + [one, one, four, four, one, one, pair, pair]
        + [pair, pair, line, line, line, line, one, one, one, one]
        + [dma((6,)), dma((6,)), dma((10,))],
        compiler_params=pltpu.CompilerParams(
            collective_id=1, has_side_effects=True, vmem_limit_bytes=62 << 20
        ),
        name="forward",
    )(*args)


def shards(
    tokens,
    teacher,
    lengths,
    deal_order,
    attention_gain,
    query_gain,
    key_gain,
    w_query,
    w_key,
    w_value,
    w_outgate,
    w_output,
    mlp_gain,
    w_gate,
    w_up,
    w_down,
):
    n_rep = lax.axis_size("rep")
    n_fsdp = lax.axis_size("fsdp")
    rows, width = tokens.shape
    mine = lax.axis_index("fsdp")
    core = lax.axis_index("rep") % 2
    others = range(1, n_fsdp)
    heads_q, heads_k = H // n_fsdp, KV // n_fsdp
    cols_q, cols_k = heads_q * HD, heads_k * HD
    deep = w_query.shape[0]
    ff = w_down.shape[0]
    rows_all = rows * n_fsdp

    freq = np.power(np.float32(ROPE_BASE), -np.arange(0, HD, 2, dtype=np.float32) / HD)
    freq = jnp.asarray(np.concatenate([freq, freq])[None])
    small = query_gain.shape[0]

    def spread(gain):
        lane = jnp.arange(HD, dtype=jnp.int32)
        return jnp.where(lane // small == mine, jnp.tile(gain, n_fsdp), 0)[None]

    gain_block = jnp.concatenate(
        [
            attention_gain.reshape(-1, HD),
            mlp_gain.reshape(-1, HD),
            spread(query_gain),
            spread(key_gain),
            jnp.zeros((14 - 2 * deep // HD, HD), jnp.bfloat16),
        ]
    )
    (
        normed_all,
        attn_raw,
        queries_b,
        keys_b,
        values_b,
        gated_b,
        w_attn,
        w_mlp,
        middle,
        normed_mlp_all,
        hidden_b,
        grad_branch_all,
        grad_mlp_b,
        grad_result,
        block_out,
        _,
        angle_cos,
        angle_sin,
        gain_rows,
        head_gains,
        losses,
    ) = forward(
        n_fsdp,
        n_rep,
        heads_k,
        (
            tokens,
            gain_block,
            w_query,
            w_outgate,
            w_key,
            w_value,
            w_gate,
            w_up,
            w_output,
            w_down,
            teacher,
            lengths,
            deal_order,
            lengths[None],
            freq,
        ),
    )
    seq_loss = losses[:2, 0]
    piece_rows, piece_cols = deep // 2, width // n_fsdp
    units, base = [], 0
    for by_owner, row_blocks, cols in (
        (False, ff // 2 // piece_rows, width),
        (True, n_fsdp, 2 * ff),
        (False, cols_q // 2 // piece_rows, width),
        (True, n_fsdp, 2 * cols_q + 2 * cols_k),
    ):
        units.append(Unit(base, by_owner, row_blocks, cols // piece_cols))
        base += units[-1].count
    pieces, _, _, _, _, tokens_grad, gain_sums = backward(
        n_fsdp,
        n_rep,
        heads_k,
        units,
        piece_rows,
        piece_cols,
        (
            hidden_b,
            normed_mlp_all,
            gated_b,
            normed_all,
            grad_branch_all,
            grad_mlp_b,
            w_mlp,
            w_output,
            w_attn,
            middle,
            grad_result,
            tokens,
            attn_raw,
            angle_cos,
            angle_sin,
            queries_b,
            keys_b,
            values_b,
            gain_rows,
            head_gains,
            lengths,
            deal_order,
        ),
    )
    down, mlp, outp, attn = units

    def by_rows(unit, weight):
        blocks, together = unit.row_blocks, unit.col_blocks
        return widened(
            pieces,
            (2, blocks),
            together,
            lambda c, r: (unit.base // together + r, c, 0, 0),
            weight.shape,
            lambda c, r: (c * blocks + r, 0),
        )

    dw_down = by_rows(down, w_down)
    dw_output = by_rows(outp, w_output)
    dw_gate, dw_up = widened_both(pieces, mlp.base, mlp.col_blocks, n_fsdp, w_gate.shape)
    dw_query, dw_outgate, dw_key, dw_value = widened_heads(
        pieces,
        attn.base,
        n_fsdp,
        (w_query.shape, w_outgate.shape, w_key.shape, w_value.shape),
    )

    def own_part(row, start, cols):
        return lax.dynamic_slice(gain_sums, (row, start + mine * cols), (1, cols))[0]

    return (
        block_out,
        seq_loss,
        tokens_grad,
        own_part(0, 0, deep),
        own_part(0, width, small),
        own_part(1, width, small),
        dw_query,
        dw_key,
        dw_value,
        dw_outgate,
        dw_output,
        own_part(1, 0, deep),
        dw_gate,
        dw_up,
        dw_down,
    )


def solution(mesh):
    return jax.shard_map(
        shards,
        mesh=mesh,
        in_specs=(
            P(("rep", "fsdp"), None),
            P(("rep", "fsdp"), None),
            P(),
            P(),
            P("fsdp"),
            P("fsdp"),
            P("fsdp"),
            P("fsdp", None),
            P("fsdp", None),
            P("fsdp", None),
            P("fsdp", None),
            P("fsdp", None),
            P("fsdp"),
            P("fsdp", None),
            P("fsdp", None),
            P("fsdp", None),
        ),
        out_specs=(
            P(("rep", "fsdp"), None),
            P(("rep", "fsdp")),
            P(("rep", "fsdp"), None),
            P("fsdp"),
            P("fsdp"),
            P("fsdp"),
            P("fsdp", None),
            P("fsdp", None),
            P("fsdp", None),
            P("fsdp", None),
            P("fsdp", None),
            P("fsdp"),
            P("fsdp", None),
            P("fsdp", None),
            P("fsdp", None),
        ),
        check_vma=False,
    )
```

```python
import functools

import jax
import jax.numpy as jnp
import numpy as np
from jax import lax
from jax.experimental import pallas as pl
from jax.experimental.pallas import tpu as pltpu
from jax.sharding import PartitionSpec as P

MESH = pl.DeviceIdType.MESH

H = 16
KV = 8
HD = 128


EPS_NORM = 1e-06
ROPE_BASE = 1000000.0
NEG_FILL = -1e30


def in_f32(values):
    return values.astype(jnp.float32)


def in_bf16(values):
    return values.astype(jnp.bfloat16)


def flipped(index, step, n):
    out, bit = index, 1
    while bit < n:
        has = (step // bit) % 2
        out = out + has * bit * (1 - 2 * ((index // bit) % 2))
        bit *= 2
    return out


def at_least(value, bound, span):
    span = max(span, bound)
    return (value + (span - bound)) // span


class Unit:
    def __init__(self, base, by_owner, row_blocks, col_blocks):
        self.base, self.by_owner = base, by_owner
        self.row_blocks, self.col_blocks = row_blocks, col_blocks
        self.count = row_blocks * col_blocks


LAG_B, LAG_C, LAG_D, LAG_E, LAG_G = 2, 4, 6, 8, 14
RING = 4


ROW_STEP = 32
TILES = 8


def norm_back(grad, raw, gain):
    scale = lax.rsqrt(jnp.mean(raw * raw, axis=-1, keepdims=True) + EPS_NORM)
    unit = raw * scale
    inner = grad * gain
    return scale * (inner - unit * jnp.mean(inner * unit, axis=-1, keepdims=True)), grad * unit


def backward_kernel(n_fsdp, n_rep, heads_k, units, piece_rows, piece_cols, *refs):
    (hidden, normed_mlp, gated, normed, grad_branch, grad_mlp, w_mlp, w_output, w_attn) = refs[:9]
    (middle, grad_result, tokens, attn_raw, all_cos, all_sin, all_q, all_k, all_v) = refs[9:18]
    (gains, head_gains, lengths_ref, deal_ref) = refs[18:22]
    (out, grad_attn, grad_raw, inb, xb, tokens_grad, gain_out) = refs[22:29]
    (lm, lo, rh, sb, kb, r1, c_slot, d_slot, big, wt, own, pbuf, land_a, land_b) = refs[29:43]
    (mid, gres, tok, ga, wo, raw, cs, sn, qb, kvb, vb, gb, gg, ob) = refs[43:57]
    (tile_sem, r1s, r1r, ins, inr, xs, xr, os_, fs, fr, gs, gr, ls) = refs[57:70]
    (load_sem, first_sem, wt_sem, ps, pr, qs, qr, ag_s, ag_r, ag_l, block_sem) = refs[70:81]
    (near_land, pair_land, in_land, far_land, near_s, near_r, line_s, line_r) = refs[81:]
    head_gain_out = gain_out.at[:, pl.ds(own.shape[1], HD)]
    lefts = (hidden, normed_mlp, gated, normed)
    rights = (grad_branch, grad_mlp, grad_attn, grad_raw)
    total = sum(unit.count for unit in units)
    rows, width = own.shape
    rows_all = n_fsdp * rows
    ff = grad_mlp.shape[1] // 2
    tile = width // TILES
    others = range(1, n_fsdp)
    rep, mine = lax.axis_index("rep"), lax.axis_index("fsdp")
    core, place = rep % 2, rep // 2
    n_line = n_rep // 2
    half = n_line // 2
    side = place // half
    depth = place * (1 - side) + (n_line - 1 - place) * side
    inward = (place + 1 - 2 * side) * 2 + core
    outward = (place - 1 + 2 * side) * 2 + core
    sib = rep + 1 - 2 * core
    at_middle = depth == half - 1

    barrier = pltpu.get_barrier_semaphore()

    def greet(to_rep, to_fsdp):
        pl.semaphore_signal(
            barrier, inc=1, device_id={"rep": to_rep, "fsdp": to_fsdp}, device_id_type=MESH
        )

    greet(sib, mine)
    greet(inward, mine)
    for s in others:
        greet(rep, flipped(mine, s, n_fsdp))

    @pl.when(depth == 0)
    def _():
        pl.semaphore_wait(barrier, 1 + n_fsdp)

    @pl.when(depth > 0)
    def _():
        greet(outward, mine)
        pl.semaphore_wait(barrier, 2 + n_fsdp)


    def r1_copy(p):
        return remote_copy(sb.at[p % RING], r1.at[p], r1s.at[p], r1r.at[p], sib, mine)

    def in_copy(p):
        return remote_copy(r1.at[p], inb.at[p], ins.at[p], inr.at[p], inward, mine)

    def x_copy(p):
        return remote_copy(r1.at[p], xb.at[p], xs.at[p], xr.at[p], inward, mine)

    def o_copy(p, src):
        return remote_copy(src.at[p], xb.at[p], os_, xr.at[p], outward, mine)

    def inside_of(p, unit):
        inside = at_least(p, unit.base, total - unit.base)
        stop = unit.base + unit.count
        if stop < total:
            inside = inside * (1 - at_least(p, stop, total - stop))
        return inside

    def owner_of(p):
        step = 0
        for unit in units:
            if unit.by_owner:
                i = p - unit.base
                step = step + inside_of(p, unit) * (n_fsdp - 1 - i // unit.col_blocks)
        return step

    def spot(p, source):
        where = p
        for unit in units:
            if unit.by_owner:
                i = p - unit.base
                spread = unit.base + source * unit.col_blocks + i % unit.col_blocks
                where = where + inside_of(p, unit) * (spread - p)
        return where

    def f_copy(p, step):
        return remote_copy(
            r1.at[p],
            out.at[spot(p, mine), core],
            fs,
            fr.at[p],
            rep,
            flipped(mine, step, n_fsdp),
        )

    def g_copy(src, where):
        return remote_copy(src, out.at[where, core], gs, gr, sib, mine)

    def l_copy(p):
        return pltpu.make_async_copy(r1.at[p], out.at[spot(p, mine), core], ls)

    def c_load(p):
        return pltpu.make_async_copy(inb.at[p], c_slot, load_sem.at[0])

    def d_load(p):
        return pltpu.make_async_copy(xb.at[p], d_slot, load_sem.at[1])

    def e_load(p):
        return pltpu.make_async_copy(xb.at[p], r1.at[p], load_sem.at[2])

    def add_into(p, other):
        r1[p] = in_bf16(in_f32(r1[p]) + in_f32(other))

    def begin_c(p):
        @pl.when(depth > 0)
        def _():
            in_copy(p).wait_recv()
            c_load(p).start()

    def begin_d(p):
        @pl.when(at_middle)
        def _():
            x_copy(p).wait_recv()
            d_load(p).start()

    def begin_e(p):
        @pl.when(depth < half - 1)
        def _():
            o_copy(p, xb).wait_recv()

            @pl.when(depth > 0)
            def _():
                o_copy(p, xb).start()

            in_copy(p).wait_send()
            e_load(p).start()

    def end_b(p):
        r1_copy(p).wait_recv()
        add_into(p, kb[p % RING])
        if half > 1:

            @pl.when(depth == 0)
            def _():
                in_copy(p).start()
        else:
            x_copy(p).start()

    def end_c(p):
        @pl.when(depth > 0)
        def _():
            c_load(p).wait()
            add_into(p, c_slot[...])

            @pl.when(depth < half - 1)
            def _():
                in_copy(p).start()

            @pl.when(at_middle)
            def _():
                x_copy(p).start()

    def end_d(p):
        @pl.when(at_middle)
        def _():
            d_load(p).wait()
            x_copy(p).wait_send()
            add_into(p, d_slot[...])

            @pl.when(depth > 0)
            def _():
                o_copy(p, r1).start()

    def end_e(p):
        @pl.when(depth < half - 1)
        def _():
            e_load(p).wait()

        step = owner_of(p)

        @pl.when(step == 0)
        def _():
            l_copy(p).start()
            g_copy(r1.at[p], spot(p, mine)).start()

        @pl.when(step > 0)
        def _():
            f_copy(p, step).start()

    def end_g(p):
        step = owner_of(p)

        @pl.when(step > 0)
        def _():
            f_copy(p, step).wait_recv()
            where = spot(p, flipped(mine, step, n_fsdp))
            g_copy(out.at[where, core], where).start()

    def run(stages, t):
        for lag, stage in stages:
            pl.when((t >= lag) & (t < total + lag))(functools.partial(stage, t - lag))

    def begin(t):
        run([(LAG_C, begin_c), (LAG_D, begin_d), (LAG_E, begin_e)], t)

    def end(t):
        run([(LAG_B, end_b), (LAG_C, end_c), (LAG_D, end_d), (LAG_E, end_e), (LAG_G, end_g)], t)

    def tiles(u, i, slot):
        unit = units[u]
        r, j = i // unit.col_blocks, i % unit.col_blocks
        if unit.by_owner:
            owner = flipped(mine, n_fsdp - 1 - r, n_fsdp)
            first = owner * 2 * piece_rows + core * piece_rows
            second = owner * 2 * piece_rows + (1 - core) * piece_rows
        else:
            first = core * unit.row_blocks * piece_rows + r * piece_rows
            second = (1 - core) * unit.row_blocks * piece_rows + r * piece_rows
        first = pl.ds(pl.multiple_of(first, piece_rows), piece_rows)
        second = pl.ds(pl.multiple_of(second, piece_rows), piece_rows)
        cols = pl.ds(pl.multiple_of(j * piece_cols, piece_cols), piece_cols)
        return [
            pltpu.make_async_copy(lefts[u].at[:, first], lm.at[slot], tile_sem.at[slot, 0]),
            pltpu.make_async_copy(lefts[u].at[:, second], lo.at[slot], tile_sem.at[slot, 1]),
            pltpu.make_async_copy(rights[u].at[:, cols], rh.at[slot], tile_sem.at[slot, 2]),
        ]


    first_pairs = (
        (grad_mlp.at[:, pl.ds(0, ff)], big.at[pl.ds(0, rows_all)]),
        (grad_mlp.at[:, pl.ds(ff, ff)], big.at[pl.ds(rows_all, rows_all)]),
        (middle, mid),
        (grad_result, gres),
        (tokens, tok),
        (w_output, wo),
    )

    def first_loads(which):
        return [pltpu.make_async_copy(*first_pairs[i], first_sem.at[i]) for i in which]

    def attn_load():
        return pltpu.make_async_copy(w_attn, big.at[pl.ds(0, width)], first_sem.at[6])

    def tile_of(j):
        return pl.ds(pl.multiple_of(j * tile, tile), tile)

    def wt_load(j):
        return pltpu.make_async_copy(w_mlp.at[tile_of(j)], wt.at[j % 2], wt_sem.at[j % 2])

    def p_copy(s, j):
        return remote_copy(
            pbuf.at[s - 1, :, tile_of(j)],
            land_a.at[s - 1, :, tile_of(j)],
            ps.at[s, j],
            pr.at[s, j],
            rep,
            flipped(mine, s, n_fsdp),
        )

    def q_copy(s):
        return remote_copy(
            pbuf.at[s - 1], land_b.at[s - 1], qs.at[s], qr.at[s], rep, flipped(mine, s, n_fsdp)
        )

    gather = GatherRows(n_fsdp, rep, mine, ga, grad_attn, (ag_s, ag_r, ag_l))

    def mlp_products(j):
        @pl.when(j == 0)
        def _():
            for copy in first_loads((0, 1)):
                copy.wait()

        wt_load(j).wait()

        @pl.when(j + 1 < TILES)
        def _():
            wt_load(j + 1).start()

        for s in (*others, 0):
            part = product_of(big[s * rows : (s + 1) * rows], wt[j % 2, :, :ff], 1, 1)
            part += product_of(
                big[rows_all + s * rows : rows_all + (s + 1) * rows], wt[j % 2, :, ff:], 1, 1
            )
            if s == 0:
                own[:, tile_of(j)] = part
            else:
                pbuf[s - 1, :, tile_of(j)] = in_bf16(part)
                p_copy(s, j).start()

    row_steps = rows // ROW_STEP

    def middle_back(part):
        if part == 0:
            middle_sums()

        def some_rows(r, carry):
            cut = pl.ds(pl.multiple_of(r * ROW_STEP, ROW_STEP), ROW_STEP)
            grad = own[cut]
            for s in others:
                grad += in_f32(land_a[s - 1, cut])
            back, gain_rows = norm_back(grad, mid[cut], gains[1:2])
            gain_out[1:2, :width] += jnp.sum(gain_rows, axis=0, keepdims=True)
            back = gres[cut] + back
            gres[cut] = back
            ga[cut] = in_bf16(back)
            return carry

        lax.fori_loop(part * row_steps // 2, (part + 1) * row_steps // 2, some_rows, 0)
        if part == 1:
            gather.start()
            for copy in block_loads(0):
                copy.start()

    def middle_sums():
        attn_load().start()
        for copy in first_loads((2, 3)):
            copy.wait()

        def wait_tiles(j, carry):
            for s in others:
                p_copy(s, j).wait()
            return carry

        lax.fori_loop(0, TILES, wait_tiles, 0)
        gain_out[...] = jnp.zeros_like(gain_out)

    def block_loads(s):
        cut = pl.ds(pl.multiple_of(s * rows, rows), rows)
        pairs = (
            (attn_raw, raw), (all_cos, cs), (all_sin, sn), (all_q, qb), (all_k, kvb), (all_v, vb)
        )
        copies = [
            pltpu.make_async_copy(src.at[cut], dst, block_sem.at[i])
            for i, (src, dst) in enumerate(pairs)
        ]
        return copies

    def grad_load(s):
        cut = pl.ds(pl.multiple_of(s * rows, rows), rows)
        return pltpu.make_async_copy(grad_attn.at[cut], gb, block_sem.at[6])

    def store(s):
        cut = pl.ds(pl.multiple_of(s * rows, rows), rows)
        return pltpu.make_async_copy(ob, grad_raw.at[cut], block_sem.at[7])

    def heads_back(s, heads):
        attend_back(
            heads_k,
            heads,
            block_mask(
                block_lengths(lengths_ref, deal_ref, rep * n_fsdp + flipped(mine, s, n_fsdp)), rows
            ),
            cs[...],
            sn[...],
            head_gains[0:1],
            head_gains[1:2],
            raw,
            qb,
            kvb,
            vb,
            gg,
            ob,
            head_gain_out,
        )

    early = heads_k // 2

    def block_first(s):
        @pl.when(s == 0)
        def _():
            first_loads((5,))[0].wait()
            gb[...] = ga[...]

        for k in others:

            @pl.when(s == k)
            def _(k=k):
                gather.arrive(k)

        @pl.when(s > 0)
        def _():
            copy = grad_load(s)
            copy.start()
            copy.wait()

        gg[...] = product_of(gb[...], wo[...], 1, 1)
        for copy in block_loads(s):
            copy.wait()
        heads_back(s, range(early))

    def block_second(s):
        heads_back(s, range(early, heads_k))
        store(s).start()

        @pl.when(s + 1 < n_fsdp)
        def _():
            for copy in block_loads(s + 1):
                copy.start()

    def block_third(s):
        store(s).wait()

        @pl.when(s == 0)
        def _():
            attn_load().wait()

        def one_tile(j, carry):
            part = product_of(ob[...], big[tile_of(j)], 1, 1)

            @pl.when(s == 0)
            def _():
                own[:, tile_of(j)] = part

            @pl.when(s > 0)
            def _():
                pbuf[s - 1, :, tile_of(j)] = in_bf16(part)

            return carry

        lax.fori_loop(0, TILES, one_tile, 0)

        @pl.when(s > 0)
        def _():
            q_copy(s).start()

    def tokens_back(part):
        if part == 0:
            gather.sent()
            first_loads((4,))[0].wait()
            for s in others:
                q_copy(s).wait()

        def some_rows(r, carry):
            cut = pl.ds(pl.multiple_of(r * ROW_STEP, ROW_STEP), ROW_STEP)
            grad = own[cut]
            for s in others:
                grad += in_f32(land_b[s - 1, cut])
            back, gain_rows = norm_back(grad, in_f32(tok[cut]), gains[0:1])
            gain_out[0:1, :width] += jnp.sum(gain_rows, axis=0, keepdims=True)
            tokens_grad[cut] = in_bf16(gres[cut] + back)
            return carry

        lax.fori_loop(part * row_steps // 2, (part + 1) * row_steps // 2, some_rows, 0)
        if part == 1:
            near_land[mine] = gain_out[...]
            for s in others:
                near_copy(s).start()


    def near_copy(s):
        return remote_copy(
            gain_out,
            near_land.at[mine],
            near_s.at[s],
            near_r.at[s],
            rep,
            flipped(mine, s, n_fsdp),
        )

    def line_copy(k, target, to_rep):
        return remote_copy(gain_out, target, line_s.at[k], line_r.at[k], to_rep, mine)

    def pair_copy():
        return line_copy(0, pair_land, sib)

    def gain_in():
        return line_copy(1, in_land, inward)

    def gain_across():
        return line_copy(2, far_land, inward)

    def gain_back():
        return line_copy(3, far_land, outward)

    def gains_near():
        for s in others:
            near_copy(s).wait()
        summed = near_land[0]
        for k in others:
            summed += near_land[k]
        gain_out[...] = summed
        pair_copy().start()

    def gains_pair():
        pair_copy().wait()
        gain_out[...] += pair_land[...]

        @pl.when(depth == 0)
        def _():
            (gain_in if half > 1 else gain_across)().start()

    def gains_in(k):
        @pl.when(depth == k)
        def _():
            gain_in().wait_recv()
            gain_out[...] += in_land[...]
            (gain_in if k < half - 1 else gain_across)().start()

    def gains_across():
        @pl.when(at_middle)
        def _():
            gain_across().wait()
            gain_out[...] += far_land[...]
            if half > 1:
                gain_back().start()

    def gains_back(k):
        @pl.when(depth == k)
        def _():
            gain_back().wait_recv()
            gain_in().wait_send()
            gain_out[...] = far_land[...]
            if k > 0:
                gain_back().start()

    def tasks(u, i):
        if u == 0:

            @pl.when(i == 1)
            def _():
                wt_load(0).start()
                for copy in first_loads((0, 1)):
                    copy.start()

            @pl.when(i == 6)
            def _():
                for copy in first_loads((2, 3, 4, 5)):
                    copy.start()

            pl.when((i >= 4) & (i < 4 + TILES))(lambda: mlp_products(i - 4))
        if u == 1:
            for part in range(2):
                pl.when(i == 7 + part)(functools.partial(middle_back, part))
            pl.when(i == 12)(gather.forward)
            pl.when(i == 15)(lambda: gather.own().wait())
            last = 15 + 3 * (n_fsdp - 1)
            busy = ((i >= 9) & (i < 12)) | ((i >= 15) & (i < last))
            s = at_least(i, 12, units[1].count) * ((i - 12) // 3)
            for phase, task in enumerate((block_first, block_second, block_third)):
                pl.when(busy & (i % 3 == phase))(functools.partial(task, s))
        if u == 3:
            for part in range(2):
                pl.when(i == 2 + part)(functools.partial(tokens_back, part))
            pl.when(i == 6)(gains_near)
            pl.when(i == 8)(gains_pair)

    def product(left, right):
        return product_of(left, right, 0, 0)

    for copy in tiles(0, 0, 0):
        copy.start()
    for u, unit in enumerate(units):

        def step(i, carry, u=u, unit=unit):
            t = unit.base + i
            slot = t % 2
            begin(t)
            for copy in tiles(u, i, slot):
                copy.wait()

            @pl.when(i + 1 < unit.count)
            def _():
                for copy in tiles(u, i + 1, 1 - slot):
                    copy.start()

            if u + 1 < len(units):

                @pl.when(i + 1 == unit.count)
                def _():
                    for copy in tiles(u + 1, 0, 1 - slot):
                        copy.start()

            @pl.when(t >= RING)
            def _():
                r1_copy(t - RING).wait_send()

            sb[t % RING] = in_bf16(product(lo[slot], rh[slot]))
            r1_copy(t).start()
            kb[t % RING] = product(lm[slot], rh[slot])
            end(t)
            tasks(u, i)
            return carry

        lax.fori_loop(0, unit.count, step, 0)

    def drain(t, carry):
        begin(t)
        end(t)
        return carry

    lax.fori_loop(total, total + LAG_G, drain, 0)

    for p in range(total - RING, total):
        r1_copy(p).wait_send()
    kept = sum(u.col_blocks if u.by_owner else u.count for u in units)
    some, rest = pl.ds(0, kept), pl.ds(0, total - kept)
    every = remote_copy(r1, out.at[:, core], gs, gr, sib, mine)
    every.wait()
    pltpu.make_async_copy(r1.at[some], out.at[some, core], ls).wait()
    remote_copy(r1.at[rest], out.at[rest, core], fs, fr.at[0], sib, mine).wait_send()

    @pl.when(depth > 0)
    def _():
        remote_copy(r1, xb, os_, xr.at[0], outward, mine).wait_send()

    for k in range(1, half):
        gains_in(k)
    gains_across()
    for k in range(half - 2, -1, -1):
        gains_back(k)
    if half > 1:

        @pl.when(depth > 0)
        def _():
            gain_back().wait_send()


def backward(n_fsdp, n_rep, heads_k, units, piece_rows, piece_cols, args):
    total = sum(unit.count for unit in units)
    rows_all, rows = args[0].shape[0], args[9].shape[0]
    width, cols = args[8].shape
    cols_q, cols_k = heads_k * (H // KV) * HD, heads_k * HD
    two_ff = args[5].shape[1]
    dma = pltpu.SemaphoreType.DMA
    piece = (piece_rows, piece_cols)
    low, full = jnp.bfloat16, jnp.float32
    any_spec = pl.BlockSpec(memory_space=pl.ANY)
    vmem = pl.BlockSpec(memory_space=pltpu.VMEM)
    flops = sum(4 * unit.count for unit in units) * rows_all * piece_rows * piece_cols
    outs = (
        ((total, 2) + piece, low),
        ((rows_all, width), low),
        ((rows_all, cols), low),
        ((total,) + piece, low),
        ((total,) + piece, low),
        ((rows, width), low),
        ((8, width + HD), full),
    )
    scratch = (
        ((2, rows_all, piece_rows), low),
        ((2, rows_all, piece_rows), low),
        ((2, rows_all, piece_cols), low),
        ((RING,) + piece, low),
        ((RING,) + piece, full),
        ((total,) + piece, low),
        (piece, low),
        (piece, low),
        ((max(2 * rows_all, width), cols), low),
        ((2, width // TILES, two_ff), low),
        ((rows, width), full),
        ((n_fsdp - 1, rows, width), low),
        ((n_fsdp - 1, rows, width), low),
        ((n_fsdp - 1, rows, width), low),
        ((rows, width), full),
        ((rows, width), full),
        ((rows, width), low),
        ((rows, width), low),
        ((cols_q, width), low),
        ((rows, cols), full),
        ((rows, HD), full),
        ((rows, HD), full),
        ((rows, cols_q), low),
        ((rows, cols_k), low),
        ((rows, cols_k), low),
        ((rows, width), low),
        ((rows, cols_q), full),
        ((rows, cols), low),
    )
    return pl.pallas_call(
        functools.partial(
            backward_kernel, n_fsdp, n_rep, heads_k, units, piece_rows, piece_cols
        ),
        out_shape=[jax.ShapeDtypeStruct(shape, kind) for shape, kind in outs],
        in_specs=[any_spec] * 18 + [vmem] * 2 + [pl.BlockSpec(memory_space=pltpu.SMEM)] * 2,
        out_specs=[any_spec] * 5 + [vmem] * 2,
        scratch_shapes=[pltpu.VMEM(shape, kind) for shape, kind in scratch]
        + [dma((2, 3))]
        + [dma((total,)) for _ in range(6)]
        + [dma, dma, dma((total,)), dma, dma, dma]
        + [
            dma((3,)),
            dma((7,)),
            dma((2,)),
            dma((n_fsdp, TILES)),
            dma((n_fsdp, TILES)),
            dma((n_fsdp,)),
            dma((n_fsdp,)),
            dma((n_fsdp, 2)),
            dma((n_fsdp, 2)),
            dma,
            dma((8,)),
            pltpu.VMEM((n_fsdp, 8, width + HD), full),
            pltpu.VMEM((8, width + HD), full),
            pltpu.VMEM((8, width + HD), full),
            pltpu.VMEM((8, width + HD), full),
            dma((n_fsdp,)),
            dma((n_fsdp,)),
            dma((4,)),
            dma((4,)),
        ],
        compiler_params=pltpu.CompilerParams(
            collective_id=0, has_side_effects=True, vmem_limit_bytes=62 << 20
        ),
        cost_estimate=pl.CostEstimate(flops=2 * flops, bytes_accessed=1 << 30, transcendentals=0),
        name="backward",
    )(*args)


def widen_kernel(in_ref, out_ref):
    cols = in_ref.shape[-1]
    for i in range(in_ref.shape[0]):
        out_ref[:, i * cols : (i + 1) * cols] = in_ref[i, 0].astype(jnp.float32)


def widened(pieces, grid, together, where, shape, place):
    rows, cols = pieces.shape[2:]
    return pl.pallas_call(
        widen_kernel,
        grid=grid,
        out_shape=jax.ShapeDtypeStruct(shape, jnp.float32),
        in_specs=[pl.BlockSpec((together, 1, rows, cols), where)],
        out_specs=pl.BlockSpec((rows, together * cols), place),
        name="widen",
    )(pieces)


def widen_both_kernel(in_ref, first_ref, second_ref):
    cols, count = in_ref.shape[-1], in_ref.shape[0] // 2
    for i in range(count):
        first_ref[:, i * cols : (i + 1) * cols] = in_f32(in_ref[i, 0])
        second_ref[:, i * cols : (i + 1) * cols] = in_f32(in_ref[count + i, 0])


def widened_both(pieces, base, together, n_fsdp, shape):
    rows, cols = pieces.shape[2:]
    return pl.pallas_call(
        widen_both_kernel,
        grid=(2, n_fsdp),
        out_shape=[jax.ShapeDtypeStruct(shape, jnp.float32)] * 2,
        in_specs=[
            pl.BlockSpec((together, 1, rows, cols), lambda c, f: (base // together + f, c, 0, 0))
        ],
        out_specs=[pl.BlockSpec((rows, together // 2 * cols), lambda c, f: (c, f))] * 2,
        compiler_params=pltpu.CompilerParams(vmem_limit_bytes=32 << 20),
        name="widen_both",
    )(pieces)


def widen_heads_kernel(query_in, gate_in, pair_in, query_out, gate_out, key_out, value_out):
    half = key_out.shape[1]
    query_out[...] = query_in[0, 0].astype(jnp.float32)
    gate_out[...] = gate_in[0, 0].astype(jnp.float32)
    key_out[...] = pair_in[0, 0, :, :half].astype(jnp.float32)
    value_out[...] = pair_in[0, 0, :, half:].astype(jnp.float32)


def widened_heads(pieces, base, n_fsdp, shapes):
    rows, cols = pieces.shape[2:]

    def where(j):
        return lambda c, f: (base + 3 * f + j, c, 0, 0)

    widths = (cols, cols, cols // 2, cols // 2)
    return pl.pallas_call(
        widen_heads_kernel,
        grid=(2, n_fsdp),
        out_shape=[jax.ShapeDtypeStruct(shape, jnp.float32) for shape in shapes],
        in_specs=[pl.BlockSpec((1, 1, rows, cols), where(j)) for j in range(3)],
        out_specs=[pl.BlockSpec((rows, wide), lambda c, f: (c, f)) for wide in widths],
        name="widen_heads",
    )(pieces, pieces, pieces)


def block_lengths(lengths_ref, deal_ref, device):
    head_len = lengths_ref[deal_ref[2 * device]]
    return head_len, head_len + lengths_ref[deal_ref[2 * device + 1]]


def block_mask(block, rows):
    head_len, both_len = block
    query_row = lax.broadcasted_iota(jnp.int32, (rows, rows), 0)
    key_row = lax.broadcasted_iota(jnp.int32, (rows, rows), 1)

    def segment(index):
        return (index >= head_len).astype(jnp.int32) + (index >= both_len).astype(jnp.int32)

    return (segment(query_row) == segment(key_row)) & (key_row <= query_row)


def turn(values):
    half_dim = values.shape[-1] // 2
    return jnp.concatenate([-values[:, half_dim:], values[:, :half_dim]], axis=-1)


def head_forward(raw, gain, angle_cos, angle_sin):
    values = raw * lax.rsqrt(jnp.mean(raw * raw, axis=-1, keepdims=True) + EPS_NORM) * gain
    return in_bf16(values * angle_cos + turn(values) * angle_sin)


def head_backward(grad, raw, gain, angle_cos, angle_sin):
    grad = grad * angle_cos - turn(grad * angle_sin)
    scale = lax.rsqrt(jnp.mean(raw * raw, axis=-1, keepdims=True) + EPS_NORM)
    unit = raw * scale
    gain_rows = grad * unit
    inner = grad * gain
    return scale * (inner - unit * jnp.mean(inner * unit, axis=-1, keepdims=True)), gain_rows


def product_of(left, right, left_dim, right_dim):
    return lax.dot_general(
        left, right, (((left_dim,), (right_dim,)), ((), ())), preferred_element_type=jnp.float32
    )


def softmax_of(queries, keys, allowed):
    scores = jnp.where(allowed, product_of(queries, keys, 1, 1) * HD ** (-0.5), NEG_FILL)
    exponent = jnp.exp(scores - jnp.max(scores, axis=-1, keepdims=True))
    return exponent / jnp.sum(exponent, axis=-1, keepdims=True)


def attend(
    heads_k,
    allowed,
    angle_cos,
    angle_sin,
    query_gain,
    key_gain,
    raw_ref,
    q_ref,
    k_ref,
    v_ref,
    gated_ref,
):
    group = H // KV
    cols_q, cols_k = heads_k * group * HD, heads_k * HD
    for j in range(heads_k):
        own = slice(j * HD, (j + 1) * HD)
        keys = head_forward(
            raw_ref[:, 2 * cols_q + j * HD : 2 * cols_q + (j + 1) * HD],
            key_gain,
            angle_cos,
            angle_sin,
        )
        start = 2 * cols_q + cols_k + j * HD
        values = in_bf16(raw_ref[:, start : start + HD])
        k_ref[:, own] = keys
        v_ref[:, own] = values
        for h in range(j * group, (j + 1) * group):
            cut = slice(h * HD, (h + 1) * HD)
            queries = head_forward(raw_ref[:, cut], query_gain, angle_cos, angle_sin)
            q_ref[:, cut] = queries
            probs = in_bf16(softmax_of(queries, keys, allowed))
            context = product_of(probs, values, 1, 0)
            gate = raw_ref[:, cols_q + h * HD : cols_q + (h + 1) * HD]
            gated_ref[:, cut] = in_bf16(context * jax.nn.sigmoid(gate))


def attend_back(
    heads_k,
    heads,
    allowed,
    angle_cos,
    angle_sin,
    query_gain,
    key_gain,
    raw_ref,
    q_ref,
    k_ref,
    v_ref,
    grad_ref,
    out_ref,
    gain_ref,
):
    group = H // KV
    cols_q, cols_k = heads_k * group * HD, heads_k * HD
    for j in heads:
        own = slice(j * HD, (j + 1) * HD)
        keys, values = k_ref[:, own], v_ref[:, own]
        grad_keys, grad_values = 0.0, 0.0
        for h in range(j * group, (j + 1) * group):
            cut = slice(h * HD, (h + 1) * HD)
            gate_cut = slice(cols_q + h * HD, cols_q + (h + 1) * HD)
            queries, grad_gated = q_ref[:, cut], grad_ref[:, cut]
            probs = softmax_of(queries, keys, allowed)
            probs_b = in_bf16(probs)
            context = product_of(probs_b, values, 1, 0)
            gate = jax.nn.sigmoid(raw_ref[:, gate_cut])
            grad_context = in_bf16(grad_gated * gate)
            out_ref[:, gate_cut] = in_bf16(grad_gated * context * gate * (1.0 - gate))
            grad_probs = product_of(grad_context, values, 1, 1)
            grad_scores = in_bf16(
                probs * (grad_probs - jnp.sum(probs * grad_probs, axis=-1, keepdims=True))
            )
            grad_values += product_of(probs_b, grad_context, 0, 0)
            grad_keys += product_of(grad_scores, queries, 0, 0)
            grad_queries = product_of(grad_scores, keys, 1, 0) * HD ** (-0.5)
            grad_raw, gain_rows = head_backward(
                grad_queries, raw_ref[:, cut], query_gain, angle_cos, angle_sin
            )
            out_ref[:, cut] = in_bf16(grad_raw)
            gain_ref[0:1, :] += jnp.sum(gain_rows, axis=0, keepdims=True)
        key_start = 2 * cols_q + j * HD
        grad_raw, gain_rows = head_backward(
            grad_keys * HD ** (-0.5),
            raw_ref[:, key_start : key_start + HD],
            key_gain,
            angle_cos,
            angle_sin,
        )
        out_ref[:, key_start : key_start + HD] = in_bf16(grad_raw)
        gain_ref[1:2, :] += jnp.sum(gain_rows, axis=0, keepdims=True)
        value_start = 2 * cols_q + cols_k + j * HD
        out_ref[:, value_start : value_start + HD] = in_bf16(grad_values)


def remote_copy(src, dst, send, recv, to_rep, to_fsdp):
    return pltpu.make_async_remote_copy(
        src_ref=src,
        dst_ref=dst,
        send_sem=send,
        recv_sem=recv,
        device_id={"rep": to_rep, "fsdp": to_fsdp},
        device_id_type=MESH,
    )


def greet_all(peers):
    barrier = pltpu.get_barrier_semaphore()
    for to_rep, to_fsdp in peers:
        pl.semaphore_signal(
            barrier, inc=1, device_id={"rep": to_rep, "fsdp": to_fsdp}, device_id_type=MESH
        )
    pl.semaphore_wait(barrier, len(peers))


class GatherRows:
    def __init__(self, n_fsdp, rep, mine, source, target, sems):
        self.n_fsdp, self.rep, self.mine = n_fsdp, rep, mine
        self.source, self.target = source, target
        self.send, self.recv, self.local = sems
        self.rows = source.shape[0]
        self.half = self.rows // 2
        self.relay = ((1, 0), (2, 1)) if n_fsdp == 4 else ()

    def copy(self, s, h, to=None, src=None):
        to = s if to is None else to
        return remote_copy(
            self.source.at[pl.ds(h * self.half, self.half)]
            if src is None
            else self.target.at[pl.ds(src * self.rows + h * self.half, self.half)],
            self.target.at[pl.ds(s * self.rows + h * self.half, self.half)],
            self.send.at[s, h],
            self.recv.at[s, h],
            self.rep,
            flipped(self.mine, to, self.n_fsdp),
        )

    def own(self):
        return pltpu.make_async_copy(
            self.source, self.target.at[pl.ds(0, self.rows)], self.local
        )

    def start(self):
        for s, h in ((1, 0), (2, 1), (1, 1), (2, 0)):
            if s < self.n_fsdp:
                self.copy(s, h).start()
        if self.n_fsdp != 4:
            for s in range(3, self.n_fsdp):
                for h in range(2):
                    self.copy(s, h).start()
        self.own().start()

    def forward(self):
        if self.n_fsdp == 4:
            self.copy(1, 0).wait_recv()
            self.copy(3, 0, to=2, src=1).start()
            self.copy(2, 1).wait_recv()
            self.copy(3, 1, to=1, src=2).start()

    def arrive(self, s):
        for h in range(2):
            if (s, h) not in self.relay:
                self.copy(s, h).wait_recv()

    def sent(self):
        for s in range(1, self.n_fsdp):
            for h in range(2):
                self.copy(s, h).wait_send()

    def finish(self):
        for s in range(1, self.n_fsdp):
            self.arrive(s)
        self.sent()
        self.own().wait()


def forward_kernel(n_fsdp, n_rep, heads_k, *refs):
    (tokens, gains, wq, wg, wk, wv, w_gate, w_up, w_output, w_down, teacher) = refs[:11]
    (lengths_ref, deal_ref, lengths_row, freq_ref) = refs[11:15]
    (normed_all, raw_all, q_all, k_all, v_all, gated_all, w_attn, w_mlp) = refs[15:23]
    (middle_out, nmlp_all, hidden_all, gbranch_all, gmlp_all, gres_out, block_out) = refs[23:30]
    (gu_all, all_cos, all_sin, gain_out, head_gain_out, loss_out) = refs[30:36]
    (tok, gl, wa, wo, wd, wm, nb, raw, cs, sn, qb, kvb, vb, gb, own, pbuf, land) = refs[36:53]
    (mid, nm, te, gu, hb, gm) = refs[53:59]
    (ts, tr, tl, us, ur, ul, bs, br, bl, gain_s, gain_r, ws, wr, zs, zr, cps, cpr) = refs[59:76]
    (ms, mr, hs, hr, ss, sr, ps, pr, qs, qr, load, keep, mine_sem) = refs[76:]
    rows, width = own.shape
    rows_all = n_fsdp * rows
    cols, ff = raw.shape[1], hb.shape[1]
    deep = wq.shape[0]
    widths = tuple(w.shape[1] // n_fsdp for w in (wq, wg, wk, wv))
    starts = [sum(widths[:i]) for i in range(4)]
    others = range(1, n_fsdp)
    n_line = n_rep // 2
    rep, mine = lax.axis_index("rep"), lax.axis_index("fsdp")
    core, place = rep % 2, rep // 2
    sib = rep + 1 - 2 * core
    partner = (place + 1 - 2 * (place % 2)) * 2 + core
    block, part = deep // 4, deep // n_rep
    band = (place % 2) * 2 + core
    other_band = (1 - place % 2) * 2 + core
    hops = range(1, n_line)
    row_steps = rows // ROW_STEP
    near = sorted({1, n_line - 1})
    greet_all(
        [(sib, mine)]
        + [(((place + k) % n_line) * 2 + core, mine) for k in near]
        + [(rep, flipped(mine, s, n_fsdp)) for s in others]
    )


    def columns(peer, wide):
        return pl.ds(pl.multiple_of(peer * wide, wide), wide)

    def mlp_copy(s, i):
        peer = flipped(mine, s, n_fsdp)
        return remote_copy(
            (w_gate, w_up)[i].at[pl.ds(rep * part, part), columns(peer, ff)],
            w_mlp.at[pl.ds(mine * deep + rep * part, part), pl.ds(i * ff, ff)],
            ms.at[s, i],
            mr.at[s, i],
            rep,
            peer,
        )

    def part_at(s, of_rep):
        return w_mlp.at[pl.ds(flipped(mine, s, n_fsdp) * deep + of_rep * part, part)]

    def line_copy(s, k, up):
        step = 1 if up else -1
        src = part_at(s, ((place - step * (k - 1) + n_line) % n_line) * 2 + core)
        to_rep = ((place + step + n_line) % n_line) * 2 + core
        way = 0 if up else 1
        return remote_copy(src, src, hs.at[way, s, k], hr.at[way, s, k], to_rep, mine)

    def line_sends(k):
        for up in (True, False):
            first, last = (k - 1, n_line - 2) if up else (1, n_line - k)

            @pl.when((place >= first) & (place <= last))
            def _(up=up):
                for s in others:
                    line_copy(s, k, up).start()

    def line_arrivals(k):
        for up in (True, False):
            first, last = (k, n_line - 1) if up else (0, n_line - 1 - k)

            @pl.when((place >= first) & (place <= last))
            def _(up=up):
                for s in others:
                    line_copy(s, k, up).wait_recv()
                    share_copy(s, k, up).start()

        if k + 1 < n_line:
            line_sends(k + 1)

    def share_copy(s, k, up):
        step = 1 if up else -1
        src = part_at(s, ((place - step * k + n_line) % n_line) * 2 + core)
        way = 0 if up else 1
        return remote_copy(src, src, ss.at[way, s, k], sr.at[way, s, k], sib, mine)

    def shares(action):
        for s in others:
            action(share_copy(s, 0, True))
        for k in hops:
            for up in (True, False):
                first, last = (k, n_line - 1) if up else (0, n_line - 1 - k)

                @pl.when((place >= first) & (place <= last))
                def _(k=k, up=up):
                    for s in others:
                        action(share_copy(s, k, up))

    def lines_sent():
        for k in hops:
            for up in (True, False):
                first, last = (k - 1, n_line - 2) if up else (1, n_line - k)

                @pl.when((place >= first) & (place <= last))
                def _(k=k, up=up):
                    for s in others:
                        line_copy(s, k, up).wait_send()

    weights = (wq, wg, wk, wv)

    def weight_copy(s, i):
        peer = flipped(mine, s, n_fsdp)
        return remote_copy(
            weights[i].at[pl.ds(band * block, block), columns(peer, widths[i])],
            w_attn.at[pl.ds(mine * deep + band * block, block), pl.ds(starts[i], widths[i])],
            ws.at[s, i],
            wr.at[s, i],
            rep,
            peer,
        )

    def band_at(s, which):
        return w_attn.at[pl.ds(flipped(mine, s, n_fsdp) * deep + which * block, block)]

    def partner_copy(s):
        return remote_copy(band_at(s, band), band_at(s, band), zs.at[s], zr.at[s], partner, mine)

    def sibling_copy(s, k):
        which = band if k == 0 else other_band
        return remote_copy(
            band_at(s, which), band_at(s, which), cps.at[s, k], cpr.at[s, k], sib, mine
        )

    def gain_copy(s):
        return remote_copy(
            gains, gl.at[mine], gain_s.at[s], gain_r.at[s], rep, flipped(mine, s, n_fsdp)
        )

    mine_rows = pl.ds(mine * deep, deep)
    mine_pairs = [
        (weights[i].at[:, columns(mine, widths[i])], w_attn.at[mine_rows, pl.ds(starts[i], widths[i])])
        for i in range(4)
    ]
    mine_pairs += [
        (w.at[:, columns(mine, ff)], w_mlp.at[mine_rows, pl.ds(i * ff, ff)])
        for i, w in enumerate((w_gate, w_up))
    ]
    mine_pairs += [(gains, gl.at[mine]), (w_output, wo), (w_down, wd), (teacher, te)]

    def local(which):
        return [pltpu.make_async_copy(*mine_pairs[i], mine_sem.at[i]) for i in which]

    def attn_load():
        return pltpu.make_async_copy(w_attn, wa, load.at[0])

    def mlp_load():
        return pltpu.make_async_copy(w_mlp, wm, load.at[1])

    token_rows = GatherRows(n_fsdp, rep, mine, tokens, tok, (ts, tr, tl))
    up_rows = GatherRows(n_fsdp, rep, mine, nm, nmlp_all, (us, ur, ul))
    back_rows = GatherRows(n_fsdp, rep, mine, nm, gbranch_all, (bs, br, bl))

    for s in others:
        gain_copy(s).start()
        for i in range(4):
            weight_copy(s, i).start()
    for copy in local(range(10)):
        copy.start()
    for s in others:
        for i in range(4):
            weight_copy(s, i).wait_recv()
        partner_copy(s).start()
        sibling_copy(s, 0).start()
    for s in others:
        for i in range(2):
            mlp_copy(s, i).start()

    def block_rows(s):
        return pl.ds(pl.multiple_of(s * rows, rows), rows)

    def lengths_of(s):
        return block_lengths(lengths_ref, deal_ref, rep * n_fsdp + flipped(mine, s, n_fsdp))

    def angles(s, carry):
        head_len, both_len = lengths_of(s)
        index = lax.broadcasted_iota(jnp.int32, (rows, HD), 0)
        start = jnp.where(index < head_len, 0, jnp.where(index < both_len, head_len, both_len))
        angle = (index - start).astype(jnp.float32) * freq_ref[...]
        cs[block_rows(s)] = jnp.cos(angle)
        sn[block_rows(s)] = jnp.sin(angle)
        return carry

    lax.fori_loop(0, n_fsdp, angles, 0)
    angle_stores = [
        pltpu.make_async_copy(cs, all_cos, load.at[2]),
        pltpu.make_async_copy(sn, all_sin, load.at[3]),
    ]
    for copy in angle_stores:
        copy.start()
    token_count = jnp.sum(in_f32(lengths_row[...]), axis=1, keepdims=True)
    local((6,))[0].wait()
    gain_out[...] = jnp.zeros_like(gain_out)
    head_gain_out[...] = jnp.zeros_like(head_gain_out)
    for s in others:
        gain_copy(s).wait()
    lines = deep // HD
    for f in range(n_fsdp):
        piece = in_f32(gl[f])
        for kind in range(2):
            for r in range(lines):
                at = f * deep + r * HD
                gain_out[kind : kind + 1, at : at + HD] = piece[
                    kind * lines + r : kind * lines + r + 1
                ]
            head_gain_out[kind : kind + 1] += piece[2 * lines + kind : 2 * lines + kind + 1]
    for s in others:
        for i in range(2):
            mlp_copy(s, i).wait_recv()
        share_copy(s, 0, True).start()
    token_rows.start()
    for s in others:
        partner_copy(s).wait_recv()
        sibling_copy(s, 1).start()
    line_sends(1)
    for s in others:
        for k in range(2):
            sibling_copy(s, k).wait_recv()
    for copy in local((0, 1, 2, 3)):
        copy.wait()
    attn_load().start()
    for copy in local((7, 8, 9)):
        copy.wait()

    def some_rows(base, r):
        return pl.ds(pl.multiple_of(base + r * ROW_STEP, ROW_STEP), ROW_STEP)

    def tiled(count, wide, body):
        def one(j, carry):
            body(pl.ds(pl.multiple_of(j * wide, wide), wide))
            return carry

        lax.fori_loop(0, count, one, 0)

    def by_rows(body):
        def one(r, carry):
            body(r)
            return carry

        lax.fori_loop(0, row_steps, one, 0)

    tile = width // 4

    def leave(s, left, right):
        def one(cut):
            product = product_of(left[...], right[:, cut], 1, 0)

            @pl.when(s == 0)
            def _():
                own[:, cut] = product

            @pl.when(s > 0)
            def _():
                pbuf[s - 1, :, cut] = in_bf16(product)

        tiled(4, tile, one)


    relayed = n_fsdp == 4

    def half_rows(h):
        return pl.ds(h * (rows // 2), rows // 2)

    def out_copy(s, h, sends, recvs):
        to, at = s, s - 1
        if relayed and s == 3:
            to, at = h + 1, 2
        return remote_copy(
            pbuf.at[s - 1, half_rows(h)],
            land.at[at, half_rows(h)],
            sends.at[s, h],
            recvs.at[s, h],
            rep,
            flipped(mine, to, n_fsdp),
        )

    def send_block(s, sends, recvs):
        for k in others:

            @pl.when(s == k)
            def _(k=k):
                for h in range(2):
                    if not relayed or (k, h) not in ((1, 1), (2, 0)):
                        out_copy(k, h, sends, recvs).start()

    def relay(sends, recvs):
        if relayed:
            for h, near in ((0, 2), (1, 1)):
                out_copy(3, h, sends, recvs).wait_recv()
                cut = half_rows(h)
                pbuf[near - 1, cut] = in_bf16(in_f32(pbuf[near - 1, cut]) + in_f32(land[2, cut]))
                out_copy(near, h, sends, recvs).start()

    def arrived(sends, recvs):
        for s in others:
            for h in range(2):
                if not (relayed and s == 3):
                    out_copy(s, h, sends, recvs).wait_recv()
                out_copy(s, h, sends, recvs).wait_send()

    def summed(cut):
        total = own[cut]
        for s in range(1, 3 if relayed else n_fsdp):
            total += in_f32(land[s - 1, cut])
        return total

    def scaled(values, gain):
        scale = lax.rsqrt(jnp.mean(values * values, axis=-1, keepdims=True) + EPS_NORM)
        return in_bf16(values * scale * gain)


    def attention_stores(s):
        cut = block_rows(s)
        pairs = (
            (nb, normed_all), (raw, raw_all), (qb, q_all), (kvb, k_all), (vb, v_all), (gb, gated_all)
        )
        return [
            pltpu.make_async_copy(src, dst.at[cut], keep.at[i])
            for i, (src, dst) in enumerate(pairs)
        ]

    def attention(s, carry):
        pl.when(s == 1)(token_rows.forward)
        for k in range(n_fsdp):

            @pl.when(s == k)
            def _(k=k):
                if k == 0:
                    token_rows.own().wait()
                else:
                    token_rows.arrive(k)

        @pl.when(s > 0)
        def _():
            for copy in attention_stores(s):
                copy.wait()

        def normed_rows(r):
            values = in_f32(tok[some_rows(s * rows, r)])
            nb[some_rows(0, r)] = scaled(values, gain_out[0:1])

        by_rows(normed_rows)

        @pl.when(s == 0)
        def _():
            attn_load().wait()

        def raw_tile(cut):
            raw[:, cut] = product_of(nb[...], wa[:, cut], 1, 0)

        tiled(3, cols // 3, raw_tile)
        attend(
            heads_k,
            block_mask(lengths_of(s), rows),
            cs[block_rows(s)],
            sn[block_rows(s)],
            head_gain_out[0:1],
            head_gain_out[1:2],
            raw,
            qb,
            kvb,
            vb,
            gb,
        )
        for copy in attention_stores(s):
            copy.start()
        leave(s, gb, wo)

        send_block(s, ps, pr)
        if n_line > 2:
            pl.when(s == n_fsdp - 2)(lambda: line_arrivals(1))
        return carry

    lax.fori_loop(0, n_fsdp, attention, 0)
    for copy in angle_stores:
        copy.wait()
    relay(ps, pr)
    for k in range(2, n_line - 1):
        line_arrivals(k)
    arrived(ps, pr)

    def middle_rows(r):
        cut = some_rows(0, r)
        values = in_f32(tok[cut]) + summed(cut)
        mid[cut] = values
        nm[cut] = scaled(values, gain_out[1:2])

    by_rows(middle_rows)
    up_rows.start()

    def middle_store():
        return pltpu.make_async_copy(mid, middle_out, load.at[4])

    middle_store().start()
    for copy in attention_stores(0):
        copy.wait()


    line_arrivals(n_line - 1)
    shares(lambda copy: copy.wait_recv())
    for copy in local((4, 5)):
        copy.wait()
    mlp_load().start()
    mlp_load().wait()

    def block_load(source, s):
        return pltpu.make_async_copy(source.at[block_rows(s)], nb, load.at[2])

    def ff_stores(s):
        cut = block_rows(s)
        return [
            pltpu.make_async_copy(hb, hidden_all.at[cut], keep.at[0]),
            pltpu.make_async_copy(gu, gu_all.at[cut], keep.at[1]),
        ]

    def into_nb(gather, source, s):
        @pl.when(s == 0)
        def _():
            nb[...] = nm[...]

        for k in others:

            @pl.when(s == k)
            def _(k=k):
                gather.arrive(k)

        @pl.when(s > 0)
        def _():
            copy = block_load(source, s)
            copy.start()
            copy.wait()

    def feed_forward(i, carry):
        s = (i + 1) % n_fsdp
        pl.when(i == 0)(up_rows.forward)
        into_nb(up_rows, nmlp_all, s)

        @pl.when(i > 0)
        def _():
            for copy in ff_stores(s):
                copy.wait()

        def pre_tile(cut):
            gu[:, cut] = product_of(nb[...], wm[:, cut], 1, 0)

        tiled(6, ff // 3, pre_tile)

        def hidden_rows(r):
            cut = some_rows(0, r)
            gate_pre = gu[cut, :ff]
            hb[cut] = in_bf16(gate_pre * jax.nn.sigmoid(gate_pre) * gu[cut, ff:])

        by_rows(hidden_rows)
        for copy in ff_stores(s):
            copy.start()
        leave(s, hb, wd)

        send_block(s, qs, qr)
        return carry

    lax.fori_loop(0, n_fsdp, feed_forward, 0)
    relay(qs, qr)
    up_rows.sent()
    up_rows.own().wait()
    middle_store().wait()
    for copy in ff_stores(0):
        copy.wait()


    def gu_load(s):
        return pltpu.make_async_copy(gu_all.at[block_rows(s)], gu, load.at[5])

    gu_load(0).start()
    arrived(qs, qr)
    head_len, both_len = lengths_of(0)
    factor = (n_rep * rows_all) / token_count
    loss_out[...] = jnp.zeros_like(loss_out)

    def error_rows(r):
        cut = some_rows(0, r)
        index = r * ROW_STEP + lax.broadcasted_iota(jnp.int32, (ROW_STEP, 1), 0)
        valid = (index < both_len).astype(jnp.float32)
        result = mid[cut] + summed(cut)
        error = (result - in_f32(te[cut])) * valid
        square = jnp.sum(error * error, axis=-1, keepdims=True)
        first = jnp.where(index < head_len, square, 0.0)
        loss_out[0:1] += jnp.sum(first, axis=0, keepdims=True)
        loss_out[1:2] += jnp.sum(square - first, axis=0, keepdims=True)
        te[cut] = in_bf16(result * valid)
        grad = error * factor
        mid[cut] = grad
        nm[cut] = in_bf16(grad)

    by_rows(error_rows)
    loss_out[...] = loss_out[...] / (2.0 * token_count)
    back_rows.start()
    last_stores = [
        pltpu.make_async_copy(te, block_out, load.at[3]),
        pltpu.make_async_copy(mid, gres_out, load.at[4]),
    ]
    for copy in last_stores:
        copy.start()

    def grad_store(s):
        return pltpu.make_async_copy(gm, gmlp_all.at[block_rows(s)], keep.at[2])

    def feed_back(s, carry):
        pl.when(s == 1)(back_rows.forward)
        into_nb(back_rows, gbranch_all, s)

        def hidden_tile(cut):
            raw[:, cut] = product_of(nb[...], wd[cut], 1, 1)

        tiled(3, ff // 3, hidden_tile)
        gu_load(s).wait()

        @pl.when(s > 0)
        def _():
            grad_store(s).wait()

        def grad_rows(r):
            cut = some_rows(0, r)
            gate_pre, grad = gu[cut, :ff], raw[cut]
            gate = jax.nn.sigmoid(gate_pre)
            silu = gate_pre * gate
            gm[cut, :ff] = in_bf16(grad * gu[cut, ff:] * (gate + silu * (1.0 - gate)))
            gm[cut, ff:] = in_bf16(grad * silu)

        by_rows(grad_rows)
        grad_store(s).start()

        @pl.when(s + 1 < n_fsdp)
        def _():
            gu_load(s + 1).start()

        return carry

    lax.fori_loop(0, n_fsdp, feed_back, 0)

    grad_store(0).wait()
    for copy in last_stores:
        copy.wait()
    back_rows.sent()
    back_rows.own().wait()
    token_rows.sent()
    for s in others:
        partner_copy(s).wait_send()
        for i in range(4):
            weight_copy(s, i).wait_send()
        for i in range(2):
            sibling_copy(s, i).wait_send()
            mlp_copy(s, i).wait_send()
    lines_sent()
    shares(lambda copy: copy.wait_send())


def forward(n_fsdp, n_rep, heads_k, args):
    rows, width = args[0].shape
    rows_all = n_fsdp * rows
    cols_q, cols_k = heads_k * (H // KV) * HD, heads_k * HD
    cols = 2 * cols_q + 2 * cols_k
    ff = args[9].shape[0]
    n_line = n_rep // 2
    low, full = jnp.bfloat16, jnp.float32
    dma = pltpu.SemaphoreType.DMA
    any_spec = pl.BlockSpec(memory_space=pl.ANY)
    vmem, smem = pl.BlockSpec(memory_space=pltpu.VMEM), pl.BlockSpec(memory_space=pltpu.SMEM)
    outs = (
        ((rows_all, width), low),
        ((rows_all, cols), full),
        ((rows_all, cols_q), low),
        ((rows_all, cols_k), low),
        ((rows_all, cols_k), low),
        ((rows_all, cols_q), low),
        ((width, cols), low),
        ((width, 2 * ff), low),
        ((rows, width), full),
        ((rows_all, width), low),
        ((rows_all, ff), low),
        ((rows_all, width), low),
        ((rows_all, 2 * ff), low),
        ((rows, width), full),
        ((rows, width), low),
        ((rows_all, 2 * ff), full),
        ((rows_all, HD), full),
        ((rows_all, HD), full),
        ((8, width), full),
        ((8, HD), full),
        ((8, HD), full),
    )
    scratch = (
        ((rows_all, width), low),
        ((n_fsdp, 16, HD), low),
        ((width, cols), low),
        ((cols_q, width), low),
        ((ff, width), low),
        ((width, 2 * ff), low),
        ((rows, width), low),
        ((rows, cols), full),
        ((rows_all, HD), full),
        ((rows_all, HD), full),
        ((rows, cols_q), low),
        ((rows, cols_k), low),
        ((rows, cols_k), low),
        ((rows, cols_q), low),
        ((rows, width), full),
        ((n_fsdp - 1, rows, width), low),
        ((n_fsdp - 1, rows, width), low),
        ((rows, width), full),
        ((rows, width), low),
        ((rows, width), low),
        ((rows, 2 * ff), full),
        ((rows, ff), low),
        ((rows, 2 * ff), low),
    )
    one, pair, four = dma((n_fsdp,)), dma((n_fsdp, 2)), dma((n_fsdp, 4))
    line = dma((2, n_fsdp, n_line))
    return pl.pallas_call(
        functools.partial(forward_kernel, n_fsdp, n_rep, heads_k),
        out_shape=[jax.ShapeDtypeStruct(shape, kind) for shape, kind in outs],
        in_specs=[any_spec] * 11 + [smem] * 2 + [vmem] * 2,
        out_specs=[any_spec] * 18 + [vmem] * 3,
        scratch_shapes=[pltpu.VMEM(shape, kind) for shape, kind in scratch]
        + [pair, pair, dma] * 3
        + [one, one, four, four, one, one, pair, pair]
        + [pair, pair, line, line, line, line, pair, pair, pair, pair]
        + [dma((6,)), dma((6,)), dma((10,))],
        compiler_params=pltpu.CompilerParams(
            collective_id=1, has_side_effects=True, vmem_limit_bytes=62 << 20
        ),
        name="forward",
    )(*args)


def shards(
    tokens,
    teacher,
    lengths,
    deal_order,
    attention_gain,
    query_gain,
    key_gain,
    w_query,
    w_key,
    w_value,
    w_outgate,
    w_output,
    mlp_gain,
    w_gate,
    w_up,
    w_down,
):
    n_rep = lax.axis_size("rep")
    n_fsdp = lax.axis_size("fsdp")
    rows, width = tokens.shape
    mine = lax.axis_index("fsdp")
    core = lax.axis_index("rep") % 2
    others = range(1, n_fsdp)
    heads_q, heads_k = H // n_fsdp, KV // n_fsdp
    cols_q, cols_k = heads_q * HD, heads_k * HD
    deep = w_query.shape[0]
    ff = w_down.shape[0]
    rows_all = rows * n_fsdp

    freq = np.power(np.float32(ROPE_BASE), -np.arange(0, HD, 2, dtype=np.float32) / HD)
    freq = jnp.asarray(np.concatenate([freq, freq])[None])
    small = query_gain.shape[0]

    def spread(gain):
        lane = jnp.arange(HD, dtype=jnp.int32)
        return jnp.where(lane // small == mine, jnp.tile(gain, n_fsdp), 0)[None]

    gain_block = jnp.concatenate(
        [
            attention_gain.reshape(-1, HD),
            mlp_gain.reshape(-1, HD),
            spread(query_gain),
            spread(key_gain),
            jnp.zeros((14 - 2 * deep // HD, HD), jnp.bfloat16),
        ]
    )
    (
        normed_all,
        attn_raw,
        queries_b,
        keys_b,
        values_b,
        gated_b,
        w_attn,
        w_mlp,
        middle,
        normed_mlp_all,
        hidden_b,
        grad_branch_all,
        grad_mlp_b,
        grad_result,
        block_out,
        _,
        angle_cos,
        angle_sin,
        gain_rows,
        head_gains,
        losses,
    ) = forward(
        n_fsdp,
        n_rep,
        heads_k,
        (
            tokens,
            gain_block,
            w_query,
            w_outgate,
            w_key,
            w_value,
            w_gate,
            w_up,
            w_output,
            w_down,
            teacher,
            lengths,
            deal_order,
            lengths[None],
            freq,
        ),
    )
    seq_loss = losses[:2, 0]
    piece_rows, piece_cols = deep // 2, width // n_fsdp
    units, base = [], 0
    for by_owner, row_blocks, cols in (
        (False, ff // 2 // piece_rows, width),
        (True, n_fsdp, 2 * ff),
        (False, cols_q // 2 // piece_rows, width),
        (True, n_fsdp, 2 * cols_q + 2 * cols_k),
    ):
        units.append(Unit(base, by_owner, row_blocks, cols // piece_cols))
        base += units[-1].count
    pieces, _, _, _, _, tokens_grad, gain_sums = backward(
        n_fsdp,
        n_rep,
        heads_k,
        units,
        piece_rows,
        piece_cols,
        (
            hidden_b,
            normed_mlp_all,
            gated_b,
            normed_all,
            grad_branch_all,
            grad_mlp_b,
            w_mlp,
            w_output,
            w_attn,
            middle,
            grad_result,
            tokens,
            attn_raw,
            angle_cos,
            angle_sin,
            queries_b,
            keys_b,
            values_b,
            gain_rows,
            head_gains,
            lengths,
            deal_order,
        ),
    )
    down, mlp, outp, attn = units

    def by_rows(unit, weight):
        blocks, together = unit.row_blocks, unit.col_blocks
        return widened(
            pieces,
            (2, blocks),
            together,
            lambda c, r: (unit.base // together + r, c, 0, 0),
            weight.shape,
            lambda c, r: (c * blocks + r, 0),
        )

    dw_down = by_rows(down, w_down)
    dw_output = by_rows(outp, w_output)
    dw_gate, dw_up = widened_both(pieces, mlp.base, mlp.col_blocks, n_fsdp, w_gate.shape)
    dw_query, dw_outgate, dw_key, dw_value = widened_heads(
        pieces,
        attn.base,
        n_fsdp,
        (w_query.shape, w_outgate.shape, w_key.shape, w_value.shape),
    )

    def own_part(row, start, cols):
        return lax.dynamic_slice(gain_sums, (row, start + mine * cols), (1, cols))[0]

    return (
        block_out,
        seq_loss,
        tokens_grad,
        own_part(0, 0, deep),
        own_part(0, width, small),
        own_part(1, width, small),
        dw_query,
        dw_key,
        dw_value,
        dw_outgate,
        dw_output,
        own_part(1, 0, deep),
        dw_gate,
        dw_up,
        dw_down,
    )


def solution(mesh):
    return jax.shard_map(
        shards,
        mesh=mesh,
        in_specs=(
            P(("rep", "fsdp"), None),
            P(("rep", "fsdp"), None),
            P(),
            P(),
            P("fsdp"),
            P("fsdp"),
            P("fsdp"),
            P("fsdp", None),
            P("fsdp", None),
            P("fsdp", None),
            P("fsdp", None),
            P("fsdp", None),
            P("fsdp"),
            P("fsdp", None),
            P("fsdp", None),
            P("fsdp", None),
        ),
        out_specs=(
            P(("rep", "fsdp"), None),
            P(("rep", "fsdp")),
            P(("rep", "fsdp"), None),
            P("fsdp"),
            P("fsdp"),
            P("fsdp"),
            P("fsdp", None),
            P("fsdp", None),
            P("fsdp", None),
            P("fsdp", None),
            P("fsdp", None),
            P("fsdp"),
            P("fsdp", None),
            P("fsdp", None),
            P("fsdp", None),
        ),
        check_vma=False,
    )
```

```python
import functools

import jax
import jax.numpy as jnp
import numpy as np
from jax import lax
from jax.experimental import pallas as pl
from jax.experimental.pallas import tpu as pltpu
from jax.sharding import PartitionSpec as P

MESH = pl.DeviceIdType.MESH

H = 16
KV = 8
HD = 128


EPS_NORM = 1e-06
ROPE_BASE = 1000000.0
NEG_FILL = -1e30


def in_f32(values):
    return values.astype(jnp.float32)


def in_bf16(values):
    return values.astype(jnp.bfloat16)


def flipped(index, step, n):
    out, bit = index, 1
    while bit < n:
        has = (step // bit) % 2
        out = out + has * bit * (1 - 2 * ((index // bit) % 2))
        bit *= 2
    return out


def at_least(value, bound, span):
    span = max(span, bound)
    return (value + (span - bound)) // span


class Unit:
    def __init__(self, base, by_owner, row_blocks, col_blocks):
        self.base, self.by_owner = base, by_owner
        self.row_blocks, self.col_blocks = row_blocks, col_blocks
        self.count = row_blocks * col_blocks


LAG_B, LAG_C, LAG_D, LAG_E, LAG_G = 1, 3, 5, 7, 13
RING = 4


ROW_STEP = 32
TILES = 8


def norm_back(grad, raw, gain):
    scale = lax.rsqrt(jnp.mean(raw * raw, axis=-1, keepdims=True) + EPS_NORM)
    unit = raw * scale
    inner = grad * gain
    return scale * (inner - unit * jnp.mean(inner * unit, axis=-1, keepdims=True)), grad * unit


def backward_kernel(n_fsdp, n_rep, heads_k, units, piece_rows, piece_cols, *refs):
    (hidden, normed_mlp, gated, normed, grad_branch, grad_mlp, w_mlp, w_output, w_attn) = refs[:9]
    (middle, grad_result, tokens, attn_raw, all_cos, all_sin, all_q, all_k, all_v) = refs[9:18]
    (gains, head_gains, lengths_ref, deal_ref) = refs[18:22]
    (out, grad_attn, grad_raw, inb, xb, tokens_grad, gain_out) = refs[22:29]
    (lm, lo, rh, sb, kb, r1, c_slot, d_slot, big, wt, own, pbuf, land_a, land_b) = refs[29:43]
    (mid, gres, tok, ga, wo, raw, cs, sn, qb, kvb, vb, gb, gg, ob) = refs[43:57]
    (tile_sem, r1s, r1r, ins, inr, xs, xr, os_, fs, fr, gs, gr, ls) = refs[57:70]
    (load_sem, first_sem, wt_sem, ps, pr, qs, qr, ag_s, ag_r, ag_l, block_sem) = refs[70:81]
    (near_land, pair_land, in_land, far_land, near_s, near_r, line_s, line_r) = refs[81:]
    head_gain_out = gain_out.at[:, pl.ds(own.shape[1], HD)]
    lefts = (hidden, normed_mlp, gated, normed)
    rights = (grad_branch, grad_mlp, grad_attn, grad_raw)
    total = sum(unit.count for unit in units)
    rows, width = own.shape
    rows_all = n_fsdp * rows
    ff = grad_mlp.shape[1] // 2
    tile = width // TILES
    others = range(1, n_fsdp)
    rep, mine = lax.axis_index("rep"), lax.axis_index("fsdp")
    core, place = rep % 2, rep // 2
    n_line = n_rep // 2
    half = n_line // 2
    side = place // half
    depth = place * (1 - side) + (n_line - 1 - place) * side
    inward = (place + 1 - 2 * side) * 2 + core
    outward = (place - 1 + 2 * side) * 2 + core
    sib = rep + 1 - 2 * core
    at_middle = depth == half - 1

    barrier = pltpu.get_barrier_semaphore()

    def greet(to_rep, to_fsdp):
        pl.semaphore_signal(
            barrier, inc=1, device_id={"rep": to_rep, "fsdp": to_fsdp}, device_id_type=MESH
        )

    greet(sib, mine)
    greet(inward, mine)
    for s in others:
        greet(rep, flipped(mine, s, n_fsdp))


    def r1_copy(p):
        return remote_copy(sb.at[p % RING], r1.at[p], r1s.at[p], r1r.at[p], sib, mine)

    def in_copy(p):
        return remote_copy(r1.at[p], inb.at[p], ins.at[p], inr.at[p], inward, mine)

    def x_copy(p):
        return remote_copy(r1.at[p], xb.at[p], xs.at[p], xr.at[p], inward, mine)

    def o_copy(p, src):
        return remote_copy(src.at[p], xb.at[p], os_, xr.at[p], outward, mine)

    def inside_of(p, unit):
        inside = at_least(p, unit.base, total - unit.base)
        stop = unit.base + unit.count
        if stop < total:
            inside = inside * (1 - at_least(p, stop, total - stop))
        return inside

    def owner_of(p):
        step = 0
        for unit in units:
            if unit.by_owner:
                i = p - unit.base
                step = step + inside_of(p, unit) * (n_fsdp - 1 - i // unit.col_blocks)
        return step

    def spot(p, source):
        where = p
        for unit in units:
            if unit.by_owner:
                i = p - unit.base
                spread = unit.base + source * unit.col_blocks + i % unit.col_blocks
                where = where + inside_of(p, unit) * (spread - p)
        return where

    def f_copy(p, step):
        return remote_copy(
            r1.at[p],
            out.at[spot(p, mine), core],
            fs,
            fr.at[p],
            rep,
            flipped(mine, step, n_fsdp),
        )

    def g_copy(src, where):
        return remote_copy(src, out.at[where, core], gs, gr, sib, mine)

    def l_copy(p):
        return pltpu.make_async_copy(r1.at[p], out.at[spot(p, mine), core], ls)

    def c_load(p):
        return pltpu.make_async_copy(inb.at[p], c_slot, load_sem.at[0])

    def d_load(p):
        return pltpu.make_async_copy(xb.at[p], d_slot, load_sem.at[1])

    def e_load(p):
        return pltpu.make_async_copy(xb.at[p], r1.at[p], load_sem.at[2])

    def add_into(p, other):
        r1[p] = in_bf16(in_f32(r1[p]) + in_f32(other))

    def begin_c(p):
        @pl.when(depth > 0)
        def _():
            in_copy(p).wait_recv()
            c_load(p).start()

    def begin_d(p):
        @pl.when(at_middle)
        def _():
            x_copy(p).wait_recv()
            d_load(p).start()

    def begin_e(p):
        @pl.when(depth < half - 1)
        def _():
            o_copy(p, xb).wait_recv()

            @pl.when(depth > 0)
            def _():
                o_copy(p, xb).start()

            in_copy(p).wait_send()
            e_load(p).start()

    def end_b(p):
        r1_copy(p).wait_recv()
        add_into(p, kb[p % RING])
        if half > 1:

            @pl.when(depth == 0)
            def _():
                in_copy(p).start()
        else:
            x_copy(p).start()

    def end_c(p):
        @pl.when(depth > 0)
        def _():
            c_load(p).wait()
            add_into(p, c_slot[...])

            @pl.when(depth < half - 1)
            def _():
                in_copy(p).start()

            @pl.when(at_middle)
            def _():
                x_copy(p).start()

    def end_d(p):
        @pl.when(at_middle)
        def _():
            d_load(p).wait()
            x_copy(p).wait_send()
            add_into(p, d_slot[...])

            @pl.when(depth > 0)
            def _():
                o_copy(p, r1).start()

    def end_e(p):
        @pl.when(depth < half - 1)
        def _():
            e_load(p).wait()

        step = owner_of(p)

        @pl.when(step == 0)
        def _():
            l_copy(p).start()
            g_copy(r1.at[p], spot(p, mine)).start()

        @pl.when(step > 0)
        def _():
            f_copy(p, step).start()

    def end_g(p):
        step = owner_of(p)

        @pl.when(step > 0)
        def _():
            f_copy(p, step).wait_recv()
            where = spot(p, flipped(mine, step, n_fsdp))
            g_copy(out.at[where, core], where).start()

    def run(stages, t):
        for lag, stage in stages:
            pl.when((t >= lag) & (t < total + lag))(functools.partial(stage, t - lag))

    def begin(t):
        run([(LAG_C, begin_c), (LAG_D, begin_d), (LAG_E, begin_e)], t)

    def end(t):
        run([(LAG_B, end_b), (LAG_C, end_c), (LAG_D, end_d), (LAG_E, end_e), (LAG_G, end_g)], t)

    def tiles(u, i, slot):
        unit = units[u]
        r, j = i // unit.col_blocks, i % unit.col_blocks
        if unit.by_owner:
            owner = flipped(mine, n_fsdp - 1 - r, n_fsdp)
            first = owner * 2 * piece_rows + core * piece_rows
            second = owner * 2 * piece_rows + (1 - core) * piece_rows
        else:
            first = core * unit.row_blocks * piece_rows + r * piece_rows
            second = (1 - core) * unit.row_blocks * piece_rows + r * piece_rows
        first = pl.ds(pl.multiple_of(first, piece_rows), piece_rows)
        second = pl.ds(pl.multiple_of(second, piece_rows), piece_rows)
        cols = pl.ds(pl.multiple_of(j * piece_cols, piece_cols), piece_cols)
        return [
            pltpu.make_async_copy(lefts[u].at[:, first], lm.at[slot], tile_sem.at[slot, 0]),
            pltpu.make_async_copy(lefts[u].at[:, second], lo.at[slot], tile_sem.at[slot, 1]),
            pltpu.make_async_copy(rights[u].at[:, cols], rh.at[slot], tile_sem.at[slot, 2]),
        ]


    first_pairs = (
        (grad_mlp.at[:, pl.ds(0, ff)], big.at[pl.ds(0, rows_all)]),
        (grad_mlp.at[:, pl.ds(ff, ff)], big.at[pl.ds(rows_all, rows_all)]),
        (middle, mid),
        (grad_result, gres),
        (tokens, tok),
        (w_output, wo),
    )

    def first_loads(which):
        return [pltpu.make_async_copy(*first_pairs[i], first_sem.at[i]) for i in which]

    def attn_load():
        return pltpu.make_async_copy(w_attn, big.at[pl.ds(0, width)], first_sem.at[6])

    def tile_of(j):
        return pl.ds(pl.multiple_of(j * tile, tile), tile)

    def wt_load(j):
        return pltpu.make_async_copy(w_mlp.at[tile_of(j)], wt.at[j % 2], wt_sem.at[j % 2])

    def p_copy(s, j):
        return remote_copy(
            pbuf.at[s - 1, :, tile_of(j)],
            land_a.at[s - 1, :, tile_of(j)],
            ps.at[s, j],
            pr.at[s, j],
            rep,
            flipped(mine, s, n_fsdp),
        )

    def q_copy(s):
        return remote_copy(
            pbuf.at[s - 1], land_b.at[s - 1], qs.at[s], qr.at[s], rep, flipped(mine, s, n_fsdp)
        )

    gather = GatherRows(n_fsdp, rep, mine, ga, grad_attn, (ag_s, ag_r, ag_l))

    def mlp_products(j):
        @pl.when(j == 0)
        def _():
            for copy in first_loads((0, 1)):
                copy.wait()

        wt_load(j).wait()

        @pl.when(j + 1 < TILES)
        def _():
            wt_load(j + 1).start()

        for s in (*others, 0):
            part = product_of(big[s * rows : (s + 1) * rows], wt[j % 2, :, :ff], 1, 1)
            part += product_of(
                big[rows_all + s * rows : rows_all + (s + 1) * rows], wt[j % 2, :, ff:], 1, 1
            )
            if s == 0:
                own[:, tile_of(j)] = part
            else:
                pbuf[s - 1, :, tile_of(j)] = in_bf16(part)
                p_copy(s, j).start()

    row_steps = rows // ROW_STEP

    def middle_back(part):
        if part == 0:
            middle_sums()

        def some_rows(r, carry):
            cut = pl.ds(pl.multiple_of(r * ROW_STEP, ROW_STEP), ROW_STEP)
            grad = own[cut]
            for s in others:
                grad += in_f32(land_a[s - 1, cut])
            back, gain_rows = norm_back(grad, mid[cut], gains[1:2])
            gain_out[1:2, :width] += jnp.sum(gain_rows, axis=0, keepdims=True)
            back = gres[cut] + back
            gres[cut] = back
            ga[cut] = in_bf16(back)
            return carry

        lax.fori_loop(part * row_steps // 2, (part + 1) * row_steps // 2, some_rows, 0)
        if part == 1:
            gather.start()
            for copy in block_loads(0):
                copy.start()

    def middle_sums():
        attn_load().start()
        for copy in first_loads((2, 3)):
            copy.wait()

        def wait_tiles(j, carry):
            for s in others:
                p_copy(s, j).wait()
            return carry

        lax.fori_loop(0, TILES, wait_tiles, 0)
        gain_out[...] = jnp.zeros_like(gain_out)

    def block_loads(s):
        cut = pl.ds(pl.multiple_of(s * rows, rows), rows)
        pairs = (
            (attn_raw, raw), (all_cos, cs), (all_sin, sn), (all_q, qb), (all_k, kvb), (all_v, vb)
        )
        copies = [
            pltpu.make_async_copy(src.at[cut], dst, block_sem.at[i])
            for i, (src, dst) in enumerate(pairs)
        ]
        return copies

    def grad_load(s):
        cut = pl.ds(pl.multiple_of(s * rows, rows), rows)
        return pltpu.make_async_copy(grad_attn.at[cut], gb, block_sem.at[6])

    def store(s):
        cut = pl.ds(pl.multiple_of(s * rows, rows), rows)
        return pltpu.make_async_copy(ob, grad_raw.at[cut], block_sem.at[7])

    def heads_back(s, heads):
        attend_back(
            heads_k,
            heads,
            block_mask(
                block_lengths(lengths_ref, deal_ref, rep * n_fsdp + flipped(mine, s, n_fsdp)), rows
            ),
            cs[...],
            sn[...],
            head_gains[0:1],
            head_gains[1:2],
            raw,
            qb,
            kvb,
            vb,
            gg,
            ob,
            head_gain_out,
        )

    early = heads_k // 2

    def block_first(s):
        @pl.when(s == 0)
        def _():
            first_loads((5,))[0].wait()
            gb[...] = ga[...]

        for k in others:

            @pl.when(s == k)
            def _(k=k):
                gather.arrive(k)

        @pl.when(s > 0)
        def _():
            copy = grad_load(s)
            copy.start()
            copy.wait()

        gg[...] = product_of(gb[...], wo[...], 1, 1)
        for copy in block_loads(s):
            copy.wait()
        heads_back(s, range(early))

    def block_second(s):
        heads_back(s, range(early, heads_k))
        store(s).start()

        @pl.when(s + 1 < n_fsdp)
        def _():
            for copy in block_loads(s + 1):
                copy.start()

    def block_third(s):
        store(s).wait()

        @pl.when(s == 0)
        def _():
            attn_load().wait()

        def one_tile(j, carry):
            part = product_of(ob[...], big[tile_of(j)], 1, 1)

            @pl.when(s == 0)
            def _():
                own[:, tile_of(j)] = part

            @pl.when(s > 0)
            def _():
                pbuf[s - 1, :, tile_of(j)] = in_bf16(part)

            return carry

        lax.fori_loop(0, TILES, one_tile, 0)

        @pl.when(s > 0)
        def _():
            q_copy(s).start()

    def tokens_back(part):
        if part == 0:
            gather.sent()
            first_loads((4,))[0].wait()
            for s in others:
                q_copy(s).wait()

        def some_rows(r, carry):
            cut = pl.ds(pl.multiple_of(r * ROW_STEP, ROW_STEP), ROW_STEP)
            grad = own[cut]
            for s in others:
                grad += in_f32(land_b[s - 1, cut])
            back, gain_rows = norm_back(grad, in_f32(tok[cut]), gains[0:1])
            gain_out[0:1, :width] += jnp.sum(gain_rows, axis=0, keepdims=True)
            tokens_grad[cut] = in_bf16(gres[cut] + back)
            return carry

        lax.fori_loop(part * row_steps // 2, (part + 1) * row_steps // 2, some_rows, 0)
        if part == 1:
            near_land[mine] = gain_out[...]
            for s in others:
                near_copy(s).start()


    def near_copy(s):
        return remote_copy(
            gain_out,
            near_land.at[mine],
            near_s.at[s],
            near_r.at[s],
            rep,
            flipped(mine, s, n_fsdp),
        )

    def line_copy(k, target, to_rep):
        return remote_copy(gain_out, target, line_s.at[k], line_r.at[k], to_rep, mine)

    def pair_copy():
        return line_copy(0, pair_land, sib)

    def gain_in():
        return line_copy(1, in_land, inward)

    def gain_across():
        return line_copy(2, far_land, inward)

    def gain_back():
        return line_copy(3, far_land, outward)

    def gains_near():
        for s in others:
            near_copy(s).wait()
        summed = near_land[0]
        for k in others:
            summed += near_land[k]
        gain_out[...] = summed
        pair_copy().start()

    def gains_pair():
        pair_copy().wait()
        gain_out[...] += pair_land[...]

        @pl.when(depth == 0)
        def _():
            (gain_in if half > 1 else gain_across)().start()

    def gains_in(k):
        @pl.when(depth == k)
        def _():
            gain_in().wait_recv()
            gain_out[...] += in_land[...]
            (gain_in if k < half - 1 else gain_across)().start()

    def gains_across():
        @pl.when(at_middle)
        def _():
            gain_across().wait()
            gain_out[...] += far_land[...]
            if half > 1:
                gain_back().start()

    def gains_back(k):
        @pl.when(depth == k)
        def _():
            gain_back().wait_recv()
            gain_in().wait_send()
            gain_out[...] = far_land[...]
            if k > 0:
                gain_back().start()

    def tasks(u, i):
        if u == 0:

            @pl.when(i == 1)
            def _():
                wt_load(0).start()
                for copy in first_loads((0, 1)):
                    copy.start()

            @pl.when(i == 6)
            def _():
                for copy in first_loads((2, 3, 4, 5)):
                    copy.start()

            pl.when((i >= 4) & (i < 4 + TILES))(lambda: mlp_products(i - 4))
        if u == 1:
            for part in range(2):
                pl.when(i == 7 + part)(functools.partial(middle_back, part))
            pl.when(i == 12)(gather.forward)
            pl.when(i == 15)(lambda: gather.own().wait())
            last = 15 + 3 * (n_fsdp - 1)
            busy = ((i >= 9) & (i < 12)) | ((i >= 15) & (i < last))
            s = at_least(i, 12, units[1].count) * ((i - 12) // 3)
            for phase, task in enumerate((block_first, block_second, block_third)):
                pl.when(busy & (i % 3 == phase))(functools.partial(task, s))
        if u == 3:
            for part in range(2):
                pl.when(i == 2 + part)(functools.partial(tokens_back, part))
            pl.when(i == 6)(gains_near)
            pl.when(i == 8)(gains_pair)

    def product(left, right):
        return product_of(left, right, 0, 0)

    for copy in tiles(0, 0, 0):
        copy.start()

    @pl.when(depth == 0)
    def _():
        pl.semaphore_wait(barrier, 1 + n_fsdp)

    @pl.when(depth > 0)
    def _():
        greet(outward, mine)
        pl.semaphore_wait(barrier, 2 + n_fsdp)

    for u, unit in enumerate(units):

        def step(i, carry, u=u, unit=unit):
            t = unit.base + i
            slot = t % 2
            begin(t)
            for copy in tiles(u, i, slot):
                copy.wait()

            @pl.when(i + 1 < unit.count)
            def _():
                for copy in tiles(u, i + 1, 1 - slot):
                    copy.start()

            if u + 1 < len(units):

                @pl.when(i + 1 == unit.count)
                def _():
                    for copy in tiles(u + 1, 0, 1 - slot):
                        copy.start()

            @pl.when(t >= RING)
            def _():
                r1_copy(t - RING).wait_send()

            sb[t % RING] = in_bf16(product(lo[slot], rh[slot]))
            r1_copy(t).start()
            kb[t % RING] = product(lm[slot], rh[slot])
            end(t)
            tasks(u, i)
            return carry

        lax.fori_loop(0, unit.count, step, 0)

    def drain(t, carry):
        begin(t)
        end(t)
        return carry

    lax.fori_loop(total, total + LAG_G, drain, 0)

    for p in range(total - RING, total):
        r1_copy(p).wait_send()
    kept = sum(u.col_blocks if u.by_owner else u.count for u in units)
    some, rest = pl.ds(0, kept), pl.ds(0, total - kept)
    every = remote_copy(r1, out.at[:, core], gs, gr, sib, mine)
    every.wait()
    pltpu.make_async_copy(r1.at[some], out.at[some, core], ls).wait()
    remote_copy(r1.at[rest], out.at[rest, core], fs, fr.at[0], sib, mine).wait_send()

    @pl.when(depth > 0)
    def _():
        remote_copy(r1, xb, os_, xr.at[0], outward, mine).wait_send()

    for k in range(1, half):
        gains_in(k)
    gains_across()
    for k in range(half - 2, -1, -1):
        gains_back(k)
    if half > 1:

        @pl.when(depth > 0)
        def _():
            gain_back().wait_send()


def backward(n_fsdp, n_rep, heads_k, units, piece_rows, piece_cols, args):
    total = sum(unit.count for unit in units)
    rows_all, rows = args[0].shape[0], args[9].shape[0]
    width, cols = args[8].shape
    cols_q, cols_k = heads_k * (H // KV) * HD, heads_k * HD
    two_ff = args[5].shape[1]
    dma = pltpu.SemaphoreType.DMA
    piece = (piece_rows, piece_cols)
    low, full = jnp.bfloat16, jnp.float32
    any_spec = pl.BlockSpec(memory_space=pl.ANY)
    vmem = pl.BlockSpec(memory_space=pltpu.VMEM)
    flops = sum(4 * unit.count for unit in units) * rows_all * piece_rows * piece_cols
    outs = (
        ((total, 2) + piece, low),
        ((rows_all, width), low),
        ((rows_all, cols), low),
        ((total,) + piece, low),
        ((total,) + piece, low),
        ((rows, width), low),
        ((8, width + HD), full),
    )
    scratch = (
        ((2, rows_all, piece_rows), low),
        ((2, rows_all, piece_rows), low),
        ((2, rows_all, piece_cols), low),
        ((RING,) + piece, low),
        ((RING,) + piece, full),
        ((total,) + piece, low),
        (piece, low),
        (piece, low),
        ((max(2 * rows_all, width), cols), low),
        ((2, width // TILES, two_ff), low),
        ((rows, width), full),
        ((n_fsdp - 1, rows, width), low),
        ((n_fsdp - 1, rows, width), low),
        ((n_fsdp - 1, rows, width), low),
        ((rows, width), full),
        ((rows, width), full),
        ((rows, width), low),
        ((rows, width), low),
        ((cols_q, width), low),
        ((rows, cols), full),
        ((rows, HD), full),
        ((rows, HD), full),
        ((rows, cols_q), low),
        ((rows, cols_k), low),
        ((rows, cols_k), low),
        ((rows, width), low),
        ((rows, cols_q), full),
        ((rows, cols), low),
    )
    return pl.pallas_call(
        functools.partial(
            backward_kernel, n_fsdp, n_rep, heads_k, units, piece_rows, piece_cols
        ),
        out_shape=[jax.ShapeDtypeStruct(shape, kind) for shape, kind in outs],
        in_specs=[any_spec] * 18 + [vmem] * 2 + [pl.BlockSpec(memory_space=pltpu.SMEM)] * 2,
        out_specs=[any_spec] * 5 + [vmem] * 2,
        scratch_shapes=[pltpu.VMEM(shape, kind) for shape, kind in scratch]
        + [dma((2, 3))]
        + [dma((total,)) for _ in range(6)]
        + [dma, dma, dma((total,)), dma, dma, dma]
        + [
            dma((3,)),
            dma((7,)),
            dma((2,)),
            dma((n_fsdp, TILES)),
            dma((n_fsdp, TILES)),
            dma((n_fsdp,)),
            dma((n_fsdp,)),
            dma((n_fsdp, 2)),
            dma((n_fsdp, 2)),
            dma,
            dma((8,)),
            pltpu.VMEM((n_fsdp, 8, width + HD), full),
            pltpu.VMEM((8, width + HD), full),
            pltpu.VMEM((8, width + HD), full),
            pltpu.VMEM((8, width + HD), full),
            dma((n_fsdp,)),
            dma((n_fsdp,)),
            dma((4,)),
            dma((4,)),
        ],
        compiler_params=pltpu.CompilerParams(
            collective_id=0, has_side_effects=True, vmem_limit_bytes=62 << 20
        ),
        cost_estimate=pl.CostEstimate(flops=2 * flops, bytes_accessed=1 << 30, transcendentals=0),
        name="backward",
    )(*args)


def widen_kernel(in_ref, out_ref):
    cols = in_ref.shape[-1]
    for i in range(in_ref.shape[0]):
        out_ref[:, i * cols : (i + 1) * cols] = in_ref[i, 0].astype(jnp.float32)


def widened(pieces, grid, together, where, shape, place):
    rows, cols = pieces.shape[2:]
    return pl.pallas_call(
        widen_kernel,
        grid=grid,
        out_shape=jax.ShapeDtypeStruct(shape, jnp.float32),
        in_specs=[pl.BlockSpec((together, 1, rows, cols), where)],
        out_specs=pl.BlockSpec((rows, together * cols), place),
        name="widen",
    )(pieces)


def widen_both_kernel(in_ref, first_ref, second_ref):
    cols, count = in_ref.shape[-1], in_ref.shape[0] // 2
    for i in range(count):
        first_ref[:, i * cols : (i + 1) * cols] = in_f32(in_ref[i, 0])
        second_ref[:, i * cols : (i + 1) * cols] = in_f32(in_ref[count + i, 0])


def widened_both(pieces, base, together, n_fsdp, shape):
    rows, cols = pieces.shape[2:]
    return pl.pallas_call(
        widen_both_kernel,
        grid=(2, n_fsdp),
        out_shape=[jax.ShapeDtypeStruct(shape, jnp.float32)] * 2,
        in_specs=[
            pl.BlockSpec((together, 1, rows, cols), lambda c, f: (base // together + f, c, 0, 0))
        ],
        out_specs=[pl.BlockSpec((rows, together // 2 * cols), lambda c, f: (c, f))] * 2,
        compiler_params=pltpu.CompilerParams(vmem_limit_bytes=32 << 20),
        name="widen_both",
    )(pieces)


def widen_heads_kernel(query_in, gate_in, pair_in, query_out, gate_out, key_out, value_out):
    half = key_out.shape[1]
    query_out[...] = query_in[0, 0].astype(jnp.float32)
    gate_out[...] = gate_in[0, 0].astype(jnp.float32)
    key_out[...] = pair_in[0, 0, :, :half].astype(jnp.float32)
    value_out[...] = pair_in[0, 0, :, half:].astype(jnp.float32)


def widened_heads(pieces, base, n_fsdp, shapes):
    rows, cols = pieces.shape[2:]

    def where(j):
        return lambda c, f: (base + 3 * f + j, c, 0, 0)

    widths = (cols, cols, cols // 2, cols // 2)
    return pl.pallas_call(
        widen_heads_kernel,
        grid=(2, n_fsdp),
        out_shape=[jax.ShapeDtypeStruct(shape, jnp.float32) for shape in shapes],
        in_specs=[pl.BlockSpec((1, 1, rows, cols), where(j)) for j in range(3)],
        out_specs=[pl.BlockSpec((rows, wide), lambda c, f: (c, f)) for wide in widths],
        name="widen_heads",
    )(pieces, pieces, pieces)


def block_lengths(lengths_ref, deal_ref, device):
    head_len = lengths_ref[deal_ref[2 * device]]
    return head_len, head_len + lengths_ref[deal_ref[2 * device + 1]]


def block_mask(block, rows):
    head_len, both_len = block
    query_row = lax.broadcasted_iota(jnp.int32, (rows, rows), 0)
    key_row = lax.broadcasted_iota(jnp.int32, (rows, rows), 1)

    def segment(index):
        return (index >= head_len).astype(jnp.int32) + (index >= both_len).astype(jnp.int32)

    return (segment(query_row) == segment(key_row)) & (key_row <= query_row)


def turn(values):
    half_dim = values.shape[-1] // 2
    return jnp.concatenate([-values[:, half_dim:], values[:, :half_dim]], axis=-1)


def head_forward(raw, gain, angle_cos, angle_sin):
    values = raw * lax.rsqrt(jnp.mean(raw * raw, axis=-1, keepdims=True) + EPS_NORM) * gain
    return in_bf16(values * angle_cos + turn(values) * angle_sin)


def head_backward(grad, raw, gain, angle_cos, angle_sin):
    grad = grad * angle_cos - turn(grad * angle_sin)
    scale = lax.rsqrt(jnp.mean(raw * raw, axis=-1, keepdims=True) + EPS_NORM)
    unit = raw * scale
    gain_rows = grad * unit
    inner = grad * gain
    return scale * (inner - unit * jnp.mean(inner * unit, axis=-1, keepdims=True)), gain_rows


def product_of(left, right, left_dim, right_dim):
    return lax.dot_general(
        left, right, (((left_dim,), (right_dim,)), ((), ())), preferred_element_type=jnp.float32
    )


def softmax_of(queries, keys, allowed):
    scores = jnp.where(allowed, product_of(queries, keys, 1, 1) * HD ** (-0.5), NEG_FILL)
    exponent = jnp.exp(scores - jnp.max(scores, axis=-1, keepdims=True))
    return exponent / jnp.sum(exponent, axis=-1, keepdims=True)


def attend(
    heads_k,
    allowed,
    angle_cos,
    angle_sin,
    query_gain,
    key_gain,
    raw_ref,
    q_ref,
    k_ref,
    v_ref,
    gated_ref,
):
    group = H // KV
    cols_q, cols_k = heads_k * group * HD, heads_k * HD
    for j in range(heads_k):
        own = slice(j * HD, (j + 1) * HD)
        keys = head_forward(
            raw_ref[:, 2 * cols_q + j * HD : 2 * cols_q + (j + 1) * HD],
            key_gain,
            angle_cos,
            angle_sin,
        )
        start = 2 * cols_q + cols_k + j * HD
        values = in_bf16(raw_ref[:, start : start + HD])
        k_ref[:, own] = keys
        v_ref[:, own] = values
        for h in range(j * group, (j + 1) * group):
            cut = slice(h * HD, (h + 1) * HD)
            queries = head_forward(raw_ref[:, cut], query_gain, angle_cos, angle_sin)
            q_ref[:, cut] = queries
            probs = in_bf16(softmax_of(queries, keys, allowed))
            context = product_of(probs, values, 1, 0)
            gate = raw_ref[:, cols_q + h * HD : cols_q + (h + 1) * HD]
            gated_ref[:, cut] = in_bf16(context * jax.nn.sigmoid(gate))


def attend_back(
    heads_k,
    heads,
    allowed,
    angle_cos,
    angle_sin,
    query_gain,
    key_gain,
    raw_ref,
    q_ref,
    k_ref,
    v_ref,
    grad_ref,
    out_ref,
    gain_ref,
):
    group = H // KV
    cols_q, cols_k = heads_k * group * HD, heads_k * HD
    for j in heads:
        own = slice(j * HD, (j + 1) * HD)
        keys, values = k_ref[:, own], v_ref[:, own]
        grad_keys, grad_values = 0.0, 0.0
        for h in range(j * group, (j + 1) * group):
            cut = slice(h * HD, (h + 1) * HD)
            gate_cut = slice(cols_q + h * HD, cols_q + (h + 1) * HD)
            queries, grad_gated = q_ref[:, cut], grad_ref[:, cut]
            probs = softmax_of(queries, keys, allowed)
            probs_b = in_bf16(probs)
            context = product_of(probs_b, values, 1, 0)
            gate = jax.nn.sigmoid(raw_ref[:, gate_cut])
            grad_context = in_bf16(grad_gated * gate)
            out_ref[:, gate_cut] = in_bf16(grad_gated * context * gate * (1.0 - gate))
            grad_probs = product_of(grad_context, values, 1, 1)
            grad_scores = in_bf16(
                probs * (grad_probs - jnp.sum(probs * grad_probs, axis=-1, keepdims=True))
            )
            grad_values += product_of(probs_b, grad_context, 0, 0)
            grad_keys += product_of(grad_scores, queries, 0, 0)
            grad_queries = product_of(grad_scores, keys, 1, 0) * HD ** (-0.5)
            grad_raw, gain_rows = head_backward(
                grad_queries, raw_ref[:, cut], query_gain, angle_cos, angle_sin
            )
            out_ref[:, cut] = in_bf16(grad_raw)
            gain_ref[0:1, :] += jnp.sum(gain_rows, axis=0, keepdims=True)
        key_start = 2 * cols_q + j * HD
        grad_raw, gain_rows = head_backward(
            grad_keys * HD ** (-0.5),
            raw_ref[:, key_start : key_start + HD],
            key_gain,
            angle_cos,
            angle_sin,
        )
        out_ref[:, key_start : key_start + HD] = in_bf16(grad_raw)
        gain_ref[1:2, :] += jnp.sum(gain_rows, axis=0, keepdims=True)
        value_start = 2 * cols_q + cols_k + j * HD
        out_ref[:, value_start : value_start + HD] = in_bf16(grad_values)


def remote_copy(src, dst, send, recv, to_rep, to_fsdp):
    return pltpu.make_async_remote_copy(
        src_ref=src,
        dst_ref=dst,
        send_sem=send,
        recv_sem=recv,
        device_id={"rep": to_rep, "fsdp": to_fsdp},
        device_id_type=MESH,
    )


def greet_all(peers):
    barrier = pltpu.get_barrier_semaphore()
    for to_rep, to_fsdp in peers:
        pl.semaphore_signal(
            barrier, inc=1, device_id={"rep": to_rep, "fsdp": to_fsdp}, device_id_type=MESH
        )
    pl.semaphore_wait(barrier, len(peers))


class GatherRows:
    def __init__(self, n_fsdp, rep, mine, source, target, sems):
        self.n_fsdp, self.rep, self.mine = n_fsdp, rep, mine
        self.source, self.target = source, target
        self.send, self.recv, self.local = sems
        self.rows = source.shape[0]
        self.half = self.rows // 2
        self.relay = ((1, 0), (2, 1)) if n_fsdp == 4 else ()

    def copy(self, s, h, to=None, src=None):
        to = s if to is None else to
        return remote_copy(
            self.source.at[pl.ds(h * self.half, self.half)]
            if src is None
            else self.target.at[pl.ds(src * self.rows + h * self.half, self.half)],
            self.target.at[pl.ds(s * self.rows + h * self.half, self.half)],
            self.send.at[s, h],
            self.recv.at[s, h],
            self.rep,
            flipped(self.mine, to, self.n_fsdp),
        )

    def own(self):
        return pltpu.make_async_copy(
            self.source, self.target.at[pl.ds(0, self.rows)], self.local
        )

    def start(self):
        for s, h in ((1, 0), (2, 1), (1, 1), (2, 0)):
            if s < self.n_fsdp:
                self.copy(s, h).start()
        if self.n_fsdp != 4:
            for s in range(3, self.n_fsdp):
                for h in range(2):
                    self.copy(s, h).start()
        self.own().start()

    def forward(self):
        if self.n_fsdp == 4:
            self.copy(1, 0).wait_recv()
            self.copy(3, 0, to=2, src=1).start()
            self.copy(2, 1).wait_recv()
            self.copy(3, 1, to=1, src=2).start()

    def arrive(self, s):
        for h in range(2):
            if (s, h) not in self.relay:
                self.copy(s, h).wait_recv()

    def sent(self):
        for s in range(1, self.n_fsdp):
            for h in range(2):
                self.copy(s, h).wait_send()

    def finish(self):
        for s in range(1, self.n_fsdp):
            self.arrive(s)
        self.sent()
        self.own().wait()


def forward_kernel(n_fsdp, n_rep, heads_k, *refs):
    (tokens, gains, wq, wg, wk, wv, w_gate, w_up, w_output, w_down, teacher) = refs[:11]
    (lengths_ref, deal_ref, lengths_row, freq_ref) = refs[11:15]
    (normed_all, raw_all, q_all, k_all, v_all, gated_all, w_attn, w_mlp) = refs[15:23]
    (middle_out, nmlp_all, hidden_all, gbranch_all, gmlp_all, gres_out, block_out) = refs[23:30]
    (gu_all, all_cos, all_sin, gain_out, head_gain_out, loss_out) = refs[30:36]
    (tok, gl, wa, wo, wd, wm, nb, raw, cs, sn, qb, kvb, vb, gb, own, pbuf, land) = refs[36:53]
    (mid, nm, te, gu, hb, gm) = refs[53:59]
    (ts, tr, tl, us, ur, ul, bs, br, bl, gain_s, gain_r, ws, wr, zs, zr, cps, cpr) = refs[59:76]
    (ms, mr, hs, hr, ss, sr, ps, pr, qs, qr, load, keep, mine_sem) = refs[76:]
    rows, width = own.shape
    rows_all = n_fsdp * rows
    cols, ff = raw.shape[1], hb.shape[1]
    deep = wq.shape[0]
    widths = tuple(w.shape[1] // n_fsdp for w in (wq, wg, wk, wv))
    starts = [sum(widths[:i]) for i in range(4)]
    others = range(1, n_fsdp)
    n_line = n_rep // 2
    rep, mine = lax.axis_index("rep"), lax.axis_index("fsdp")
    core, place = rep % 2, rep // 2
    sib = rep + 1 - 2 * core
    partner = (place + 1 - 2 * (place % 2)) * 2 + core
    block, part = deep // 4, deep // n_rep
    band = (place % 2) * 2 + core
    other_band = (1 - place % 2) * 2 + core
    hops = range(1, n_line)
    row_steps = rows // ROW_STEP
    near = sorted({1, n_line - 1})
    greet_all(
        [(sib, mine)]
        + [(((place + k) % n_line) * 2 + core, mine) for k in near]
        + [(rep, flipped(mine, s, n_fsdp)) for s in others]
    )


    def columns(peer, wide):
        return pl.ds(pl.multiple_of(peer * wide, wide), wide)

    def mlp_copy(s, i):
        peer = flipped(mine, s, n_fsdp)
        return remote_copy(
            (w_gate, w_up)[i].at[pl.ds(rep * part, part), columns(peer, ff)],
            w_mlp.at[pl.ds(mine * deep + rep * part, part), pl.ds(i * ff, ff)],
            ms.at[s, i],
            mr.at[s, i],
            rep,
            peer,
        )

    def part_at(s, of_rep):
        return w_mlp.at[pl.ds(flipped(mine, s, n_fsdp) * deep + of_rep * part, part)]

    def line_copy(s, k, up):
        step = 1 if up else -1
        src = part_at(s, ((place - step * (k - 1) + n_line) % n_line) * 2 + core)
        to_rep = ((place + step + n_line) % n_line) * 2 + core
        way = 0 if up else 1
        return remote_copy(src, src, hs.at[way, s, k], hr.at[way, s, k], to_rep, mine)

    def line_sends(k):
        for up in (True, False):
            first, last = (k - 1, n_line - 2) if up else (1, n_line - k)

            @pl.when((place >= first) & (place <= last))
            def _(up=up):
                for s in others:
                    line_copy(s, k, up).start()

    def line_arrivals(k):
        for up in (True, False):
            first, last = (k, n_line - 1) if up else (0, n_line - 1 - k)

            @pl.when((place >= first) & (place <= last))
            def _(up=up):
                for s in others:
                    line_copy(s, k, up).wait_recv()
                    share_copy(s, k, up).start()

        if k + 1 < n_line:
            line_sends(k + 1)

    def share_copy(s, k, up):
        step = 1 if up else -1
        src = part_at(s, ((place - step * k + n_line) % n_line) * 2 + core)
        way = 0 if up else 1
        return remote_copy(src, src, ss.at[way, s, k], sr.at[way, s, k], sib, mine)

    def shares(action):
        for s in others:
            action(share_copy(s, 0, True))
        for k in hops:
            for up in (True, False):
                first, last = (k, n_line - 1) if up else (0, n_line - 1 - k)

                @pl.when((place >= first) & (place <= last))
                def _(k=k, up=up):
                    for s in others:
                        action(share_copy(s, k, up))

    def lines_sent():
        for k in hops:
            for up in (True, False):
                first, last = (k - 1, n_line - 2) if up else (1, n_line - k)

                @pl.when((place >= first) & (place <= last))
                def _(k=k, up=up):
                    for s in others:
                        line_copy(s, k, up).wait_send()

    weights = (wq, wg, wk, wv)

    def weight_copy(s, i):
        peer = flipped(mine, s, n_fsdp)
        return remote_copy(
            weights[i].at[pl.ds(band * block, block), columns(peer, widths[i])],
            w_attn.at[pl.ds(mine * deep + band * block, block), pl.ds(starts[i], widths[i])],
            ws.at[s, i],
            wr.at[s, i],
            rep,
            peer,
        )

    def band_at(s, which):
        return w_attn.at[pl.ds(flipped(mine, s, n_fsdp) * deep + which * block, block)]

    def partner_copy(s):
        return remote_copy(band_at(s, band), band_at(s, band), zs.at[s], zr.at[s], partner, mine)

    def sibling_copy(s, k):
        which = band if k == 0 else other_band
        return remote_copy(
            band_at(s, which), band_at(s, which), cps.at[s, k], cpr.at[s, k], sib, mine
        )

    def gain_copy(s):
        return remote_copy(
            gains, gl.at[mine], gain_s.at[s], gain_r.at[s], rep, flipped(mine, s, n_fsdp)
        )

    mine_rows = pl.ds(mine * deep, deep)
    mine_pairs = [
        (weights[i].at[:, columns(mine, widths[i])], w_attn.at[mine_rows, pl.ds(starts[i], widths[i])])
        for i in range(4)
    ]
    mine_pairs += [
        (w.at[:, columns(mine, ff)], w_mlp.at[mine_rows, pl.ds(i * ff, ff)])
        for i, w in enumerate((w_gate, w_up))
    ]
    mine_pairs += [(gains, gl.at[mine]), (w_output, wo), (w_down, wd), (teacher, te)]

    def local(which):
        return [pltpu.make_async_copy(*mine_pairs[i], mine_sem.at[i]) for i in which]

    def attn_load():
        return pltpu.make_async_copy(w_attn, wa, load.at[0])

    def mlp_load():
        return pltpu.make_async_copy(w_mlp, wm, load.at[1])

    token_rows = GatherRows(n_fsdp, rep, mine, tokens, tok, (ts, tr, tl))
    up_rows = GatherRows(n_fsdp, rep, mine, nm, nmlp_all, (us, ur, ul))
    back_rows = GatherRows(n_fsdp, rep, mine, nm, gbranch_all, (bs, br, bl))

    for s in others:
        gain_copy(s).start()
        for i in range(4):
            weight_copy(s, i).start()
    for copy in local(range(10)):
        copy.start()
    for s in others:
        for i in range(4):
            weight_copy(s, i).wait_recv()
        partner_copy(s).start()
        sibling_copy(s, 0).start()
    for s in others:
        for i in range(2):
            mlp_copy(s, i).start()

    def block_rows(s):
        return pl.ds(pl.multiple_of(s * rows, rows), rows)

    def lengths_of(s):
        return block_lengths(lengths_ref, deal_ref, rep * n_fsdp + flipped(mine, s, n_fsdp))

    def angles(s, carry):
        head_len, both_len = lengths_of(s)
        index = lax.broadcasted_iota(jnp.int32, (rows, HD), 0)
        start = jnp.where(index < head_len, 0, jnp.where(index < both_len, head_len, both_len))
        angle = (index - start).astype(jnp.float32) * freq_ref[...]
        cs[block_rows(s)] = jnp.cos(angle)
        sn[block_rows(s)] = jnp.sin(angle)
        return carry

    lax.fori_loop(0, n_fsdp, angles, 0)
    angle_stores = [
        pltpu.make_async_copy(cs, all_cos, load.at[2]),
        pltpu.make_async_copy(sn, all_sin, load.at[3]),
    ]
    for copy in angle_stores:
        copy.start()
    token_count = jnp.sum(in_f32(lengths_row[...]), axis=1, keepdims=True)
    local((6,))[0].wait()
    gain_out[...] = jnp.zeros_like(gain_out)
    head_gain_out[...] = jnp.zeros_like(head_gain_out)
    for s in others:
        gain_copy(s).wait()
    lines = deep // HD
    for f in range(n_fsdp):
        piece = in_f32(gl[f])
        for kind in range(2):
            for r in range(lines):
                at = f * deep + r * HD
                gain_out[kind : kind + 1, at : at + HD] = piece[
                    kind * lines + r : kind * lines + r + 1
                ]
            head_gain_out[kind : kind + 1] += piece[2 * lines + kind : 2 * lines + kind + 1]
    for s in others:
        for i in range(2):
            mlp_copy(s, i).wait_recv()
        share_copy(s, 0, True).start()
    token_rows.start()
    for s in others:
        partner_copy(s).wait_recv()
        sibling_copy(s, 1).start()
    line_sends(1)
    for s in others:
        for k in range(2):
            sibling_copy(s, k).wait_recv()
    for copy in local((0, 1, 2, 3)):
        copy.wait()
    attn_load().start()
    for copy in local((7, 8, 9)):
        copy.wait()

    def some_rows(base, r):
        return pl.ds(pl.multiple_of(base + r * ROW_STEP, ROW_STEP), ROW_STEP)

    def tiled(count, wide, body):
        def one(j, carry):
            body(pl.ds(pl.multiple_of(j * wide, wide), wide))
            return carry

        lax.fori_loop(0, count, one, 0)

    def by_rows(body):
        def one(r, carry):
            body(r)
            return carry

        lax.fori_loop(0, row_steps, one, 0)

    tile = width // 4

    def leave(s, left, right):
        def one(cut):
            product = product_of(left[...], right[:, cut], 1, 0)

            @pl.when(s == 0)
            def _():
                own[:, cut] = product

            @pl.when(s > 0)
            def _():
                pbuf[s - 1, :, cut] = in_bf16(product)

        tiled(4, tile, one)


    relayed = n_fsdp == 4

    def half_rows(h):
        return pl.ds(h * (rows // 2), rows // 2)

    def out_copy(s, h, sends, recvs):
        to, at = s, s - 1
        if relayed and s == 3:
            to, at = h + 1, 2
        return remote_copy(
            pbuf.at[s - 1, half_rows(h)],
            land.at[at, half_rows(h)],
            sends.at[s, h],
            recvs.at[s, h],
            rep,
            flipped(mine, to, n_fsdp),
        )

    def send_block(s, sends, recvs):
        for k in others:

            @pl.when(s == k)
            def _(k=k):
                for h in range(2):
                    if not relayed or (k, h) not in ((1, 1), (2, 0)):
                        out_copy(k, h, sends, recvs).start()

    def relay(sends, recvs):
        if relayed:
            for h, near in ((0, 2), (1, 1)):
                out_copy(3, h, sends, recvs).wait_recv()
                cut = half_rows(h)
                pbuf[near - 1, cut] = in_bf16(in_f32(pbuf[near - 1, cut]) + in_f32(land[2, cut]))
                out_copy(near, h, sends, recvs).start()

    def arrived(sends, recvs):
        for s in others:
            for h in range(2):
                if not (relayed and s == 3):
                    out_copy(s, h, sends, recvs).wait_recv()
                out_copy(s, h, sends, recvs).wait_send()

    def summed(cut):
        total = own[cut]
        for s in range(1, 3 if relayed else n_fsdp):
            total += in_f32(land[s - 1, cut])
        return total

    def scaled(values, gain):
        scale = lax.rsqrt(jnp.mean(values * values, axis=-1, keepdims=True) + EPS_NORM)
        return in_bf16(values * scale * gain)


    def attention_stores(s):
        cut = block_rows(s)
        pairs = (
            (nb, normed_all), (raw, raw_all), (qb, q_all), (kvb, k_all), (vb, v_all), (gb, gated_all)
        )
        return [
            pltpu.make_async_copy(src, dst.at[cut], keep.at[i])
            for i, (src, dst) in enumerate(pairs)
        ]

    def attention(s, carry):
        pl.when(s == 1)(token_rows.forward)
        for k in range(n_fsdp):

            @pl.when(s == k)
            def _(k=k):
                if k == 0:
                    token_rows.own().wait()
                else:
                    token_rows.arrive(k)

        @pl.when(s > 0)
        def _():
            for copy in attention_stores(s):
                copy.wait()

        def normed_rows(r):
            values = in_f32(tok[some_rows(s * rows, r)])
            nb[some_rows(0, r)] = scaled(values, gain_out[0:1])

        by_rows(normed_rows)

        @pl.when(s == 0)
        def _():
            attn_load().wait()

        def raw_tile(cut):
            raw[:, cut] = product_of(nb[...], wa[:, cut], 1, 0)

        tiled(3, cols // 3, raw_tile)
        attend(
            heads_k,
            block_mask(lengths_of(s), rows),
            cs[block_rows(s)],
            sn[block_rows(s)],
            head_gain_out[0:1],
            head_gain_out[1:2],
            raw,
            qb,
            kvb,
            vb,
            gb,
        )
        for copy in attention_stores(s):
            copy.start()
        leave(s, gb, wo)

        send_block(s, ps, pr)
        if n_line > 2:
            pl.when(s == n_fsdp - 2)(lambda: line_arrivals(1))
        return carry

    lax.fori_loop(0, n_fsdp, attention, 0)
    for copy in angle_stores:
        copy.wait()
    relay(ps, pr)
    for k in range(2, n_line - 1):
        line_arrivals(k)
    arrived(ps, pr)

    def middle_rows(r):
        cut = some_rows(0, r)
        values = in_f32(tok[cut]) + summed(cut)
        mid[cut] = values
        nm[cut] = scaled(values, gain_out[1:2])

    by_rows(middle_rows)
    up_rows.start()

    def middle_store():
        return pltpu.make_async_copy(mid, middle_out, load.at[4])

    middle_store().start()
    for copy in attention_stores(0):
        copy.wait()


    line_arrivals(n_line - 1)
    shares(lambda copy: copy.wait_recv())
    for copy in local((4, 5)):
        copy.wait()
    mlp_load().start()
    mlp_load().wait()

    def block_load(source, s):
        return pltpu.make_async_copy(source.at[block_rows(s)], nb, load.at[2])

    def ff_stores(s):
        cut = block_rows(s)
        return [
            pltpu.make_async_copy(hb, hidden_all.at[cut], keep.at[0]),
            pltpu.make_async_copy(gu, gu_all.at[cut], keep.at[1]),
        ]

    def into_nb(gather, source, s):
        @pl.when(s == 0)
        def _():
            nb[...] = nm[...]

        for k in others:

            @pl.when(s == k)
            def _(k=k):
                gather.arrive(k)

        @pl.when(s > 0)
        def _():
            copy = block_load(source, s)
            copy.start()
            copy.wait()

    def feed_forward(i, carry):
        s = (i + 1) % n_fsdp
        pl.when(i == 0)(up_rows.forward)
        into_nb(up_rows, nmlp_all, s)

        @pl.when(i > 0)
        def _():
            for copy in ff_stores(s):
                copy.wait()

        def pre_tile(cut):
            gu[:, cut] = product_of(nb[...], wm[:, cut], 1, 0)

        tiled(6, ff // 3, pre_tile)

        def hidden_rows(r):
            cut = some_rows(0, r)
            gate_pre = gu[cut, :ff]
            hb[cut] = in_bf16(gate_pre * jax.nn.sigmoid(gate_pre) * gu[cut, ff:])

        by_rows(hidden_rows)
        for copy in ff_stores(s):
            copy.start()
        leave(s, hb, wd)

        send_block(s, qs, qr)
        return carry

    lax.fori_loop(0, n_fsdp, feed_forward, 0)
    relay(qs, qr)
    up_rows.sent()
    up_rows.own().wait()
    middle_store().wait()
    for copy in ff_stores(0):
        copy.wait()


    def gu_load(s):
        return pltpu.make_async_copy(gu_all.at[block_rows(s)], gu, load.at[5])

    gu_load(0).start()
    arrived(qs, qr)
    head_len, both_len = lengths_of(0)
    factor = (n_rep * rows_all) / token_count
    loss_out[...] = jnp.zeros_like(loss_out)

    def error_rows(r):
        cut = some_rows(0, r)
        index = r * ROW_STEP + lax.broadcasted_iota(jnp.int32, (ROW_STEP, 1), 0)
        valid = (index < both_len).astype(jnp.float32)
        result = mid[cut] + summed(cut)
        error = (result - in_f32(te[cut])) * valid
        square = jnp.sum(error * error, axis=-1, keepdims=True)
        first = jnp.where(index < head_len, square, 0.0)
        loss_out[0:1] += jnp.sum(first, axis=0, keepdims=True)
        loss_out[1:2] += jnp.sum(square - first, axis=0, keepdims=True)
        te[cut] = in_bf16(result * valid)
        grad = error * factor
        mid[cut] = grad
        nm[cut] = in_bf16(grad)

    by_rows(error_rows)
    loss_out[...] = loss_out[...] / (2.0 * token_count)
    back_rows.start()
    last_stores = [
        pltpu.make_async_copy(te, block_out, load.at[3]),
        pltpu.make_async_copy(mid, gres_out, load.at[4]),
    ]
    for copy in last_stores:
        copy.start()

    def grad_store(s):
        return pltpu.make_async_copy(gm, gmlp_all.at[block_rows(s)], keep.at[2])

    def feed_back(s, carry):
        pl.when(s == 1)(back_rows.forward)
        into_nb(back_rows, gbranch_all, s)

        def hidden_tile(cut):
            raw[:, cut] = product_of(nb[...], wd[cut], 1, 1)

        tiled(3, ff // 3, hidden_tile)
        gu_load(s).wait()

        @pl.when(s > 0)
        def _():
            grad_store(s).wait()

        def grad_rows(r):
            cut = some_rows(0, r)
            gate_pre, grad = gu[cut, :ff], raw[cut]
            gate = jax.nn.sigmoid(gate_pre)
            silu = gate_pre * gate
            gm[cut, :ff] = in_bf16(grad * gu[cut, ff:] * (gate + silu * (1.0 - gate)))
            gm[cut, ff:] = in_bf16(grad * silu)

        by_rows(grad_rows)
        grad_store(s).start()

        @pl.when(s + 1 < n_fsdp)
        def _():
            gu_load(s + 1).start()

        return carry

    lax.fori_loop(0, n_fsdp, feed_back, 0)

    grad_store(0).wait()
    for copy in last_stores:
        copy.wait()
    back_rows.sent()
    back_rows.own().wait()
    token_rows.sent()
    for s in others:
        partner_copy(s).wait_send()
        for i in range(4):
            weight_copy(s, i).wait_send()
        for i in range(2):
            sibling_copy(s, i).wait_send()
            mlp_copy(s, i).wait_send()
    lines_sent()
    shares(lambda copy: copy.wait_send())


def forward(n_fsdp, n_rep, heads_k, args):
    rows, width = args[0].shape
    rows_all = n_fsdp * rows
    cols_q, cols_k = heads_k * (H // KV) * HD, heads_k * HD
    cols = 2 * cols_q + 2 * cols_k
    ff = args[9].shape[0]
    n_line = n_rep // 2
    low, full = jnp.bfloat16, jnp.float32
    dma = pltpu.SemaphoreType.DMA
    any_spec = pl.BlockSpec(memory_space=pl.ANY)
    vmem, smem = pl.BlockSpec(memory_space=pltpu.VMEM), pl.BlockSpec(memory_space=pltpu.SMEM)
    outs = (
        ((rows_all, width), low),
        ((rows_all, cols), full),
        ((rows_all, cols_q), low),
        ((rows_all, cols_k), low),
        ((rows_all, cols_k), low),
        ((rows_all, cols_q), low),
        ((width, cols), low),
        ((width, 2 * ff), low),
        ((rows, width), full),
        ((rows_all, width), low),
        ((rows_all, ff), low),
        ((rows_all, width), low),
        ((rows_all, 2 * ff), low),
        ((rows, width), full),
        ((rows, width), low),
        ((rows_all, 2 * ff), full),
        ((rows_all, HD), full),
        ((rows_all, HD), full),
        ((8, width), full),
        ((8, HD), full),
        ((8, HD), full),
    )
    scratch = (
        ((rows_all, width), low),
        ((n_fsdp, 16, HD), low),
        ((width, cols), low),
        ((cols_q, width), low),
        ((ff, width), low),
        ((width, 2 * ff), low),
        ((rows, width), low),
        ((rows, cols), full),
        ((rows_all, HD), full),
        ((rows_all, HD), full),
        ((rows, cols_q), low),
        ((rows, cols_k), low),
        ((rows, cols_k), low),
        ((rows, cols_q), low),
        ((rows, width), full),
        ((n_fsdp - 1, rows, width), low),
        ((n_fsdp - 1, rows, width), low),
        ((rows, width), full),
        ((rows, width), low),
        ((rows, width), low),
        ((rows, 2 * ff), full),
        ((rows, ff), low),
        ((rows, 2 * ff), low),
    )
    one, pair, four = dma((n_fsdp,)), dma((n_fsdp, 2)), dma((n_fsdp, 4))
    line = dma((2, n_fsdp, n_line))
    return pl.pallas_call(
        functools.partial(forward_kernel, n_fsdp, n_rep, heads_k),
        out_shape=[jax.ShapeDtypeStruct(shape, kind) for shape, kind in outs],
        in_specs=[any_spec] * 11 + [smem] * 2 + [vmem] * 2,
        out_specs=[any_spec] * 18 + [vmem] * 3,
        scratch_shapes=[pltpu.VMEM(shape, kind) for shape, kind in scratch]
        + [pair, pair, dma] * 3
        + [one, one, four, four, one, one, pair, pair]
        + [pair, pair, line, line, line, line, pair, pair, pair, pair]
        + [dma((6,)), dma((6,)), dma((10,))],
        compiler_params=pltpu.CompilerParams(
            collective_id=1, has_side_effects=True, vmem_limit_bytes=62 << 20
        ),
        name="forward",
    )(*args)


def shards(
    tokens,
    teacher,
    lengths,
    deal_order,
    attention_gain,
    query_gain,
    key_gain,
    w_query,
    w_key,
    w_value,
    w_outgate,
    w_output,
    mlp_gain,
    w_gate,
    w_up,
    w_down,
):
    n_rep = lax.axis_size("rep")
    n_fsdp = lax.axis_size("fsdp")
    rows, width = tokens.shape
    mine = lax.axis_index("fsdp")
    core = lax.axis_index("rep") % 2
    others = range(1, n_fsdp)
    heads_q, heads_k = H // n_fsdp, KV // n_fsdp
    cols_q, cols_k = heads_q * HD, heads_k * HD
    deep = w_query.shape[0]
    ff = w_down.shape[0]
    rows_all = rows * n_fsdp

    freq = np.power(np.float32(ROPE_BASE), -np.arange(0, HD, 2, dtype=np.float32) / HD)
    freq = jnp.asarray(np.concatenate([freq, freq])[None])
    small = query_gain.shape[0]

    def spread(gain):
        lane = jnp.arange(HD, dtype=jnp.int32)
        return jnp.where(lane // small == mine, jnp.tile(gain, n_fsdp), 0)[None]

    gain_block = jnp.concatenate(
        [
            attention_gain.reshape(-1, HD),
            mlp_gain.reshape(-1, HD),
            spread(query_gain),
            spread(key_gain),
            jnp.zeros((14 - 2 * deep // HD, HD), jnp.bfloat16),
        ]
    )
    (
        normed_all,
        attn_raw,
        queries_b,
        keys_b,
        values_b,
        gated_b,
        w_attn,
        w_mlp,
        middle,
        normed_mlp_all,
        hidden_b,
        grad_branch_all,
        grad_mlp_b,
        grad_result,
        block_out,
        _,
        angle_cos,
        angle_sin,
        gain_rows,
        head_gains,
        losses,
    ) = forward(
        n_fsdp,
        n_rep,
        heads_k,
        (
            tokens,
            gain_block,
            w_query,
            w_outgate,
            w_key,
            w_value,
            w_gate,
            w_up,
            w_output,
            w_down,
            teacher,
            lengths,
            deal_order,
            lengths[None],
            freq,
        ),
    )
    seq_loss = losses[:2, 0]
    piece_rows, piece_cols = deep // 2, width // n_fsdp
    units, base = [], 0
    for by_owner, row_blocks, cols in (
        (False, ff // 2 // piece_rows, width),
        (True, n_fsdp, 2 * ff),
        (False, cols_q // 2 // piece_rows, width),
        (True, n_fsdp, 2 * cols_q + 2 * cols_k),
    ):
        units.append(Unit(base, by_owner, row_blocks, cols // piece_cols))
        base += units[-1].count
    pieces, _, _, _, _, tokens_grad, gain_sums = backward(
        n_fsdp,
        n_rep,
        heads_k,
        units,
        piece_rows,
        piece_cols,
        (
            hidden_b,
            normed_mlp_all,
            gated_b,
            normed_all,
            grad_branch_all,
            grad_mlp_b,
            w_mlp,
            w_output,
            w_attn,
            middle,
            grad_result,
            tokens,
            attn_raw,
            angle_cos,
            angle_sin,
            queries_b,
            keys_b,
            values_b,
            gain_rows,
            head_gains,
            lengths,
            deal_order,
        ),
    )
    down, mlp, outp, attn = units

    def by_rows(unit, weight):
        blocks, together = unit.row_blocks, unit.col_blocks
        return widened(
            pieces,
            (2, blocks),
            together,
            lambda c, r: (unit.base // together + r, c, 0, 0),
            weight.shape,
            lambda c, r: (c * blocks + r, 0),
        )

    dw_down = by_rows(down, w_down)
    dw_output = by_rows(outp, w_output)
    dw_gate, dw_up = widened_both(pieces, mlp.base, mlp.col_blocks, n_fsdp, w_gate.shape)
    dw_query, dw_outgate, dw_key, dw_value = widened_heads(
        pieces,
        attn.base,
        n_fsdp,
        (w_query.shape, w_outgate.shape, w_key.shape, w_value.shape),
    )

    def own_part(row, start, cols):
        return lax.dynamic_slice(gain_sums, (row, start + mine * cols), (1, cols))[0]

    return (
        block_out,
        seq_loss,
        tokens_grad,
        own_part(0, 0, deep),
        own_part(0, width, small),
        own_part(1, width, small),
        dw_query,
        dw_key,
        dw_value,
        dw_outgate,
        dw_output,
        own_part(1, 0, deep),
        dw_gate,
        dw_up,
        dw_down,
    )


def solution(mesh):
    return jax.shard_map(
        shards,
        mesh=mesh,
        in_specs=(
            P(("rep", "fsdp"), None),
            P(("rep", "fsdp"), None),
            P(),
            P(),
            P("fsdp"),
            P("fsdp"),
            P("fsdp"),
            P("fsdp", None),
            P("fsdp", None),
            P("fsdp", None),
            P("fsdp", None),
            P("fsdp", None),
            P("fsdp"),
            P("fsdp", None),
            P("fsdp", None),
            P("fsdp", None),
        ),
        out_specs=(
            P(("rep", "fsdp"), None),
            P(("rep", "fsdp")),
            P(("rep", "fsdp"), None),
            P("fsdp"),
            P("fsdp"),
            P("fsdp"),
            P("fsdp", None),
            P("fsdp", None),
            P("fsdp", None),
            P("fsdp", None),
            P("fsdp", None),
            P("fsdp"),
            P("fsdp", None),
            P("fsdp", None),
            P("fsdp", None),
        ),
        check_vma=False,
    )
```

```python
import functools

import jax
import jax.numpy as jnp
import numpy as np
from jax import lax
from jax.experimental import pallas as pl
from jax.experimental.pallas import tpu as pltpu
from jax.sharding import PartitionSpec as P

MESH = pl.DeviceIdType.MESH

H = 16
KV = 8
HD = 128


EPS_NORM = 1e-06
ROPE_BASE = 1000000.0
NEG_FILL = -1e30


def in_f32(values):
    return values.astype(jnp.float32)


def in_bf16(values):
    return values.astype(jnp.bfloat16)


def flipped(index, step, n):
    out, bit = index, 1
    while bit < n:
        has = (step // bit) % 2
        out = out + has * bit * (1 - 2 * ((index // bit) % 2))
        bit *= 2
    return out


def at_least(value, bound, span):
    span = max(span, bound)
    return (value + (span - bound)) // span


class Unit:
    def __init__(self, base, by_owner, row_blocks, col_blocks):
        self.base, self.by_owner = base, by_owner
        self.row_blocks, self.col_blocks = row_blocks, col_blocks
        self.count = row_blocks * col_blocks


LAG_B, LAG_C, LAG_D, LAG_E, LAG_G = 1, 3, 5, 7, 13
RING = 4


ROW_STEP = 64
TILES = 8


def norm_back(grad, raw, gain):
    scale = lax.rsqrt(jnp.mean(raw * raw, axis=-1, keepdims=True) + EPS_NORM)
    unit = raw * scale
    inner = grad * gain
    return scale * (inner - unit * jnp.mean(inner * unit, axis=-1, keepdims=True)), grad * unit


def backward_kernel(n_fsdp, n_rep, heads_k, units, piece_rows, piece_cols, *refs):
    (hidden, normed_mlp, gated, normed, grad_branch, grad_mlp, w_mlp, w_output, w_attn) = refs[:9]
    (middle, grad_result, tokens, attn_raw, all_cos, all_sin, all_q, all_k, all_v) = refs[9:18]
    (gains, head_gains, lengths_ref, deal_ref) = refs[18:22]
    (out, grad_attn, grad_raw, inb, xb, tokens_grad, gain_out) = refs[22:29]
    (lm, lo, rh, sb, kb, r1, c_slot, d_slot, big, wt, own, pbuf, land_a, land_b) = refs[29:43]
    (mid, gres, tok, ga, wo, raw, cs, sn, qb, kvb, vb, gb, gg, ob) = refs[43:57]
    (tile_sem, r1s, r1r, ins, inr, xs, xr, os_, fs, fr, gs, gr, ls) = refs[57:70]
    (load_sem, first_sem, wt_sem, ps, pr, qs, qr, ag_s, ag_r, ag_l, block_sem) = refs[70:81]
    (near_land, pair_land, in_land, far_land, near_s, near_r, line_s, line_r) = refs[81:]
    head_gain_out = gain_out.at[:, pl.ds(own.shape[1], HD)]
    lefts = (hidden, normed_mlp, gated, normed)
    rights = (grad_branch, grad_mlp, grad_attn, grad_raw)
    total = sum(unit.count for unit in units)
    rows, width = own.shape
    rows_all = n_fsdp * rows
    ff = grad_mlp.shape[1] // 2
    tile = width // TILES
    others = range(1, n_fsdp)
    rep, mine = lax.axis_index("rep"), lax.axis_index("fsdp")
    core, place = rep % 2, rep // 2
    n_line = n_rep // 2
    half = n_line // 2
    side = place // half
    depth = place * (1 - side) + (n_line - 1 - place) * side
    inward = (place + 1 - 2 * side) * 2 + core
    outward = (place - 1 + 2 * side) * 2 + core
    sib = rep + 1 - 2 * core
    at_middle = depth == half - 1

    barrier = pltpu.get_barrier_semaphore()

    def greet(to_rep, to_fsdp):
        pl.semaphore_signal(
            barrier, inc=1, device_id={"rep": to_rep, "fsdp": to_fsdp}, device_id_type=MESH
        )

    greet(sib, mine)
    greet(inward, mine)
    for s in others:
        greet(rep, flipped(mine, s, n_fsdp))


    def r1_copy(p):
        return remote_copy(sb.at[p % RING], r1.at[p], r1s.at[p], r1r.at[p], sib, mine)

    def in_copy(p):
        return remote_copy(r1.at[p], inb.at[p], ins.at[p], inr.at[p], inward, mine)

    def x_copy(p):
        return remote_copy(r1.at[p], xb.at[p], xs.at[p], xr.at[p], inward, mine)

    def o_copy(p, src):
        return remote_copy(src.at[p], xb.at[p], os_, xr.at[p], outward, mine)

    def inside_of(p, unit):
        inside = at_least(p, unit.base, total - unit.base)
        stop = unit.base + unit.count
        if stop < total:
            inside = inside * (1 - at_least(p, stop, total - stop))
        return inside

    def owner_of(p):
        step = 0
        for unit in units:
            if unit.by_owner:
                i = p - unit.base
                step = step + inside_of(p, unit) * (n_fsdp - 1 - i // unit.col_blocks)
        return step

    def spot(p, source):
        where = p
        for unit in units:
            if unit.by_owner:
                i = p - unit.base
                spread = unit.base + source * unit.col_blocks + i % unit.col_blocks
                where = where + inside_of(p, unit) * (spread - p)
        return where

    def f_copy(p, step):
        return remote_copy(
            r1.at[p],
            out.at[spot(p, mine), core],
            fs,
            fr.at[p],
            rep,
            flipped(mine, step, n_fsdp),
        )

    def g_copy(src, where):
        return remote_copy(src, out.at[where, core], gs, gr, sib, mine)

    def l_copy(p):
        return pltpu.make_async_copy(r1.at[p], out.at[spot(p, mine), core], ls)

    def c_load(p):
        return pltpu.make_async_copy(inb.at[p], c_slot, load_sem.at[0])

    def d_load(p):
        return pltpu.make_async_copy(xb.at[p], d_slot, load_sem.at[1])

    def e_load(p):
        return pltpu.make_async_copy(xb.at[p], r1.at[p], load_sem.at[2])

    def add_into(p, other):
        r1[p] = in_bf16(in_f32(r1[p]) + in_f32(other))

    def begin_c(p):
        @pl.when(depth > 0)
        def _():
            in_copy(p).wait_recv()
            c_load(p).start()

    def begin_d(p):
        @pl.when(at_middle)
        def _():
            x_copy(p).wait_recv()
            d_load(p).start()

    def begin_e(p):
        @pl.when(depth < half - 1)
        def _():
            o_copy(p, xb).wait_recv()

            @pl.when(depth > 0)
            def _():
                o_copy(p, xb).start()

            in_copy(p).wait_send()
            e_load(p).start()

    def end_b(p):
        r1_copy(p).wait_recv()
        add_into(p, kb[p % RING])
        if half > 1:

            @pl.when(depth == 0)
            def _():
                in_copy(p).start()
        else:
            x_copy(p).start()

    def end_c(p):
        @pl.when(depth > 0)
        def _():
            c_load(p).wait()
            add_into(p, c_slot[...])

            @pl.when(depth < half - 1)
            def _():
                in_copy(p).start()

            @pl.when(at_middle)
            def _():
                x_copy(p).start()

    def end_d(p):
        @pl.when(at_middle)
        def _():
            d_load(p).wait()
            x_copy(p).wait_send()
            add_into(p, d_slot[...])

            @pl.when(depth > 0)
            def _():
                o_copy(p, r1).start()

    def end_e(p):
        @pl.when(depth < half - 1)
        def _():
            e_load(p).wait()

        step = owner_of(p)

        @pl.when(step == 0)
        def _():
            l_copy(p).start()
            g_copy(r1.at[p], spot(p, mine)).start()

        @pl.when(step > 0)
        def _():
            f_copy(p, step).start()

    def end_g(p):
        step = owner_of(p)

        @pl.when(step > 0)
        def _():
            f_copy(p, step).wait_recv()
            where = spot(p, flipped(mine, step, n_fsdp))
            g_copy(out.at[where, core], where).start()

    def run(stages, t):
        for lag, stage in stages:
            pl.when((t >= lag) & (t < total + lag))(functools.partial(stage, t - lag))

    def begin(t):
        run([(LAG_C, begin_c), (LAG_D, begin_d), (LAG_E, begin_e)], t)

    def end(t):
        run([(LAG_B, end_b), (LAG_C, end_c), (LAG_D, end_d), (LAG_E, end_e), (LAG_G, end_g)], t)

    def tiles(u, i, slot):
        unit = units[u]
        r, j = i // unit.col_blocks, i % unit.col_blocks
        if unit.by_owner:
            owner = flipped(mine, n_fsdp - 1 - r, n_fsdp)
            first = owner * 2 * piece_rows + core * piece_rows
            second = owner * 2 * piece_rows + (1 - core) * piece_rows
        else:
            first = core * unit.row_blocks * piece_rows + r * piece_rows
            second = (1 - core) * unit.row_blocks * piece_rows + r * piece_rows
        first = pl.ds(pl.multiple_of(first, piece_rows), piece_rows)
        second = pl.ds(pl.multiple_of(second, piece_rows), piece_rows)
        cols = pl.ds(pl.multiple_of(j * piece_cols, piece_cols), piece_cols)
        return [
            pltpu.make_async_copy(lefts[u].at[:, first], lm.at[slot], tile_sem.at[slot, 0]),
            pltpu.make_async_copy(lefts[u].at[:, second], lo.at[slot], tile_sem.at[slot, 1]),
            pltpu.make_async_copy(rights[u].at[:, cols], rh.at[slot], tile_sem.at[slot, 2]),
        ]


    first_pairs = (
        (grad_mlp.at[:, pl.ds(0, ff)], big.at[pl.ds(0, rows_all)]),
        (grad_mlp.at[:, pl.ds(ff, ff)], big.at[pl.ds(rows_all, rows_all)]),
        (middle, mid),
        (grad_result, gres),
        (tokens, tok),
        (w_output, wo),
    )

    def first_loads(which):
        return [pltpu.make_async_copy(*first_pairs[i], first_sem.at[i]) for i in which]

    def attn_load():
        return pltpu.make_async_copy(w_attn, big.at[pl.ds(0, width)], first_sem.at[6])

    def tile_of(j):
        return pl.ds(pl.multiple_of(j * tile, tile), tile)

    def wt_load(j):
        return pltpu.make_async_copy(w_mlp.at[tile_of(j)], wt.at[j % 2], wt_sem.at[j % 2])

    def p_copy(s, j):
        return remote_copy(
            pbuf.at[s - 1, :, tile_of(j)],
            land_a.at[s - 1, :, tile_of(j)],
            ps.at[s, j],
            pr.at[s, j],
            rep,
            flipped(mine, s, n_fsdp),
        )

    def q_copy(s):
        return remote_copy(
            pbuf.at[s - 1], land_b.at[s - 1], qs.at[s], qr.at[s], rep, flipped(mine, s, n_fsdp)
        )

    gather = GatherRows(n_fsdp, rep, mine, ga, grad_attn, (ag_s, ag_r, ag_l))

    def mlp_products(j):
        @pl.when(j == 0)
        def _():
            for copy in first_loads((0, 1)):
                copy.wait()

        wt_load(j).wait()

        @pl.when(j + 1 < TILES)
        def _():
            wt_load(j + 1).start()

        for s in (*others, 0):
            part = product_of(big[s * rows : (s + 1) * rows], wt[j % 2, :, :ff], 1, 1)
            part += product_of(
                big[rows_all + s * rows : rows_all + (s + 1) * rows], wt[j % 2, :, ff:], 1, 1
            )
            if s == 0:
                own[:, tile_of(j)] = part
            else:
                pbuf[s - 1, :, tile_of(j)] = in_bf16(part)
                p_copy(s, j).start()

    row_steps = rows // ROW_STEP

    def middle_back(part):
        if part == 0:
            middle_sums()

        def some_rows(r, carry):
            cut = pl.ds(pl.multiple_of(r * ROW_STEP, ROW_STEP), ROW_STEP)
            grad = own[cut]
            for s in others:
                grad += in_f32(land_a[s - 1, cut])
            back, gain_rows = norm_back(grad, mid[cut], gains[1:2])
            gain_out[1:2, :width] += jnp.sum(gain_rows, axis=0, keepdims=True)
            back = gres[cut] + back
            gres[cut] = back
            ga[cut] = in_bf16(back)
            return carry

        lax.fori_loop(part * row_steps // 2, (part + 1) * row_steps // 2, some_rows, 0)
        if part == 1:
            gather.start()
            for copy in block_loads(0):
                copy.start()

    def middle_sums():
        attn_load().start()
        for copy in first_loads((2, 3)):
            copy.wait()

        def wait_tiles(j, carry):
            for s in others:
                p_copy(s, j).wait()
            return carry

        lax.fori_loop(0, TILES, wait_tiles, 0)
        gain_out[...] = jnp.zeros_like(gain_out)

    def block_loads(s):
        cut = pl.ds(pl.multiple_of(s * rows, rows), rows)
        pairs = (
            (attn_raw, raw), (all_cos, cs), (all_sin, sn), (all_q, qb), (all_k, kvb), (all_v, vb)
        )
        copies = [
            pltpu.make_async_copy(src.at[cut], dst, block_sem.at[i])
            for i, (src, dst) in enumerate(pairs)
        ]
        return copies

    def grad_load(s):
        cut = pl.ds(pl.multiple_of(s * rows, rows), rows)
        return pltpu.make_async_copy(grad_attn.at[cut], gb, block_sem.at[6])

    def store(s):
        cut = pl.ds(pl.multiple_of(s * rows, rows), rows)
        return pltpu.make_async_copy(ob, grad_raw.at[cut], block_sem.at[7])

    def heads_back(s, heads):
        attend_back(
            heads_k,
            heads,
            block_mask(
                block_lengths(lengths_ref, deal_ref, rep * n_fsdp + flipped(mine, s, n_fsdp)), rows
            ),
            cs[...],
            sn[...],
            head_gains[0:1],
            head_gains[1:2],
            raw,
            qb,
            kvb,
            vb,
            gg,
            ob,
            head_gain_out,
        )

    early = heads_k // 2

    def block_first(s):
        @pl.when(s == 0)
        def _():
            first_loads((5,))[0].wait()
            gb[...] = ga[...]

        for k in others:

            @pl.when(s == k)
            def _(k=k):
                gather.arrive(k)

        @pl.when(s > 0)
        def _():
            copy = grad_load(s)
            copy.start()
            copy.wait()

        gg[...] = product_of(gb[...], wo[...], 1, 1)
        for copy in block_loads(s):
            copy.wait()
        heads_back(s, range(early))

    def block_second(s):
        heads_back(s, range(early, heads_k))
        store(s).start()

        @pl.when(s + 1 < n_fsdp)
        def _():
            for copy in block_loads(s + 1):
                copy.start()

    def block_third(s):
        store(s).wait()

        @pl.when(s == 0)
        def _():
            attn_load().wait()

        def one_tile(j, carry):
            part = product_of(ob[...], big[tile_of(j)], 1, 1)

            @pl.when(s == 0)
            def _():
                own[:, tile_of(j)] = part

            @pl.when(s > 0)
            def _():
                pbuf[s - 1, :, tile_of(j)] = in_bf16(part)

            return carry

        lax.fori_loop(0, TILES, one_tile, 0)

        @pl.when(s > 0)
        def _():
            q_copy(s).start()

    def tokens_back(part):
        if part == 0:
            gather.sent()
            first_loads((4,))[0].wait()
            for s in others:
                q_copy(s).wait()

        def some_rows(r, carry):
            cut = pl.ds(pl.multiple_of(r * ROW_STEP, ROW_STEP), ROW_STEP)
            grad = own[cut]
            for s in others:
                grad += in_f32(land_b[s - 1, cut])
            back, gain_rows = norm_back(grad, in_f32(tok[cut]), gains[0:1])
            gain_out[0:1, :width] += jnp.sum(gain_rows, axis=0, keepdims=True)
            tokens_grad[cut] = in_bf16(gres[cut] + back)
            return carry

        lax.fori_loop(part * row_steps // 2, (part + 1) * row_steps // 2, some_rows, 0)
        if part == 1:
            near_land[mine] = gain_out[...]
            for s in others:
                near_copy(s).start()


    def near_copy(s):
        return remote_copy(
            gain_out,
            near_land.at[mine],
            near_s.at[s],
            near_r.at[s],
            rep,
            flipped(mine, s, n_fsdp),
        )

    def line_copy(k, target, to_rep):
        return remote_copy(gain_out, target, line_s.at[k], line_r.at[k], to_rep, mine)

    def pair_copy():
        return line_copy(0, pair_land, sib)

    def gain_in():
        return line_copy(1, in_land, inward)

    def gain_across():
        return line_copy(2, far_land, inward)

    def gain_back():
        return line_copy(3, far_land, outward)

    def gains_near():
        for s in others:
            near_copy(s).wait()
        summed = near_land[0]
        for k in others:
            summed += near_land[k]
        gain_out[...] = summed
        pair_copy().start()

    def gains_pair():
        pair_copy().wait()
        gain_out[...] += pair_land[...]

        @pl.when(depth == 0)
        def _():
            (gain_in if half > 1 else gain_across)().start()

    def gains_in(k):
        @pl.when(depth == k)
        def _():
            gain_in().wait_recv()
            gain_out[...] += in_land[...]
            (gain_in if k < half - 1 else gain_across)().start()

    def gains_across():
        @pl.when(at_middle)
        def _():
            gain_across().wait()
            gain_out[...] += far_land[...]
            if half > 1:
                gain_back().start()

    def gains_back(k):
        @pl.when(depth == k)
        def _():
            gain_back().wait_recv()
            gain_in().wait_send()
            gain_out[...] = far_land[...]
            if k > 0:
                gain_back().start()

    def tasks(u, i):
        if u == 0:

            @pl.when(i == 1)
            def _():
                wt_load(0).start()
                for copy in first_loads((0, 1)):
                    copy.start()

            @pl.when(i == 6)
            def _():
                for copy in first_loads((2, 3, 4, 5)):
                    copy.start()

            pl.when((i >= 4) & (i < 4 + TILES))(lambda: mlp_products(i - 4))
        if u == 1:
            for part in range(2):
                pl.when(i == 7 + part)(functools.partial(middle_back, part))
            pl.when(i == 12)(gather.forward)
            pl.when(i == 15)(lambda: gather.own().wait())
            last = 15 + 3 * (n_fsdp - 1)
            busy = ((i >= 9) & (i < 12)) | ((i >= 15) & (i < last))
            s = at_least(i, 12, units[1].count) * ((i - 12) // 3)
            for phase, task in enumerate((block_first, block_second, block_third)):
                pl.when(busy & (i % 3 == phase))(functools.partial(task, s))
        if u == 3:
            for part in range(2):
                pl.when(i == 2 + part)(functools.partial(tokens_back, part))
            pl.when(i == 6)(gains_near)
            pl.when(i == 8)(gains_pair)

    def product(left, right):
        return product_of(left, right, 0, 0)

    for copy in tiles(0, 0, 0):
        copy.start()

    @pl.when(depth == 0)
    def _():
        pl.semaphore_wait(barrier, 1 + n_fsdp)

    @pl.when(depth > 0)
    def _():
        greet(outward, mine)
        pl.semaphore_wait(barrier, 2 + n_fsdp)

    for u, unit in enumerate(units):

        def step(i, carry, u=u, unit=unit):
            t = unit.base + i
            slot = t % 2
            begin(t)
            for copy in tiles(u, i, slot):
                copy.wait()

            @pl.when(i + 1 < unit.count)
            def _():
                for copy in tiles(u, i + 1, 1 - slot):
                    copy.start()

            if u + 1 < len(units):

                @pl.when(i + 1 == unit.count)
                def _():
                    for copy in tiles(u + 1, 0, 1 - slot):
                        copy.start()

            @pl.when(t >= RING)
            def _():
                r1_copy(t - RING).wait_send()

            sb[t % RING] = in_bf16(product(lo[slot], rh[slot]))
            r1_copy(t).start()
            kb[t % RING] = product(lm[slot], rh[slot])
            end(t)
            tasks(u, i)
            return carry

        lax.fori_loop(0, unit.count, step, 0)

    def drain(t, carry):
        begin(t)
        end(t)
        return carry

    lax.fori_loop(total, total + LAG_G, drain, 0)

    for p in range(total - RING, total):
        r1_copy(p).wait_send()
    kept = sum(u.col_blocks if u.by_owner else u.count for u in units)
    some, rest = pl.ds(0, kept), pl.ds(0, total - kept)
    every = remote_copy(r1, out.at[:, core], gs, gr, sib, mine)
    every.wait()
    pltpu.make_async_copy(r1.at[some], out.at[some, core], ls).wait()
    remote_copy(r1.at[rest], out.at[rest, core], fs, fr.at[0], sib, mine).wait_send()

    @pl.when(depth > 0)
    def _():
        remote_copy(r1, xb, os_, xr.at[0], outward, mine).wait_send()

    for k in range(1, half):
        gains_in(k)
    gains_across()
    for k in range(half - 2, -1, -1):
        gains_back(k)
    if half > 1:

        @pl.when(depth > 0)
        def _():
            gain_back().wait_send()


def backward(n_fsdp, n_rep, heads_k, units, piece_rows, piece_cols, args):
    total = sum(unit.count for unit in units)
    rows_all, rows = args[0].shape[0], args[9].shape[0]
    width, cols = args[8].shape
    cols_q, cols_k = heads_k * (H // KV) * HD, heads_k * HD
    two_ff = args[5].shape[1]
    dma = pltpu.SemaphoreType.DMA
    piece = (piece_rows, piece_cols)
    low, full = jnp.bfloat16, jnp.float32
    any_spec = pl.BlockSpec(memory_space=pl.ANY)
    vmem = pl.BlockSpec(memory_space=pltpu.VMEM)
    flops = sum(4 * unit.count for unit in units) * rows_all * piece_rows * piece_cols
    outs = (
        ((total, 2) + piece, low),
        ((rows_all, width), low),
        ((rows_all, cols), low),
        ((total,) + piece, low),
        ((total,) + piece, low),
        ((rows, width), low),
        ((8, width + HD), full),
    )
    scratch = (
        ((2, rows_all, piece_rows), low),
        ((2, rows_all, piece_rows), low),
        ((2, rows_all, piece_cols), low),
        ((RING,) + piece, low),
        ((RING,) + piece, full),
        ((total,) + piece, low),
        (piece, low),
        (piece, low),
        ((max(2 * rows_all, width), cols), low),
        ((2, width // TILES, two_ff), low),
        ((rows, width), full),
        ((n_fsdp - 1, rows, width), low),
        ((n_fsdp - 1, rows, width), low),
        ((n_fsdp - 1, rows, width), low),
        ((rows, width), full),
        ((rows, width), full),
        ((rows, width), low),
        ((rows, width), low),
        ((cols_q, width), low),
        ((rows, cols), full),
        ((rows, HD), full),
        ((rows, HD), full),
        ((rows, cols_q), low),
        ((rows, cols_k), low),
        ((rows, cols_k), low),
        ((rows, width), low),
        ((rows, cols_q), full),
        ((rows, cols), low),
    )
    return pl.pallas_call(
        functools.partial(
            backward_kernel, n_fsdp, n_rep, heads_k, units, piece_rows, piece_cols
        ),
        out_shape=[jax.ShapeDtypeStruct(shape, kind) for shape, kind in outs],
        in_specs=[any_spec] * 18 + [vmem] * 2 + [pl.BlockSpec(memory_space=pltpu.SMEM)] * 2,
        out_specs=[any_spec] * 5 + [vmem] * 2,
        scratch_shapes=[pltpu.VMEM(shape, kind) for shape, kind in scratch]
        + [dma((2, 3))]
        + [dma((total,)) for _ in range(6)]
        + [dma, dma, dma((total,)), dma, dma, dma]
        + [
            dma((3,)),
            dma((7,)),
            dma((2,)),
            dma((n_fsdp, TILES)),
            dma((n_fsdp, TILES)),
            dma((n_fsdp,)),
            dma((n_fsdp,)),
            dma((n_fsdp, 2)),
            dma((n_fsdp, 2)),
            dma,
            dma((8,)),
            pltpu.VMEM((n_fsdp, 8, width + HD), full),
            pltpu.VMEM((8, width + HD), full),
            pltpu.VMEM((8, width + HD), full),
            pltpu.VMEM((8, width + HD), full),
            dma((n_fsdp,)),
            dma((n_fsdp,)),
            dma((4,)),
            dma((4,)),
        ],
        compiler_params=pltpu.CompilerParams(
            collective_id=0, has_side_effects=True, vmem_limit_bytes=62 << 20
        ),
        cost_estimate=pl.CostEstimate(flops=2 * flops, bytes_accessed=1 << 30, transcendentals=0),
        name="backward",
    )(*args)


def widen_kernel(in_ref, out_ref):
    cols = in_ref.shape[-1]
    for i in range(in_ref.shape[0]):
        out_ref[:, i * cols : (i + 1) * cols] = in_ref[i, 0].astype(jnp.float32)


def widened(pieces, grid, together, where, shape, place):
    rows, cols = pieces.shape[2:]
    return pl.pallas_call(
        widen_kernel,
        grid=grid,
        out_shape=jax.ShapeDtypeStruct(shape, jnp.float32),
        in_specs=[pl.BlockSpec((together, 1, rows, cols), where)],
        out_specs=pl.BlockSpec((rows, together * cols), place),
        name="widen",
    )(pieces)


def widen_both_kernel(in_ref, first_ref, second_ref):
    cols, count = in_ref.shape[-1], in_ref.shape[0] // 2
    for i in range(count):
        first_ref[:, i * cols : (i + 1) * cols] = in_f32(in_ref[i, 0])
        second_ref[:, i * cols : (i + 1) * cols] = in_f32(in_ref[count + i, 0])


def widened_both(pieces, base, together, n_fsdp, shape):
    rows, cols = pieces.shape[2:]
    return pl.pallas_call(
        widen_both_kernel,
        grid=(2, n_fsdp),
        out_shape=[jax.ShapeDtypeStruct(shape, jnp.float32)] * 2,
        in_specs=[
            pl.BlockSpec((together, 1, rows, cols), lambda c, f: (base // together + f, c, 0, 0))
        ],
        out_specs=[pl.BlockSpec((rows, together // 2 * cols), lambda c, f: (c, f))] * 2,
        compiler_params=pltpu.CompilerParams(vmem_limit_bytes=32 << 20),
        name="widen_both",
    )(pieces)


def widen_heads_kernel(query_in, gate_in, pair_in, query_out, gate_out, key_out, value_out):
    half = key_out.shape[1]
    query_out[...] = query_in[0, 0].astype(jnp.float32)
    gate_out[...] = gate_in[0, 0].astype(jnp.float32)
    key_out[...] = pair_in[0, 0, :, :half].astype(jnp.float32)
    value_out[...] = pair_in[0, 0, :, half:].astype(jnp.float32)


def widened_heads(pieces, base, n_fsdp, shapes):
    rows, cols = pieces.shape[2:]

    def where(j):
        return lambda c, f: (base + 3 * f + j, c, 0, 0)

    widths = (cols, cols, cols // 2, cols // 2)
    return pl.pallas_call(
        widen_heads_kernel,
        grid=(2, n_fsdp),
        out_shape=[jax.ShapeDtypeStruct(shape, jnp.float32) for shape in shapes],
        in_specs=[pl.BlockSpec((1, 1, rows, cols), where(j)) for j in range(3)],
        out_specs=[pl.BlockSpec((rows, wide), lambda c, f: (c, f)) for wide in widths],
        name="widen_heads",
    )(pieces, pieces, pieces)


def block_lengths(lengths_ref, deal_ref, device):
    head_len = lengths_ref[deal_ref[2 * device]]
    return head_len, head_len + lengths_ref[deal_ref[2 * device + 1]]


def block_mask(block, rows):
    head_len, both_len = block
    query_row = lax.broadcasted_iota(jnp.int32, (rows, rows), 0)
    key_row = lax.broadcasted_iota(jnp.int32, (rows, rows), 1)

    def segment(index):
        return (index >= head_len).astype(jnp.int32) + (index >= both_len).astype(jnp.int32)

    return (segment(query_row) == segment(key_row)) & (key_row <= query_row)


def turn(values):
    half_dim = values.shape[-1] // 2
    return jnp.concatenate([-values[:, half_dim:], values[:, :half_dim]], axis=-1)


def head_forward(raw, gain, angle_cos, angle_sin):
    values = raw * lax.rsqrt(jnp.mean(raw * raw, axis=-1, keepdims=True) + EPS_NORM) * gain
    return in_bf16(values * angle_cos + turn(values) * angle_sin)


def head_backward(grad, raw, gain, angle_cos, angle_sin):
    grad = grad * angle_cos - turn(grad * angle_sin)
    scale = lax.rsqrt(jnp.mean(raw * raw, axis=-1, keepdims=True) + EPS_NORM)
    unit = raw * scale
    gain_rows = grad * unit
    inner = grad * gain
    return scale * (inner - unit * jnp.mean(inner * unit, axis=-1, keepdims=True)), gain_rows


def product_of(left, right, left_dim, right_dim):
    return lax.dot_general(
        left, right, (((left_dim,), (right_dim,)), ((), ())), preferred_element_type=jnp.float32
    )


def softmax_of(queries, keys, allowed):
    scores = jnp.where(allowed, product_of(queries, keys, 1, 1) * HD ** (-0.5), NEG_FILL)
    exponent = jnp.exp(scores - jnp.max(scores, axis=-1, keepdims=True))
    return exponent / jnp.sum(exponent, axis=-1, keepdims=True)


def attend(
    heads_k,
    allowed,
    angle_cos,
    angle_sin,
    query_gain,
    key_gain,
    raw_ref,
    q_ref,
    k_ref,
    v_ref,
    gated_ref,
):
    group = H // KV
    cols_q, cols_k = heads_k * group * HD, heads_k * HD
    for j in range(heads_k):
        own = slice(j * HD, (j + 1) * HD)
        keys = head_forward(
            raw_ref[:, 2 * cols_q + j * HD : 2 * cols_q + (j + 1) * HD],
            key_gain,
            angle_cos,
            angle_sin,
        )
        start = 2 * cols_q + cols_k + j * HD
        values = in_bf16(raw_ref[:, start : start + HD])
        k_ref[:, own] = keys
        v_ref[:, own] = values
        for h in range(j * group, (j + 1) * group):
            cut = slice(h * HD, (h + 1) * HD)
            queries = head_forward(raw_ref[:, cut], query_gain, angle_cos, angle_sin)
            q_ref[:, cut] = queries
            probs = in_bf16(softmax_of(queries, keys, allowed))
            context = product_of(probs, values, 1, 0)
            gate = raw_ref[:, cols_q + h * HD : cols_q + (h + 1) * HD]
            gated_ref[:, cut] = in_bf16(context * jax.nn.sigmoid(gate))


def attend_back(
    heads_k,
    heads,
    allowed,
    angle_cos,
    angle_sin,
    query_gain,
    key_gain,
    raw_ref,
    q_ref,
    k_ref,
    v_ref,
    grad_ref,
    out_ref,
    gain_ref,
):
    group = H // KV
    cols_q, cols_k = heads_k * group * HD, heads_k * HD
    for j in heads:
        own = slice(j * HD, (j + 1) * HD)
        keys, values = k_ref[:, own], v_ref[:, own]
        grad_keys, grad_values = 0.0, 0.0
        for h in range(j * group, (j + 1) * group):
            cut = slice(h * HD, (h + 1) * HD)
            gate_cut = slice(cols_q + h * HD, cols_q + (h + 1) * HD)
            queries, grad_gated = q_ref[:, cut], grad_ref[:, cut]
            probs = softmax_of(queries, keys, allowed)
            probs_b = in_bf16(probs)
            context = product_of(probs_b, values, 1, 0)
            gate = jax.nn.sigmoid(raw_ref[:, gate_cut])
            grad_context = in_bf16(grad_gated * gate)
            out_ref[:, gate_cut] = in_bf16(grad_gated * context * gate * (1.0 - gate))
            grad_probs = product_of(grad_context, values, 1, 1)
            grad_scores = in_bf16(
                probs * (grad_probs - jnp.sum(probs * grad_probs, axis=-1, keepdims=True))
            )
            grad_values += product_of(probs_b, grad_context, 0, 0)
            grad_keys += product_of(grad_scores, queries, 0, 0)
            grad_queries = product_of(grad_scores, keys, 1, 0) * HD ** (-0.5)
            grad_raw, gain_rows = head_backward(
                grad_queries, raw_ref[:, cut], query_gain, angle_cos, angle_sin
            )
            out_ref[:, cut] = in_bf16(grad_raw)
            gain_ref[0:1, :] += jnp.sum(gain_rows, axis=0, keepdims=True)
        key_start = 2 * cols_q + j * HD
        grad_raw, gain_rows = head_backward(
            grad_keys * HD ** (-0.5),
            raw_ref[:, key_start : key_start + HD],
            key_gain,
            angle_cos,
            angle_sin,
        )
        out_ref[:, key_start : key_start + HD] = in_bf16(grad_raw)
        gain_ref[1:2, :] += jnp.sum(gain_rows, axis=0, keepdims=True)
        value_start = 2 * cols_q + cols_k + j * HD
        out_ref[:, value_start : value_start + HD] = in_bf16(grad_values)


def remote_copy(src, dst, send, recv, to_rep, to_fsdp):
    return pltpu.make_async_remote_copy(
        src_ref=src,
        dst_ref=dst,
        send_sem=send,
        recv_sem=recv,
        device_id={"rep": to_rep, "fsdp": to_fsdp},
        device_id_type=MESH,
    )


def greet_all(peers):
    barrier = pltpu.get_barrier_semaphore()
    for to_rep, to_fsdp in peers:
        pl.semaphore_signal(
            barrier, inc=1, device_id={"rep": to_rep, "fsdp": to_fsdp}, device_id_type=MESH
        )
    pl.semaphore_wait(barrier, len(peers))


class GatherRows:
    def __init__(self, n_fsdp, rep, mine, source, target, sems):
        self.n_fsdp, self.rep, self.mine = n_fsdp, rep, mine
        self.source, self.target = source, target
        self.send, self.recv, self.local = sems
        self.rows = source.shape[0]
        self.half = self.rows // 2
        self.relay = ((1, 0), (2, 1)) if n_fsdp == 4 else ()

    def copy(self, s, h, to=None, src=None):
        to = s if to is None else to
        return remote_copy(
            self.source.at[pl.ds(h * self.half, self.half)]
            if src is None
            else self.target.at[pl.ds(src * self.rows + h * self.half, self.half)],
            self.target.at[pl.ds(s * self.rows + h * self.half, self.half)],
            self.send.at[s, h],
            self.recv.at[s, h],
            self.rep,
            flipped(self.mine, to, self.n_fsdp),
        )

    def own(self):
        return pltpu.make_async_copy(
            self.source, self.target.at[pl.ds(0, self.rows)], self.local
        )

    def start(self):
        for s, h in ((1, 0), (2, 1), (1, 1), (2, 0)):
            if s < self.n_fsdp:
                self.copy(s, h).start()
        if self.n_fsdp != 4:
            for s in range(3, self.n_fsdp):
                for h in range(2):
                    self.copy(s, h).start()
        self.own().start()

    def forward(self):
        if self.n_fsdp == 4:
            self.copy(1, 0).wait_recv()
            self.copy(3, 0, to=2, src=1).start()
            self.copy(2, 1).wait_recv()
            self.copy(3, 1, to=1, src=2).start()

    def arrive(self, s):
        for h in range(2):
            if (s, h) not in self.relay:
                self.copy(s, h).wait_recv()

    def sent(self):
        for s in range(1, self.n_fsdp):
            for h in range(2):
                self.copy(s, h).wait_send()

    def finish(self):
        for s in range(1, self.n_fsdp):
            self.arrive(s)
        self.sent()
        self.own().wait()


def forward_kernel(n_fsdp, n_rep, heads_k, *refs):
    (tokens, gains, wq, wg, wk, wv, w_gate, w_up, w_output, w_down, teacher) = refs[:11]
    (lengths_ref, deal_ref, lengths_row, freq_ref) = refs[11:15]
    (normed_all, raw_all, q_all, k_all, v_all, gated_all, w_attn, w_mlp) = refs[15:23]
    (middle_out, nmlp_all, hidden_all, gbranch_all, gmlp_all, gres_out, block_out) = refs[23:30]
    (gu_all, all_cos, all_sin, gain_out, head_gain_out, loss_out) = refs[30:36]
    (tok, gl, wa, wo, wd, wm, nb, raw, cs, sn, qb, kvb, vb, gb, own, pbuf, land) = refs[36:53]
    (mid, nm, te, gu, hb, gm) = refs[53:59]
    (ts, tr, tl, us, ur, ul, bs, br, bl, gain_s, gain_r, ws, wr, zs, zr, cps, cpr) = refs[59:76]
    (ms, mr, hs, hr, ss, sr, ps, pr, qs, qr, load, keep, mine_sem) = refs[76:]
    rows, width = own.shape
    rows_all = n_fsdp * rows
    cols, ff = raw.shape[1], hb.shape[1]
    deep = wq.shape[0]
    widths = tuple(w.shape[1] // n_fsdp for w in (wq, wg, wk, wv))
    starts = [sum(widths[:i]) for i in range(4)]
    others = range(1, n_fsdp)
    n_line = n_rep // 2
    rep, mine = lax.axis_index("rep"), lax.axis_index("fsdp")
    core, place = rep % 2, rep // 2
    sib = rep + 1 - 2 * core
    partner = (place + 1 - 2 * (place % 2)) * 2 + core
    block, part = deep // 4, deep // n_rep
    band = (place % 2) * 2 + core
    other_band = (1 - place % 2) * 2 + core
    hops = range(1, n_line)
    row_steps = rows // ROW_STEP
    near = sorted({1, n_line - 1})
    greet_all(
        [(sib, mine)]
        + [(((place + k) % n_line) * 2 + core, mine) for k in near]
        + [(rep, flipped(mine, s, n_fsdp)) for s in others]
    )


    def columns(peer, wide):
        return pl.ds(pl.multiple_of(peer * wide, wide), wide)

    def mlp_copy(s, i):
        peer = flipped(mine, s, n_fsdp)
        return remote_copy(
            (w_gate, w_up)[i].at[pl.ds(rep * part, part), columns(peer, ff)],
            w_mlp.at[pl.ds(mine * deep + rep * part, part), pl.ds(i * ff, ff)],
            ms.at[s, i],
            mr.at[s, i],
            rep,
            peer,
        )

    def part_at(s, of_rep):
        return w_mlp.at[pl.ds(flipped(mine, s, n_fsdp) * deep + of_rep * part, part)]

    def line_copy(s, k, up):
        step = 1 if up else -1
        src = part_at(s, ((place - step * (k - 1) + n_line) % n_line) * 2 + core)
        to_rep = ((place + step + n_line) % n_line) * 2 + core
        way = 0 if up else 1
        return remote_copy(src, src, hs.at[way, s, k], hr.at[way, s, k], to_rep, mine)

    def line_sends(k):
        for up in (True, False):
            first, last = (k - 1, n_line - 2) if up else (1, n_line - k)

            @pl.when((place >= first) & (place <= last))
            def _(up=up):
                for s in others:
                    line_copy(s, k, up).start()

    def line_arrivals(k):
        for up in (True, False):
            first, last = (k, n_line - 1) if up else (0, n_line - 1 - k)

            @pl.when((place >= first) & (place <= last))
            def _(up=up):
                for s in others:
                    line_copy(s, k, up).wait_recv()
                    share_copy(s, k, up).start()

        if k + 1 < n_line:
            line_sends(k + 1)

    def share_copy(s, k, up):
        step = 1 if up else -1
        src = part_at(s, ((place - step * k + n_line) % n_line) * 2 + core)
        way = 0 if up else 1
        return remote_copy(src, src, ss.at[way, s, k], sr.at[way, s, k], sib, mine)

    def shares(action):
        for s in others:
            action(share_copy(s, 0, True))
        for k in hops:
            for up in (True, False):
                first, last = (k, n_line - 1) if up else (0, n_line - 1 - k)

                @pl.when((place >= first) & (place <= last))
                def _(k=k, up=up):
                    for s in others:
                        action(share_copy(s, k, up))

    def lines_sent():
        for k in hops:
            for up in (True, False):
                first, last = (k - 1, n_line - 2) if up else (1, n_line - k)

                @pl.when((place >= first) & (place <= last))
                def _(k=k, up=up):
                    for s in others:
                        line_copy(s, k, up).wait_send()

    weights = (wq, wg, wk, wv)

    def weight_copy(s, i):
        peer = flipped(mine, s, n_fsdp)
        return remote_copy(
            weights[i].at[pl.ds(band * block, block), columns(peer, widths[i])],
            w_attn.at[pl.ds(mine * deep + band * block, block), pl.ds(starts[i], widths[i])],
            ws.at[s, i],
            wr.at[s, i],
            rep,
            peer,
        )

    def band_at(s, which):
        return w_attn.at[pl.ds(flipped(mine, s, n_fsdp) * deep + which * block, block)]

    def partner_copy(s):
        return remote_copy(band_at(s, band), band_at(s, band), zs.at[s], zr.at[s], partner, mine)

    def sibling_copy(s, k):
        which = band if k == 0 else other_band
        return remote_copy(
            band_at(s, which), band_at(s, which), cps.at[s, k], cpr.at[s, k], sib, mine
        )

    def gain_copy(s):
        return remote_copy(
            gains, gl.at[mine], gain_s.at[s], gain_r.at[s], rep, flipped(mine, s, n_fsdp)
        )

    mine_rows = pl.ds(mine * deep, deep)
    mine_pairs = [
        (weights[i].at[:, columns(mine, widths[i])], w_attn.at[mine_rows, pl.ds(starts[i], widths[i])])
        for i in range(4)
    ]
    mine_pairs += [
        (w.at[:, columns(mine, ff)], w_mlp.at[mine_rows, pl.ds(i * ff, ff)])
        for i, w in enumerate((w_gate, w_up))
    ]
    mine_pairs += [(gains, gl.at[mine]), (w_output, wo), (w_down, wd), (teacher, te)]

    def local(which):
        return [pltpu.make_async_copy(*mine_pairs[i], mine_sem.at[i]) for i in which]

    def attn_load():
        return pltpu.make_async_copy(w_attn, wa, load.at[0])

    def mlp_load():
        return pltpu.make_async_copy(w_mlp, wm, load.at[1])

    token_rows = GatherRows(n_fsdp, rep, mine, tokens, tok, (ts, tr, tl))
    up_rows = GatherRows(n_fsdp, rep, mine, nm, nmlp_all, (us, ur, ul))
    back_rows = GatherRows(n_fsdp, rep, mine, nm, gbranch_all, (bs, br, bl))

    for s in others:
        gain_copy(s).start()
        for i in range(4):
            weight_copy(s, i).start()
    for copy in local(range(10)):
        copy.start()
    for s in others:
        for i in range(4):
            weight_copy(s, i).wait_recv()
        partner_copy(s).start()
        sibling_copy(s, 0).start()
    for s in others:
        for i in range(2):
            mlp_copy(s, i).start()

    def block_rows(s):
        return pl.ds(pl.multiple_of(s * rows, rows), rows)

    def lengths_of(s):
        return block_lengths(lengths_ref, deal_ref, rep * n_fsdp + flipped(mine, s, n_fsdp))

    def angles(s, carry):
        head_len, both_len = lengths_of(s)
        index = lax.broadcasted_iota(jnp.int32, (rows, HD), 0)
        start = jnp.where(index < head_len, 0, jnp.where(index < both_len, head_len, both_len))
        angle = (index - start).astype(jnp.float32) * freq_ref[...]
        cs[block_rows(s)] = jnp.cos(angle)
        sn[block_rows(s)] = jnp.sin(angle)
        return carry

    lax.fori_loop(0, n_fsdp, angles, 0)
    angle_stores = [
        pltpu.make_async_copy(cs, all_cos, load.at[2]),
        pltpu.make_async_copy(sn, all_sin, load.at[3]),
    ]
    for copy in angle_stores:
        copy.start()
    token_count = jnp.sum(in_f32(lengths_row[...]), axis=1, keepdims=True)
    local((6,))[0].wait()
    gain_out[...] = jnp.zeros_like(gain_out)
    head_gain_out[...] = jnp.zeros_like(head_gain_out)
    for s in others:
        gain_copy(s).wait()
    lines = deep // HD
    for f in range(n_fsdp):
        piece = in_f32(gl[f])
        for kind in range(2):
            for r in range(lines):
                at = f * deep + r * HD
                gain_out[kind : kind + 1, at : at + HD] = piece[
                    kind * lines + r : kind * lines + r + 1
                ]
            head_gain_out[kind : kind + 1] += piece[2 * lines + kind : 2 * lines + kind + 1]
    for s in others:
        for i in range(2):
            mlp_copy(s, i).wait_recv()
        share_copy(s, 0, True).start()
    token_rows.start()
    for s in others:
        partner_copy(s).wait_recv()
        sibling_copy(s, 1).start()
    line_sends(1)
    for s in others:
        for k in range(2):
            sibling_copy(s, k).wait_recv()
    for copy in local((0, 1, 2, 3)):
        copy.wait()
    attn_load().start()
    for copy in local((7, 8, 9)):
        copy.wait()

    def some_rows(base, r):
        return pl.ds(pl.multiple_of(base + r * ROW_STEP, ROW_STEP), ROW_STEP)

    def tiled(count, wide, body):
        def one(j, carry):
            body(pl.ds(pl.multiple_of(j * wide, wide), wide))
            return carry

        lax.fori_loop(0, count, one, 0)

    def by_rows(body):
        def one(r, carry):
            body(r)
            return carry

        lax.fori_loop(0, row_steps, one, 0)

    tile = width // 4

    def leave(s, left, right):
        def one(cut):
            product = product_of(left[...], right[:, cut], 1, 0)

            @pl.when(s == 0)
            def _():
                own[:, cut] = product

            @pl.when(s > 0)
            def _():
                pbuf[s - 1, :, cut] = in_bf16(product)

        tiled(4, tile, one)


    relayed = n_fsdp == 4

    def half_rows(h):
        return pl.ds(h * (rows // 2), rows // 2)

    def out_copy(s, h, sends, recvs):
        to, at = s, s - 1
        if relayed and s == 3:
            to, at = h + 1, 2
        return remote_copy(
            pbuf.at[s - 1, half_rows(h)],
            land.at[at, half_rows(h)],
            sends.at[s, h],
            recvs.at[s, h],
            rep,
            flipped(mine, to, n_fsdp),
        )

    def send_block(s, sends, recvs):
        for k in others:

            @pl.when(s == k)
            def _(k=k):
                for h in range(2):
                    if not relayed or (k, h) not in ((1, 1), (2, 0)):
                        out_copy(k, h, sends, recvs).start()

    def relay(sends, recvs):
        if relayed:
            for h, near in ((0, 2), (1, 1)):
                out_copy(3, h, sends, recvs).wait_recv()
                cut = half_rows(h)
                pbuf[near - 1, cut] = in_bf16(in_f32(pbuf[near - 1, cut]) + in_f32(land[2, cut]))
                out_copy(near, h, sends, recvs).start()

    def arrived(sends, recvs):
        for s in others:
            for h in range(2):
                if not (relayed and s == 3):
                    out_copy(s, h, sends, recvs).wait_recv()
                out_copy(s, h, sends, recvs).wait_send()

    def summed(cut):
        total = own[cut]
        for s in range(1, 3 if relayed else n_fsdp):
            total += in_f32(land[s - 1, cut])
        return total

    def scaled(values, gain):
        scale = lax.rsqrt(jnp.mean(values * values, axis=-1, keepdims=True) + EPS_NORM)
        return in_bf16(values * scale * gain)


    def attention_stores(s):
        cut = block_rows(s)
        pairs = (
            (nb, normed_all), (raw, raw_all), (qb, q_all), (kvb, k_all), (vb, v_all), (gb, gated_all)
        )
        return [
            pltpu.make_async_copy(src, dst.at[cut], keep.at[i])
            for i, (src, dst) in enumerate(pairs)
        ]

    def attention(s, carry):
        pl.when(s == 1)(token_rows.forward)
        for k in range(n_fsdp):

            @pl.when(s == k)
            def _(k=k):
                if k == 0:
                    token_rows.own().wait()
                else:
                    token_rows.arrive(k)

        @pl.when(s > 0)
        def _():
            for copy in attention_stores(s):
                copy.wait()

        def normed_rows(r):
            values = in_f32(tok[some_rows(s * rows, r)])
            nb[some_rows(0, r)] = scaled(values, gain_out[0:1])

        by_rows(normed_rows)

        @pl.when(s == 0)
        def _():
            attn_load().wait()

        def raw_tile(cut):
            raw[:, cut] = product_of(nb[...], wa[:, cut], 1, 0)

        tiled(3, cols // 3, raw_tile)
        attend(
            heads_k,
            block_mask(lengths_of(s), rows),
            cs[block_rows(s)],
            sn[block_rows(s)],
            head_gain_out[0:1],
            head_gain_out[1:2],
            raw,
            qb,
            kvb,
            vb,
            gb,
        )
        for copy in attention_stores(s):
            copy.start()
        leave(s, gb, wo)

        send_block(s, ps, pr)
        if n_line > 2:
            pl.when(s == n_fsdp - 2)(lambda: line_arrivals(1))
        return carry

    lax.fori_loop(0, n_fsdp, attention, 0)
    for copy in angle_stores:
        copy.wait()
    relay(ps, pr)
    for k in range(2, n_line - 1):
        line_arrivals(k)
    arrived(ps, pr)

    def middle_rows(r):
        cut = some_rows(0, r)
        values = in_f32(tok[cut]) + summed(cut)
        mid[cut] = values
        nm[cut] = scaled(values, gain_out[1:2])

    by_rows(middle_rows)
    up_rows.start()

    def middle_store():
        return pltpu.make_async_copy(mid, middle_out, load.at[4])

    middle_store().start()
    for copy in attention_stores(0):
        copy.wait()


    line_arrivals(n_line - 1)
    shares(lambda copy: copy.wait_recv())
    for copy in local((4, 5)):
        copy.wait()
    mlp_load().start()
    mlp_load().wait()

    def block_load(source, s):
        return pltpu.make_async_copy(source.at[block_rows(s)], nb, load.at[2])

    def ff_stores(s):
        cut = block_rows(s)
        return [
            pltpu.make_async_copy(hb, hidden_all.at[cut], keep.at[0]),
            pltpu.make_async_copy(gu, gu_all.at[cut], keep.at[1]),
        ]

    def into_nb(gather, source, s):
        @pl.when(s == 0)
        def _():
            nb[...] = nm[...]

        for k in others:

            @pl.when(s == k)
            def _(k=k):
                gather.arrive(k)

        @pl.when(s > 0)
        def _():
            copy = block_load(source, s)
            copy.start()
            copy.wait()

    def feed_forward(i, carry):
        s = (i + 1) % n_fsdp
        pl.when(i == 0)(up_rows.forward)
        into_nb(up_rows, nmlp_all, s)

        @pl.when(i > 0)
        def _():
            for copy in ff_stores(s):
                copy.wait()

        def pre_tile(cut):
            gu[:, cut] = product_of(nb[...], wm[:, cut], 1, 0)

        tiled(6, ff // 3, pre_tile)

        def hidden_rows(r):
            cut = some_rows(0, r)
            gate_pre = gu[cut, :ff]
            hb[cut] = in_bf16(gate_pre * jax.nn.sigmoid(gate_pre) * gu[cut, ff:])

        by_rows(hidden_rows)
        for copy in ff_stores(s):
            copy.start()
        leave(s, hb, wd)

        send_block(s, qs, qr)
        return carry

    lax.fori_loop(0, n_fsdp, feed_forward, 0)
    relay(qs, qr)
    up_rows.sent()
    up_rows.own().wait()
    middle_store().wait()
    for copy in ff_stores(0):
        copy.wait()


    def gu_load(s):
        return pltpu.make_async_copy(gu_all.at[block_rows(s)], gu, load.at[5])

    gu_load(0).start()
    arrived(qs, qr)
    head_len, both_len = lengths_of(0)
    factor = (n_rep * rows_all) / token_count
    loss_out[...] = jnp.zeros_like(loss_out)

    def error_rows(r):
        cut = some_rows(0, r)
        index = r * ROW_STEP + lax.broadcasted_iota(jnp.int32, (ROW_STEP, 1), 0)
        valid = (index < both_len).astype(jnp.float32)
        result = mid[cut] + summed(cut)
        error = (result - in_f32(te[cut])) * valid
        square = jnp.sum(error * error, axis=-1, keepdims=True)
        first = jnp.where(index < head_len, square, 0.0)
        loss_out[0:1] += jnp.sum(first, axis=0, keepdims=True)
        loss_out[1:2] += jnp.sum(square - first, axis=0, keepdims=True)
        te[cut] = in_bf16(result * valid)
        grad = error * factor
        mid[cut] = grad
        nm[cut] = in_bf16(grad)

    by_rows(error_rows)
    loss_out[...] = loss_out[...] / (2.0 * token_count)
    back_rows.start()
    last_stores = [
        pltpu.make_async_copy(te, block_out, load.at[3]),
        pltpu.make_async_copy(mid, gres_out, load.at[4]),
    ]
    for copy in last_stores:
        copy.start()

    def grad_store(s):
        return pltpu.make_async_copy(gm, gmlp_all.at[block_rows(s)], keep.at[2])

    def feed_back(s, carry):
        pl.when(s == 1)(back_rows.forward)
        into_nb(back_rows, gbranch_all, s)

        def hidden_tile(cut):
            raw[:, cut] = product_of(nb[...], wd[cut], 1, 1)

        tiled(3, ff // 3, hidden_tile)
        gu_load(s).wait()

        @pl.when(s > 0)
        def _():
            grad_store(s).wait()

        def grad_rows(r):
            cut = some_rows(0, r)
            gate_pre, grad = gu[cut, :ff], raw[cut]
            gate = jax.nn.sigmoid(gate_pre)
            silu = gate_pre * gate
            gm[cut, :ff] = in_bf16(grad * gu[cut, ff:] * (gate + silu * (1.0 - gate)))
            gm[cut, ff:] = in_bf16(grad * silu)

        by_rows(grad_rows)
        grad_store(s).start()

        @pl.when(s + 1 < n_fsdp)
        def _():
            gu_load(s + 1).start()

        return carry

    lax.fori_loop(0, n_fsdp, feed_back, 0)

    grad_store(0).wait()
    for copy in last_stores:
        copy.wait()
    back_rows.sent()
    back_rows.own().wait()
    token_rows.sent()
    for s in others:
        partner_copy(s).wait_send()
        for i in range(4):
            weight_copy(s, i).wait_send()
        for i in range(2):
            sibling_copy(s, i).wait_send()
            mlp_copy(s, i).wait_send()
    lines_sent()
    shares(lambda copy: copy.wait_send())


def forward(n_fsdp, n_rep, heads_k, args):
    rows, width = args[0].shape
    rows_all = n_fsdp * rows
    cols_q, cols_k = heads_k * (H // KV) * HD, heads_k * HD
    cols = 2 * cols_q + 2 * cols_k
    ff = args[9].shape[0]
    n_line = n_rep // 2
    low, full = jnp.bfloat16, jnp.float32
    dma = pltpu.SemaphoreType.DMA
    any_spec = pl.BlockSpec(memory_space=pl.ANY)
    vmem, smem = pl.BlockSpec(memory_space=pltpu.VMEM), pl.BlockSpec(memory_space=pltpu.SMEM)
    outs = (
        ((rows_all, width), low),
        ((rows_all, cols), full),
        ((rows_all, cols_q), low),
        ((rows_all, cols_k), low),
        ((rows_all, cols_k), low),
        ((rows_all, cols_q), low),
        ((width, cols), low),
        ((width, 2 * ff), low),
        ((rows, width), full),
        ((rows_all, width), low),
        ((rows_all, ff), low),
        ((rows_all, width), low),
        ((rows_all, 2 * ff), low),
        ((rows, width), full),
        ((rows, width), low),
        ((rows_all, 2 * ff), full),
        ((rows_all, HD), full),
        ((rows_all, HD), full),
        ((8, width), full),
        ((8, HD), full),
        ((8, HD), full),
    )
    scratch = (
        ((rows_all, width), low),
        ((n_fsdp, 16, HD), low),
        ((width, cols), low),
        ((cols_q, width), low),
        ((ff, width), low),
        ((width, 2 * ff), low),
        ((rows, width), low),
        ((rows, cols), full),
        ((rows_all, HD), full),
        ((rows_all, HD), full),
        ((rows, cols_q), low),
        ((rows, cols_k), low),
        ((rows, cols_k), low),
        ((rows, cols_q), low),
        ((rows, width), full),
        ((n_fsdp - 1, rows, width), low),
        ((n_fsdp - 1, rows, width), low),
        ((rows, width), full),
        ((rows, width), low),
        ((rows, width), low),
        ((rows, 2 * ff), full),
        ((rows, ff), low),
        ((rows, 2 * ff), low),
    )
    one, pair, four = dma((n_fsdp,)), dma((n_fsdp, 2)), dma((n_fsdp, 4))
    line = dma((2, n_fsdp, n_line))
    return pl.pallas_call(
        functools.partial(forward_kernel, n_fsdp, n_rep, heads_k),
        out_shape=[jax.ShapeDtypeStruct(shape, kind) for shape, kind in outs],
        in_specs=[any_spec] * 11 + [smem] * 2 + [vmem] * 2,
        out_specs=[any_spec] * 18 + [vmem] * 3,
        scratch_shapes=[pltpu.VMEM(shape, kind) for shape, kind in scratch]
        + [pair, pair, dma] * 3
        + [one, one, four, four, one, one, pair, pair]
        + [pair, pair, line, line, line, line, pair, pair, pair, pair]
        + [dma((6,)), dma((6,)), dma((10,))],
        compiler_params=pltpu.CompilerParams(
            collective_id=1, has_side_effects=True, vmem_limit_bytes=62 << 20
        ),
        name="forward",
    )(*args)


def shards(
    tokens,
    teacher,
    lengths,
    deal_order,
    attention_gain,
    query_gain,
    key_gain,
    w_query,
    w_key,
    w_value,
    w_outgate,
    w_output,
    mlp_gain,
    w_gate,
    w_up,
    w_down,
):
    n_rep = lax.axis_size("rep")
    n_fsdp = lax.axis_size("fsdp")
    rows, width = tokens.shape
    mine = lax.axis_index("fsdp")
    core = lax.axis_index("rep") % 2
    others = range(1, n_fsdp)
    heads_q, heads_k = H // n_fsdp, KV // n_fsdp
    cols_q, cols_k = heads_q * HD, heads_k * HD
    deep = w_query.shape[0]
    ff = w_down.shape[0]
    rows_all = rows * n_fsdp

    freq = np.power(np.float32(ROPE_BASE), -np.arange(0, HD, 2, dtype=np.float32) / HD)
    freq = jnp.asarray(np.concatenate([freq, freq])[None])
    small = query_gain.shape[0]

    def spread(gain):
        lane = jnp.arange(HD, dtype=jnp.int32)
        return jnp.where(lane // small == mine, jnp.tile(gain, n_fsdp), 0)[None]

    gain_block = jnp.concatenate(
        [
            attention_gain.reshape(-1, HD),
            mlp_gain.reshape(-1, HD),
            spread(query_gain),
            spread(key_gain),
            jnp.zeros((14 - 2 * deep // HD, HD), jnp.bfloat16),
        ]
    )
    (
        normed_all,
        attn_raw,
        queries_b,
        keys_b,
        values_b,
        gated_b,
        w_attn,
        w_mlp,
        middle,
        normed_mlp_all,
        hidden_b,
        grad_branch_all,
        grad_mlp_b,
        grad_result,
        block_out,
        _,
        angle_cos,
        angle_sin,
        gain_rows,
        head_gains,
        losses,
    ) = forward(
        n_fsdp,
        n_rep,
        heads_k,
        (
            tokens,
            gain_block,
            w_query,
            w_outgate,
            w_key,
            w_value,
            w_gate,
            w_up,
            w_output,
            w_down,
            teacher,
            lengths,
            deal_order,
            lengths[None],
            freq,
        ),
    )
    seq_loss = losses[:2, 0]
    piece_rows, piece_cols = deep // 2, width // n_fsdp
    units, base = [], 0
    for by_owner, row_blocks, cols in (
        (False, ff // 2 // piece_rows, width),
        (True, n_fsdp, 2 * ff),
        (False, cols_q // 2 // piece_rows, width),
        (True, n_fsdp, 2 * cols_q + 2 * cols_k),
    ):
        units.append(Unit(base, by_owner, row_blocks, cols // piece_cols))
        base += units[-1].count
    pieces, _, _, _, _, tokens_grad, gain_sums = backward(
        n_fsdp,
        n_rep,
        heads_k,
        units,
        piece_rows,
        piece_cols,
        (
            hidden_b,
            normed_mlp_all,
            gated_b,
            normed_all,
            grad_branch_all,
            grad_mlp_b,
            w_mlp,
            w_output,
            w_attn,
            middle,
            grad_result,
            tokens,
            attn_raw,
            angle_cos,
            angle_sin,
            queries_b,
            keys_b,
            values_b,
            gain_rows,
            head_gains,
            lengths,
            deal_order,
        ),
    )
    down, mlp, outp, attn = units

    def by_rows(unit, weight):
        blocks, together = unit.row_blocks, unit.col_blocks
        return widened(
            pieces,
            (2, blocks),
            together,
            lambda c, r: (unit.base // together + r, c, 0, 0),
            weight.shape,
            lambda c, r: (c * blocks + r, 0),
        )

    dw_down = by_rows(down, w_down)
    dw_output = by_rows(outp, w_output)
    dw_gate, dw_up = widened_both(pieces, mlp.base, mlp.col_blocks, n_fsdp, w_gate.shape)
    dw_query, dw_outgate, dw_key, dw_value = widened_heads(
        pieces,
        attn.base,
        n_fsdp,
        (w_query.shape, w_outgate.shape, w_key.shape, w_value.shape),
    )

    def own_part(row, start, cols):
        return lax.dynamic_slice(gain_sums, (row, start + mine * cols), (1, cols))[0]

    return (
        block_out,
        seq_loss,
        tokens_grad,
        own_part(0, 0, deep),
        own_part(0, width, small),
        own_part(1, width, small),
        dw_query,
        dw_key,
        dw_value,
        dw_outgate,
        dw_output,
        own_part(1, 0, deep),
        dw_gate,
        dw_up,
        dw_down,
    )


def solution(mesh):
    return jax.shard_map(
        shards,
        mesh=mesh,
        in_specs=(
            P(("rep", "fsdp"), None),
            P(("rep", "fsdp"), None),
            P(),
            P(),
            P("fsdp"),
            P("fsdp"),
            P("fsdp"),
            P("fsdp", None),
            P("fsdp", None),
            P("fsdp", None),
            P("fsdp", None),
            P("fsdp", None),
            P("fsdp"),
            P("fsdp", None),
            P("fsdp", None),
            P("fsdp", None),
        ),
        out_specs=(
            P(("rep", "fsdp"), None),
            P(("rep", "fsdp")),
            P(("rep", "fsdp"), None),
            P("fsdp"),
            P("fsdp"),
            P("fsdp"),
            P("fsdp", None),
            P("fsdp", None),
            P("fsdp", None),
            P("fsdp", None),
            P("fsdp", None),
            P("fsdp"),
            P("fsdp", None),
            P("fsdp", None),
            P("fsdp", None),
        ),
        check_vma=False,
    )
```
